32 devices in a mesh: dp: 8 (over z, x), bn: 4 (over y, core).
Axes of the slice: x: 2, y: 2, z: 4, core: 2. Of those that a mesh axis runs over, the one named last changes fastest.
Arguments:
- features: bfloat16 [128, 19, 19, 1024], P(('dp', 'bn')), may hold values from -8 to 8
- image_counts: int32 [32], P(('dp', 'bn')), may hold values from 2 to 4, as said below
- map_sides: int32 [128], P(('dp', 'bn')), may hold values from 13 to 19, as said below
- split_kernel: bfloat16 [1024, 1024], replicated, may hold values from -0.1875 to 0.1875
- split_gain: float32 [1024], replicated, may hold values from 0.5 to 1.5
- split_shift: float32 [1024], replicated, may hold values from -2 to 2
- inner_kernel: bfloat16 [512, 512], replicated, may hold values from -0.25 to 0.25
- inner_gain: float32 [512], replicated, may hold values from 0.5 to 1.5
- inner_shift: float32 [512], replicated, may hold values from -2 to 2
- spread_kernel: bfloat16 [3, 3, 512, 512], replicated, may hold values from -0.09375 to 0.09375
- spread_gain: float32 [512], replicated, may hold values from 0.5 to 1.5
- spread_shift: float32 [512], replicated, may hold values from -2 to 2
- transition_kernel: bfloat16 [512, 512], replicated, may hold values from -0.25 to 0.25
- transition_gain: float32 [512], replicated, may hold values from 0.5 to 1.5
- transition_shift: float32 [512], replicated, may hold values from -2 to 2
- output_kernel: bfloat16 [1024, 1024], replicated, may hold values from -0.1875 to 0.1875
- output_gain: float32 [1024], replicated, may hold values from 0.5 to 1.5
- output_shift: float32 [1024], replicated, may hold values from -2 to 2
- cotangent: float32 [128, 19, 19, 1024], P(('dp', 'bn')), may hold values from -6 to 6
Outputs:
- result_map: float32 [128, 19, 19, 1024], P(('dp', 'bn'))
- grad_features: float32 [128, 19, 19, 1024], P(('dp', 'bn'))
- grad_split_kernel: float32 [1024, 1024], replicated
- grad_split_gain: float32 [1024], replicated
- grad_split_shift: float32 [1024], replicated
- grad_inner_kernel: float32 [512, 512], replicated
- grad_inner_gain: float32 [512], replicated
- grad_inner_shift: float32 [512], replicated
- grad_spread_kernel: float32 [3, 3, 512, 512], replicated
- grad_spread_gain: float32 [512], replicated
- grad_spread_shift: float32 [512], replicated
- grad_transition_kernel: float32 [512, 512], replicated
- grad_transition_gain: float32 [512], replicated
- grad_transition_shift: float32 [512], replicated
- grad_output_kernel: float32 [1024, 1024], replicated
- grad_output_gain: float32 [1024], replicated
- grad_output_shift: float32 [1024], replicated
The draws below stay inside these ranges and needn't reach their ends.
Inputs may be any that keep to these rules, and one draw needn't show every extreme that they name: `image_counts`: each device has at least 2 live slots; some device has all 4. `map_sides`: each slot's side is 19, 16 or 13; sides of slots that are not live are to be ignored.
All inputs are finite; a program needn't handle non-finite values.
Results may differ from the reference program's by a relative error of at most 0.0003.
Values sent between devices are 32-bit elements; how exact they have to be, the bound alone decides.
A program may use at most 192 MiB of HBM per device.

```python
import jax
import jax.numpy as jnp
from jax import lax

C_OUT = 1024
C_HALF = 512
SLOTS = 4
MAP = 19
HOLDERS = 32
BN_GROUP = 4
IMAGES = 128
N_DP = 8
N_BN = 4


def draw_image_counts(key, part):
    lowest = max(SLOTS // 2, 1)
    values = jax.random.randint(key, (HOLDERS,), lowest, SLOTS + 1)
    return jnp.where(jnp.arange(HOLDERS) == 0, SLOTS, values).astype(jnp.int32)


def draw_map_sides(key, part):
    steps = jax.random.randint(key, (IMAGES,), 0, 3)
    sides = MAP - 3 * steps
    return jnp.where(jnp.arange(IMAGES) == 0, MAP, sides).astype(jnp.int32)


def draw_features(key, part):
    first, second = jax.random.split(key, 2)
    image = jnp.arange(IMAGES)
    member = (image // SLOTS % BN_GROUP).astype(jnp.float32) / max(BN_GROUP - 1, 1)
    scale = 0.5 + member
    offset = jax.random.uniform(second, (C_OUT,), jnp.float32, -0.5, 0.5)
    noise = jax.random.normal(first, (IMAGES, MAP, MAP, C_OUT), jnp.float32)
    return jnp.clip((noise + offset) * scale[:, None, None, None], -8.0, 8.0).astype(jnp.bfloat16)


def steps_of(stream_key, shape, cuts, smallest, largest):
    level, own = 1.0, jax.random.fold_in(stream_key, 6)
    for dim, blocks in cuts:
        heights = jnp.exp(jax.random.uniform(jax.random.fold_in(own, dim), (blocks,), jnp.float32, smallest / len(cuts), largest / len(cuts)))
        level = level * jnp.repeat(heights, shape[dim] // blocks).reshape([-1 if axis == dim else 1 for axis in range(len(shape))])
    return level


def gaussian(own_key, extent, deviation, limit, cuts=(), held_as=jnp.bfloat16):
    loudness = steps_of(own_key, extent, cuts, -0.22, 0.18) if cuts else 1.0
    array = jax.random.normal(own_key, extent, jnp.float32) * deviation * loudness
    return jnp.minimum(jnp.maximum(array, -limit), limit).astype(held_as)


def setup_inputs(seed: int = 0) -> dict:
    key_list = jax.random.split(jax.random.key(seed), 20)
    return {
        "features": draw_features(jax.random.fold_in(key_list[19], 71), 0),
        "image_counts": draw_image_counts(jax.random.fold_in(key_list[19], 71), 0),
        "map_sides": draw_map_sides(jax.random.fold_in(key_list[19], 71), 0),
        "split_kernel": gaussian(key_list[3], (C_OUT, 2 * C_HALF), C_OUT ** -0.5, 0.1875),
        "split_gain": jnp.clip(1.0 + 0.1 * jax.random.normal(key_list[4], (2 * C_HALF,), jnp.float32), 0.5, 1.5),
        "split_shift": gaussian(key_list[5], (2 * C_HALF,), 0.5, 2.0, (), jnp.float32),
        "inner_kernel": gaussian(key_list[6], (C_HALF, C_HALF), C_HALF ** -0.5, 0.25),
        "inner_gain": jnp.clip(1.0 + 0.1 * jax.random.normal(key_list[7], (C_HALF,), jnp.float32), 0.5, 1.5),
        "inner_shift": gaussian(key_list[8], (C_HALF,), 0.5, 2.0, (), jnp.float32),
        "spread_kernel": gaussian(key_list[9], (3, 3, C_HALF, C_HALF), (9 * C_HALF) ** -0.5, 0.09375),
        "spread_gain": jnp.clip(1.0 + 0.1 * jax.random.normal(key_list[10], (C_HALF,), jnp.float32), 0.5, 1.5),
        "spread_shift": gaussian(key_list[11], (C_HALF,), 0.5, 2.0, (), jnp.float32),
        "transition_kernel": gaussian(key_list[12], (C_HALF, C_HALF), C_HALF ** -0.5, 0.25),
        "transition_gain": jnp.clip(1.0 + 0.1 * jax.random.normal(key_list[13], (C_HALF,), jnp.float32), 0.5, 1.5),
        "transition_shift": gaussian(key_list[14], (C_HALF,), 0.5, 2.0, (), jnp.float32),
        "output_kernel": gaussian(key_list[15], (C_OUT, C_OUT), C_OUT ** -0.5, 0.1875),
        "output_gain": jnp.clip(1.0 + 0.1 * jax.random.normal(key_list[16], (C_OUT,), jnp.float32), 0.5, 1.5),
        "output_shift": gaussian(key_list[17], (C_OUT,), 0.5, 2.0, (), jnp.float32),
        "cotangent": gaussian(key_list[18], (IMAGES, MAP, MAP, C_OUT), 1.0, 6.0, ((0, 32),), jnp.float32),
    }


epsilon = 1e-05

def mish(value):
    return value * jnp.tanh(jax.nn.softplus(value))

def convolve(inputs, kernel):
    return lax.conv_general_dilated(inputs, kernel, (1, 1), ((1, 1), (1, 1)), dimension_numbers=('NHWC', 'HWIO', 'NHWC'), precision=lax.Precision.HIGHEST)

def pointwise(inputs, kernel):
    return jnp.einsum('nhwc,cd->nhwd', inputs, kernel, precision=lax.Precision.HIGHEST)

def masks(count_list, side_list):
    image = jnp.arange(side_list.shape[0])
    live = image % SLOTS < count_list[image // SLOTS]
    places = jnp.arange(MAP)
    inside = places[None, :] < side_list[:, None]
    keep = live[:, None, None] & inside[:, :, None] & inside[:, None, :]
    return keep.astype(jnp.float32)[..., None]

def normalize(z, gain, shift, mask, total):
    mean = lax.optimization_barrier(jnp.sum(z * mask, axis=(0, 1, 2))) / total
    square = lax.optimization_barrier(jnp.sum(z * z * mask, axis=(0, 1, 2))) / total
    scaled = (z - mean) * lax.rsqrt(square - mean * mean + epsilon)
    return mish(gain * scaled + shift) * mask

def group_forward(params, image, count_list, side_list):
    split_kernel, split_gain, split_shift, inner_kernel, inner_gain, inner_shift, spread_kernel, spread_gain, spread_shift, transition_kernel, transition_gain, transition_shift, output_kernel, output_gain, output_shift = params
    mask = masks(count_list, side_list)
    total = jnp.sum(mask)
    split = normalize(pointwise(image * mask, split_kernel), split_gain, split_shift, mask, total)
    part = split[..., :C_HALF]
    main = split[..., C_HALF:]
    inner = normalize(pointwise(main, inner_kernel), inner_gain, inner_shift, mask, total)
    joined = main + normalize(convolve(inner, spread_kernel), spread_gain, spread_shift, mask, total)
    trans = normalize(pointwise(joined, transition_kernel), transition_gain, transition_shift, mask, total)
    stacked = jnp.concatenate([trans, part], axis=-1)
    return normalize(pointwise(stacked, output_kernel), output_gain, output_shift, mask, total)

def reference(features, image_counts, map_sides, split_kernel, split_gain, split_shift, inner_kernel, inner_gain, inner_shift, spread_kernel, spread_gain, spread_shift, transition_kernel, transition_gain, transition_shift, output_kernel, output_gain, output_shift, cotangent):
    params = tuple((item.astype(jnp.float32) for item in (split_kernel, split_gain, split_shift, inner_kernel, inner_gain, inner_shift, spread_kernel, spread_gain, spread_shift, transition_kernel, transition_gain, transition_shift, output_kernel, output_gain, output_shift)))
    group = N_BN * SLOTS
    feature_groups = features.astype(jnp.float32).reshape(N_DP, group, MAP, MAP, C_OUT)
    cot_groups = cotangent.reshape(N_DP, group, MAP, MAP, C_OUT)
    count_groups = image_counts.reshape(N_DP, N_BN)
    side_groups = map_sides.reshape(N_DP, group)

    def advance(running, pieces):
        image_part, count_part, side_part, cot_part = pieces

        def forward(weights, image):
            return group_forward(weights, image, count_part, side_part)
        result, pull = jax.vjp(forward, params, image_part)
        grad_params, grad_image = pull(cot_part)
        running = jax.tree.map(lambda left, right: left + right, running, grad_params)
        return (running, (result, grad_image))
    zeros = jax.tree.map(jnp.zeros_like, params)
    grads, (result, grad_image) = lax.scan(advance, zeros, (feature_groups, count_groups, side_groups, cot_groups))
    return (result.reshape(IMAGES, MAP, MAP, C_OUT), grad_image.reshape(IMAGES, MAP, MAP, C_OUT), grads[0], grads[1], grads[2], grads[3], grads[4], grads[5], grads[6], grads[7], grads[8], grads[9], grads[10], grads[11], grads[12], grads[13], grads[14])
```

```python
import functools

import jax
import jax.numpy as jnp
from jax import lax
from jax.experimental import pallas as pl
from jax.experimental.pallas import tpu as pltpu
from jax.sharding import PartitionSpec as P

EPS = 1e-05
GUARD = 24
CHUNK = 16
F32 = jnp.float32
BF16 = jnp.bfloat16


def round_up(value, step):
    return -(-value // step) * step


def params(megabytes=56):
    return pltpu.CompilerParams(vmem_limit_bytes=megabytes * 1024 * 1024)


def whole(array):
    zeros = (0,) * len(array.shape)
    return pl.BlockSpec(array.shape, lambda *_: zeros, pipeline_mode=pl.Buffered(1))


def out_whole(shape):
    zeros = (0,) * len(shape)
    return pl.BlockSpec(shape, lambda *_: zeros)


def rows(pitch, width, column=0):
    return pl.BlockSpec((pitch, width), lambda i: (i, column))


def rows2(pitch, width):
    return pl.BlockSpec((2, pitch, width), lambda i: (0, i, 0))


def image(shape):
    return pl.BlockSpec((1,) + tuple(shape[1:]), lambda i: (i, 0, 0, 0))


def sds(shape, dtype=F32):
    return jax.ShapeDtypeStruct(tuple(shape), dtype)


def dot(left, right):
    return jnp.dot(left, right, preferred_element_type=F32)


def dot_t(left, right):
    return lax.dot_general(left, right, (((1,), (1,)), ((), ())), preferred_element_type=F32)


def split_store(ref, place, value):
    high = value.astype(BF16)
    ref[(0,) + place] = high
    ref[(1,) + place] = (value - high.astype(F32)).astype(BF16)


def moments(stats_ref, total, columns):
    mean = stats_ref[0:1, columns] / total
    square = stats_ref[1:2, columns] / total
    return mean, lax.rsqrt(square - mean * mean + EPS)


def mish(y):
    t = jnp.exp(jnp.minimum(y, 30.0))
    n = t * (t + 2.0)
    return y * (n / (n + 2.0))


def mish_slope(y):
    t = jnp.exp(jnp.minimum(y, 30.0))
    n = t * (t + 2.0)
    r = 1.0 / (n + 2.0)
    return n * r + y * (((4.0 * t) * (t + 1.0) * r) * r)


def fold(value):
    return jnp.sum(value.reshape(value.shape[0] // 8, 8, value.shape[1]), axis=0)


def over_rows(count, body, carry=None, unroll=2):
    def step(k, c):
        return body(pl.ds(pl.multiple_of(k * CHUNK, CHUNK), CHUNK), c)

    return lax.fori_loop(0, count // CHUNK, step, carry, unroll=unroll)


def column_blocks(width, block=512):
    return [slice(c, c + block) for c in range(0, width, block)]


def add_sums(sums_ref, columns, pieces):
    for k, piece in enumerate(pieces):
        sums_ref[k : k + 1, columns] += jnp.sum(piece, axis=0, keepdims=True)


def start_sums(sums_ref):
    @pl.when(pl.program_id(0) == 0)
    def _():
        sums_ref[...] = jnp.zeros_like(sums_ref)


def sum_squares(z_ref, sums_ref, mask_ref=None):
    for columns in column_blocks(z_ref.shape[1]):
        width = columns.stop - columns.start

        def body(r, carry):
            value = z_ref[r, columns]
            kept = value if mask_ref is None else value * mask_ref[r, 0:1]
            return (carry[0] + fold(kept), carry[1] + fold(kept * value))

        zero = jnp.zeros((8, width), F32)
        add_sums(sums_ref, columns, over_rows(z_ref.shape[0], body, (zero, zero)))


def product2(ref, place, weight):
    high = ref[(0,) + place]
    low = ref[(1,) + place]
    return dot(high, weight) + dot(low, weight)


def product2_t(ref, place, weight):
    high = ref[(0,) + place]
    low = ref[(1,) + place]
    return dot_t(high, weight) + dot_t(low, weight)


def compact(source_ref, scratch_ref):
    side = source_ref.shape[1]
    for y in range(side):
        scratch_ref[y * side : (y + 1) * side, :] = source_ref[0, y].astype(F32)
    scratch_ref[side * side :, :] = jnp.zeros((scratch_ref.shape[0] - side * side, scratch_ref.shape[1]), F32)


def spread_out(scratch_ref, target_ref):
    side = target_ref.shape[1]
    for y in range(side):
        target_ref[0, y] = scratch_ref[y * side : (y + 1) * side, :]


def split_kernel_body(features_ref, mask_ref, w_ref, x_ref, z_ref, sums_ref, scratch_ref):
    compact(features_ref, scratch_ref)

    def body(r, _):
        x_ref[r, :] = (scratch_ref[r, :] * mask_ref[r, 0:1]).astype(BF16)

    over_rows(x_ref.shape[0], body)
    z_ref[...] = dot(x_ref[...], w_ref[...])
    start_sums(sums_ref)
    sum_squares(z_ref, sums_ref)
    count = jnp.sum(mask_ref[...], axis=0, keepdims=True)
    sums_ref[2:3, 0:128] += count


def inner_body(z_ref, stats_ref, gain_ref, shift_ref, mask_ref, w_ref, part_ref, main_ref, main2_ref, zi_ref, sums_ref):
    total = stats_ref[2:3, 0:1]
    half = w_ref.shape[0]
    for index, columns in enumerate(column_blocks(2 * half, half)):
        mean, inverse = moments(stats_ref, total, columns)
        scale, shift = gain_ref[0:1, columns] * inverse, shift_ref[0:1, columns]

        def body(r, _):
            act = mish((z_ref[r, columns] - mean) * scale + shift) * mask_ref[r, 0:1]
            if index == 0:
                split_store(part_ref, (r,), act)
            else:
                main_ref[r, :] = act
                split_store(main2_ref, (r,), act)

        over_rows(z_ref.shape[0], body)
    zi_ref[...] = product2(main2_ref, (), w_ref[...])
    start_sums(sums_ref)
    sum_squares(zi_ref, sums_ref)


def taps(side):
    return [(dy * side + dx, dx) for dy in (-1, 0, 1) for dx in (-1, 0, 1)]


def spread_body(side, z_ref, total_ref, stats_ref, gain_ref, shift_ref, mask_ref, edge_ref, w_ref, inner_ref, zs_ref, sums_ref, padded_ref, pair_ref):
    total = total_ref[2:3, 0:1]
    pitch = z_ref.shape[0]
    columns = slice(None)
    mean, inverse = moments(stats_ref, total, columns)
    scale, shift = gain_ref[...] * inverse, shift_ref[...]
    padded_ref[0:GUARD, :] = jnp.zeros((GUARD, padded_ref.shape[1]), F32)
    padded_ref[GUARD + pitch :, :] = jnp.zeros((GUARD, padded_ref.shape[1]), F32)

    def body(r, _):
        act = mish((z_ref[r, :] - mean) * scale + shift) * mask_ref[r, 0:1]
        padded_ref[pl.ds(r.start + GUARD, CHUNK), :] = act
        split_store(inner_ref, (r,), act)

    over_rows(pitch, body)
    for tap, (move, dx) in enumerate(taps(side)):
        if move == 0:
            part = product2(inner_ref, (), w_ref[tap])
        else:
            moved = padded_ref[GUARD + move : GUARD + move + pitch, :]
            if dx:
                moved = moved * edge_ref[:, dx + 1 : dx + 2]
            split_store(pair_ref, (slice(None),), moved)
            part = product2(pair_ref, (), w_ref[tap])
        if tap == 0:
            zs_ref[...] = part
        else:
            zs_ref[...] += part
    start_sums(sums_ref)
    sum_squares(zs_ref, sums_ref, mask_ref)


def transition_body(z_ref, total_ref, stats_ref, gain_ref, shift_ref, mask_ref, main_ref, w_ref, joined_ref, zt_ref, sums_ref):
    total = total_ref[2:3, 0:1]
    mean, inverse = moments(stats_ref, total, slice(None))
    scale, shift = gain_ref[...] * inverse, shift_ref[...]

    def body(r, _):
        act = mish((z_ref[r, :] - mean) * scale + shift) * mask_ref[r, 0:1]
        split_store(joined_ref, (r,), act + main_ref[r, :])

    over_rows(z_ref.shape[0], body)
    zt_ref[...] = product2(joined_ref, (), w_ref[...])
    start_sums(sums_ref)
    sum_squares(zt_ref, sums_ref)


def output_body(z_ref, total_ref, stats_ref, gain_ref, shift_ref, mask_ref, part_ref, w_ref, trans_ref, zo_ref, sums_ref):
    total = total_ref[2:3, 0:1]
    mean, inverse = moments(stats_ref, total, slice(None))
    scale, shift = gain_ref[...] * inverse, shift_ref[...]
    half = z_ref.shape[1]

    def body(r, _):
        act = mish((z_ref[r, :] - mean) * scale + shift) * mask_ref[r, 0:1]
        split_store(trans_ref, (r,), act)

    over_rows(z_ref.shape[0], body)
    zo_ref[...] = product2(part_ref, (), w_ref[half:, :])
    zo_ref[...] += product2(trans_ref, (), w_ref[:half, :])
    start_sums(sums_ref)
    sum_squares(zo_ref, sums_ref)


def result_body(z_ref, total_ref, stats_ref, gain_ref, shift_ref, mask_ref, cotangent_ref, result_ref, dy_ref, sums_ref, scratch_ref):
    total = total_ref[2:3, 0:1]
    compact(cotangent_ref, scratch_ref)
    start_sums(sums_ref)
    for columns in column_blocks(z_ref.shape[1]):
        mean, inverse = moments(stats_ref, total, columns)
        gain, shift = gain_ref[0:1, columns], shift_ref[0:1, columns]

        def body(r, carry):
            mask = mask_ref[r, 0:1]
            scaled = (z_ref[r, columns] - mean) * inverse
            y = scaled * gain + shift
            t = jnp.exp(jnp.minimum(y, 30.0))
            n = t * (t + 2.0)
            inv = 1.0 / (n + 2.0)
            ratio = n * inv
            slope = ratio + y * (((4.0 * t) * (t + 1.0) * inv) * inv)
            dy = scratch_ref[r, columns] * mask * slope
            scratch_ref[r, columns] = y * ratio * mask
            dy_ref[r, columns] = dy
            return (carry[0] + fold(dy), carry[1] + fold(dy * scaled))

        zero = jnp.zeros((8, columns.stop - columns.start), F32)
        add_sums(sums_ref, columns, over_rows(z_ref.shape[0], body, (zero, zero)))
    spread_out(scratch_ref, result_ref)


def norm_slope(z_ref, grad, mask_ref, r, columns, mean, inverse, gain, shift):
    scaled = (z_ref[r, columns] - mean) * inverse
    dy = grad * mask_ref[r, 0:1] * mish_slope(scaled * gain + shift)
    return dy, (fold(dy), fold(dy * scaled))


def settle(dy, z, mask, mean, inverse, factor, first, second):
    scaled = (z - mean) * inverse
    return mask * factor * (dy - (first + scaled * second))


def output_back_body(dy_ref, zo_ref, so_ref, go_ref, qo_ref, total_ref, mask_ref, w_ref, zt_ref, st_ref, gt_ref, bt_ref, zp_ref, gp_ref, bp_ref, dz_ref, dyt_ref, dyp_ref, sums_ref, grad_ref):
    total = total_ref[2:3, 0:1]
    for columns in column_blocks(zo_ref.shape[1]):
        mean, inverse = moments(so_ref, total, columns)
        factor = go_ref[0:1, columns] * inverse
        first, second = qo_ref[0:1, columns] / total, qo_ref[1:2, columns] / total

        def body(r, _):
            dz = settle(dy_ref[r, columns], zo_ref[r, columns], mask_ref[r, 0:1], mean, inverse, factor, first, second)
            split_store(dz_ref, (r, columns), dz)

        over_rows(zo_ref.shape[0], body)
    grad_ref[...] = product2_t(dz_ref, (), w_ref[...])
    start_sums(sums_ref)
    half = zt_ref.shape[1]
    for index, (z_ref, s_ref, g_ref, b_ref, out_ref) in enumerate(((zt_ref, st_ref, gt_ref, bt_ref, dyt_ref), (zp_ref, total_ref, gp_ref, bp_ref, dyp_ref))):
        columns = slice(index * half, (index + 1) * half)
        own = slice(0, half)
        mean, inverse = moments(s_ref, total, own)
        gain, shift = g_ref[0:1, own], b_ref[0:1, own]

        def body(r, carry):
            dy, sums = norm_slope(z_ref, grad_ref[r, columns], mask_ref, r, own, mean, inverse, gain, shift)
            out_ref[r, :] = dy
            return (carry[0] + sums[0], carry[1] + sums[1])

        zero = jnp.zeros((8, half), F32)
        add_sums(sums_ref, columns, over_rows(zt_ref.shape[0], body, (zero, zero)))


def transition_back_body(dyt_ref, dyp_ref, zt_ref, st_ref, gt_ref, q_ref, total_ref, mask_ref, w_ref, zp_ref, gp_ref, zs_ref, ss_ref, gs_ref, bs_ref, dz_ref, dzp_ref, grad_ref, dys_ref, sums_ref):
    total = total_ref[2:3, 0:1]
    half = zt_ref.shape[1]
    own = slice(0, half)
    for index, (dy_ref, z_ref, s_ref, g_ref, out_ref) in enumerate(((dyt_ref, zt_ref, st_ref, gt_ref, dz_ref), (dyp_ref, zp_ref, total_ref, gp_ref, dzp_ref))):
        columns = slice(index * half, (index + 1) * half)
        mean, inverse = moments(s_ref, total, own)
        factor = g_ref[0:1, own] * inverse
        first, second = q_ref[0:1, columns] / total, q_ref[1:2, columns] / total

        def body(r, _):
            dz = settle(dy_ref[r, :], z_ref[r, :], mask_ref[r, 0:1], mean, inverse, factor, first, second)
            split_store(out_ref, (r,), dz)

        over_rows(zt_ref.shape[0], body)
    grad_ref[...] = product2_t(dz_ref, (), w_ref[...])
    start_sums(sums_ref)
    mean, inverse = moments(ss_ref, total, own)
    gain, shift = gs_ref[...], bs_ref[...]

    def tail(r, carry):
        dy, sums = norm_slope(zs_ref, grad_ref[r, :], mask_ref, r, own, mean, inverse, gain, shift)
        dys_ref[r, :] = dy
        return (carry[0] + sums[0], carry[1] + sums[1])

    zero = jnp.zeros((8, half), F32)
    add_sums(sums_ref, own, over_rows(zt_ref.shape[0], tail, (zero, zero)))


def spread_back_body(side, dy_ref, z_ref, s_ref, g_ref, q_ref, total_ref, mask_ref, edge_ref, w_ref, inner_ref, zi_ref, si_ref, gi_ref, bi_ref, dw_ref, dyi_ref, sums_ref, padded_ref, pair_ref, turned_ref, grad_ref):
    total = total_ref[2:3, 0:1]
    count, half = z_ref.shape
    tap = pl.program_id(0)

    @pl.when(tap == 0)
    def _():
        padded_ref[0:GUARD, :] = jnp.zeros((GUARD, half), F32)
        padded_ref[GUARD + count :, :] = jnp.zeros((GUARD, half), F32)
        mean, inverse = moments(s_ref, total, slice(None))
        factor = g_ref[...] * inverse
        first, second = q_ref[0:1, :] / total, q_ref[1:2, :] / total

        def body(r, _):
            dz = settle(dy_ref[r, :], z_ref[r, :], mask_ref[r, 0:1], mean, inverse, factor, first, second)
            padded_ref[pl.ds(r.start + GUARD, CHUNK), :] = dz

        over_rows(count, body)
        turned_ref[0:half, :] = inner_ref[0].T
        turned_ref[half:, :] = inner_ref[1].T
        grad_ref[...] = jnp.zeros_like(grad_ref)

    for index, (move, dx) in enumerate(taps(side)):

        @pl.when(tap == index)
        def _(move=move, dx=dx):
            moved = padded_ref[GUARD - move : GUARD - move + count, :]
            if dx:
                moved = moved * edge_ref[:, 1 - dx : 2 - dx]
            split_store(pair_ref, (slice(None),), moved)

    both = dot(turned_ref[...], pair_ref[0])
    dw_ref[0] = both[0:half] + both[half:] + dot(turned_ref[0:half, :], pair_ref[1])
    grad_ref[...] += product2_t(pair_ref, (), w_ref[0])

    @pl.when(tap == pl.num_programs(0) - 1)
    def _():
        sums_ref[...] = jnp.zeros_like(sums_ref)
        own = slice(0, half)
        mean, inverse = moments(si_ref, total, own)
        gain, shift = gi_ref[...], bi_ref[...]

        def tail(r, carry):
            dy, sums = norm_slope(zi_ref, grad_ref[r, :], mask_ref, r, own, mean, inverse, gain, shift)
            dyi_ref[r, :] = dy
            return (carry[0] + sums[0], carry[1] + sums[1])

        zero = jnp.zeros((8, half), F32)
        add_sums(sums_ref, own, over_rows(count, tail, (zero, zero)))


def inner_back_body(dy_ref, zi_ref, si_ref, gi_ref, q_ref, total_ref, mask_ref, w_ref, joined_ref, zm_ref, gm_ref, bm_ref, dz_ref, dym_ref, sums_ref, grad_ref):
    total = total_ref[2:3, 0:1]
    half = zi_ref.shape[1]
    own = slice(0, half)
    upper = slice(half, 2 * half)
    mean, inverse = moments(si_ref, total, own)
    factor = gi_ref[...] * inverse
    first, second = q_ref[0:1, :] / total, q_ref[1:2, :] / total

    def body(r, _):
        dz = settle(dy_ref[r, :], zi_ref[r, :], mask_ref[r, 0:1], mean, inverse, factor, first, second)
        split_store(dz_ref, (r,), dz)

    over_rows(zi_ref.shape[0], body)
    grad_ref[...] = product2_t(dz_ref, (), w_ref[...])
    start_sums(sums_ref)
    mean, inverse = moments(total_ref, total, upper)
    gain, shift = gm_ref[0:1, upper], bm_ref[0:1, upper]

    def tail(r, carry):
        dy, sums = norm_slope(zm_ref, grad_ref[r, :] + joined_ref[r, :], mask_ref, r, own, mean, inverse, gain, shift)
        dym_ref[r, :] = dy
        return (carry[0] + sums[0], carry[1] + sums[1])

    zero = jnp.zeros((8, half), F32)
    add_sums(sums_ref, own, over_rows(zi_ref.shape[0], tail, (zero, zero)))


def split_back_body(dy_ref, zm_ref, q_ref, total_ref, g_ref, mask_ref, dzp_ref, w_ref, dz_ref, grad_ref, scratch_ref):
    total = total_ref[2:3, 0:1]
    half = zm_ref.shape[1]
    upper = slice(half, 2 * half)
    mean, inverse = moments(total_ref, total, upper)
    factor = g_ref[0:1, upper] * inverse
    first, second = q_ref[0:1, :] / total, q_ref[1:2, :] / total

    def body(r, _):
        dz = settle(dy_ref[r, :], zm_ref[r, :], mask_ref[r, 0:1], mean, inverse, factor, first, second)
        split_store(dz_ref, (r,), dz)

    over_rows(zm_ref.shape[0], body)
    scratch_ref[...] = product2_t(dzp_ref, (), w_ref[:, :half])
    scratch_ref[...] += product2_t(dz_ref, (), w_ref[:, half:])
    spread_out(scratch_ref, grad_ref)


def weight_body(x_ref, dz_ref, dw_ref):
    turned = x_ref[0].T
    value = dot(turned, dz_ref[0]) + dot(turned, dz_ref[1])
    if x_ref.shape[0] == 2:
        value += dot(x_ref[1].T, dz_ref[0])
    dw_ref[...] = value


def weight_grad(x, dz, block=256):
    parts, count, width = x.shape
    wide = dz.shape[2]
    return pl.pallas_call(
        weight_body,
        grid=(width // block,),
        in_specs=[pl.BlockSpec((parts, count, block), lambda i: (0, 0, i)), whole(dz)],
        out_specs=pl.BlockSpec((block, wide), lambda i: (i, 0)),
        out_shape=sds((width, wide)),
        compiler_params=params(),
    )(x, dz)


def local(
    features, image_counts, map_sides,
    split_kernel, split_gain, split_shift, inner_kernel, inner_gain, inner_shift,
    spread_kernel, spread_gain, spread_shift, transition_kernel, transition_gain, transition_shift,
    output_kernel, output_gain, output_shift, cotangent,
):
    slots, side, _, full = features.shape
    half = inner_kernel.shape[0]
    pitch = round_up(side * side, 128)
    count = slots * pitch
    grid = (slots,)
    row = jnp.arange(pitch)
    y, x = row // side, row % side
    live = jnp.arange(slots) < image_counts[0]
    keep = live[:, None] & (y[None, :] < map_sides[:, None]) & (x[None, :] < map_sides[:, None])
    mask = jnp.broadcast_to(keep.astype(F32).reshape(count, 1), (count, 128))
    lane = jnp.arange(128)[None, :]
    edges = jnp.where(lane == 0, (x > 0)[:, None], jnp.where(lane == 2, (x < side - 1)[:, None], True)).astype(F32)
    edges = jnp.tile(edges, (slots, 1))
    (split_gain, split_shift, inner_gain, inner_shift, spread_gain, spread_shift, transition_gain, transition_shift, output_gain, output_shift) = (
        item.reshape(1, -1)
        for item in (split_gain, split_shift, inner_gain, inner_shift, spread_gain, spread_shift, transition_gain, transition_shift, output_gain, output_shift)
    )
    spread_weight = spread_kernel.reshape(9, half, half)

    def group(sums):
        return lax.psum(sums, "bn")

    sums_full, sums_half = out_whole((8, full)), out_whole((8, half))
    r_half, r_full, r_mask = rows(pitch, half), rows(pitch, full), rows(pitch, 128)
    pair_half, pair_full = rows2(pitch, half), rows2(pitch, full)

    def call(body, ins, outs, scratch=(), steps=grid):
        return pl.pallas_call(
            body,
            grid=steps,
            in_specs=[spec for _, spec in ins],
            out_specs=[spec for _, spec in outs],
            out_shape=[shape for shape, _ in outs],
            scratch_shapes=list(scratch),
            compiler_params=params(),
        )(*[array for array, _ in ins])

    def fixed(array):
        return (array, whole(array))

    x0, z_split, s_split = call(
        split_kernel_body,
        [(features, image(features.shape)), (mask, r_mask), fixed(split_kernel)],
        [(sds((count, full), BF16), r_full), (sds((count, full)), r_full), (sds((8, full)), sums_full)],
        [pltpu.VMEM((pitch, full), F32)],
    )
    s_split = group(s_split)
    part2, main, main2, z_inner, s_inner = call(
        inner_body,
        [(z_split, r_full), fixed(s_split), fixed(split_gain), fixed(split_shift), (mask, r_mask), fixed(inner_kernel)],
        [
            (sds((2, count, half), BF16), pair_half), (sds((count, half)), r_half), (sds((2, count, half), BF16), pair_half),
            (sds((count, half)), r_half), (sds((8, half)), sums_half),
        ],
    )
    s_inner = group(s_inner)
    inner2, z_spread, s_spread = call(
        functools.partial(spread_body, side),
        [(z_inner, r_half), fixed(s_split), fixed(s_inner), fixed(inner_gain), fixed(inner_shift), (mask, r_mask), (edges, r_mask), fixed(spread_weight)],
        [(sds((2, count, half), BF16), pair_half), (sds((count, half)), r_half), (sds((8, half)), sums_half)],
        [pltpu.VMEM((pitch + 2 * GUARD, half), F32), pltpu.VMEM((2, pitch, half), BF16)],
    )
    s_spread = group(s_spread)
    joined2, z_trans, s_trans = call(
        transition_body,
        [(z_spread, r_half), fixed(s_split), fixed(s_spread), fixed(spread_gain), fixed(spread_shift), (mask, r_mask), (main, r_half), fixed(transition_kernel)],
        [(sds((2, count, half), BF16), pair_half), (sds((count, half)), r_half), (sds((8, half)), sums_half)],
    )
    s_trans = group(s_trans)
    trans2, z_out, s_out = call(
        output_body,
        [(z_trans, r_half), fixed(s_split), fixed(s_trans), fixed(transition_gain), fixed(transition_shift), (mask, r_mask), (part2, pair_half), fixed(output_kernel)],
        [(sds((2, count, half), BF16), pair_half), (sds((count, full)), r_full), (sds((8, full)), sums_full)],
    )
    s_out = group(s_out)
    result, dy_out, q_out = call(
        result_body,
        [(z_out, r_full), fixed(s_split), fixed(s_out), fixed(output_gain), fixed(output_shift), (mask, r_mask), (cotangent, image(cotangent.shape))],
        [(sds(cotangent.shape), image(cotangent.shape)), (sds((count, full)), r_full), (sds((8, full)), sums_full)],
        [pltpu.VMEM((pitch, full), F32)],
    )
    own_out = q_out
    q_out = group(q_out)
    dz_out, dy_trans, dy_part, q_mid = call(
        output_back_body,
        [
            (dy_out, r_full), (z_out, r_full), fixed(s_out), fixed(output_gain), fixed(q_out), fixed(s_split), (mask, r_mask), fixed(output_kernel),
            (z_trans, r_half), fixed(s_trans), fixed(transition_gain), fixed(transition_shift), (z_split, rows(pitch, half, 0)), fixed(split_gain), fixed(split_shift),
        ],
        [(sds((2, count, full), BF16), pair_full), (sds((count, half)), r_half), (sds((count, half)), r_half), (sds((8, full)), sums_full)],
        [pltpu.VMEM((pitch, full), F32)],
    )
    own_mid = q_mid
    q_mid = group(q_mid)
    grad_output = jnp.concatenate([weight_grad(trans2, dz_out), weight_grad(part2, dz_out)], axis=0)
    dz_trans, dz_part, grad_joined, dy_spread, q_spread = call(
        transition_back_body,
        [
            (dy_trans, r_half), (dy_part, r_half), (z_trans, r_half), fixed(s_trans), fixed(transition_gain), fixed(q_mid), fixed(s_split), (mask, r_mask), fixed(transition_kernel),
            (z_split, rows(pitch, half, 0)), fixed(split_gain), (z_spread, r_half), fixed(s_spread), fixed(spread_gain), fixed(spread_shift),
        ],
        [
            (sds((2, count, half), BF16), pair_half), (sds((2, count, half), BF16), pair_half), (sds((count, half)), r_half),
            (sds((count, half)), r_half), (sds((8, half)), sums_half),
        ],
    )
    own_spread = q_spread
    q_spread = group(q_spread)
    grad_transition = weight_grad(joined2, dz_trans)
    grad_part = weight_grad(x0[None], dz_part)
    tap_spec = pl.BlockSpec((1, half, half), lambda i: (i, 0, 0))
    grad_spread, dy_inner, q_inner = call(
        functools.partial(spread_back_body, side),
        [
            fixed(dy_spread), fixed(z_spread), fixed(s_spread), fixed(spread_gain), fixed(q_spread), fixed(s_split), fixed(mask), fixed(edges), (spread_weight, tap_spec),
            fixed(inner2), fixed(z_inner), fixed(s_inner), fixed(inner_gain), fixed(inner_shift),
        ],
        [(sds((9, half, half)), tap_spec), (sds((count, half)), out_whole((count, half))), (sds((8, half)), sums_half)],
        [pltpu.VMEM((count + 2 * GUARD, half), F32), pltpu.VMEM((2, count, half), BF16), pltpu.VMEM((2 * half, count), BF16), pltpu.VMEM((count, half), F32)],
        (9,),
    )
    own_inner = q_inner
    q_inner = group(q_inner)
    dz_inner, dy_main, q_main = call(
        inner_back_body,
        [
            (dy_inner, r_half), (z_inner, r_half), fixed(s_inner), fixed(inner_gain), fixed(q_inner), fixed(s_split), (mask, r_mask), fixed(inner_kernel),
            (grad_joined, r_half), (z_split, rows(pitch, half, 1)), fixed(split_gain), fixed(split_shift),
        ],
        [(sds((2, count, half), BF16), pair_half), (sds((count, half)), r_half), (sds((8, half)), sums_half)],
        [pltpu.VMEM((pitch, half), F32)],
    )
    own_main = q_main
    q_main = group(q_main)
    grad_inner = weight_grad(main2, dz_inner)
    dz_main, grad_features = call(
        split_back_body,
        [(dy_main, r_half), (z_split, rows(pitch, half, 1)), fixed(q_main), fixed(s_split), fixed(split_gain), (mask, r_mask), (dz_part, pair_half), fixed(split_kernel)],
        [(sds((2, count, half), BF16), pair_half), (sds(cotangent.shape), image(cotangent.shape))],
        [pltpu.VMEM((pitch, full), F32)],
    )
    grad_main = weight_grad(x0[None], dz_main)
    grad_split = jnp.concatenate([grad_part, grad_main], axis=1)
    small = jnp.concatenate([own_mid[0:2, half:], own_main[0:2], own_inner[0:2], own_spread[0:2], own_mid[0:2, :half], own_out[0:2]], axis=1)
    grad_split, grad_inner, grad_spread, grad_transition, grad_output, small = lax.psum(
        (grad_split, grad_inner, grad_spread, grad_transition, grad_output, small), ("dp", "bn")
    )
    cuts = [0, full, full + half, full + 2 * half, full + 3 * half, 2 * full + 3 * half]
    shifts = [small[0, a:b] for a, b in zip(cuts[:-1], cuts[1:])]
    gains = [small[1, a:b] for a, b in zip(cuts[:-1], cuts[1:])]
    return (
        result, grad_features,
        grad_split, gains[0], shifts[0], grad_inner, gains[1], shifts[1],
        grad_spread.reshape(3, 3, half, half), gains[2], shifts[2], grad_transition, gains[3], shifts[3], grad_output, gains[4], shifts[4],
    )


def solution(mesh):
    shard, copy = P(("dp", "bn")), P()
    return jax.shard_map(
        local,
        mesh=mesh,
        in_specs=(shard, shard, shard) + (copy,) * 15 + (shard,),
        out_specs=(shard, shard) + (copy,) * 15,
        check_vma=False,
    )
```

```python
import functools

import jax
import jax.numpy as jnp
from jax import lax
from jax.experimental import pallas as pl
from jax.experimental.pallas import tpu as pltpu
from jax.sharding import PartitionSpec as P

EPS = 1e-05
GUARD = 80
CHUNK = 16
TILES = 4
MESH = pl.DeviceIdType.MESH
F32 = jnp.float32
BF16 = jnp.bfloat16


def round_up(value, step):
    return -(-value // step) * step


def params(megabytes=56):
    return pltpu.CompilerParams(vmem_limit_bytes=megabytes * 1024 * 1024)


def whole(array):
    zeros = (0,) * len(array.shape)
    return pl.BlockSpec(array.shape, lambda *_: zeros, pipeline_mode=pl.Buffered(1))


def out_whole(shape):
    zeros = (0,) * len(shape)
    return pl.BlockSpec(shape, lambda *_: zeros)


def rows(pitch, width, column=0):
    return pl.BlockSpec((pitch, width), lambda i: (i, column))


def rows2(pitch, width):
    return pl.BlockSpec((2, pitch, width), lambda i: (0, i, 0))


def pixels(pitch, shape):
    return pl.BlockSpec((pitch // shape[1],) + tuple(shape[1:]), lambda i: (i, 0, 0))


def sds(shape, dtype=F32):
    return jax.ShapeDtypeStruct(tuple(shape), dtype)


def dot(left, right):
    return jnp.dot(left, right, preferred_element_type=F32)


def dot_t(left, right):
    return lax.dot_general(left, right, (((1,), (1,)), ((), ())), preferred_element_type=F32)


def split_store(ref, place, value):
    high = value.astype(BF16)
    ref[(0,) + place] = high
    ref[(1,) + place] = (value - high.astype(F32)).astype(BF16)


def moments(stats_ref, total, columns):
    mean = stats_ref[0:1, columns] / total
    square = stats_ref[1:2, columns] / total
    return mean, lax.rsqrt(square - mean * mean + EPS)


def mish(y):
    t = jnp.exp(jnp.minimum(y, 30.0))
    n = t * (t + 2.0)
    return y * (n / (n + 2.0))


def mish_slope(y):
    t = jnp.exp(jnp.minimum(y, 30.0))
    n = t * (t + 2.0)
    r = 1.0 / (n + 2.0)
    return n * r + y * (((4.0 * t) * (t + 1.0) * r) * r)


def fold(value):
    return jnp.sum(value.reshape(value.shape[0] // 8, 8, value.shape[1]), axis=0)


def over_rows(count, body, carry=None, unroll=2):
    def step(k, c):
        return body(pl.ds(pl.multiple_of(k * CHUNK, CHUNK), CHUNK), c)

    return lax.fori_loop(0, count // CHUNK, step, carry, unroll=unroll)


def column_blocks(width, block=512):
    return [slice(c, c + block) for c in range(0, width, block)]


def add_sums(sums_ref, columns, pieces):
    for k, piece in enumerate(pieces):
        sums_ref[k : k + 1, columns] += jnp.sum(piece, axis=0, keepdims=True)


def start_sums(sums_ref):
    @pl.when(pl.program_id(0) == 0)
    def _():
        sums_ref[...] = jnp.zeros_like(sums_ref)


def sum_squares(z_ref, sums_ref, mask_ref=None):
    for columns in column_blocks(z_ref.shape[1]):
        width = columns.stop - columns.start

        def body(r, carry):
            value = z_ref[r, columns]
            kept = value if mask_ref is None else value * mask_ref[r, 0:1]
            return (carry[0] + fold(kept), carry[1] + fold(kept * value))

        zero = jnp.zeros((8, width), F32)
        add_sums(sums_ref, columns, over_rows(z_ref.shape[0], body, (zero, zero)))


def product2(ref, place, weight):
    high = ref[(0,) + place]
    low = ref[(1,) + place]
    return dot(high, weight) + dot(low, weight)


def product2_t(ref, place, weight):
    high = ref[(0,) + place]
    low = ref[(1,) + place]
    return dot_t(high, weight) + dot_t(low, weight)


def compact(source_ref, scratch_ref):
    places, slots, _ = source_ref.shape
    for p in range(places):
        scratch_ref[p * slots : (p + 1) * slots, :] = source_ref[p].astype(F32)


def spread_out(scratch_ref, target_ref):
    places, slots, _ = target_ref.shape
    for p in range(places):
        target_ref[p] = scratch_ref[p * slots : (p + 1) * slots, :]


def split_kernel_body(features_ref, mask_ref, w_ref, x_ref, z_ref, sums_ref, scratch_ref):
    compact(features_ref, scratch_ref)

    def body(r, _):
        x_ref[r, :] = jnp.where(mask_ref[r, 0:1] > 0.0, scratch_ref[r, :], 0.0).astype(BF16)

    over_rows(x_ref.shape[0], body)
    z_ref[...] = dot(x_ref[...], w_ref[...])
    start_sums(sums_ref)
    sum_squares(z_ref, sums_ref)
    count = jnp.sum(mask_ref[...], axis=0, keepdims=True)
    sums_ref[2:3, 0:128] += count


def inner_body(z_ref, stats_ref, gain_ref, shift_ref, mask_ref, w_ref, part_ref, main_ref, main2_ref, zi_ref, sums_ref):
    total = stats_ref[2:3, 0:1]
    half = w_ref.shape[0]
    for index, columns in enumerate(column_blocks(2 * half, half)):
        mean, inverse = moments(stats_ref, total, columns)
        scale, shift = gain_ref[0:1, columns] * inverse, shift_ref[0:1, columns]

        def body(r, _):
            act = mish((z_ref[r, columns] - mean) * scale + shift) * mask_ref[r, 0:1]
            if index == 0:
                split_store(part_ref, (r,), act)
            else:
                main_ref[r, :] = act
                split_store(main2_ref, (r,), act)

        over_rows(z_ref.shape[0], body)
    zi_ref[...] = product2(main2_ref, (), w_ref[...])
    start_sums(sums_ref)
    sum_squares(zi_ref, sums_ref)


def taps(side, slots):
    return [((dy * side + dx) * slots, dx) for dy in (-1, 0, 1) for dx in (-1, 0, 1)]


def move_rows(padded_ref, edge_ref, pair_ref, side, slots, sign):
    count = pair_ref.shape[1]
    for index, (move, dx) in enumerate(taps(side, slots)):

        @pl.when(pl.program_id(0) == index)
        def _(move=sign * move, dx=sign * dx):
            moved = padded_ref[GUARD + move : GUARD + move + count, :]
            if dx:
                moved = moved * edge_ref[:, dx + 1 : dx + 2]
            split_store(pair_ref, (slice(None),), moved)


def spread_body(side, slots, z_ref, total_ref, stats_ref, gain_ref, shift_ref, mask_ref, edge_ref, w_ref, inner_ref, zs_ref, sums_ref, padded_ref, pair_ref):
    total = total_ref[2:3, 0:1]
    count = z_ref.shape[0]
    tap = pl.program_id(0)

    @pl.when(tap == 0)
    def _():
        mean, inverse = moments(stats_ref, total, slice(None))
        scale, shift = gain_ref[...] * inverse, shift_ref[...]
        padded_ref[0:GUARD, :] = jnp.zeros((GUARD, padded_ref.shape[1]), F32)
        padded_ref[GUARD + count :, :] = jnp.zeros((GUARD, padded_ref.shape[1]), F32)

        def body(r, _):
            act = mish((z_ref[r, :] - mean) * scale + shift) * mask_ref[r, 0:1]
            padded_ref[pl.ds(r.start + GUARD, CHUNK), :] = act
            split_store(inner_ref, (r,), act)

        over_rows(count, body)
        zs_ref[...] = jnp.zeros_like(zs_ref)

    move_rows(padded_ref, edge_ref, pair_ref, side, slots, 1)
    zs_ref[...] += product2(pair_ref, (), w_ref[0])

    @pl.when(tap == pl.num_programs(0) - 1)
    def _():
        sums_ref[...] = jnp.zeros_like(sums_ref)
        sum_squares(zs_ref, sums_ref, mask_ref)


def transition_body(z_ref, total_ref, stats_ref, gain_ref, shift_ref, mask_ref, main_ref, w_ref, joined_ref, zt_ref, sums_ref):
    total = total_ref[2:3, 0:1]
    mean, inverse = moments(stats_ref, total, slice(None))
    scale, shift = gain_ref[...] * inverse, shift_ref[...]

    def body(r, _):
        act = mish((z_ref[r, :] - mean) * scale + shift) * mask_ref[r, 0:1]
        split_store(joined_ref, (r,), act + main_ref[r, :])

    over_rows(z_ref.shape[0], body)
    zt_ref[...] = product2(joined_ref, (), w_ref[...])
    start_sums(sums_ref)
    sum_squares(zt_ref, sums_ref)


def output_body(z_ref, total_ref, stats_ref, gain_ref, shift_ref, mask_ref, part_ref, w_ref, trans_ref, zo_ref, sums_ref):
    total = total_ref[2:3, 0:1]
    mean, inverse = moments(stats_ref, total, slice(None))
    scale, shift = gain_ref[...] * inverse, shift_ref[...]
    half = z_ref.shape[1]

    def body(r, _):
        act = mish((z_ref[r, :] - mean) * scale + shift) * mask_ref[r, 0:1]
        split_store(trans_ref, (r,), act)

    over_rows(z_ref.shape[0], body)
    zo_ref[...] = product2(part_ref, (), w_ref[half:, :])
    zo_ref[...] += product2(trans_ref, (), w_ref[:half, :])
    start_sums(sums_ref)
    sum_squares(zo_ref, sums_ref)


def result_body(z_ref, total_ref, stats_ref, gain_ref, shift_ref, mask_ref, cotangent_ref, result_ref, dy_ref, sums_ref, scratch_ref):
    total = total_ref[2:3, 0:1]
    compact(cotangent_ref, scratch_ref)
    start_sums(sums_ref)
    for columns in column_blocks(z_ref.shape[1]):
        mean, inverse = moments(stats_ref, total, columns)
        gain, shift = gain_ref[0:1, columns], shift_ref[0:1, columns]

        def body(r, carry):
            mask = mask_ref[r, 0:1]
            scaled = (z_ref[r, columns] - mean) * inverse
            y = scaled * gain + shift
            t = jnp.exp(jnp.minimum(y, 30.0))
            n = t * (t + 2.0)
            inv = 1.0 / (n + 2.0)
            ratio = n * inv
            slope = ratio + y * (((4.0 * t) * (t + 1.0) * inv) * inv)
            dy = jnp.where(mask > 0.0, scratch_ref[r, columns], 0.0) * slope
            scratch_ref[r, columns] = y * ratio * mask
            dy_ref[r, columns] = dy
            return (carry[0] + fold(dy), carry[1] + fold(dy * scaled))

        zero = jnp.zeros((8, columns.stop - columns.start), F32)
        add_sums(sums_ref, columns, over_rows(z_ref.shape[0], body, (zero, zero)))
    spread_out(scratch_ref, result_ref)


def norm_slope(z_ref, grad, mask_ref, r, columns, mean, inverse, gain, shift):
    scaled = (z_ref[r, columns] - mean) * inverse
    dy = grad * mask_ref[r, 0:1] * mish_slope(scaled * gain + shift)
    return dy, (fold(dy), fold(dy * scaled))


def settle(dy, z, mask, mean, inverse, factor, first, second):
    scaled = (z - mean) * inverse
    return mask * factor * (dy - (first + scaled * second))


def output_back_body(dy_ref, zo_ref, so_ref, go_ref, qo_ref, total_ref, mask_ref, w_ref, zt_ref, st_ref, gt_ref, bt_ref, zp_ref, gp_ref, bp_ref, dz_ref, dyt_ref, dyp_ref, sums_ref, grad_ref):
    total = total_ref[2:3, 0:1]
    for columns in column_blocks(zo_ref.shape[1]):
        mean, inverse = moments(so_ref, total, columns)
        factor = go_ref[0:1, columns] * inverse
        first, second = qo_ref[0:1, columns] / total, qo_ref[1:2, columns] / total

        def body(r, _):
            dz = settle(dy_ref[r, columns], zo_ref[r, columns], mask_ref[r, 0:1], mean, inverse, factor, first, second)
            split_store(dz_ref, (r, columns), dz)

        over_rows(zo_ref.shape[0], body)
    grad_ref[...] = product2_t(dz_ref, (), w_ref[...])
    start_sums(sums_ref)
    half = zt_ref.shape[1]
    for index, (z_ref, s_ref, g_ref, b_ref, out_ref) in enumerate(((zt_ref, st_ref, gt_ref, bt_ref, dyt_ref), (zp_ref, total_ref, gp_ref, bp_ref, dyp_ref))):
        columns = slice(index * half, (index + 1) * half)
        own = slice(0, half)
        mean, inverse = moments(s_ref, total, own)
        gain, shift = g_ref[0:1, own], b_ref[0:1, own]

        def body(r, carry):
            dy, sums = norm_slope(z_ref, grad_ref[r, columns], mask_ref, r, own, mean, inverse, gain, shift)
            out_ref[r, :] = dy
            return (carry[0] + sums[0], carry[1] + sums[1])

        zero = jnp.zeros((8, half), F32)
        add_sums(sums_ref, columns, over_rows(zt_ref.shape[0], body, (zero, zero)))


def transition_back_body(dyt_ref, dyp_ref, zt_ref, st_ref, gt_ref, q_ref, total_ref, mask_ref, w_ref, zp_ref, gp_ref, zs_ref, ss_ref, gs_ref, bs_ref, dz_ref, dzp_ref, grad_ref, dys_ref, sums_ref):
    total = total_ref[2:3, 0:1]
    half = zt_ref.shape[1]
    own = slice(0, half)
    for index, (dy_ref, z_ref, s_ref, g_ref, out_ref) in enumerate(((dyt_ref, zt_ref, st_ref, gt_ref, dz_ref), (dyp_ref, zp_ref, total_ref, gp_ref, dzp_ref))):
        columns = slice(index * half, (index + 1) * half)
        mean, inverse = moments(s_ref, total, own)
        factor = g_ref[0:1, own] * inverse
        first, second = q_ref[0:1, columns] / total, q_ref[1:2, columns] / total

        def body(r, _):
            dz = settle(dy_ref[r, :], z_ref[r, :], mask_ref[r, 0:1], mean, inverse, factor, first, second)
            split_store(out_ref, (r,), dz)

        over_rows(zt_ref.shape[0], body)
    grad_ref[...] = product2_t(dz_ref, (), w_ref[...])
    start_sums(sums_ref)
    mean, inverse = moments(ss_ref, total, own)
    gain, shift = gs_ref[...], bs_ref[...]

    def tail(r, carry):
        dy, sums = norm_slope(zs_ref, grad_ref[r, :], mask_ref, r, own, mean, inverse, gain, shift)
        dys_ref[r, :] = dy
        return (carry[0] + sums[0], carry[1] + sums[1])

    zero = jnp.zeros((8, half), F32)
    add_sums(sums_ref, own, over_rows(zt_ref.shape[0], tail, (zero, zero)))


def spread_back_body(side, slots, dy_ref, z_ref, s_ref, g_ref, q_ref, total_ref, mask_ref, edge_ref, w_ref, zi_ref, si_ref, gi_ref, bi_ref, moved_ref, dyi_ref, sums_ref, padded_ref, grad_ref):
    total = total_ref[2:3, 0:1]
    count, half = z_ref.shape
    tap = pl.program_id(0)

    @pl.when(tap == 0)
    def _():
        padded_ref[0:GUARD, :] = jnp.zeros((GUARD, half), F32)
        padded_ref[GUARD + count :, :] = jnp.zeros((GUARD, half), F32)
        mean, inverse = moments(s_ref, total, slice(None))
        factor = g_ref[...] * inverse
        first, second = q_ref[0:1, :] / total, q_ref[1:2, :] / total

        def body(r, _):
            dz = settle(dy_ref[r, :], z_ref[r, :], mask_ref[r, 0:1], mean, inverse, factor, first, second)
            padded_ref[pl.ds(r.start + GUARD, CHUNK), :] = dz

        over_rows(count, body)
        grad_ref[...] = jnp.zeros_like(grad_ref)

    move_rows(padded_ref, edge_ref, moved_ref.at[0], side, slots, -1)
    grad_ref[...] += product2_t(moved_ref.at[0], (), w_ref[0])

    @pl.when(tap == pl.num_programs(0) - 1)
    def _():
        sums_ref[...] = jnp.zeros_like(sums_ref)
        own = slice(0, half)
        mean, inverse = moments(si_ref, total, own)
        gain, shift = gi_ref[...], bi_ref[...]

        def tail(r, carry):
            dy, sums = norm_slope(zi_ref, grad_ref[r, :], mask_ref, r, own, mean, inverse, gain, shift)
            dyi_ref[r, :] = dy
            return (carry[0] + sums[0], carry[1] + sums[1])

        zero = jnp.zeros((8, half), F32)
        add_sums(sums_ref, own, over_rows(count, tail, (zero, zero)))


def inner_back_body(dy_ref, zi_ref, si_ref, gi_ref, q_ref, total_ref, mask_ref, w_ref, joined_ref, zm_ref, gm_ref, bm_ref, dz_ref, dym_ref, sums_ref, grad_ref):
    total = total_ref[2:3, 0:1]
    half = zi_ref.shape[1]
    own = slice(0, half)
    upper = slice(half, 2 * half)
    mean, inverse = moments(si_ref, total, own)
    factor = gi_ref[...] * inverse
    first, second = q_ref[0:1, :] / total, q_ref[1:2, :] / total

    def body(r, _):
        dz = settle(dy_ref[r, :], zi_ref[r, :], mask_ref[r, 0:1], mean, inverse, factor, first, second)
        split_store(dz_ref, (r,), dz)

    over_rows(zi_ref.shape[0], body)
    grad_ref[...] = product2_t(dz_ref, (), w_ref[...])
    start_sums(sums_ref)
    mean, inverse = moments(total_ref, total, upper)
    gain, shift = gm_ref[0:1, upper], bm_ref[0:1, upper]

    def tail(r, carry):
        dy, sums = norm_slope(zm_ref, grad_ref[r, :] + joined_ref[r, :], mask_ref, r, own, mean, inverse, gain, shift)
        dym_ref[r, :] = dy
        return (carry[0] + sums[0], carry[1] + sums[1])

    zero = jnp.zeros((8, half), F32)
    add_sums(sums_ref, own, over_rows(zi_ref.shape[0], tail, (zero, zero)))


def split_back_body(dy_ref, zm_ref, q_ref, total_ref, g_ref, mask_ref, dzp_ref, w_ref, dz_ref, grad_ref, scratch_ref):
    total = total_ref[2:3, 0:1]
    half = zm_ref.shape[1]
    upper = slice(half, 2 * half)
    mean, inverse = moments(total_ref, total, upper)
    factor = g_ref[0:1, upper] * inverse
    first, second = q_ref[0:1, :] / total, q_ref[1:2, :] / total

    def body(r, _):
        dz = settle(dy_ref[r, :], zm_ref[r, :], mask_ref[r, 0:1], mean, inverse, factor, first, second)
        split_store(dz_ref, (r,), dz)

    over_rows(zm_ref.shape[0], body)
    scratch_ref[...] = product2_t(dzp_ref, (), w_ref[:, :half])
    scratch_ref[...] += product2_t(dz_ref, (), w_ref[:, half:])
    spread_out(scratch_ref, grad_ref)


def weight_body(x_ref, dz_ref, dw_ref):
    turned = x_ref[0].T
    value = dot(turned, dz_ref[0]) + dot(turned, dz_ref[1])
    if x_ref.shape[0] == 2:
        value += dot(x_ref[1].T, dz_ref[0])
    dw_ref[...] = value


def weight_grad(x, dz, block=256):
    parts, count, width = x.shape
    wide = dz.shape[2]
    return pl.pallas_call(
        weight_body,
        grid=(width // block,),
        in_specs=[pl.BlockSpec((parts, count, block), lambda i: (0, 0, i)), whole(dz)],
        out_specs=pl.BlockSpec((block, wide), lambda i: (i, 0)),
        out_shape=sds((width, wide)),
        compiler_params=params(),
    )(x, dz)


LAG = 8
KEPT = 6


def reduce_body(jobs, left_count, right_count, *refs):
    lefts, rights = refs[:left_count], refs[left_count : left_count + right_count]
    refs = refs[left_count + right_count :]
    outs = refs[:5]
    (x_ref, z_ref, turned_ref, own_ref, r0_ref, half_ref, r1_ref, quarter_ref, r2_ref, eighth_ref, r3_ref, full_ref, load_sem, store_sem) = refs[5:19]
    sems = refs[19:]
    block = own_ref.shape[1]
    mid = block // 2
    dp, bn = lax.axis_index("dp"), lax.axis_index("bn")
    z, x, y, core = dp // 2, dp % 2, bn // 2, bn % 2

    def at(new_z, new_x, new_y, new_core):
        return {"dp": new_z * 2 + new_x, "bn": new_y * 2 + new_core}

    to_core, to_x, to_y = at(z, x, y, 1 - core), at(z, 1 - x, y, core), at(z, x, 1 - y, core)
    depth = [(z + k) % 4 for k in (1, 2, 3)]
    to_z = [at(new_z, x, y, core) for new_z in depth]
    columns = (pl.ds(0, mid), pl.ds(mid, mid))

    def part(start, size):
        return pl.ds(pl.multiple_of(start, size), size)

    def far(stage, k, slot, source, target, peer):
        send, recv = sems[2 * stage], sems[2 * stage + 1]
        return pltpu.make_async_remote_copy(
            src_ref=source, dst_ref=target, send_sem=send.at[k, slot], recv_sem=recv.at[k, slot], device_id=peer, device_id_type=MESH
        )

    first = (x, y)
    second = (y, x)
    sides = (to_x, to_y)

    def copies(stage, c):
        slot, keep = c % 2, c % KEPT
        base = core * (block // 2)
        if stage == 0:
            return [far(0, 0, slot, own_ref.at[slot, part((1 - core) * (block // 2), block // 2)], r0_ref.at[slot], to_core)]
        if stage == 1:
            return [
                far(1, k, slot, half_ref.at[slot, part((1 - first[k]) * (block // 4), block // 4), columns[k]], r1_ref.at[slot, :, columns[k]], sides[k])
                for k in (0, 1)
            ]
        if stage == 2:
            return [
                far(2, k, slot, quarter_ref.at[slot, part((1 - second[k]) * (block // 8), block // 8), columns[k]], r2_ref.at[slot, :, columns[k]], sides[1 - k])
                for k in (0, 1)
            ]
        if stage == 3:
            return [
                far(3, k, slot, eighth_ref.at[slot, part(depth[k] * (block // 32), block // 32)], r3_ref.at[slot, k], to_z[k]) for k in (0, 1, 2)
            ]
        made = []
        for k in (0, 1):
            eighth = base + first[k] * (block // 4) + second[k] * (block // 8)
            if stage == 4:
                spot = full_ref.at[keep, part(eighth + z * (block // 32), block // 32), columns[k]]
                made += [far(4, 3 * k + d, slot, spot, spot, to_z[d]) for d in (0, 1, 2)]
            elif stage == 5:
                spot = full_ref.at[keep, part(eighth, block // 8), columns[k]]
                made.append(far(5, k, slot, spot, spot, sides[1 - k]))
            elif stage == 6:
                spot = full_ref.at[keep, part(base + first[k] * (block // 4), block // 4), columns[k]]
                made.append(far(6, k, slot, spot, spot, sides[k]))
        if stage == 7:
            spot = full_ref.at[keep, part(base, block // 2)]
            made.append(far(7, 0, slot, spot, spot, to_core))
        return made

    def begin(stage, c):
        for copy in copies(stage, c):
            copy.start()

    def finish(stage, c):
        for copy in copies(stage, c):
            copy.wait()

    def load(j):
        (left, left_columns, parts), (right, right_columns), _ = jobs[j]
        slot = j % 2
        return [
            pltpu.make_async_copy(lefts[left].at[0:parts, :, left_columns], x_ref.at[slot, 0:parts], load_sem.at[slot, 0]),
            pltpu.make_async_copy(rights[right].at[(slice(None),) * (len(rights[right].shape) - 2) + (slice(None), right_columns)] if right_columns is not None else rights[right[0]].at[right[1]], z_ref.at[slot], load_sem.at[slot, 1]),
        ]

    def store(j):
        out, spot = jobs[j][2]
        return pltpu.make_async_copy(full_ref.at[j % KEPT], outs[out].at[spot], store_sem.at[j % KEPT])

    for copy in load(0):
        copy.start()
    barrier = pltpu.get_barrier_semaphore()
    peers = [to_core, to_x, to_y] + to_z
    for peer in peers:
        pl.semaphore_signal(barrier, inc=1, device_id=peer, device_id_type=MESH)
    pl.semaphore_wait(barrier, len(peers))
    total = len(jobs)

    @pl.loop(0, total + LAG + 1)
    def _(t):
        for j in range(total):

            @pl.when(t == j + LAG + 1)
            def _(j=j):
                store(j).wait()

        def stage(number, lag):
            def wrap(body):
                c = t - lag
                pl.when(jnp.logical_and(c >= 0, c < total))(lambda: body(c))

            return wrap

        @stage(7, 8)
        def _(c):
            finish(7, c)

        for j in range(total):

            @pl.when(t == j + LAG)
            def _(j=j):
                store(j).start()

        for number in (6, 5, 4):

            @stage(number, number + 1)
            def _(c, number=number):
                finish(number, c)
                begin(number + 1, c)

        @stage(3, 4)
        def _(c):
            finish(3, c)
            slot, keep = c % 2, c % KEPT
            value = eighth_ref[slot, part(z * (block // 32), block // 32), :]
            for k in (0, 1, 2):
                value = value + r3_ref[slot, k]
            for k in (0, 1):
                row = core * (block // 2) + first[k] * (block // 4) + second[k] * (block // 8) + z * (block // 32)
                full_ref[keep, part(row, block // 32), k * mid : (k + 1) * mid] = value[:, k * mid : (k + 1) * mid]
            begin(4, c)

        @stage(2, 3)
        def _(c):
            finish(2, c)
            slot = c % 2
            for k in (0, 1):
                eighth_ref[slot, :, columns[k]] = quarter_ref[slot, part(second[k] * (block // 8), block // 8), columns[k]] + r2_ref[slot, :, columns[k]]
            begin(3, c)

        @stage(1, 2)
        def _(c):
            finish(1, c)
            slot = c % 2
            for k in (0, 1):
                quarter_ref[slot, :, columns[k]] = half_ref[slot, part(first[k] * (block // 4), block // 4), columns[k]] + r1_ref[slot, :, columns[k]]
            begin(2, c)

        @stage(0, 1)
        def _(c):
            finish(0, c)
            slot = c % 2
            half_ref[slot] = own_ref[slot, part(core * (block // 2), block // 2), :] + r0_ref[slot]
            begin(1, c)

        for j in range(total):

            @pl.when(t == j)
            def _(j=j):
                for copy in load(j):
                    copy.wait()
                if j + 1 < total:
                    for copy in load(j + 1):
                        copy.start()

        exact = functools.reduce(jnp.logical_or, [t == j for j in range(total) if jobs[j][0][2] == 1])

        @stage(None, 0)
        def _(c):
            slot = c % 2
            turned_ref[...] = x_ref[slot, 0].T
            own_ref[slot] = dot(turned_ref[...], z_ref[slot, 0]) + dot(turned_ref[...], z_ref[slot, 1])

            @pl.when(jnp.logical_not(exact))
            def _():
                turned_ref[...] = x_ref[slot, 1].T
                own_ref[slot] += dot(turned_ref[...], z_ref[slot, 0])

            begin(0, c)


def reduce_call(jobs, lefts, rights, shapes, count, block):
    hbm = pl.BlockSpec(memory_space=pl.ANY)
    vmem = pltpu.VMEM
    scratch = [
        vmem((2, 2, count, block), BF16), vmem((2, 2, count, block), BF16), vmem((block, count), BF16),
        vmem((2, block, block), F32), vmem((2, block // 2, block), F32), vmem((2, block // 2, block), F32),
        vmem((2, block // 4, block), F32), vmem((2, block // 4, block), F32), vmem((2, block // 8, block), F32), vmem((2, block // 8, block), F32),
        vmem((2, 3, block // 32, block), F32), vmem((KEPT, block, block), F32),
        pltpu.SemaphoreType.DMA((2, 2)), pltpu.SemaphoreType.DMA((KEPT,)),
    ]
    for width in (1, 2, 2, 3, 6, 2, 2, 1):
        scratch += [pltpu.SemaphoreType.DMA((width, 2)), pltpu.SemaphoreType.DMA((width, 2))]
    return pl.pallas_call(
        functools.partial(reduce_body, jobs, len(lefts), len(rights)),
        in_specs=[hbm] * (len(lefts) + len(rights)),
        out_specs=[hbm] * len(shapes),
        out_shape=[sds(shape) for shape in shapes],
        scratch_shapes=scratch,
        compiler_params=pltpu.CompilerParams(collective_id=3, has_side_effects=True, vmem_limit_bytes=56 * 1024 * 1024),
    )(*lefts, *rights)


def gather_sums_body(axis, sums_ref, out_ref, slots_ref, send_sem, recv_sem):
    members = slots_ref.shape[0]
    me = lax.axis_index(axis)
    peers = [lax.rem(me + k, members) for k in range(1, members)]
    barrier = pltpu.get_barrier_semaphore()
    for peer in peers:
        pl.semaphore_signal(barrier, inc=1, device_id={axis: peer}, device_id_type=MESH)
    pl.semaphore_wait(barrier, members - 1)
    copies = [
        pltpu.make_async_remote_copy(
            src_ref=sums_ref, dst_ref=slots_ref.at[me], send_sem=send_sem.at[k], recv_sem=recv_sem.at[k], device_id={axis: peer}, device_id_type=MESH
        )
        for k, peer in enumerate(peers)
    ]
    for copy in copies:
        copy.start()
    slots_ref[me] = sums_ref[...]
    for copy in copies:
        copy.wait()
    value = slots_ref[0]
    for k in range(1, members):
        value = value + slots_ref[k]
    out_ref[...] = value


def gather_sums(sums, members, collective, axis="bn"):
    if members == 1:
        return sums
    spec = pl.BlockSpec(memory_space=pltpu.VMEM)
    return pl.pallas_call(
        functools.partial(gather_sums_body, axis),
        in_specs=[spec],
        out_specs=spec,
        out_shape=sds(sums.shape),
        scratch_shapes=[pltpu.VMEM((members,) + sums.shape, F32), pltpu.SemaphoreType.DMA((members - 1,)), pltpu.SemaphoreType.DMA((members - 1,))],
        compiler_params=pltpu.CompilerParams(collective_id=collective, has_side_effects=True),
    )(sums)


def local(
    shape,
    features, image_counts, map_sides,
    split_kernel, split_gain, split_shift, inner_kernel, inner_gain, inner_shift,
    spread_kernel, spread_gain, spread_shift, transition_kernel, transition_gain, transition_shift,
    output_kernel, output_gain, output_shift, cotangent,
):
    slots, side, _, full = features.shape
    half = inner_kernel.shape[0]
    pitch = round_up(-(-slots * side * side // TILES), 16)
    count = TILES * pitch
    grid = (TILES,)
    row = jnp.arange(count)
    slot, place = row % slots, row // slots
    y, x = place // side, place % side
    sides = map_sides[slot]
    keep = (slot < image_counts[0]) & (y < sides) & (x < sides) & (place < side * side)
    mask = jnp.broadcast_to(keep.astype(F32)[:, None], (count, 128))
    lane = jnp.arange(128)[None, :]
    edges = jnp.where(lane == 0, (x > 0)[:, None], jnp.where(lane == 2, (x < side - 1)[:, None], True)).astype(F32)
    features = features.transpose(1, 2, 0, 3).reshape(side * side, slots, full)
    cotangent = cotangent.transpose(1, 2, 0, 3).reshape(side * side, slots, full)
    (split_gain, split_shift, inner_gain, inner_shift, spread_gain, spread_shift, transition_gain, transition_shift, output_gain, output_shift) = (
        item.reshape(1, -1)
        for item in (split_gain, split_shift, inner_gain, inner_shift, spread_gain, spread_shift, transition_gain, transition_shift, output_gain, output_shift)
    )
    spread_weight = spread_kernel.reshape(9, half, half)

    def group(sums):
        return gather_sums(sums, shape[1], 1 if sums.shape[1] == full else 2)

    sums_full, sums_half = out_whole((8, full)), out_whole((8, half))
    r_half, r_full, r_mask = rows(pitch, half), rows(pitch, full), rows(pitch, 128)
    pair_half, pair_full = rows2(pitch, half), rows2(pitch, full)

    def call(body, ins, outs, scratch=(), steps=grid):
        return pl.pallas_call(
            body,
            grid=steps,
            in_specs=[spec for _, spec in ins],
            out_specs=[spec for _, spec in outs],
            out_shape=[shape for shape, _ in outs],
            scratch_shapes=list(scratch),
            compiler_params=params(),
        )(*[array for array, _ in ins])

    def fixed(array):
        return (array, whole(array))

    x0, z_split, s_split = call(
        split_kernel_body,
        [(features, pixels(pitch, features.shape)), (mask, r_mask), fixed(split_kernel)],
        [(sds((count, full), BF16), r_full), (sds((count, full)), r_full), (sds((8, full)), sums_full)],
        [pltpu.VMEM((pitch, full), F32)],
    )
    s_split = group(s_split)
    part2, main, main2, z_inner, s_inner = call(
        inner_body,
        [(z_split, r_full), fixed(s_split), fixed(split_gain), fixed(split_shift), (mask, r_mask), fixed(inner_kernel)],
        [
            (sds((2, count, half), BF16), pair_half), (sds((count, half)), r_half), (sds((2, count, half), BF16), pair_half),
            (sds((count, half)), r_half), (sds((8, half)), sums_half),
        ],
    )
    s_inner = group(s_inner)
    tap_spec = pl.BlockSpec((1, half, half), lambda i: (i, 0, 0))
    inner2, z_spread, s_spread = call(
        functools.partial(spread_body, side, slots),
        [fixed(z_inner), fixed(s_split), fixed(s_inner), fixed(inner_gain), fixed(inner_shift), fixed(mask), fixed(edges), (spread_weight, tap_spec)],
        [(sds((2, count, half), BF16), out_whole((2, count, half))), (sds((count, half)), out_whole((count, half))), (sds((8, half)), sums_half)],
        [pltpu.VMEM((count + 2 * GUARD, half), F32), pltpu.VMEM((2, count, half), BF16)],
        (9,),
    )
    s_spread = group(s_spread)
    joined2, z_trans, s_trans = call(
        transition_body,
        [(z_spread, r_half), fixed(s_split), fixed(s_spread), fixed(spread_gain), fixed(spread_shift), (mask, r_mask), (main, r_half), fixed(transition_kernel)],
        [(sds((2, count, half), BF16), pair_half), (sds((count, half)), r_half), (sds((8, half)), sums_half)],
    )
    s_trans = group(s_trans)
    trans2, z_out, s_out = call(
        output_body,
        [(z_trans, r_half), fixed(s_split), fixed(s_trans), fixed(transition_gain), fixed(transition_shift), (mask, r_mask), (part2, pair_half), fixed(output_kernel)],
        [(sds((2, count, half), BF16), pair_half), (sds((count, full)), r_full), (sds((8, full)), sums_full)],
    )
    s_out = group(s_out)
    result, dy_out, q_out = call(
        result_body,
        [(z_out, r_full), fixed(s_split), fixed(s_out), fixed(output_gain), fixed(output_shift), (mask, r_mask), (cotangent, pixels(pitch, cotangent.shape))],
        [(sds(cotangent.shape), pixels(pitch, cotangent.shape)), (sds((count, full)), r_full), (sds((8, full)), sums_full)],
        [pltpu.VMEM((pitch, full), F32)],
    )
    q_out = group(q_out)
    dz_out, dy_trans, dy_part, q_mid = call(
        output_back_body,
        [
            (dy_out, r_full), (z_out, r_full), fixed(s_out), fixed(output_gain), fixed(q_out), fixed(s_split), (mask, r_mask), fixed(output_kernel),
            (z_trans, r_half), fixed(s_trans), fixed(transition_gain), fixed(transition_shift), (z_split, rows(pitch, half, 0)), fixed(split_gain), fixed(split_shift),
        ],
        [(sds((2, count, full), BF16), pair_full), (sds((count, half)), r_half), (sds((count, half)), r_half), (sds((8, full)), sums_full)],
        [pltpu.VMEM((pitch, full), F32)],
    )
    q_mid = group(q_mid)
    dz_trans, dz_part, grad_joined, dy_spread, q_spread = call(
        transition_back_body,
        [
            (dy_trans, r_half), (dy_part, r_half), (z_trans, r_half), fixed(s_trans), fixed(transition_gain), fixed(q_mid), fixed(s_split), (mask, r_mask), fixed(transition_kernel),
            (z_split, rows(pitch, half, 0)), fixed(split_gain), (z_spread, r_half), fixed(s_spread), fixed(spread_gain), fixed(spread_shift),
        ],
        [
            (sds((2, count, half), BF16), pair_half), (sds((2, count, half), BF16), pair_half), (sds((count, half)), r_half),
            (sds((count, half)), r_half), (sds((8, half)), sums_half),
        ],
    )
    q_spread = group(q_spread)
    moved_spec = pl.BlockSpec((1, 2, count, half), lambda i: (i, 0, 0, 0))
    moved, dy_inner, q_inner = call(
        functools.partial(spread_back_body, side, slots),
        [
            fixed(dy_spread), fixed(z_spread), fixed(s_spread), fixed(spread_gain), fixed(q_spread), fixed(s_split), fixed(mask), fixed(edges), (spread_weight, tap_spec),
            fixed(z_inner), fixed(s_inner), fixed(inner_gain), fixed(inner_shift),
        ],
        [(sds((9, 2, count, half), BF16), moved_spec), (sds((count, half)), out_whole((count, half))), (sds((8, half)), sums_half)],
        [pltpu.VMEM((count + 2 * GUARD, half), F32), pltpu.VMEM((count, half), F32)],
        (9,),
    )
    q_inner = group(q_inner)
    dz_inner, dy_main, q_main = call(
        inner_back_body,
        [
            (dy_inner, r_half), (z_inner, r_half), fixed(s_inner), fixed(inner_gain), fixed(q_inner), fixed(s_split), (mask, r_mask), fixed(inner_kernel),
            (grad_joined, r_half), (z_split, rows(pitch, half, 1)), fixed(split_gain), fixed(split_shift),
        ],
        [(sds((2, count, half), BF16), pair_half), (sds((count, half)), r_half), (sds((8, half)), sums_half)],
        [pltpu.VMEM((pitch, half), F32)],
    )
    q_main = group(q_main)
    dz_main, grad_features = call(
        split_back_body,
        [(dy_main, r_half), (z_split, rows(pitch, half, 1)), fixed(q_main), fixed(s_split), fixed(split_gain), (mask, r_mask), (dz_part, pair_half), fixed(split_kernel)],
        [(sds((2, count, half), BF16), pair_half), (sds(cotangent.shape), pixels(pitch, cotangent.shape))],
        [pltpu.VMEM((pitch, full), F32)],
    )
    small = jnp.concatenate([q_mid[0:2, half:], q_main[0:2], q_inner[0:2], q_spread[0:2], q_mid[0:2, :half], q_out[0:2]], axis=1)
    if shape == (8, 4):
        low, high = slice(0, half), slice(half, full)
        every = slice(None)
        lefts = [trans2, part2, joined2, x0[None], inner2, main2]
        rights = [dz_out, dz_trans, dz_part, moved, dz_inner, dz_main]
        jobs = [((0, every, 2), (0, low), (4, (low, low))), ((0, every, 2), (0, high), (4, (low, high)))]
        jobs += [((1, every, 2), (0, low), (4, (high, low))), ((1, every, 2), (0, high), (4, (high, high)))]
        jobs += [((2, every, 2), (1, every), (3, (every, every)))]
        jobs += [((3, low, 1), (2, every), (0, (low, low))), ((3, high, 1), (2, every), (0, (high, low)))]
        jobs += [((4, every, 2), ((3, tap), None), (2, (tap,))) for tap in range(9)]
        jobs += [((5, every, 2), (4, every), (1, (every, every)))]
        jobs += [((3, low, 1), (5, every), (0, (low, high))), ((3, high, 1), (5, every), (0, (high, high)))]
        shapes = [(full, full), (half, half), (9, half, half), (half, half), (full, full)]
        grad_split, grad_inner, grad_spread, grad_transition, grad_output = reduce_call(jobs, lefts, rights, shapes, count, half)
        small = gather_sums(jnp.pad(small, ((0, 6), (0, 0))), shape[0], 4, "dp")
    else:
        grad_output = jnp.concatenate([weight_grad(trans2, dz_out), weight_grad(part2, dz_out)], axis=0)
        grad_transition, grad_inner = weight_grad(joined2, dz_trans), weight_grad(main2, dz_inner)
        grad_split = jnp.concatenate([weight_grad(x0[None], dz_part), weight_grad(x0[None], dz_main)], axis=1)
        grad_spread = jnp.stack([weight_grad(inner2, moved[tap]) for tap in range(9)])
        grad_split, grad_inner, grad_spread, grad_transition, grad_output = lax.psum(
            (grad_split, grad_inner, grad_spread, grad_transition, grad_output), ("dp", "bn")
        )
        small = lax.psum(small, "dp")
    cuts = [0, full, full + half, full + 2 * half, full + 3 * half, 2 * full + 3 * half]
    shifts = [small[0, a:b] for a, b in zip(cuts[:-1], cuts[1:])]
    gains = [small[1, a:b] for a, b in zip(cuts[:-1], cuts[1:])]
    result, grad_features = (item.reshape(side, side, slots, full).transpose(2, 0, 1, 3) for item in (result, grad_features))
    return (
        result, grad_features,
        grad_split, gains[0], shifts[0], grad_inner, gains[1], shifts[1],
        grad_spread.reshape(3, 3, half, half), gains[2], shifts[2], grad_transition, gains[3], shifts[3], grad_output, gains[4], shifts[4],
    )


def solution(mesh):
    shard, copy = P(("dp", "bn")), P()
    return jax.shard_map(
        functools.partial(local, (mesh.shape["dp"], mesh.shape["bn"])),
        mesh=mesh,
        in_specs=(shard, shard, shard) + (copy,) * 15 + (shard,),
        out_specs=(shard, shard) + (copy,) * 15,
        check_vma=False,
    )
```

```python
import functools

import jax
import jax.numpy as jnp
from jax import lax
from jax.experimental import pallas as pl
from jax.experimental.pallas import tpu as pltpu
from jax.sharding import PartitionSpec as P

EPS = 1e-05
GUARD = 80
CHUNK = 16
TILES = 4
MESH = pl.DeviceIdType.MESH
F32 = jnp.float32
BF16 = jnp.bfloat16


def round_up(value, step):
    return -(-value // step) * step


def params(megabytes=56):
    return pltpu.CompilerParams(vmem_limit_bytes=megabytes * 1024 * 1024)


def whole(array):
    zeros = (0,) * len(array.shape)
    return pl.BlockSpec(array.shape, lambda *_: zeros, pipeline_mode=pl.Buffered(1))


def out_whole(shape):
    zeros = (0,) * len(shape)
    return pl.BlockSpec(shape, lambda *_: zeros)


def rows(pitch, width, column=0):
    return pl.BlockSpec((pitch, width), lambda i: (i, column))


def rows2(pitch, width):
    return pl.BlockSpec((2, pitch, width), lambda i: (0, i, 0))


def pixels(pitch, shape):
    return pl.BlockSpec((pitch // shape[1],) + tuple(shape[1:]), lambda i: (i, 0, 0))


def sds(shape, dtype=F32):
    return jax.ShapeDtypeStruct(tuple(shape), dtype)


def dot(left, right):
    return jnp.dot(left, right, preferred_element_type=F32)


def dot_t(left, right):
    return lax.dot_general(left, right, (((1,), (1,)), ((), ())), preferred_element_type=F32)


def split_store(ref, place, value):
    high = value.astype(BF16)
    ref[(0,) + place] = high
    ref[(1,) + place] = (value - high.astype(F32)).astype(BF16)


def moments(stats_ref, total, columns):
    mean = stats_ref[0:1, columns] / total
    square = stats_ref[1:2, columns] / total
    return mean, lax.rsqrt(square - mean * mean + EPS)


def mish(y):
    t = jnp.exp(jnp.minimum(y, 30.0))
    n = t * (t + 2.0)
    return y * (n / (n + 2.0))


def mish_slope(y):
    t = jnp.exp(jnp.minimum(y, 30.0))
    n = t * (t + 2.0)
    r = 1.0 / (n + 2.0)
    return n * r + y * (((4.0 * t) * (t + 1.0) * r) * r)


def fold(value):
    return jnp.sum(value.reshape(value.shape[0] // 8, 8, value.shape[1]), axis=0)


def over_rows(count, body, carry=None, unroll=2):
    def step(k, c):
        return body(pl.ds(pl.multiple_of(k * CHUNK, CHUNK), CHUNK), c)

    return lax.fori_loop(0, count // CHUNK, step, carry, unroll=unroll)


def column_blocks(width, block=512):
    return [slice(c, c + block) for c in range(0, width, block)]


def add_sums(sums_ref, columns, pieces):
    for k, piece in enumerate(pieces):
        sums_ref[k : k + 1, columns] += jnp.sum(piece, axis=0, keepdims=True)


def start_sums(sums_ref):
    @pl.when(pl.program_id(0) == 0)
    def _():
        sums_ref[...] = jnp.zeros_like(sums_ref)


def sum_squares(z_ref, sums_ref, mask_ref=None):
    for columns in column_blocks(z_ref.shape[1]):
        width = columns.stop - columns.start

        def body(r, carry):
            value = z_ref[r, columns]
            kept = value if mask_ref is None else value * mask_ref[r, 0:1]
            return (carry[0] + fold(kept), carry[1] + fold(kept * value))

        zero = jnp.zeros((8, width), F32)
        add_sums(sums_ref, columns, over_rows(z_ref.shape[0], body, (zero, zero)))


def product2(ref, place, weight):
    high = ref[(0,) + place]
    low = ref[(1,) + place]
    return dot(high, weight) + dot(low, weight)


def product2_t(ref, place, weight):
    high = ref[(0,) + place]
    low = ref[(1,) + place]
    return dot_t(high, weight) + dot_t(low, weight)


def compact(source_ref, scratch_ref):
    places, slots, _ = source_ref.shape
    for p in range(places):
        scratch_ref[p * slots : (p + 1) * slots, :] = source_ref[p].astype(F32)


def spread_out(scratch_ref, target_ref):
    places, slots, _ = target_ref.shape
    for p in range(places):
        target_ref[p] = scratch_ref[p * slots : (p + 1) * slots, :]


def split_kernel_body(features_ref, mask_ref, w_ref, x_ref, z_ref, sums_ref, scratch_ref):
    compact(features_ref, scratch_ref)

    def body(r, _):
        x_ref[r, :] = jnp.where(mask_ref[r, 0:1] > 0.0, scratch_ref[r, :], 0.0).astype(BF16)

    over_rows(x_ref.shape[0], body)
    z_ref[...] = dot(x_ref[...], w_ref[...])
    start_sums(sums_ref)
    sum_squares(z_ref, sums_ref)
    count = jnp.sum(mask_ref[...], axis=0, keepdims=True)
    sums_ref[2:3, 0:128] += count


def inner_body(z_ref, stats_ref, gain_ref, shift_ref, mask_ref, w_ref, part_ref, main_ref, main2_ref, zi_ref, sums_ref):
    total = stats_ref[2:3, 0:1]
    half = w_ref.shape[0]
    for index, columns in enumerate(column_blocks(2 * half, half)):
        mean, inverse = moments(stats_ref, total, columns)
        scale, shift = gain_ref[0:1, columns] * inverse, shift_ref[0:1, columns]

        def body(r, _):
            act = mish((z_ref[r, columns] - mean) * scale + shift) * mask_ref[r, 0:1]
            if index == 0:
                split_store(part_ref, (r,), act)
            else:
                main_ref[r, :] = act
                split_store(main2_ref, (r,), act)

        over_rows(z_ref.shape[0], body)
    zi_ref[...] = product2(main2_ref, (), w_ref[...])
    start_sums(sums_ref)
    sum_squares(zi_ref, sums_ref)


def taps(side, slots):
    return [((dy * side + dx) * slots, dx) for dy in (-1, 0, 1) for dx in (-1, 0, 1)]


def move_rows(padded_ref, edge_ref, pair_ref, side, slots, sign):
    count = pair_ref.shape[1]
    for index, (move, dx) in enumerate(taps(side, slots)):

        @pl.when(pl.program_id(0) == index)
        def _(move=sign * move, dx=sign * dx):
            moved = padded_ref[GUARD + move : GUARD + move + count, :]
            if dx:
                moved = moved * edge_ref[:, dx + 1 : dx + 2]
            split_store(pair_ref, (slice(None),), moved)


def spread_body(side, slots, z_ref, total_ref, stats_ref, gain_ref, shift_ref, mask_ref, edge_ref, w_ref, inner_ref, zs_ref, sums_ref, padded_ref, pair_ref):
    total = total_ref[2:3, 0:1]
    count = z_ref.shape[0]
    tap = pl.program_id(0)

    @pl.when(tap == 0)
    def _():
        mean, inverse = moments(stats_ref, total, slice(None))
        scale, shift = gain_ref[...] * inverse, shift_ref[...]
        padded_ref[0:GUARD, :] = jnp.zeros((GUARD, padded_ref.shape[1]), F32)
        padded_ref[GUARD + count :, :] = jnp.zeros((GUARD, padded_ref.shape[1]), F32)

        def body(r, _):
            act = mish((z_ref[r, :] - mean) * scale + shift) * mask_ref[r, 0:1]
            padded_ref[pl.ds(r.start + GUARD, CHUNK), :] = act
            split_store(inner_ref, (r,), act)

        over_rows(count, body)
        zs_ref[...] = jnp.zeros_like(zs_ref)

    move_rows(padded_ref, edge_ref, pair_ref, side, slots, 1)
    zs_ref[...] += product2(pair_ref, (), w_ref[0])

    @pl.when(tap == pl.num_programs(0) - 1)
    def _():
        sums_ref[...] = jnp.zeros_like(sums_ref)
        sum_squares(zs_ref, sums_ref, mask_ref)


def transition_body(z_ref, total_ref, stats_ref, gain_ref, shift_ref, mask_ref, main_ref, w_ref, joined_ref, zt_ref, sums_ref):
    total = total_ref[2:3, 0:1]
    mean, inverse = moments(stats_ref, total, slice(None))
    scale, shift = gain_ref[...] * inverse, shift_ref[...]

    def body(r, _):
        act = mish((z_ref[r, :] - mean) * scale + shift) * mask_ref[r, 0:1]
        split_store(joined_ref, (r,), act + main_ref[r, :])

    over_rows(z_ref.shape[0], body)
    zt_ref[...] = product2(joined_ref, (), w_ref[...])
    start_sums(sums_ref)
    sum_squares(zt_ref, sums_ref)


def output_body(z_ref, total_ref, stats_ref, gain_ref, shift_ref, mask_ref, part_ref, w_ref, trans_ref, zo_ref, sums_ref):
    total = total_ref[2:3, 0:1]
    mean, inverse = moments(stats_ref, total, slice(None))
    scale, shift = gain_ref[...] * inverse, shift_ref[...]
    half = z_ref.shape[1]

    def body(r, _):
        act = mish((z_ref[r, :] - mean) * scale + shift) * mask_ref[r, 0:1]
        split_store(trans_ref, (r,), act)

    over_rows(z_ref.shape[0], body)
    zo_ref[...] = product2(part_ref, (), w_ref[half:, :])
    zo_ref[...] += product2(trans_ref, (), w_ref[:half, :])
    start_sums(sums_ref)
    sum_squares(zo_ref, sums_ref)


def result_body(z_ref, total_ref, stats_ref, gain_ref, shift_ref, mask_ref, cotangent_ref, result_ref, dy_ref, sums_ref, scratch_ref):
    total = total_ref[2:3, 0:1]
    compact(cotangent_ref, scratch_ref)
    start_sums(sums_ref)
    for columns in column_blocks(z_ref.shape[1]):
        mean, inverse = moments(stats_ref, total, columns)
        gain, shift = gain_ref[0:1, columns], shift_ref[0:1, columns]

        def body(r, carry):
            mask = mask_ref[r, 0:1]
            scaled = (z_ref[r, columns] - mean) * inverse
            y = scaled * gain + shift
            t = jnp.exp(jnp.minimum(y, 30.0))
            n = t * (t + 2.0)
            inv = 1.0 / (n + 2.0)
            ratio = n * inv
            slope = ratio + y * (((4.0 * t) * (t + 1.0) * inv) * inv)
            dy = jnp.where(mask > 0.0, scratch_ref[r, columns], 0.0) * slope
            scratch_ref[r, columns] = y * ratio * mask
            dy_ref[r, columns] = dy
            return (carry[0] + fold(dy), carry[1] + fold(dy * scaled))

        zero = jnp.zeros((8, columns.stop - columns.start), F32)
        add_sums(sums_ref, columns, over_rows(z_ref.shape[0], body, (zero, zero)))
    spread_out(scratch_ref, result_ref)


def norm_slope(z_ref, grad, mask_ref, r, columns, mean, inverse, gain, shift):
    scaled = (z_ref[r, columns] - mean) * inverse
    dy = grad * mask_ref[r, 0:1] * mish_slope(scaled * gain + shift)
    return dy, (fold(dy), fold(dy * scaled))


def settle(dy, z, mask, mean, inverse, factor, first, second):
    scaled = (z - mean) * inverse
    return mask * factor * (dy - (first + scaled * second))


def output_back_body(dy_ref, zo_ref, so_ref, go_ref, qo_ref, total_ref, mask_ref, w_ref, zt_ref, st_ref, gt_ref, bt_ref, zp_ref, gp_ref, bp_ref, dz_ref, dyt_ref, dyp_ref, sums_ref, grad_ref):
    total = total_ref[2:3, 0:1]
    for columns in column_blocks(zo_ref.shape[1]):
        mean, inverse = moments(so_ref, total, columns)
        factor = go_ref[0:1, columns] * inverse
        first, second = qo_ref[0:1, columns] / total, qo_ref[1:2, columns] / total

        def body(r, _):
            dz = settle(dy_ref[r, columns], zo_ref[r, columns], mask_ref[r, 0:1], mean, inverse, factor, first, second)
            split_store(dz_ref, (r, columns), dz)

        over_rows(zo_ref.shape[0], body)
    grad_ref[...] = product2_t(dz_ref, (), w_ref[...])
    start_sums(sums_ref)
    half = zt_ref.shape[1]
    for index, (z_ref, s_ref, g_ref, b_ref, out_ref) in enumerate(((zt_ref, st_ref, gt_ref, bt_ref, dyt_ref), (zp_ref, total_ref, gp_ref, bp_ref, dyp_ref))):
        columns = slice(index * half, (index + 1) * half)
        own = slice(0, half)
        mean, inverse = moments(s_ref, total, own)
        gain, shift = g_ref[0:1, own], b_ref[0:1, own]

        def body(r, carry):
            dy, sums = norm_slope(z_ref, grad_ref[r, columns], mask_ref, r, own, mean, inverse, gain, shift)
            out_ref[r, :] = dy
            return (carry[0] + sums[0], carry[1] + sums[1])

        zero = jnp.zeros((8, half), F32)
        add_sums(sums_ref, columns, over_rows(zt_ref.shape[0], body, (zero, zero)))


def transition_back_body(dyt_ref, dyp_ref, zt_ref, st_ref, gt_ref, q_ref, total_ref, mask_ref, w_ref, zp_ref, gp_ref, zs_ref, ss_ref, gs_ref, bs_ref, dz_ref, dzp_ref, grad_ref, dys_ref, sums_ref):
    total = total_ref[2:3, 0:1]
    half = zt_ref.shape[1]
    own = slice(0, half)
    for index, (dy_ref, z_ref, s_ref, g_ref, out_ref) in enumerate(((dyt_ref, zt_ref, st_ref, gt_ref, dz_ref), (dyp_ref, zp_ref, total_ref, gp_ref, dzp_ref))):
        columns = slice(index * half, (index + 1) * half)
        mean, inverse = moments(s_ref, total, own)
        factor = g_ref[0:1, own] * inverse
        first, second = q_ref[0:1, columns] / total, q_ref[1:2, columns] / total

        def body(r, _):
            dz = settle(dy_ref[r, :], z_ref[r, :], mask_ref[r, 0:1], mean, inverse, factor, first, second)
            split_store(out_ref, (r,), dz)

        over_rows(zt_ref.shape[0], body)
    grad_ref[...] = product2_t(dz_ref, (), w_ref[...])
    start_sums(sums_ref)
    mean, inverse = moments(ss_ref, total, own)
    gain, shift = gs_ref[...], bs_ref[...]

    def tail(r, carry):
        dy, sums = norm_slope(zs_ref, grad_ref[r, :], mask_ref, r, own, mean, inverse, gain, shift)
        dys_ref[r, :] = dy
        return (carry[0] + sums[0], carry[1] + sums[1])

    zero = jnp.zeros((8, half), F32)
    add_sums(sums_ref, own, over_rows(zt_ref.shape[0], tail, (zero, zero)))


def spread_back_body(side, slots, dy_ref, z_ref, s_ref, g_ref, q_ref, total_ref, mask_ref, edge_ref, w_ref, zi_ref, si_ref, gi_ref, bi_ref, moved_ref, dyi_ref, sums_ref, padded_ref, grad_ref):
    total = total_ref[2:3, 0:1]
    count, half = z_ref.shape
    tap = pl.program_id(0)

    @pl.when(tap == 0)
    def _():
        padded_ref[0:GUARD, :] = jnp.zeros((GUARD, half), F32)
        padded_ref[GUARD + count :, :] = jnp.zeros((GUARD, half), F32)
        mean, inverse = moments(s_ref, total, slice(None))
        factor = g_ref[...] * inverse
        first, second = q_ref[0:1, :] / total, q_ref[1:2, :] / total

        def body(r, _):
            dz = settle(dy_ref[r, :], z_ref[r, :], mask_ref[r, 0:1], mean, inverse, factor, first, second)
            padded_ref[pl.ds(r.start + GUARD, CHUNK), :] = dz

        over_rows(count, body)
        grad_ref[...] = jnp.zeros_like(grad_ref)

    move_rows(padded_ref, edge_ref, moved_ref.at[0], side, slots, -1)
    grad_ref[...] += product2_t(moved_ref.at[0], (), w_ref[0])

    @pl.when(tap == pl.num_programs(0) - 1)
    def _():
        sums_ref[...] = jnp.zeros_like(sums_ref)
        own = slice(0, half)
        mean, inverse = moments(si_ref, total, own)
        gain, shift = gi_ref[...], bi_ref[...]

        def tail(r, carry):
            dy, sums = norm_slope(zi_ref, grad_ref[r, :], mask_ref, r, own, mean, inverse, gain, shift)
            dyi_ref[r, :] = dy
            return (carry[0] + sums[0], carry[1] + sums[1])

        zero = jnp.zeros((8, half), F32)
        add_sums(sums_ref, own, over_rows(count, tail, (zero, zero)))


def inner_back_body(dy_ref, zi_ref, si_ref, gi_ref, q_ref, total_ref, mask_ref, w_ref, joined_ref, zm_ref, gm_ref, bm_ref, dz_ref, dym_ref, sums_ref, grad_ref):
    total = total_ref[2:3, 0:1]
    half = zi_ref.shape[1]
    own = slice(0, half)
    upper = slice(half, 2 * half)
    mean, inverse = moments(si_ref, total, own)
    factor = gi_ref[...] * inverse
    first, second = q_ref[0:1, :] / total, q_ref[1:2, :] / total

    def body(r, _):
        dz = settle(dy_ref[r, :], zi_ref[r, :], mask_ref[r, 0:1], mean, inverse, factor, first, second)
        split_store(dz_ref, (r,), dz)

    over_rows(zi_ref.shape[0], body)
    grad_ref[...] = product2_t(dz_ref, (), w_ref[...])
    start_sums(sums_ref)
    mean, inverse = moments(total_ref, total, upper)
    gain, shift = gm_ref[0:1, upper], bm_ref[0:1, upper]

    def tail(r, carry):
        dy, sums = norm_slope(zm_ref, grad_ref[r, :] + joined_ref[r, :], mask_ref, r, own, mean, inverse, gain, shift)
        dym_ref[r, :] = dy
        return (carry[0] + sums[0], carry[1] + sums[1])

    zero = jnp.zeros((8, half), F32)
    add_sums(sums_ref, own, over_rows(zi_ref.shape[0], tail, (zero, zero)))


def split_back_body(dy_ref, zm_ref, q_ref, total_ref, g_ref, mask_ref, dzp_ref, w_ref, dz_ref, grad_ref, scratch_ref):
    total = total_ref[2:3, 0:1]
    half = zm_ref.shape[1]
    upper = slice(half, 2 * half)
    mean, inverse = moments(total_ref, total, upper)
    factor = g_ref[0:1, upper] * inverse
    first, second = q_ref[0:1, :] / total, q_ref[1:2, :] / total

    def body(r, _):
        dz = settle(dy_ref[r, :], zm_ref[r, :], mask_ref[r, 0:1], mean, inverse, factor, first, second)
        split_store(dz_ref, (r,), dz)

    over_rows(zm_ref.shape[0], body)
    scratch_ref[...] = product2_t(dzp_ref, (), w_ref[:, :half])
    scratch_ref[...] += product2_t(dz_ref, (), w_ref[:, half:])
    spread_out(scratch_ref, grad_ref)


def weight_body(x_ref, dz_ref, dw_ref):
    turned = x_ref[0].T
    value = dot(turned, dz_ref[0]) + dot(turned, dz_ref[1])
    if x_ref.shape[0] == 2:
        value += dot(x_ref[1].T, dz_ref[0])
    dw_ref[...] = value


def weight_grad(x, dz, block=256):
    parts, count, width = x.shape
    wide = dz.shape[2]
    return pl.pallas_call(
        weight_body,
        grid=(width // block,),
        in_specs=[pl.BlockSpec((parts, count, block), lambda i: (0, 0, i)), whole(dz)],
        out_specs=pl.BlockSpec((block, wide), lambda i: (i, 0)),
        out_shape=sds((width, wide)),
        compiler_params=params(),
    )(x, dz)


LAG = 8
KEPT = 6


def reduce_body(jobs, side, slots, *refs):
    lefts, rights, refs = refs[:6], refs[6:9], refs[9:]
    (dys_hbm, zs_hbm, zi_hbm, gj_hbm, zm_hbm, ws_hbm), refs = refs[:6], refs[6:]
    (s_split, s_spread, g_spread, q_spread, s_inner, g_inner, b_inner, g_split, b_split, q_out, q_mid, mask_ref, edge_ref, wi_ref, w_ref), refs = refs[:15], refs[15:]
    outs, features_hbm, vectors_ref, refs = refs[:5], refs[5], refs[6], refs[7:]
    (x_ref, z_ref, turned_ref, own_ref, r0_ref, half_ref, r1_ref, quarter_ref, r2_ref, eighth_ref, r3_ref, full_ref, load_sem, store_sem) = refs[:14]
    (padded_ref, grad_ref, page_ref, tile_ref, zm_ref, pair_ref, part_ref, wide_ref, staged_ref, tap_ref, sums_ref, shared_ref, small_ref, spread_ref) = refs[14:28]
    (page_sem, tap_sem, part_sem, staged_sem, sum_send, sum_recv, small_send, small_recv) = refs[28:36]
    sems = refs[36:]
    count, half = grad_ref.shape
    pitch = tile_ref.shape[1]
    tiles = count // pitch
    stats_total = s_split[2:3, 0:1]
    block = own_ref.shape[1]
    mid = block // 2
    dp, bn = lax.axis_index("dp"), lax.axis_index("bn")
    z, x, y, core = dp // 2, dp % 2, bn // 2, bn % 2

    def at(new_z, new_x, new_y, new_core):
        return {"dp": new_z * 2 + new_x, "bn": new_y * 2 + new_core}

    to_core, to_x, to_y = at(z, x, y, 1 - core), at(z, 1 - x, y, core), at(z, x, 1 - y, core)
    depth = [(z + k) % 4 for k in (1, 2, 3)]
    to_z = [at(new_z, x, y, core) for new_z in depth]
    to_far = [at(new_z, 1 - x, y, core) for new_z in depth]
    to_diagonal = at(z, x, 1 - y, 1 - core)
    columns = (pl.ds(0, mid), pl.ds(mid, mid))

    def part(start, size):
        return pl.ds(pl.multiple_of(start, size), size)

    def far(stage, k, slot, source, target, peer):
        send, recv = sems[2 * stage], sems[2 * stage + 1]
        return pltpu.make_async_remote_copy(
            src_ref=source, dst_ref=target, send_sem=send.at[k, slot], recv_sem=recv.at[k, slot], device_id=peer, device_id_type=MESH
        )

    first = (x, y)
    second = (y, x)
    sides = (to_x, to_y)

    def copies(stage, c):
        slot, keep = c % 2, c % KEPT
        base = core * (block // 2)
        if stage == 0:
            return [far(0, 0, slot, own_ref.at[slot, part((1 - core) * (block // 2), block // 2)], r0_ref.at[slot], to_core)]
        if stage == 1:
            return [
                far(1, k, slot, half_ref.at[slot, part((1 - first[k]) * (block // 4), block // 4), columns[k]], r1_ref.at[slot, :, columns[k]], sides[k])
                for k in (0, 1)
            ]
        if stage == 2:
            return [
                far(2, k, slot, quarter_ref.at[slot, part((1 - second[k]) * (block // 8), block // 8), columns[k]], r2_ref.at[slot, :, columns[k]], sides[1 - k])
                for k in (0, 1)
            ]
        if stage == 3:
            return [
                far(3, k, slot, eighth_ref.at[slot, part(depth[k] * (block // 32), block // 32)], r3_ref.at[slot, k], to_z[k]) for k in (0, 1, 2)
            ]
        made = []
        for k in (0, 1):
            eighth = base + first[k] * (block // 4) + second[k] * (block // 8)
            if stage == 4:
                spot = full_ref.at[keep, part(eighth + z * (block // 32), block // 32), columns[k]]
                made += [far(4, 3 * k + d, slot, spot, spot, to_z[d]) for d in (0, 1, 2)]
            elif stage == 5:
                spot = full_ref.at[keep, part(eighth, block // 8), columns[k]]
                made.append(far(5, k, slot, spot, spot, sides[1 - k]))
            elif stage == 6:
                spot = full_ref.at[keep, part(base + first[k] * (block // 4), block // 4), columns[k]]
                made.append(far(6, k, slot, spot, spot, sides[k]))
        if stage == 7:
            spot = full_ref.at[keep, part(base, block // 2)]
            made.append(far(7, 0, slot, spot, spot, to_core))
        return made

    def begin(stage, c):
        for copy in copies(stage, c):
            copy.start()

    def finish(stage, c):
        for copy in copies(stage, c):
            copy.wait()

    def load(j):
        (left, left_columns, parts), right, _ = jobs[j]
        slot = j % 2
        made = [pltpu.make_async_copy(lefts[left].at[0:parts, :, left_columns], x_ref.at[slot, 0:parts], load_sem.at[slot, 0])]
        if right == "pair":
            made.append(pltpu.make_async_copy(pair_ref, z_ref.at[slot], load_sem.at[slot, 1]))
        elif right is not None:
            made.append(pltpu.make_async_copy(rights[right[0]].at[:, :, right[1]], z_ref.at[slot], load_sem.at[slot, 1]))
        return made

    def store(j):
        out, spot = jobs[j][2]
        return pltpu.make_async_copy(full_ref.at[j % KEPT], outs[out].at[spot], store_sem.at[j % KEPT])


    everything = slice(None)

    def page(source, target, k):
        return pltpu.make_async_copy(source, target, page_sem.at[k])

    def tap_load(tap):
        return pltpu.make_async_copy(ws_hbm.at[tap], tap_ref.at[tap % 2], tap_sem.at[tap % 2])

    upper = slice(half, 2 * half)
    load_dy, load_zs = page(dys_hbm, grad_ref, 0), page(zs_hbm, page_ref, 1)
    load_zi, load_zm = page(zi_hbm, page_ref, 1), page(zm_hbm.at[:, upper], zm_ref, 2)

    def joined_load(k):
        return pltpu.make_async_copy(gj_hbm.at[k * pitch : (k + 1) * pitch], tile_ref.at[k % 2], part_sem.at[0, k % 2])

    def part_load(k):
        return pltpu.make_async_copy(rights[2].at[:, k * pitch : (k + 1) * pitch], part_ref.at[k % 2], part_sem.at[1, k % 2])

    places = staged_ref.shape[0]

    def staged_store(k):
        size = min(places, features_hbm.shape[0] - k * places)
        return pltpu.make_async_copy(staged_ref.at[0:size], features_hbm.at[k * places : k * places + size], staged_sem)

    group = [at(z, x, y, 1 - core), at(z, x, 1 - y, core), to_diagonal]

    def sum_copies(which):
        return [
            pltpu.make_async_remote_copy(
                src_ref=sums_ref.at[which], dst_ref=shared_ref.at[which, bn], send_sem=sum_send.at[which, k], recv_sem=sum_recv.at[which, k], device_id=peer, device_id_type=MESH
            )
            for k, peer in enumerate(group)
        ]

    def sum_start(which):
        for copy in sum_copies(which):
            copy.start()
        shared_ref[which, bn] = sums_ref[which]

    def sum_finish(which):
        for copy in sum_copies(which):
            copy.wait()
        value = shared_ref[which, 0]
        for k in range(1, shared_ref.shape[1]):
            value = value + shared_ref[which, k]
        sums_ref[which] = value

    everyone = [to_x] + to_z + to_far

    def small_copies():
        return [
            pltpu.make_async_remote_copy(
                src_ref=small_ref, dst_ref=spread_ref.at[dp], send_sem=small_send.at[k], recv_sem=small_recv.at[k], device_id=peer, device_id_type=MESH
            )
            for k, peer in enumerate(everyone)
        ]

    def prepare():
        load_dy.wait()
        load_zs.wait()
        padded_ref[0:GUARD, :] = jnp.zeros((GUARD, half), F32)
        padded_ref[GUARD + count :, :] = jnp.zeros((GUARD, half), F32)
        mean, inverse = moments(s_spread, stats_total, everything)
        factor = g_spread[...] * inverse
        first_sum, second_sum = q_spread[0:1, :] / stats_total, q_spread[1:2, :] / stats_total

        def body(r, _):
            dz = settle(grad_ref[r, :], page_ref[r, :], mask_ref[r, 0:1], mean, inverse, factor, first_sum, second_sum)
            padded_ref[pl.ds(r.start + GUARD, CHUNK), :] = dz

        over_rows(count, body)
        load_zi.start()
        load_zm.start()

    def tap_work(tap):
        move, dx = taps(side, slots)[tap]
        slot = tap % 2
        moved = padded_ref[GUARD - move : GUARD - move + count, :]
        if dx:
            moved = moved * edge_ref[:, 1 - dx : 2 - dx]
        high = moved.astype(BF16)
        z_ref[slot, 0] = high
        z_ref[slot, 1] = (moved - high.astype(F32)).astype(BF16)
        tap_load(tap).wait()
        if tap < 8:
            tap_load(tap + 1).start()

    def tap_gradient(slot):
        grad_ref[...] += dot_t(z_ref[slot, 0], tap_ref[slot]) + dot_t(z_ref[slot, 1], tap_ref[slot])

    def inner_slope():
        load_zi.wait()
        joined_load(0).start()
        joined_load(1).start()
        mean, inverse = moments(s_inner, stats_total, everything)
        gain, shift = g_inner[...], b_inner[...]

        def tail(r, carry):
            dy, sums = norm_slope(page_ref, grad_ref[r, :], mask_ref, r, everything, mean, inverse, gain, shift)
            grad_ref[r, :] = dy
            return (carry[0] + sums[0], carry[1] + sums[1])

        zero = jnp.zeros((8, half), F32)
        sums_ref[...] = jnp.zeros_like(sums_ref)
        add_sums(sums_ref.at[0], everything, over_rows(count, tail, (zero, zero)))
        sum_start(0)

    def shifted(k):
        return lambda r: pl.ds(pl.multiple_of(r.start + k * pitch, CHUNK), CHUNK)

    def inner_tile(k):
        mean, inverse = moments(s_inner, stats_total, everything)
        factor = g_inner[...] * inverse
        first_sum, second_sum = sums_ref[0, 0:1, :] / stats_total, sums_ref[0, 1:2, :] / stats_total
        here = shifted(k)

        def body(r, _):
            q = here(r)
            dz = settle(grad_ref[q, :], page_ref[q, :], mask_ref[q, 0:1], mean, inverse, factor, first_sum, second_sum)
            split_store(pair_ref, (q,), dz)

        over_rows(pitch, body)
        rows_k = slice(k * pitch, (k + 1) * pitch)
        wide_ref[:, 0:half] = product2_t(pair_ref, (rows_k,), wi_ref[...])
        joined_load(k).wait()
        mean, inverse = moments(s_split, stats_total, upper)
        gain, shift = g_split[0:1, upper], b_split[0:1, upper]

        def tail(r, carry):
            q = here(r)
            dy, sums = norm_slope(zm_ref, wide_ref[r, 0:half] + tile_ref[k % 2, r, :], mask_ref, q, everything, mean, inverse, gain, shift)
            grad_ref[q, :] = dy
            return (carry[0] + sums[0], carry[1] + sums[1])

        zero = jnp.zeros((8, half), F32)
        add_sums(sums_ref.at[1], everything, over_rows(pitch, tail, (zero, zero)))
        if k + 2 < tiles:
            joined_load(k + 2).start()

    def small_start():
        pieces = [
            (q_mid, slice(half, 2 * half)), (sums_ref.at[1], everything), (sums_ref.at[0], everything), (q_spread, everything),
            (q_mid, slice(0, half)), (q_out, slice(0, half)), (q_out, slice(half, 2 * half)),
        ]
        small_ref[...] = jnp.zeros_like(small_ref)
        for k, (ref, columns_k) in enumerate(pieces):
            small_ref[k : k + 1, :] = ref[0:1, columns_k]
            small_ref[8 + k : 9 + k, :] = ref[1:2, columns_k]
        for copy in small_copies():
            copy.start()
        spread_ref[dp] = small_ref[...]

    def small_finish():
        for copy in small_copies():
            copy.wait()
        value = spread_ref[0]
        for k in range(1, spread_ref.shape[0]):
            value = value + spread_ref[k]
        vectors_ref[...] = value

    def split_tile(k):
        mean, inverse = moments(s_split, stats_total, upper)
        factor = g_split[0:1, upper] * inverse
        first_sum, second_sum = sums_ref[1, 0:1, :] / stats_total, sums_ref[1, 1:2, :] / stats_total
        here = shifted(k)

        def body(r, _):
            q = here(r)
            dz = settle(grad_ref[q, :], zm_ref[q, :], mask_ref[q, 0:1], mean, inverse, factor, first_sum, second_sum)
            split_store(pair_ref, (q,), dz)

        over_rows(pitch, body)
        part_load(k).wait()
        wide_ref[...] = dot_t(part_ref[k % 2, 0], w_ref[:, 0:half]) + dot_t(part_ref[k % 2, 1], w_ref[:, 0:half])
        wide_ref[...] += product2_t(pair_ref, (slice(k * pitch, (k + 1) * pitch),), w_ref[:, half:])
        if k + 2 < tiles:
            part_load(k + 2).start()
        if k:
            staged_store(k - 1).wait()
        spread_out(wide_ref, staged_ref)
        staged_store(k).start()

    def first_parts():
        part_load(0).start()
        part_load(1).start()

    hosted = {
        9: [inner_slope],
        10: [lambda: (load_zm.wait(), sum_finish(0)), functools.partial(inner_tile, 0), functools.partial(inner_tile, 1)],
        11: [functools.partial(inner_tile, 2), functools.partial(inner_tile, 3), lambda: sum_start(1)],
        12: [lambda: sum_finish(1), small_start, first_parts],
        14: [functools.partial(split_tile, 0), functools.partial(split_tile, 1)],
        15: [functools.partial(split_tile, 2), functools.partial(split_tile, 3)],
        16: [lambda: staged_store(3).wait()],
        18: [small_finish],
    }

    load_dy.start()
    load_zs.start()
    tap_load(0).start()
    for copy in load(0):
        copy.start()
    barrier = pltpu.get_barrier_semaphore()
    peers = [to_core, to_x, to_y] + to_z + to_far + [to_diagonal]
    for peer in peers:
        pl.semaphore_signal(barrier, inc=1, device_id=peer, device_id_type=MESH)
    pl.semaphore_wait(barrier, len(peers))
    prepare()
    grad_ref[...] = jnp.zeros_like(grad_ref)
    total = len(jobs)

    @pl.loop(0, total + LAG + 1)
    def _(t):
        for j in range(total):

            @pl.when(t == j + LAG + 1)
            def _(j=j):
                store(j).wait()

        def stage(number, lag):
            def wrap(body):
                c = t - lag
                pl.when(jnp.logical_and(c >= 0, c < total))(lambda: body(c))

            return wrap

        @stage(7, 8)
        def _(c):
            finish(7, c)

        for j in range(total):

            @pl.when(t == j + LAG)
            def _(j=j):
                store(j).start()

        for number in (6, 5, 4):

            @stage(number, number + 1)
            def _(c, number=number):
                finish(number, c)
                begin(number + 1, c)

        @stage(3, 4)
        def _(c):
            finish(3, c)
            slot, keep = c % 2, c % KEPT
            value = eighth_ref[slot, part(z * (block // 32), block // 32), :]
            for k in (0, 1, 2):
                value = value + r3_ref[slot, k]
            for k in (0, 1):
                row = core * (block // 2) + first[k] * (block // 4) + second[k] * (block // 8) + z * (block // 32)
                full_ref[keep, part(row, block // 32), k * mid : (k + 1) * mid] = value[:, k * mid : (k + 1) * mid]
            begin(4, c)

        @stage(2, 3)
        def _(c):
            finish(2, c)
            slot = c % 2
            for k in (0, 1):
                eighth_ref[slot, :, columns[k]] = quarter_ref[slot, part(second[k] * (block // 8), block // 8), columns[k]] + r2_ref[slot, :, columns[k]]
            begin(3, c)

        @stage(1, 2)
        def _(c):
            finish(1, c)
            slot = c % 2
            for k in (0, 1):
                quarter_ref[slot, :, columns[k]] = half_ref[slot, part(first[k] * (block // 4), block // 4), columns[k]] + r1_ref[slot, :, columns[k]]
            begin(2, c)

        @stage(0, 1)
        def _(c):
            finish(0, c)
            slot = c % 2
            half_ref[slot] = own_ref[slot, part(core * (block // 2), block // 2), :] + r0_ref[slot]
            begin(1, c)

        for j in range(total):

            @pl.when(t == j)
            def _(j=j):
                for copy in load(j):
                    copy.wait()
                for task in hosted.get(j, ()):
                    task()
                if j + 1 < total:
                    for copy in load(j + 1):
                        copy.start()
                if j < 9:
                    tap_work(j)

        @pl.when(t < 9)
        def _():
            tap_gradient(t % 2)

        exact = functools.reduce(jnp.logical_or, [t == j for j in range(total) if jobs[j][0][2] == 1])

        @stage(None, 0)
        def _(c):
            slot = c % 2
            turned_ref[...] = x_ref[slot, 0].T
            own_ref[slot] = dot(turned_ref[...], z_ref[slot, 0]) + dot(turned_ref[...], z_ref[slot, 1])

            @pl.when(jnp.logical_not(exact))
            def _():
                turned_ref[...] = x_ref[slot, 1].T
                own_ref[slot] += dot(turned_ref[...], z_ref[slot, 0])

            begin(0, c)


def reduce_call(jobs, lefts, rights, hosted, constants, shapes, side, slots, pixel_shape):
    hbm, vmem_spec = pl.BlockSpec(memory_space=pl.ANY), pl.BlockSpec(memory_space=pltpu.VMEM)
    vmem, dma = pltpu.VMEM, pltpu.SemaphoreType.DMA
    count, block = hosted[0].shape
    pitch = count // TILES
    scratch = [
        vmem((2, 2, count, block), BF16), vmem((2, 2, count, block), BF16), vmem((block, count), BF16),
        vmem((2, block, block), F32), vmem((2, block // 2, block), F32), vmem((2, block // 2, block), F32),
        vmem((2, block // 4, block), F32), vmem((2, block // 4, block), F32), vmem((2, block // 8, block), F32), vmem((2, block // 8, block), F32),
        vmem((2, 3, block // 32, block), F32), vmem((KEPT, block, block), F32),
        dma((2, 2)), dma((KEPT,)),
        vmem((count + 2 * GUARD, block), F32), vmem((count, block), F32), vmem((count, block), F32), vmem((2, pitch, block), F32),
        vmem((count, block), F32), vmem((2, count, block), BF16), vmem((2, 2, pitch, block), BF16), vmem((pitch, 2 * block), F32),
        vmem((pitch // slots, slots, 2 * block), F32), vmem((2, block, block), BF16), vmem((2, 8, block), F32), vmem((2, 4, 8, block), F32),
        vmem((16, block), F32), vmem((8, 16, block), F32),
        dma((3,)), dma((2,)), dma((2, 2)), dma(()), dma((2, 3)), dma((2, 3)), dma((7,)), dma((7,)),
    ]
    for width in (1, 2, 2, 3, 6, 2, 2, 1):
        scratch += [dma((width, 2)), dma((width, 2))]
    return pl.pallas_call(
        functools.partial(reduce_body, jobs, side, slots),
        in_specs=[hbm] * (len(lefts) + len(rights) + len(hosted)) + [vmem_spec] * len(constants),
        out_specs=[hbm] * (len(shapes) + 1) + [vmem_spec],
        out_shape=[sds(shape) for shape in shapes] + [sds(pixel_shape), sds((16, block))],
        scratch_shapes=scratch,
        compiler_params=pltpu.CompilerParams(collective_id=3, has_side_effects=True, vmem_limit_bytes=60 * 1024 * 1024),
    )(*lefts, *rights, *hosted, *constants)


def gather_sums_body(axis, sums_ref, out_ref, slots_ref, send_sem, recv_sem):
    members = slots_ref.shape[0]
    me = lax.axis_index(axis)
    peers = [lax.rem(me + k, members) for k in range(1, members)]
    barrier = pltpu.get_barrier_semaphore()
    for peer in peers:
        pl.semaphore_signal(barrier, inc=1, device_id={axis: peer}, device_id_type=MESH)
    pl.semaphore_wait(barrier, members - 1)
    copies = [
        pltpu.make_async_remote_copy(
            src_ref=sums_ref, dst_ref=slots_ref.at[me], send_sem=send_sem.at[k], recv_sem=recv_sem.at[k], device_id={axis: peer}, device_id_type=MESH
        )
        for k, peer in enumerate(peers)
    ]
    for copy in copies:
        copy.start()
    slots_ref[me] = sums_ref[...]
    for copy in copies:
        copy.wait()
    value = slots_ref[0]
    for k in range(1, members):
        value = value + slots_ref[k]
    out_ref[...] = value


def gather_sums(sums, members, collective, axis="bn"):
    if members == 1:
        return sums
    spec = pl.BlockSpec(memory_space=pltpu.VMEM)
    return pl.pallas_call(
        functools.partial(gather_sums_body, axis),
        in_specs=[spec],
        out_specs=spec,
        out_shape=sds(sums.shape),
        scratch_shapes=[pltpu.VMEM((members,) + sums.shape, F32), pltpu.SemaphoreType.DMA((members - 1,)), pltpu.SemaphoreType.DMA((members - 1,))],
        compiler_params=pltpu.CompilerParams(collective_id=collective, has_side_effects=True),
    )(sums)


def local(
    shape,
    features, image_counts, map_sides,
    split_kernel, split_gain, split_shift, inner_kernel, inner_gain, inner_shift,
    spread_kernel, spread_gain, spread_shift, transition_kernel, transition_gain, transition_shift,
    output_kernel, output_gain, output_shift, cotangent,
):
    slots, side, _, full = features.shape
    half = inner_kernel.shape[0]
    pitch = round_up(-(-slots * side * side // TILES), 16)
    count = TILES * pitch
    grid = (TILES,)
    row = jnp.arange(count)
    slot, place = row % slots, row // slots
    y, x = place // side, place % side
    sides = map_sides[slot]
    keep = (slot < image_counts[0]) & (y < sides) & (x < sides) & (place < side * side)
    mask = jnp.broadcast_to(keep.astype(F32)[:, None], (count, 128))
    lane = jnp.arange(128)[None, :]
    edges = jnp.where(lane == 0, (x > 0)[:, None], jnp.where(lane == 2, (x < side - 1)[:, None], True)).astype(F32)
    features = features.transpose(1, 2, 0, 3).reshape(side * side, slots, full)
    cotangent = cotangent.transpose(1, 2, 0, 3).reshape(side * side, slots, full)
    (split_gain, split_shift, inner_gain, inner_shift, spread_gain, spread_shift, transition_gain, transition_shift, output_gain, output_shift) = (
        item.reshape(1, -1)
        for item in (split_gain, split_shift, inner_gain, inner_shift, spread_gain, spread_shift, transition_gain, transition_shift, output_gain, output_shift)
    )
    spread_weight = spread_kernel.reshape(9, half, half)

    def group(sums):
        return gather_sums(sums, shape[1], 1 if sums.shape[1] == full else 2)

    sums_full, sums_half = out_whole((8, full)), out_whole((8, half))
    r_half, r_full, r_mask = rows(pitch, half), rows(pitch, full), rows(pitch, 128)
    pair_half, pair_full = rows2(pitch, half), rows2(pitch, full)

    def call(body, ins, outs, scratch=(), steps=grid):
        return pl.pallas_call(
            body,
            grid=steps,
            in_specs=[spec for _, spec in ins],
            out_specs=[spec for _, spec in outs],
            out_shape=[shape for shape, _ in outs],
            scratch_shapes=list(scratch),
            compiler_params=params(),
        )(*[array for array, _ in ins])

    def fixed(array):
        return (array, whole(array))

    x0, z_split, s_split = call(
        split_kernel_body,
        [(features, pixels(pitch, features.shape)), (mask, r_mask), fixed(split_kernel)],
        [(sds((count, full), BF16), r_full), (sds((count, full)), r_full), (sds((8, full)), sums_full)],
        [pltpu.VMEM((pitch, full), F32)],
    )
    s_split = group(s_split)
    part2, main, main2, z_inner, s_inner = call(
        inner_body,
        [(z_split, r_full), fixed(s_split), fixed(split_gain), fixed(split_shift), (mask, r_mask), fixed(inner_kernel)],
        [
            (sds((2, count, half), BF16), pair_half), (sds((count, half)), r_half), (sds((2, count, half), BF16), pair_half),
            (sds((count, half)), r_half), (sds((8, half)), sums_half),
        ],
    )
    s_inner = group(s_inner)
    tap_spec = pl.BlockSpec((1, half, half), lambda i: (i, 0, 0))
    inner2, z_spread, s_spread = call(
        functools.partial(spread_body, side, slots),
        [fixed(z_inner), fixed(s_split), fixed(s_inner), fixed(inner_gain), fixed(inner_shift), fixed(mask), fixed(edges), (spread_weight, tap_spec)],
        [(sds((2, count, half), BF16), out_whole((2, count, half))), (sds((count, half)), out_whole((count, half))), (sds((8, half)), sums_half)],
        [pltpu.VMEM((count + 2 * GUARD, half), F32), pltpu.VMEM((2, count, half), BF16)],
        (9,),
    )
    s_spread = group(s_spread)
    joined2, z_trans, s_trans = call(
        transition_body,
        [(z_spread, r_half), fixed(s_split), fixed(s_spread), fixed(spread_gain), fixed(spread_shift), (mask, r_mask), (main, r_half), fixed(transition_kernel)],
        [(sds((2, count, half), BF16), pair_half), (sds((count, half)), r_half), (sds((8, half)), sums_half)],
    )
    s_trans = group(s_trans)
    trans2, z_out, s_out = call(
        output_body,
        [(z_trans, r_half), fixed(s_split), fixed(s_trans), fixed(transition_gain), fixed(transition_shift), (mask, r_mask), (part2, pair_half), fixed(output_kernel)],
        [(sds((2, count, half), BF16), pair_half), (sds((count, full)), r_full), (sds((8, full)), sums_full)],
    )
    s_out = group(s_out)
    result, dy_out, q_out = call(
        result_body,
        [(z_out, r_full), fixed(s_split), fixed(s_out), fixed(output_gain), fixed(output_shift), (mask, r_mask), (cotangent, pixels(pitch, cotangent.shape))],
        [(sds(cotangent.shape), pixels(pitch, cotangent.shape)), (sds((count, full)), r_full), (sds((8, full)), sums_full)],
        [pltpu.VMEM((pitch, full), F32)],
    )
    q_out = group(q_out)
    dz_out, dy_trans, dy_part, q_mid = call(
        output_back_body,
        [
            (dy_out, r_full), (z_out, r_full), fixed(s_out), fixed(output_gain), fixed(q_out), fixed(s_split), (mask, r_mask), fixed(output_kernel),
            (z_trans, r_half), fixed(s_trans), fixed(transition_gain), fixed(transition_shift), (z_split, rows(pitch, half, 0)), fixed(split_gain), fixed(split_shift),
        ],
        [(sds((2, count, full), BF16), pair_full), (sds((count, half)), r_half), (sds((count, half)), r_half), (sds((8, full)), sums_full)],
        [pltpu.VMEM((pitch, full), F32)],
    )
    q_mid = group(q_mid)
    dz_trans, dz_part, grad_joined, dy_spread, q_spread = call(
        transition_back_body,
        [
            (dy_trans, r_half), (dy_part, r_half), (z_trans, r_half), fixed(s_trans), fixed(transition_gain), fixed(q_mid), fixed(s_split), (mask, r_mask), fixed(transition_kernel),
            (z_split, rows(pitch, half, 0)), fixed(split_gain), (z_spread, r_half), fixed(s_spread), fixed(spread_gain), fixed(spread_shift),
        ],
        [
            (sds((2, count, half), BF16), pair_half), (sds((2, count, half), BF16), pair_half), (sds((count, half)), r_half),
            (sds((count, half)), r_half), (sds((8, half)), sums_half),
        ],
    )
    q_spread = group(q_spread)
    if shape == (8, 4):
        low, high = slice(0, half), slice(half, full)
        every = slice(None)
        jobs = [((4, every, 2), None, (2, (tap,))) for tap in range(9)]
        jobs += [((0, every, 2), (0, low), (4, (low, low))), ((0, every, 2), (0, high), (4, (low, high)))]
        jobs += [((1, every, 2), (0, low), (4, (high, low))), ((1, every, 2), (0, high), (4, (high, high)))]
        jobs += [((5, every, 2), "pair", (1, (every, every))), ((2, every, 2), (1, every), (3, (every, every)))]
        jobs += [((3, low, 1), (2, every), (0, (low, low))), ((3, high, 1), (2, every), (0, (high, low)))]
        jobs += [((3, low, 1), "pair", (0, (low, high))), ((3, high, 1), "pair", (0, (high, high)))]
        grad_split, grad_inner, grad_spread, grad_transition, grad_output, grad_features, vectors = reduce_call(
            jobs,
            [trans2, part2, joined2, x0[None], inner2, main2],
            [dz_out, dz_trans, dz_part],
            [dy_spread, z_spread, z_inner, grad_joined, z_split, spread_weight],
            [
                s_split, s_spread, spread_gain, q_spread, s_inner, inner_gain, inner_shift, split_gain, split_shift, q_out, q_mid,
                mask, edges, inner_kernel, split_kernel,
            ],
            [(full, full), (half, half), (9, half, half), (half, half), (full, full)],
            side, slots, cotangent.shape,
        )
        small = vectors.reshape(2, 8 * half)
    else:
        moved_spec = pl.BlockSpec((1, 2, count, half), lambda i: (i, 0, 0, 0))
        moved, dy_inner, q_inner = call(
            functools.partial(spread_back_body, side, slots),
            [
                fixed(dy_spread), fixed(z_spread), fixed(s_spread), fixed(spread_gain), fixed(q_spread), fixed(s_split), fixed(mask), fixed(edges), (spread_weight, tap_spec),
                fixed(z_inner), fixed(s_inner), fixed(inner_gain), fixed(inner_shift),
            ],
            [(sds((9, 2, count, half), BF16), moved_spec), (sds((count, half)), out_whole((count, half))), (sds((8, half)), sums_half)],
            [pltpu.VMEM((count + 2 * GUARD, half), F32), pltpu.VMEM((count, half), F32)],
            (9,),
        )
        q_inner = group(q_inner)
        dz_inner, dy_main, q_main = call(
            inner_back_body,
            [
                (dy_inner, r_half), (z_inner, r_half), fixed(s_inner), fixed(inner_gain), fixed(q_inner), fixed(s_split), (mask, r_mask), fixed(inner_kernel),
                (grad_joined, r_half), (z_split, rows(pitch, half, 1)), fixed(split_gain), fixed(split_shift),
            ],
            [(sds((2, count, half), BF16), pair_half), (sds((count, half)), r_half), (sds((8, half)), sums_half)],
            [pltpu.VMEM((pitch, half), F32)],
        )
        q_main = group(q_main)
        dz_main, grad_features = call(
            split_back_body,
            [(dy_main, r_half), (z_split, rows(pitch, half, 1)), fixed(q_main), fixed(s_split), fixed(split_gain), (mask, r_mask), (dz_part, pair_half), fixed(split_kernel)],
            [(sds((2, count, half), BF16), pair_half), (sds(cotangent.shape), pixels(pitch, cotangent.shape))],
            [pltpu.VMEM((pitch, full), F32)],
        )
        small = jnp.concatenate([q_mid[0:2, half:], q_main[0:2], q_inner[0:2], q_spread[0:2], q_mid[0:2, :half], q_out[0:2]], axis=1)
        grad_output = jnp.concatenate([weight_grad(trans2, dz_out), weight_grad(part2, dz_out)], axis=0)
        grad_transition, grad_inner = weight_grad(joined2, dz_trans), weight_grad(main2, dz_inner)
        grad_split = jnp.concatenate([weight_grad(x0[None], dz_part), weight_grad(x0[None], dz_main)], axis=1)
        grad_spread = jnp.stack([weight_grad(inner2, moved[tap]) for tap in range(9)])
        grad_split, grad_inner, grad_spread, grad_transition, grad_output = lax.psum(
            (grad_split, grad_inner, grad_spread, grad_transition, grad_output), ("dp", "bn")
        )
        small = lax.psum(small, "dp")
    cuts = [0, full, full + half, full + 2 * half, full + 3 * half, 2 * full + 3 * half]
    shifts = [small[0, a:b] for a, b in zip(cuts[:-1], cuts[1:])]
    gains = [small[1, a:b] for a, b in zip(cuts[:-1], cuts[1:])]
    result, grad_features = (item.reshape(side, side, slots, full).transpose(2, 0, 1, 3) for item in (result, grad_features))
    return (
        result, grad_features,
        grad_split, gains[0], shifts[0], grad_inner, gains[1], shifts[1],
        grad_spread.reshape(3, 3, half, half), gains[2], shifts[2], grad_transition, gains[3], shifts[3], grad_output, gains[4], shifts[4],
    )


def solution(mesh):
    shard, copy = P(("dp", "bn")), P()
    return jax.shard_map(
        functools.partial(local, (mesh.shape["dp"], mesh.shape["bn"])),
        mesh=mesh,
        in_specs=(shard, shard, shard) + (copy,) * 15 + (shard,),
        out_specs=(shard, shard) + (copy,) * 15,
        check_vma=False,
    )
```

```python
import functools

import jax
import jax.numpy as jnp
import numpy as np
from jax import lax
from jax.experimental import pallas as pl
from jax.experimental.pallas import tpu as pltpu
from jax.sharding import PartitionSpec as P

EPS = 1e-05
GUARD = 80
CHUNK = 16
TILES = 4
MESH = pl.DeviceIdType.MESH
F32 = jnp.float32
BF16 = jnp.bfloat16


def round_up(value, step):
    return -(-value // step) * step


def params(megabytes=56):
    return pltpu.CompilerParams(vmem_limit_bytes=megabytes * 1024 * 1024)


def whole(array):
    zeros = (0,) * len(array.shape)
    return pl.BlockSpec(array.shape, lambda *_: zeros, pipeline_mode=pl.Buffered(1))


def out_whole(shape):
    zeros = (0,) * len(shape)
    return pl.BlockSpec(shape, lambda *_: zeros)


def rows(pitch, width, column=0):
    return pl.BlockSpec((pitch, width), lambda i: (i, column))


def rows2(pitch, width):
    return pl.BlockSpec((2, pitch, width), lambda i: (0, i, 0))


def pixels(pitch, shape):
    return pl.BlockSpec((pitch // shape[1],) + tuple(shape[1:]), lambda i: (i, 0, 0))


def sds(shape, dtype=F32):
    return jax.ShapeDtypeStruct(tuple(shape), dtype)


def dot(left, right):
    return jnp.dot(left, right, preferred_element_type=F32)


def dot_t(left, right):
    return lax.dot_general(left, right, (((1,), (1,)), ((), ())), preferred_element_type=F32)


def split_store(ref, place, value):
    high = value.astype(BF16)
    ref[(0,) + place] = high
    ref[(1,) + place] = (value - high.astype(F32)).astype(BF16)


def moments(stats_ref, total, columns):
    mean = stats_ref[0:1, columns] / total
    square = stats_ref[1:2, columns] / total
    return mean, lax.rsqrt(square - mean * mean + EPS)


def mish(y):
    t = jnp.exp(jnp.minimum(y, 30.0))
    n = t * (t + 2.0)
    return y * (n / (n + 2.0))


def mish_slope(y):
    t = jnp.exp(jnp.minimum(y, 30.0))
    n = t * (t + 2.0)
    r = 1.0 / (n + 2.0)
    return n * r + y * (((4.0 * t) * (t + 1.0) * r) * r)


def fold(value):
    return jnp.sum(value.reshape(value.shape[0] // 8, 8, value.shape[1]), axis=0)


def over_rows(count, body, carry=None, unroll=4):
    def step(k, c):
        return body(pl.ds(pl.multiple_of(k * CHUNK, CHUNK), CHUNK), c)

    return lax.fori_loop(0, count // CHUNK, step, carry, unroll=unroll)


def column_blocks(width, block=512):
    return [slice(c, c + block) for c in range(0, width, block)]


def add_sums(sums_ref, columns, pieces):
    for k, piece in enumerate(pieces):
        sums_ref[k : k + 1, columns] += jnp.sum(piece, axis=0, keepdims=True)


def start_sums(sums_ref):
    @pl.when(pl.program_id(0) == 0)
    def _():
        sums_ref[...] = jnp.zeros_like(sums_ref)


def sum_squares(z_ref, sums_ref, mask_ref=None):
    for columns in column_blocks(z_ref.shape[1]):
        width = columns.stop - columns.start

        def body(r, carry):
            value = z_ref[r, columns]
            kept = value if mask_ref is None else value * mask_ref[r, 0:1]
            return (carry[0] + fold(kept), carry[1] + fold(kept * value))

        zero = jnp.zeros((8, width), F32)
        add_sums(sums_ref, columns, over_rows(z_ref.shape[0], body, (zero, zero)))


def product2(ref, place, weight):
    high = ref[(0,) + place]
    low = ref[(1,) + place]
    return dot(high, weight) + dot(low, weight)


def product2_t(ref, place, weight):
    high = ref[(0,) + place]
    low = ref[(1,) + place]
    return dot_t(high, weight) + dot_t(low, weight)


def compact(source_ref, scratch_ref):
    places, slots, _ = source_ref.shape
    for p in range(places):
        scratch_ref[p * slots : (p + 1) * slots, :] = source_ref[p].astype(F32)


def spread_out(scratch_ref, target_ref):
    places, slots, _ = target_ref.shape
    for p in range(places):
        target_ref[p] = scratch_ref[p * slots : (p + 1) * slots, :]


def split_kernel_body(features_ref, mask_ref, w_ref, x_ref, z_ref, sums_ref, scratch_ref):
    compact(features_ref, scratch_ref)

    def body(r, _):
        x_ref[r, :] = jnp.where(mask_ref[r, 0:1] > 0.0, scratch_ref[r, :], 0.0).astype(BF16)

    over_rows(x_ref.shape[0], body)
    z_ref[...] = dot(x_ref[...], w_ref[...])
    start_sums(sums_ref)
    sum_squares(z_ref, sums_ref)
    count = jnp.sum(mask_ref[...], axis=0, keepdims=True)
    sums_ref[2:3, 0:128] += count


def inner_body(z_ref, stats_ref, gain_ref, shift_ref, mask_ref, w_ref, part_ref, main_ref, main2_ref, zi_ref, sums_ref):
    total = stats_ref[2:3, 0:1]
    half = w_ref.shape[0]
    for index, columns in enumerate(column_blocks(2 * half, half)):
        mean, inverse = moments(stats_ref, total, columns)
        scale, shift = gain_ref[0:1, columns] * inverse, shift_ref[0:1, columns]

        def body(r, _):
            act = mish((z_ref[r, columns] - mean) * scale + shift) * mask_ref[r, 0:1]
            if index == 0:
                split_store(part_ref, (r,), act)
            else:
                main_ref[r, :] = act
                split_store(main2_ref, (r,), act)

        over_rows(z_ref.shape[0], body)
    zi_ref[...] = product2(main2_ref, (), w_ref[...])
    start_sums(sums_ref)
    sum_squares(zi_ref, sums_ref)


def taps(side, slots):
    return [((dy * side + dx) * slots, dx) for dy in (-1, 0, 1) for dx in (-1, 0, 1)]


def move_rows(padded_ref, edge_ref, pair_ref, side, slots, sign):
    count = pair_ref.shape[1]
    for index, (move, dx) in enumerate(taps(side, slots)):

        @pl.when(pl.program_id(0) == index)
        def _(move=sign * move, dx=sign * dx):
            moved = padded_ref[GUARD + move : GUARD + move + count, :]
            if dx:
                moved = moved * edge_ref[:, dx + 1 : dx + 2]
            split_store(pair_ref, (slice(None),), moved)


def spread_body(side, slots, z_ref, total_ref, stats_ref, gain_ref, shift_ref, mask_ref, edge_ref, w_ref, inner_ref, zs_ref, sums_ref, padded_ref, pair_ref):
    total = total_ref[2:3, 0:1]
    count = z_ref.shape[0]
    tap = pl.program_id(0)

    @pl.when(tap == 0)
    def _():
        mean, inverse = moments(stats_ref, total, slice(None))
        scale, shift = gain_ref[...] * inverse, shift_ref[...]
        padded_ref[0:GUARD, :] = jnp.zeros((GUARD, padded_ref.shape[1]), F32)
        padded_ref[GUARD + count :, :] = jnp.zeros((GUARD, padded_ref.shape[1]), F32)

        def body(r, _):
            act = mish((z_ref[r, :] - mean) * scale + shift) * mask_ref[r, 0:1]
            padded_ref[pl.ds(r.start + GUARD, CHUNK), :] = act
            split_store(inner_ref, (r,), act)

        over_rows(count, body)
        zs_ref[...] = jnp.zeros_like(zs_ref)

    move_rows(padded_ref, edge_ref, pair_ref, side, slots, 1)
    zs_ref[...] += product2(pair_ref, (), w_ref[0])

    @pl.when(tap == pl.num_programs(0) - 1)
    def _():
        sums_ref[...] = jnp.zeros_like(sums_ref)
        sum_squares(zs_ref, sums_ref, mask_ref)


def transition_body(z_ref, total_ref, stats_ref, gain_ref, shift_ref, mask_ref, main_ref, w_ref, joined_ref, zt_ref, sums_ref):
    total = total_ref[2:3, 0:1]
    mean, inverse = moments(stats_ref, total, slice(None))
    scale, shift = gain_ref[...] * inverse, shift_ref[...]

    def body(r, _):
        act = mish((z_ref[r, :] - mean) * scale + shift) * mask_ref[r, 0:1]
        split_store(joined_ref, (r,), act + main_ref[r, :])

    over_rows(z_ref.shape[0], body)
    zt_ref[...] = product2(joined_ref, (), w_ref[...])
    start_sums(sums_ref)
    sum_squares(zt_ref, sums_ref)


def output_body(z_ref, total_ref, stats_ref, gain_ref, shift_ref, mask_ref, part_ref, w_ref, trans_ref, zo_ref, sums_ref):
    total = total_ref[2:3, 0:1]
    mean, inverse = moments(stats_ref, total, slice(None))
    scale, shift = gain_ref[...] * inverse, shift_ref[...]
    half = z_ref.shape[1]

    def body(r, _):
        act = mish((z_ref[r, :] - mean) * scale + shift) * mask_ref[r, 0:1]
        split_store(trans_ref, (r,), act)

    over_rows(z_ref.shape[0], body)
    zo_ref[...] = product2(part_ref, (), w_ref[half:, :])
    zo_ref[...] += product2(trans_ref, (), w_ref[:half, :])
    start_sums(sums_ref)
    sum_squares(zo_ref, sums_ref)


def result_body(z_ref, total_ref, stats_ref, gain_ref, shift_ref, mask_ref, cotangent_ref, result_ref, dy_ref, sums_ref, scratch_ref):
    total = total_ref[2:3, 0:1]
    compact(cotangent_ref, scratch_ref)
    start_sums(sums_ref)
    for columns in column_blocks(z_ref.shape[1]):
        mean, inverse = moments(stats_ref, total, columns)
        gain, shift = gain_ref[0:1, columns], shift_ref[0:1, columns]

        def body(r, carry):
            mask = mask_ref[r, 0:1]
            scaled = (z_ref[r, columns] - mean) * inverse
            y = scaled * gain + shift
            t = jnp.exp(jnp.minimum(y, 30.0))
            n = t * (t + 2.0)
            inv = 1.0 / (n + 2.0)
            ratio = n * inv
            slope = ratio + y * (((4.0 * t) * (t + 1.0) * inv) * inv)
            dy = jnp.where(mask > 0.0, scratch_ref[r, columns], 0.0) * slope
            scratch_ref[r, columns] = y * ratio * mask
            dy_ref[r, columns] = dy
            return (carry[0] + fold(dy), carry[1] + fold(dy * scaled))

        zero = jnp.zeros((8, columns.stop - columns.start), F32)
        add_sums(sums_ref, columns, over_rows(z_ref.shape[0], body, (zero, zero)))
    spread_out(scratch_ref, result_ref)


def norm_slope(z_ref, grad, mask_ref, r, columns, mean, inverse, gain, shift):
    scaled = (z_ref[r, columns] - mean) * inverse
    dy = grad * mask_ref[r, 0:1] * mish_slope(scaled * gain + shift)
    return dy, (fold(dy), fold(dy * scaled))


def settle(dy, z, mask, mean, inverse, factor, first, second):
    scaled = (z - mean) * inverse
    return mask * factor * (dy - (first + scaled * second))


def output_back_body(dy_ref, zo_ref, so_ref, go_ref, qo_ref, total_ref, mask_ref, w_ref, zt_ref, st_ref, gt_ref, bt_ref, zp_ref, gp_ref, bp_ref, dz_ref, dyt_ref, dyp_ref, sums_ref, grad_ref):
    total = total_ref[2:3, 0:1]
    for columns in column_blocks(zo_ref.shape[1]):
        mean, inverse = moments(so_ref, total, columns)
        factor = go_ref[0:1, columns] * inverse
        first, second = qo_ref[0:1, columns] / total, qo_ref[1:2, columns] / total

        def body(r, _):
            dz = settle(dy_ref[r, columns], zo_ref[r, columns], mask_ref[r, 0:1], mean, inverse, factor, first, second)
            split_store(dz_ref, (r, columns), dz)

        over_rows(zo_ref.shape[0], body)
    grad_ref[...] = product2_t(dz_ref, (), w_ref[...])
    start_sums(sums_ref)
    half = zt_ref.shape[1]
    for index, (z_ref, s_ref, g_ref, b_ref, out_ref) in enumerate(((zt_ref, st_ref, gt_ref, bt_ref, dyt_ref), (zp_ref, total_ref, gp_ref, bp_ref, dyp_ref))):
        columns = slice(index * half, (index + 1) * half)
        own = slice(0, half)
        mean, inverse = moments(s_ref, total, own)
        gain, shift = g_ref[0:1, own], b_ref[0:1, own]

        def body(r, carry):
            dy, sums = norm_slope(z_ref, grad_ref[r, columns], mask_ref, r, own, mean, inverse, gain, shift)
            out_ref[r, :] = dy
            return (carry[0] + sums[0], carry[1] + sums[1])

        zero = jnp.zeros((8, half), F32)
        add_sums(sums_ref, columns, over_rows(zt_ref.shape[0], body, (zero, zero)))


def transition_back_body(dyt_ref, dyp_ref, zt_ref, st_ref, gt_ref, q_ref, total_ref, mask_ref, w_ref, zp_ref, gp_ref, zs_ref, ss_ref, gs_ref, bs_ref, dz_ref, dzp_ref, grad_ref, dys_ref, sums_ref):
    total = total_ref[2:3, 0:1]
    half = zt_ref.shape[1]
    own = slice(0, half)
    for index, (dy_ref, z_ref, s_ref, g_ref, out_ref) in enumerate(((dyt_ref, zt_ref, st_ref, gt_ref, dz_ref), (dyp_ref, zp_ref, total_ref, gp_ref, dzp_ref))):
        columns = slice(index * half, (index + 1) * half)
        mean, inverse = moments(s_ref, total, own)
        factor = g_ref[0:1, own] * inverse
        first, second = q_ref[0:1, columns] / total, q_ref[1:2, columns] / total

        def body(r, _):
            dz = settle(dy_ref[r, :], z_ref[r, :], mask_ref[r, 0:1], mean, inverse, factor, first, second)
            split_store(out_ref, (r,), dz)

        over_rows(zt_ref.shape[0], body)
    grad_ref[...] = product2_t(dz_ref, (), w_ref[...])
    start_sums(sums_ref)
    mean, inverse = moments(ss_ref, total, own)
    gain, shift = gs_ref[...], bs_ref[...]

    def tail(r, carry):
        dy, sums = norm_slope(zs_ref, grad_ref[r, :], mask_ref, r, own, mean, inverse, gain, shift)
        dys_ref[r, :] = dy
        return (carry[0] + sums[0], carry[1] + sums[1])

    zero = jnp.zeros((8, half), F32)
    add_sums(sums_ref, own, over_rows(zt_ref.shape[0], tail, (zero, zero)))


def spread_back_body(side, slots, dy_ref, z_ref, s_ref, g_ref, q_ref, total_ref, mask_ref, edge_ref, w_ref, zi_ref, si_ref, gi_ref, bi_ref, moved_ref, dyi_ref, sums_ref, padded_ref, grad_ref):
    total = total_ref[2:3, 0:1]
    count, half = z_ref.shape
    tap = pl.program_id(0)

    @pl.when(tap == 0)
    def _():
        padded_ref[0:GUARD, :] = jnp.zeros((GUARD, half), F32)
        padded_ref[GUARD + count :, :] = jnp.zeros((GUARD, half), F32)
        mean, inverse = moments(s_ref, total, slice(None))
        factor = g_ref[...] * inverse
        first, second = q_ref[0:1, :] / total, q_ref[1:2, :] / total

        def body(r, _):
            dz = settle(dy_ref[r, :], z_ref[r, :], mask_ref[r, 0:1], mean, inverse, factor, first, second)
            padded_ref[pl.ds(r.start + GUARD, CHUNK), :] = dz

        over_rows(count, body)
        grad_ref[...] = jnp.zeros_like(grad_ref)

    move_rows(padded_ref, edge_ref, moved_ref.at[0], side, slots, -1)
    grad_ref[...] += product2_t(moved_ref.at[0], (), w_ref[0])

    @pl.when(tap == pl.num_programs(0) - 1)
    def _():
        sums_ref[...] = jnp.zeros_like(sums_ref)
        own = slice(0, half)
        mean, inverse = moments(si_ref, total, own)
        gain, shift = gi_ref[...], bi_ref[...]

        def tail(r, carry):
            dy, sums = norm_slope(zi_ref, grad_ref[r, :], mask_ref, r, own, mean, inverse, gain, shift)
            dyi_ref[r, :] = dy
            return (carry[0] + sums[0], carry[1] + sums[1])

        zero = jnp.zeros((8, half), F32)
        add_sums(sums_ref, own, over_rows(count, tail, (zero, zero)))


def inner_back_body(dy_ref, zi_ref, si_ref, gi_ref, q_ref, total_ref, mask_ref, w_ref, joined_ref, zm_ref, gm_ref, bm_ref, dz_ref, dym_ref, sums_ref, grad_ref):
    total = total_ref[2:3, 0:1]
    half = zi_ref.shape[1]
    own = slice(0, half)
    upper = slice(half, 2 * half)
    mean, inverse = moments(si_ref, total, own)
    factor = gi_ref[...] * inverse
    first, second = q_ref[0:1, :] / total, q_ref[1:2, :] / total

    def body(r, _):
        dz = settle(dy_ref[r, :], zi_ref[r, :], mask_ref[r, 0:1], mean, inverse, factor, first, second)
        split_store(dz_ref, (r,), dz)

    over_rows(zi_ref.shape[0], body)
    grad_ref[...] = product2_t(dz_ref, (), w_ref[...])
    start_sums(sums_ref)
    mean, inverse = moments(total_ref, total, upper)
    gain, shift = gm_ref[0:1, upper], bm_ref[0:1, upper]

    def tail(r, carry):
        dy, sums = norm_slope(zm_ref, grad_ref[r, :] + joined_ref[r, :], mask_ref, r, own, mean, inverse, gain, shift)
        dym_ref[r, :] = dy
        return (carry[0] + sums[0], carry[1] + sums[1])

    zero = jnp.zeros((8, half), F32)
    add_sums(sums_ref, own, over_rows(zi_ref.shape[0], tail, (zero, zero)))


def split_back_body(dy_ref, zm_ref, q_ref, total_ref, g_ref, mask_ref, dzp_ref, w_ref, dz_ref, grad_ref, scratch_ref):
    total = total_ref[2:3, 0:1]
    half = zm_ref.shape[1]
    upper = slice(half, 2 * half)
    mean, inverse = moments(total_ref, total, upper)
    factor = g_ref[0:1, upper] * inverse
    first, second = q_ref[0:1, :] / total, q_ref[1:2, :] / total

    def body(r, _):
        dz = settle(dy_ref[r, :], zm_ref[r, :], mask_ref[r, 0:1], mean, inverse, factor, first, second)
        split_store(dz_ref, (r,), dz)

    over_rows(zm_ref.shape[0], body)
    scratch_ref[...] = product2_t(dzp_ref, (), w_ref[:, :half])
    scratch_ref[...] += product2_t(dz_ref, (), w_ref[:, half:])
    spread_out(scratch_ref, grad_ref)


def features_body(dzp_ref, dzm_ref, w_ref, grad_ref, scratch_ref):
    half = dzp_ref.shape[2]
    scratch_ref[...] = product2_t(dzp_ref, (), w_ref[:, :half])
    scratch_ref[...] += product2_t(dzm_ref, (), w_ref[:, half:])
    spread_out(scratch_ref, grad_ref)


def weight_body(x_ref, dz_ref, dw_ref):
    turned = x_ref[0].T
    value = dot(turned, dz_ref[0]) + dot(turned, dz_ref[1])
    if x_ref.shape[0] == 2:
        value += dot(x_ref[1].T, dz_ref[0])
    dw_ref[...] = value


def weight_grad(x, dz, block=256):
    parts, count, width = x.shape
    wide = dz.shape[2]
    return pl.pallas_call(
        weight_body,
        grid=(width // block,),
        in_specs=[pl.BlockSpec((parts, count, block), lambda i: (0, 0, i)), whole(dz)],
        out_specs=pl.BlockSpec((block, wide), lambda i: (i, 0)),
        out_shape=sds((width, wide)),
        compiler_params=params(),
    )(x, dz)


SPLIT, INNER, SPREAD, TRANS, OUT, BACK_OUT = range(6)


def front_body(side, slots, *refs):
    (features_hbm, cotangent_hbm, w_split_hbm, w_inner_hbm, w_spread_hbm, w_trans_hbm, w_out_hbm), refs = refs[:7], refs[7:]
    (g_split, b_split, g_inner, b_inner, g_spread, b_spread, g_trans, b_trans, g_out, b_out, edge_ref, counts_ref, sides_ref), refs = refs[:13], refs[13:]
    (x_out, zp_out, zm_out, main_out, part_out, zi_out, inner_out, zs_out, joined_out, zt_out, trans_out, result_hbm, dlow_out, dhigh_out, total_ref, mask_ref), refs = refs[:16], refs[16:]
    (p0, p1, p2, p3, p4, p5, p6, p7, q0, q1, q2, q3, wide_ref, feature_ref, cot_ref, staged_ref), refs = refs[:16], refs[16:]
    (w_split, w_inner, w_spread, w_trans, w_out, local_ref, shared_ref), refs = refs[:7], refs[7:]
    weight_sem, feature_sem, cot_sem, staged_sem, out_sem, sum_send, sum_recv = refs
    count, half = p0.shape
    pitch = count // TILES
    places = pitch // slots
    low, high, everything = slice(0, half), slice(half, 2 * half), slice(None)
    dp, bn = lax.axis_index("dp"), lax.axis_index("bn")
    members = shared_ref.shape[1]
    group = [lax.rem(bn + k, members) for k in range(1, members)]

    weights = [
        pltpu.make_async_copy(source, target, weight_sem.at[k])
        for k, (source, target) in enumerate(
            ((w_split_hbm, w_split), (w_inner_hbm, w_inner), (w_spread_hbm, w_spread), (w_trans_hbm, w_trans), (w_out_hbm, w_out))
        )
    ]

    def rows_of(k):
        return min(places, features_hbm.shape[0] - k * places)

    def feature_load(k):
        size = rows_of(k)
        return pltpu.make_async_copy(features_hbm.at[k * places : k * places + size], feature_ref.at[k % 2, 0:size], feature_sem.at[k % 2])

    def cot_load(k):
        size = rows_of(k)
        return pltpu.make_async_copy(cotangent_hbm.at[k * places : k * places + size], cot_ref.at[0:size], cot_sem)

    def result_store(k):
        size = rows_of(k)
        return pltpu.make_async_copy(staged_ref.at[0:size], result_hbm.at[k * places : k * places + size], staged_sem)

    pending = {}

    def write(name, source, target):
        copy = pltpu.make_async_copy(source, target, out_sem.at[len(pending)])
        copy.start()
        pending[name] = [copy, True]

    def written(name):
        if pending[name][1]:
            pending[name][0].wait()
            pending[name][1] = False

    def sum_copies(which, width):
        return [
            pltpu.make_async_remote_copy(
                src_ref=local_ref.at[which, :, 0:width], dst_ref=shared_ref.at[which, bn, :, 0:width],
                send_sem=sum_send.at[which, k], recv_sem=sum_recv.at[which, k], device_id={"bn": peer}, device_id_type=MESH,
            )
            for k, peer in enumerate(group)
        ]

    def exchange(which, width, beside=None):
        copies = sum_copies(which, width)
        for copy in copies:
            copy.start()
        shared_ref[which, bn, :, 0:width] = local_ref[which, :, 0:width]
        if beside is not None:
            beside()
        for copy in copies:
            copy.wait()
        value = shared_ref[which, 0, :, 0:width]
        for k in range(1, members):
            value = value + shared_ref[which, k, :, 0:width]
        total_ref[which, :, 0:width] = value

    def stats(which):
        return total_ref.at[which]

    def affine(which, gain_ref, shift_ref, columns):
        mean, inverse = moments(stats(which), total_ref[SPLIT, 2:3, 0:1], columns)
        return mean, gain_ref[0:1, columns] * inverse, shift_ref[0:1, columns]

    def activate(z_ref, r, mean, scale, shift):
        return mish((z_ref[r, :] - mean) * scale + shift) * mask_ref[r, 0:1]

    feature_load(0).start()
    for k in (0, 1):
        weights[k].start()
    feature_load(1).start()
    barrier = pltpu.get_barrier_semaphore()
    for peer in group:
        pl.semaphore_signal(barrier, inc=1, device_id={"bn": peer}, device_id_type=MESH)
    local_ref[...] = jnp.zeros_like(local_ref)
    limits = [jnp.where(k < counts_ref[0], sides_ref[k], 0).astype(F32) for k in range(slots)]

    def mask_rows(r, _):
        index = (r.start + lax.broadcasted_iota(jnp.int32, (CHUNK, 128), 0)).astype(F32)
        place = jnp.floor((index + 0.5) * (1.0 / slots))
        slot = index - place * slots
        y = jnp.floor((place + 0.5) * (1.0 / side))
        x = place - y * side
        limit = jnp.zeros_like(index)
        for k in range(slots):
            limit = jnp.where(slot == k, limits[k], limit)
        mask_ref[r, :] = jnp.where(jnp.maximum(x, y) < limit, 1.0, 0.0)

    over_rows(count, mask_rows)
    for k in range(TILES):
        feature_load(k).wait()
        compact(feature_ref.at[k % 2], wide_ref)
        if k + 2 < TILES:
            feature_load(k + 2).start()
        here = pl.ds(k * pitch, pitch)

        def body(r, _, k=k):
            q = pl.ds(pl.multiple_of(r.start + k * pitch, CHUNK), CHUNK)
            for h, columns in enumerate((low, high)):
                q0[h, q, :] = jnp.where(mask_ref[q, 0:1] > 0.0, wide_ref[r, columns], 0.0).astype(BF16)

        over_rows(pitch, body)
    for k in (2, 3, 4):
        weights[k].start()
    cot_load(0).start()
    write("x", q0, x_out)
    weights[0].wait()
    p0[...] = dot(q0[0], w_split[low, low]) + dot(q0[1], w_split[high, low])
    p1[0:count, :] = dot(q0[0], w_split[low, high]) + dot(q0[1], w_split[high, high])
    write("zm", p1.at[0:count], zm_out)
    write("zp", p0, zp_out)

    def add_squares(which, z_ref, columns, masked=False):
        def body(r, carry):
            value = z_ref[r, :]
            kept = value * mask_ref[r, 0:1] if masked else value
            return (carry[0] + fold(kept), carry[1] + fold(kept * value))

        zero = jnp.zeros((8, half), F32)
        add_sums(local_ref.at[which], columns, over_rows(count, body, (zero, zero)))

    add_squares(SPLIT, p0, low)
    add_squares(SPLIT, p1, high)
    local_ref[SPLIT, 2:3, 0:128] = jnp.sum(mask_ref[...], axis=0, keepdims=True)
    pl.semaphore_wait(barrier, members - 1)
    exchange(SPLIT, 2 * half)

    mean, scale, shift = affine(SPLIT, g_split, b_split, high)

    def main_rows(r, _):
        act = activate(p1, r, mean, scale, shift)
        p2[r, :] = act
        split_store(q2, (r,), act)

    over_rows(count, main_rows)
    write("main", q2, main_out)
    weights[1].wait()
    p3[...] = product2(q2, (), w_inner[...])
    write("zi", p3, zi_out)
    add_squares(INNER, p3, low)
    mean_p, scale_p, shift_p = affine(SPLIT, g_split, b_split, low)

    def part_rows(r, _):
        split_store(q1, (r,), activate(p0, r, mean_p, scale_p, shift_p))

    exchange(INNER, half, lambda: over_rows(count, part_rows))
    write("part", q1, part_out)

    written("zm")
    written("x")
    mean_i, scale_i, shift_i = affine(INNER, g_inner, b_inner, low)
    p1[0:GUARD, :] = jnp.zeros((GUARD, half), F32)
    p1[GUARD + count :, :] = jnp.zeros((GUARD, half), F32)

    def inner_rows(r, _):
        act = activate(p3, r, mean_i, scale_i, shift_i)
        p1[pl.ds(r.start + GUARD, CHUNK), :] = act
        split_store(q0, (r,), act)

    over_rows(count, inner_rows)
    write("inner", q0, inner_out)
    weights[2].wait()
    written("zi")
    written("main")
    for tap, (move, dx) in enumerate(taps(side, slots)):
        if move:
            pair_ref = (q2, q3)[tap % 2]
            moved = p1[GUARD + move : GUARD + move + count, :]
            if dx:
                moved = moved * edge_ref[:, dx + 1 : dx + 2]
            split_store(pair_ref, (slice(None),), moved)
        else:
            pair_ref = q0
        part = product2(pair_ref, (), w_spread[tap])
        if tap == 0:
            p3[...] = part
        else:
            p3[...] += part
    write("zs", p3, zs_out)
    add_squares(SPREAD, p3, low, True)
    exchange(SPREAD, half)

    mean_s, scale_s, shift_s = affine(SPREAD, g_spread, b_spread, low)

    def joined_rows(r, _):
        split_store(q2, (r,), activate(p3, r, mean_s, scale_s, shift_s) + p2[r, :])

    over_rows(count, joined_rows)
    write("joined", q2, joined_out)
    weights[3].wait()
    p2[...] = product2(q2, (), w_trans[...])
    write("zt", p2, zt_out)
    add_squares(TRANS, p2, low)
    exchange(TRANS, half)

    mean_t, scale_t, shift_t = affine(TRANS, g_trans, b_trans, low)

    def trans_rows(r, _):
        split_store(q3, (r,), activate(p2, r, mean_t, scale_t, shift_t))

    over_rows(count, trans_rows)
    write("trans", q3, trans_out)
    weights[4].wait()
    for page, columns in ((p4, low), (p5, high)):
        page[...] = product2(q3, (), w_out[low, columns]) + product2(q1, (), w_out[high, columns])
        add_squares(OUT, page, columns)
    exchange(OUT, 2 * half)

    total = total_ref[SPLIT, 2:3, 0:1]
    for k in range(TILES):
        cot_load(k).wait()
        compact(cot_ref, wide_ref)
        if k + 1 < TILES:
            cot_load(k + 1).start()
        for page, slope_page, columns in ((p4, p6, low), (p5, p7, high)):
            mean_o, inverse_o = moments(stats(OUT), total, columns)
            gain, shift_o = g_out[0:1, columns], b_out[0:1, columns]

            def body(r, carry, k=k, page=page, slope_page=slope_page, columns=columns):
                q = pl.ds(pl.multiple_of(r.start + k * pitch, CHUNK), CHUNK)
                mask = mask_ref[q, 0:1]
                scaled = (page[q, :] - mean_o) * inverse_o
                y = scaled * gain + shift_o
                t = jnp.exp(jnp.minimum(y, 30.0))
                n = t * (t + 2.0)
                inv = 1.0 / (n + 2.0)
                ratio = n * inv
                slope = ratio + y * (((4.0 * t) * (t + 1.0) * inv) * inv)
                dy = jnp.where(mask > 0.0, wide_ref[r, columns], 0.0) * slope
                wide_ref[r, columns] = y * ratio * mask
                slope_page[q, :] = dy
                return (carry[0] + fold(dy), carry[1] + fold(dy * scaled))

            zero = jnp.zeros((8, half), F32)
            add_sums(local_ref.at[BACK_OUT], columns, over_rows(pitch, body, (zero, zero)))
        if k:
            result_store(k - 1).wait()
        spread_out(wide_ref, staged_ref)
        result_store(k).start()
    exchange(BACK_OUT, 2 * half)

    def settled(page, z_page, pair_ref, which, back, gain_ref, columns, back_columns):
        mean_k, inverse_k = moments(stats(which), total, columns)
        factor = gain_ref[0:1, columns] * inverse_k
        first, second = total_ref[back, 0:1, back_columns] / total, total_ref[back, 1:2, back_columns] / total

        def body(r, _):
            split_store(pair_ref, (r,), settle(page[r, :], z_page[r, :], mask_ref[r, 0:1], mean_k, inverse_k, factor, first, second))

        over_rows(count, body)

    written("inner")
    written("joined")
    settled(p6, p4, q0, OUT, BACK_OUT, g_out, low, low)
    settled(p7, p5, q2, OUT, BACK_OUT, g_out, high, high)
    write("dlow", q0, dlow_out)
    write("dhigh", q2, dhigh_out)
    result_store(TILES - 1).wait()
    for name in list(pending):
        written(name)


def front_call(arrays, constants, scalars, slots, side, count, members):
    hbm, vmem_spec = pl.BlockSpec(memory_space=pl.ANY), pl.BlockSpec(memory_space=pltpu.VMEM)
    vmem, dma = pltpu.VMEM, pltpu.SemaphoreType.DMA
    full = arrays[0].shape[2]
    half = full // 2
    pitch = count // TILES
    pair, page = sds((2, count, half), BF16), sds((count, half))
    outs = [pair, page, page, pair, pair, page, pair, page, pair, page, pair, sds(arrays[1].shape), pair, pair]
    scratch = [vmem((count, half), F32), vmem((count + 2 * GUARD, half), F32)] + [vmem((count, half), F32)] * 6
    scratch += [vmem((2, count, half), BF16)] * 4
    scratch += [
        vmem((pitch, full), F32), vmem((2, pitch // slots, slots, full), BF16), vmem((pitch // slots, slots, full), F32), vmem((pitch // slots, slots, full), F32),
        vmem((full, full), BF16), vmem((half, half), BF16), vmem((9, half, half), BF16), vmem((half, half), BF16), vmem((full, full), BF16),
        vmem((6, 8, full), F32), vmem((6, members, 8, full), F32),
        dma((5,)), dma((2,)), dma(()), dma(()), dma((16,)), dma((6, members - 1)), dma((6, members - 1)),
    ]
    return pl.pallas_call(
        functools.partial(front_body, side, slots),
        in_specs=[hbm] * len(arrays) + [vmem_spec] * len(constants) + [pl.BlockSpec(memory_space=pltpu.SMEM)] * 2,
        out_specs=[hbm] * len(outs) + [vmem_spec] * 2,
        out_shape=outs + [sds((6, 8, full)), sds((count, 128))],
        scratch_shapes=scratch,
        compiler_params=pltpu.CompilerParams(collective_id=1, has_side_effects=True, vmem_limit_bytes=60 * 1024 * 1024),
    )(*arrays, *constants, *scalars)


LAG = 8
KEPT = 6


def reduce_body(jobs, side, slots, *refs):
    lefts, rights, refs = refs[:6], refs[6:8], refs[8:]
    (zt_hbm, zp_hbm, zs_hbm, zi_hbm, zm_hbm, ws_hbm), refs = refs[:6], refs[6:]
    (totals_ref, g_split, b_split, g_inner, b_inner, g_spread, b_spread, g_trans, b_trans, mask_ref, edge_ref, wi_ref, wt_ref, wo_ref), refs = refs[:14], refs[14:]
    outs, dpart_out, dmain_out, vectors_ref, refs = refs[:5], refs[5], refs[6], refs[7], refs[8:]
    (x_ref, z_ref, turned_ref, own_ref, r0_ref, half_ref, r1_ref, quarter_ref, r2_ref, eighth_ref, r3_ref, full_ref, load_sem, store_sem) = refs[:14]
    (padded_ref, grad_ref, page_ref, joined_ref, zm_ref, pair_ref, part_ref, wide_ref, tap_ref, sums_ref, shared_ref, small_ref, spread_ref) = refs[14:27]
    (page_sem, tap_sem, write_sem, sum_send, sum_recv, small_send, small_recv) = refs[27:34]
    sems = refs[34:]
    count, half = grad_ref.shape
    pitch = wide_ref.shape[0]
    tiles = count // pitch
    s_split, q_out = totals_ref.at[SPLIT], totals_ref.at[BACK_OUT]
    s_spread, s_trans, s_inner = (totals_ref.at[k, :, 0:half] for k in (SPREAD, TRANS, INNER))
    stats_total = s_split[2:3, 0:1]
    block = own_ref.shape[1]
    mid = block // 2
    dp, bn = lax.axis_index("dp"), lax.axis_index("bn")
    z, x, y, core = dp // 2, dp % 2, bn // 2, bn % 2

    def at(new_z, new_x, new_y, new_core):
        return {"dp": new_z * 2 + new_x, "bn": new_y * 2 + new_core}

    to_core, to_x, to_y = at(z, x, y, 1 - core), at(z, 1 - x, y, core), at(z, x, 1 - y, core)
    depth = [(z + k) % 4 for k in (1, 2, 3)]
    to_z = [at(new_z, x, y, core) for new_z in depth]
    to_far = [at(new_z, 1 - x, y, core) for new_z in depth]
    to_diagonal = at(z, x, 1 - y, 1 - core)
    columns = (pl.ds(0, mid), pl.ds(mid, mid))

    def part(start, size):
        return pl.ds(pl.multiple_of(start, size), size)

    def far(stage, k, slot, source, target, peer):
        send, recv = sems[2 * stage], sems[2 * stage + 1]
        return pltpu.make_async_remote_copy(
            src_ref=source, dst_ref=target, send_sem=send.at[k, slot], recv_sem=recv.at[k, slot], device_id=peer, device_id_type=MESH
        )

    first = (x, y)
    second = (y, x)
    sides = (to_x, to_y)

    def copies(stage, c):
        slot, keep = c % 2, c % KEPT
        base = core * (block // 2)
        if stage == 0:
            return [far(0, 0, slot, own_ref.at[slot, part((1 - core) * (block // 2), block // 2)], r0_ref.at[slot], to_core)]
        if stage == 1:
            return [
                far(1, k, slot, half_ref.at[slot, part((1 - first[k]) * (block // 4), block // 4), columns[k]], r1_ref.at[slot, :, columns[k]], sides[k])
                for k in (0, 1)
            ]
        if stage == 2:
            return [
                far(2, k, slot, quarter_ref.at[slot, part((1 - second[k]) * (block // 8), block // 8), columns[k]], r2_ref.at[slot, :, columns[k]], sides[1 - k])
                for k in (0, 1)
            ]
        if stage == 3:
            return [
                far(3, k, slot, eighth_ref.at[slot, part(depth[k] * (block // 32), block // 32)], r3_ref.at[slot, k], to_z[k]) for k in (0, 1, 2)
            ]
        made = []
        for k in (0, 1):
            eighth = base + first[k] * (block // 4) + second[k] * (block // 8)
            if stage == 4:
                spot = full_ref.at[keep, part(eighth + z * (block // 32), block // 32), columns[k]]
                made += [far(4, 3 * k + d, slot, spot, spot, to_z[d]) for d in (0, 1, 2)]
            elif stage == 5:
                spot = full_ref.at[keep, part(eighth, block // 8), columns[k]]
                made.append(far(5, k, slot, spot, spot, sides[1 - k]))
            elif stage == 6:
                spot = full_ref.at[keep, part(base + first[k] * (block // 4), block // 4), columns[k]]
                made.append(far(6, k, slot, spot, spot, sides[k]))
        if stage == 7:
            spot = full_ref.at[keep, part(base, block // 2)]
            made.append(far(7, 0, slot, spot, spot, to_core))
        return made

    def begin(stage, c):
        for copy in copies(stage, c):
            copy.start()

    def finish(stage, c):
        for copy in copies(stage, c):
            copy.wait()

    def load(j):
        (left, begin_part, parts), right, _ = jobs[j]
        slot = j % 2
        made = [pltpu.make_async_copy(lefts[left].at[begin_part : begin_part + parts], x_ref.at[slot, 0:parts], load_sem.at[slot, 0])]
        source = {"pair": pair_ref, "part": part_ref, 0: rights[0], 1: rights[1]}.get(right)
        if source is not None:
            made.append(pltpu.make_async_copy(source, z_ref.at[slot], load_sem.at[slot, 1]))
        return made

    def store(j):
        out, spot = jobs[j][2]
        return pltpu.make_async_copy(full_ref.at[j % KEPT], outs[out].at[spot], store_sem.at[j % KEPT])


    everything = slice(None)

    def page(source, target, k):
        return pltpu.make_async_copy(source, target, page_sem.at[k])

    def tap_load(tap):
        return pltpu.make_async_copy(ws_hbm.at[tap], tap_ref.at[tap % 2], tap_sem.at[tap % 2])

    upper = slice(half, 2 * half)
    load_zt, load_zp, load_zs = page(zt_hbm, page_ref, 0), page(zp_hbm, joined_ref, 1), page(zs_hbm, page_ref, 0)
    load_zi, load_zm = page(zi_hbm, page_ref, 0), page(zm_hbm, zm_ref, 2)
    write_part = pltpu.make_async_copy(part_ref, dpart_out, write_sem.at[0])
    write_main = pltpu.make_async_copy(z_ref.at[1], dmain_out, write_sem.at[1])

    group = [at(z, x, y, 1 - core), at(z, x, 1 - y, core), to_diagonal]

    def sum_copies(which):
        return [
            pltpu.make_async_remote_copy(
                src_ref=sums_ref.at[which], dst_ref=shared_ref.at[which, bn], send_sem=sum_send.at[which, k], recv_sem=sum_recv.at[which, k], device_id=peer, device_id_type=MESH
            )
            for k, peer in enumerate(group)
        ]

    def sum_start(which):
        for copy in sum_copies(which):
            copy.start()
        shared_ref[which, bn] = sums_ref[which]

    def sum_finish(which):
        for copy in sum_copies(which):
            copy.wait()
        value = shared_ref[which, 0]
        for k in range(1, shared_ref.shape[1]):
            value = value + shared_ref[which, k]
        sums_ref[which] = value

    everyone = [to_x] + to_z + to_far

    def small_copies():
        return [
            pltpu.make_async_remote_copy(
                src_ref=small_ref, dst_ref=spread_ref.at[dp], send_sem=small_send.at[k], recv_sem=small_recv.at[k], device_id=peer, device_id_type=MESH
            )
            for k, peer in enumerate(everyone)
        ]

    def settled(dy_ref, z_page, which, back, gain_ref, columns, keep):
        mean, inverse = moments(which, stats_total, columns)
        factor = gain_ref[0:1, columns] * inverse
        first_sum, second_sum = sums_ref[back, 0:1, :] / stats_total, sums_ref[back, 1:2, :] / stats_total

        def body(r, _):
            keep(r, settle(dy_ref[r, :], z_page[r, :], mask_ref[r, 0:1], mean, inverse, factor, first_sum, second_sum))

        over_rows(count, body)

    def sloped(grad, target_ref, z_page, which, back, gain_ref, shift_ref, columns):
        mean, inverse = moments(which, stats_total, columns)
        gain, shift = gain_ref[0:1, columns], shift_ref[0:1, columns]

        def body(r, carry):
            dy, sums = norm_slope(z_page, grad[r, :], mask_ref, r, everything, mean, inverse, gain, shift)
            target_ref[r, :] = dy
            return (carry[0] + sums[0], carry[1] + sums[1])

        zero = jnp.zeros((8, half), F32)
        add_sums(sums_ref.at[back], everything, over_rows(count, body, (zero, zero)))
        sum_start(back)

    own, lower = everything, slice(0, half)

    def stacked(step):
        columns_k = slice(step * half, (step + 1) * half)
        for target_ref, rows_k in ((grad_ref, lower), (zm_ref, upper)):
            value = product2_t(z_ref.at[step % 2], (), wo_ref[rows_k, columns_k])
            if step == 0:
                target_ref[...] = value
            else:
                target_ref[...] += value

    def middle_slopes():
        load_zt.wait()
        load_zp.wait()
        sloped(grad_ref, grad_ref, page_ref, s_trans, 2, g_trans, b_trans, own)
        sloped(zm_ref, zm_ref, joined_ref, s_split, 3, g_split, b_split, lower)

    def middle():
        sum_finish(2)
        sum_finish(3)
        settled(grad_ref, page_ref, s_trans, 2, g_trans, own, lambda r, dz: split_store(pair_ref, (r,), dz))
        load_zs.start()
        settled(zm_ref, joined_ref, s_split, 3, g_split, lower, lambda r, dz: split_store(part_ref, (r,), dz))
        load_zm.start()
        write_part.start()
        joined_ref[...] = product2_t(pair_ref, (), wt_ref[...])
        load_zs.wait()
        sloped(joined_ref, grad_ref, page_ref, s_spread, 4, g_spread, b_spread, own)

    def prepare():
        sum_finish(4)
        padded_ref[0:GUARD, :] = jnp.zeros((GUARD, half), F32)
        padded_ref[GUARD + count :, :] = jnp.zeros((GUARD, half), F32)

        def keep(r, dz):
            padded_ref[pl.ds(r.start + GUARD, CHUNK), :] = dz

        settled(grad_ref, page_ref, s_spread, 4, g_spread, own, keep)
        load_zi.start()
        grad_ref[...] = jnp.zeros_like(grad_ref)

    def tap_work(tap):
        move, dx = taps(side, slots)[tap]
        slot = tap % 2
        moved = padded_ref[GUARD - move : GUARD - move + count, :]
        if dx:
            moved = moved * edge_ref[:, 1 - dx : 2 - dx]
        high = moved.astype(BF16)
        z_ref[slot, 0] = high
        z_ref[slot, 1] = (moved - high.astype(F32)).astype(BF16)
        tap_load(tap).wait()
        if tap < 8:
            tap_load(tap + 1).start()

    def tap_gradient(slot):
        grad_ref[...] += dot_t(z_ref[slot, 0], tap_ref[slot]) + dot_t(z_ref[slot, 1], tap_ref[slot])

    def inner_slope():
        load_zi.wait()
        sloped(grad_ref, grad_ref, page_ref, s_inner, 0, g_inner, b_inner, own)

    def shifted(k):
        return lambda r: pl.ds(pl.multiple_of(r.start + k * pitch, CHUNK), CHUNK)

    def inner_tile(k):
        mean, inverse = moments(s_inner, stats_total, everything)
        factor = g_inner[...] * inverse
        first_sum, second_sum = sums_ref[0, 0:1, :] / stats_total, sums_ref[0, 1:2, :] / stats_total
        here = shifted(k)

        def body(r, _):
            q = here(r)
            dz = settle(grad_ref[q, :], page_ref[q, :], mask_ref[q, 0:1], mean, inverse, factor, first_sum, second_sum)
            split_store(pair_ref, (q,), dz)

        over_rows(pitch, body)
        rows_k = slice(k * pitch, (k + 1) * pitch)
        wide_ref[...] = product2_t(pair_ref, (rows_k,), wi_ref[...])
        mean, inverse = moments(s_split, stats_total, upper)
        gain, shift = g_split[0:1, upper], b_split[0:1, upper]

        def tail(r, carry):
            q = here(r)
            dy, sums = norm_slope(zm_ref, wide_ref[r, :] + joined_ref[q, :], mask_ref, q, everything, mean, inverse, gain, shift)
            grad_ref[q, :] = dy
            return (carry[0] + sums[0], carry[1] + sums[1])

        zero = jnp.zeros((8, half), F32)
        add_sums(sums_ref.at[1], everything, over_rows(pitch, tail, (zero, zero)))

    def small_start():
        pieces = [
            (sums_ref.at[3], everything), (sums_ref.at[1], everything), (sums_ref.at[0], everything), (sums_ref.at[4], everything),
            (sums_ref.at[2], everything), (q_out, slice(0, half)), (q_out, slice(half, 2 * half)),
        ]
        small_ref[...] = jnp.zeros_like(small_ref)
        for k, (ref, columns_k) in enumerate(pieces):
            small_ref[k : k + 1, :] = ref[0:1, columns_k]
            small_ref[8 + k : 9 + k, :] = ref[1:2, columns_k]
        for copy in small_copies():
            copy.start()
        spread_ref[dp] = small_ref[...]

    def small_finish():
        for copy in small_copies():
            copy.wait()
        value = spread_ref[0]
        for k in range(1, spread_ref.shape[0]):
            value = value + spread_ref[k]
        vectors_ref[...] = value

    def main_settle():
        def keep(r, dz):
            high = dz.astype(BF16)
            rest = (dz - high.astype(F32)).astype(BF16)
            for slot in (0, 1):
                z_ref[slot, 0, r, :] = high
                z_ref[slot, 1, r, :] = rest

        settled(grad_ref, zm_ref, s_split, 1, g_split, upper, keep)
        write_main.start()

    FIRST_TAP = 4
    hosted = {
        0: [functools.partial(stacked, 0)],
        1: [functools.partial(stacked, 1), middle_slopes],
        2: [middle],
        3: [prepare],
        13: [inner_slope],
        14: [load_zm.wait, lambda: sum_finish(0), functools.partial(inner_tile, 0), functools.partial(inner_tile, 1)],
        15: [functools.partial(inner_tile, 2), functools.partial(inner_tile, 3), lambda: sum_start(1)],
        16: [lambda: sum_finish(1), small_start],
        17: [main_settle],
        18: [small_finish, write_part.wait, write_main.wait],
    }

    sums_ref[...] = jnp.zeros_like(sums_ref)
    load_zt.start()
    load_zp.start()
    tap_load(0).start()
    for copy in load(0):
        copy.start()
    barrier = pltpu.get_barrier_semaphore()
    peers = [to_core, to_x, to_y] + to_z + to_far + [to_diagonal]
    for peer in peers:
        pl.semaphore_signal(barrier, inc=1, device_id=peer, device_id_type=MESH)
    pl.semaphore_wait(barrier, len(peers))
    total = len(jobs)

    @pl.loop(0, total + LAG + 1)
    def _(t):
        for j in range(total):

            @pl.when(t == j + LAG + 1)
            def _(j=j):
                store(j).wait()

        def stage(number, lag):
            def wrap(body):
                c = t - lag
                pl.when(jnp.logical_and(c >= 0, c < total))(lambda: body(c))

            return wrap

        @stage(7, 8)
        def _(c):
            finish(7, c)

        for j in range(total):

            @pl.when(t == j + LAG)
            def _(j=j):
                store(j).start()

        for number in (6, 5, 4):

            @stage(number, number + 1)
            def _(c, number=number):
                finish(number, c)
                begin(number + 1, c)

        for j in range(total):

            @pl.when(t == j)
            def _(j=j):
                for copy in load(j):
                    copy.wait()
                for task in hosted.get(j, ()):
                    task()
                if j + 1 < total:
                    for copy in load(j + 1):
                        copy.start()
                if 0 <= j - FIRST_TAP < 9:
                    tap_work(j - FIRST_TAP)

        @pl.when(jnp.logical_and(t >= FIRST_TAP, t < FIRST_TAP + 9))
        def _():
            tap_gradient(t % 2)

        @stage(3, 4)
        def _(c):
            finish(3, c)
            slot, keep = c % 2, c % KEPT
            value = eighth_ref[slot, part(z * (block // 32), block // 32), :]
            for k in (0, 1, 2):
                value = value + r3_ref[slot, k]
            for k in (0, 1):
                row = core * (block // 2) + first[k] * (block // 4) + second[k] * (block // 8) + z * (block // 32)
                full_ref[keep, part(row, block // 32), k * mid : (k + 1) * mid] = value[:, k * mid : (k + 1) * mid]
            begin(4, c)

        @stage(2, 3)
        def _(c):
            finish(2, c)
            slot = c % 2
            for k in (0, 1):
                eighth_ref[slot, :, columns[k]] = quarter_ref[slot, part(second[k] * (block // 8), block // 8), columns[k]] + r2_ref[slot, :, columns[k]]
            begin(3, c)

        @stage(1, 2)
        def _(c):
            finish(1, c)
            slot = c % 2
            for k in (0, 1):
                quarter_ref[slot, :, columns[k]] = half_ref[slot, part(first[k] * (block // 4), block // 4), columns[k]] + r1_ref[slot, :, columns[k]]
            begin(2, c)

        @stage(0, 1)
        def _(c):
            finish(0, c)
            slot = c % 2
            half_ref[slot] = own_ref[slot, part(core * (block // 2), block // 2), :] + r0_ref[slot]
            begin(1, c)

        exact = functools.reduce(jnp.logical_or, [t == j for j in range(total) if jobs[j][0][2] == 1])

        @stage(None, 0)
        def _(c):
            slot = c % 2
            turned_ref[...] = x_ref[slot, 0].T
            own_ref[slot] = dot(turned_ref[...], z_ref[slot, 0]) + dot(turned_ref[...], z_ref[slot, 1])

            @pl.when(jnp.logical_not(exact))
            def _():
                turned_ref[...] = x_ref[slot, 1].T
                own_ref[slot] += dot(turned_ref[...], z_ref[slot, 0])

            begin(0, c)


def reduce_call(jobs, lefts, rights, hosted, constants, shapes, side, slots):
    hbm, vmem_spec = pl.BlockSpec(memory_space=pl.ANY), pl.BlockSpec(memory_space=pltpu.VMEM)
    vmem, dma = pltpu.VMEM, pltpu.SemaphoreType.DMA
    count, block = hosted[0].shape
    pitch = count // TILES
    scratch = [
        vmem((2, 2, count, block), BF16), vmem((2, 2, count, block), BF16), vmem((block, count), BF16),
        vmem((2, block, block), F32), vmem((2, block // 2, block), F32), vmem((2, block // 2, block), F32),
        vmem((2, block // 4, block), F32), vmem((2, block // 4, block), F32), vmem((2, block // 8, block), F32), vmem((2, block // 8, block), F32),
        vmem((2, 3, block // 32, block), F32), vmem((KEPT, block, block), F32),
        dma((2, 2)), dma((KEPT,)),
        vmem((count + 2 * GUARD, block), F32), vmem((count, block), F32), vmem((count, block), F32), vmem((count, block), F32),
        vmem((count, block), F32), vmem((2, count, block), BF16), vmem((2, count, block), BF16), vmem((pitch, block), F32),
        vmem((2, block, block), BF16), vmem((5, 8, block), F32), vmem((5, 4, 8, block), F32),
        vmem((16, block), F32), vmem((8, 16, block), F32),
        dma((3,)), dma((2,)), dma((2,)), dma((5, 3)), dma((5, 3)), dma((7,)), dma((7,)),
    ]
    for width in (1, 2, 2, 3, 6, 2, 2, 1):
        scratch += [dma((width, 2)), dma((width, 2))]
    return pl.pallas_call(
        functools.partial(reduce_body, jobs, side, slots),
        in_specs=[hbm] * (len(lefts) + len(rights) + len(hosted)) + [vmem_spec] * len(constants),
        out_specs=[hbm] * (len(shapes) + 2) + [vmem_spec],
        out_shape=[sds(shape) for shape in shapes] + [sds((2, count, block), BF16)] * 2 + [sds((16, block))],
        scratch_shapes=scratch,
        compiler_params=pltpu.CompilerParams(collective_id=3, has_side_effects=True, vmem_limit_bytes=60 * 1024 * 1024),
    )(*lefts, *rights, *hosted, *constants)


def gather_sums_body(axis, sums_ref, out_ref, slots_ref, send_sem, recv_sem):
    members = slots_ref.shape[0]
    me = lax.axis_index(axis)
    peers = [lax.rem(me + k, members) for k in range(1, members)]
    barrier = pltpu.get_barrier_semaphore()
    for peer in peers:
        pl.semaphore_signal(barrier, inc=1, device_id={axis: peer}, device_id_type=MESH)
    pl.semaphore_wait(barrier, members - 1)
    copies = [
        pltpu.make_async_remote_copy(
            src_ref=sums_ref, dst_ref=slots_ref.at[me], send_sem=send_sem.at[k], recv_sem=recv_sem.at[k], device_id={axis: peer}, device_id_type=MESH
        )
        for k, peer in enumerate(peers)
    ]
    for copy in copies:
        copy.start()
    slots_ref[me] = sums_ref[...]
    for copy in copies:
        copy.wait()
    value = slots_ref[0]
    for k in range(1, members):
        value = value + slots_ref[k]
    out_ref[...] = value


def gather_sums(sums, members, collective, axis="bn"):
    if members == 1:
        return sums
    spec = pl.BlockSpec(memory_space=pltpu.VMEM)
    return pl.pallas_call(
        functools.partial(gather_sums_body, axis),
        in_specs=[spec],
        out_specs=spec,
        out_shape=sds(sums.shape),
        scratch_shapes=[pltpu.VMEM((members,) + sums.shape, F32), pltpu.SemaphoreType.DMA((members - 1,)), pltpu.SemaphoreType.DMA((members - 1,))],
        compiler_params=pltpu.CompilerParams(collective_id=collective, has_side_effects=True),
    )(sums)


def local(
    shape,
    features, image_counts, map_sides,
    split_kernel, split_gain, split_shift, inner_kernel, inner_gain, inner_shift,
    spread_kernel, spread_gain, spread_shift, transition_kernel, transition_gain, transition_shift,
    output_kernel, output_gain, output_shift, cotangent,
):
    slots, side, _, full = features.shape
    half = inner_kernel.shape[0]
    pitch = round_up(-(-slots * side * side // TILES), 16)
    count = TILES * pitch
    grid = (TILES,)
    columns = np.arange(count)[:, None] // slots % side
    lanes = np.arange(128)[None, :]
    edges = jnp.asarray(np.where(lanes == 0, columns > 0, np.where(lanes == 2, columns < side - 1, True)).astype(np.float32))
    features = features.transpose(1, 2, 0, 3).reshape(side * side, slots, full)
    cotangent = cotangent.transpose(1, 2, 0, 3).reshape(side * side, slots, full)
    (split_gain, split_shift, inner_gain, inner_shift, spread_gain, spread_shift, transition_gain, transition_shift, output_gain, output_shift) = (
        item.reshape(1, -1)
        for item in (split_gain, split_shift, inner_gain, inner_shift, spread_gain, spread_shift, transition_gain, transition_shift, output_gain, output_shift)
    )
    spread_weight = spread_kernel.reshape(9, half, half)

    def group(sums):
        return gather_sums(sums, shape[1], 1 if sums.shape[1] == full else 2)

    sums_full, sums_half = out_whole((8, full)), out_whole((8, half))
    r_half, r_full, r_mask = rows(pitch, half), rows(pitch, full), rows(pitch, 128)
    pair_half, pair_full = rows2(pitch, half), rows2(pitch, full)

    def call(body, ins, outs, scratch=(), steps=grid):
        return pl.pallas_call(
            body,
            grid=steps,
            in_specs=[spec for _, spec in ins],
            out_specs=[spec for _, spec in outs],
            out_shape=[shape for shape, _ in outs],
            scratch_shapes=list(scratch),
            compiler_params=params(),
        )(*[array for array, _ in ins])

    def fixed(array):
        return (array, whole(array))

    if shape == (8, 4):
        low, high = slice(0, half), slice(half, full)
        every = slice(None)
        (x0, z_part, z_main, main2, part2, z_inner, inner2, z_spread, joined2, z_trans, trans2, result, dz_low, dz_high, totals, mask) = front_call(
            [features, cotangent, split_kernel, inner_kernel, spread_weight, transition_kernel, output_kernel],
            [split_gain, split_shift, inner_gain, inner_shift, spread_gain, spread_shift, transition_gain, transition_shift, output_gain, output_shift, edges],
            [image_counts, map_sides],
            slots, side, count, shape[1],
        )
        jobs = [((0, 0, 2), 0, (4, (low, low))), ((0, 0, 2), 1, (4, (low, high)))]
        jobs += [((1, 0, 2), 0, (4, (high, low))), ((1, 0, 2), 1, (4, (high, high)))]
        jobs += [((4, 0, 2), None, (2, (tap,))) for tap in range(9)]
        jobs += [((2, 0, 2), "pair", (3, (every, every)))]
        jobs += [((3, 0, 1), "part", (0, (low, low))), ((3, 1, 1), "part", (0, (high, low)))]
        jobs += [((5, 0, 2), "pair", (1, (every, every)))]
        jobs += [((3, 0, 1), None, (0, (low, high))), ((3, 1, 1), None, (0, (high, high)))]
        grad_split, grad_inner, grad_spread, grad_transition, grad_output, dz_part, dz_main, vectors = reduce_call(
            jobs,
            [trans2, part2, joined2, x0, inner2, main2],
            [dz_low, dz_high],
            [z_trans, z_part, z_spread, z_inner, z_main, spread_weight],
            [
                totals, split_gain, split_shift, inner_gain, inner_shift, spread_gain, spread_shift, transition_gain, transition_shift,
                mask, edges, inner_kernel, transition_kernel, output_kernel,
            ],
            [(full, full), (half, half), (9, half, half), (half, half), (full, full)],
            side, slots,
        )
        (grad_features,) = call(
            features_body,
            [(dz_part, pair_half), (dz_main, pair_half), fixed(split_kernel)],
            [(sds(cotangent.shape), pixels(pitch, cotangent.shape))],
            [pltpu.VMEM((pitch, full), F32)],
        )
        small = vectors.reshape(2, 8 * half)
    else:
        row = jnp.arange(count)[:, None] + jnp.zeros((1, 128), jnp.int32)
        slot, place = row % slots, row // slots
        y, x = place // side, place % side
        sides = sum(jnp.where(slot == k, map_sides[k], 0) for k in range(slots))
        keep = (slot < image_counts[0]) & (y < sides) & (x < sides) & (place < side * side)
        mask = keep.astype(F32)
        x0, z_split, s_split = call(
            split_kernel_body,
            [(features, pixels(pitch, features.shape)), (mask, r_mask), fixed(split_kernel)],
            [(sds((count, full), BF16), r_full), (sds((count, full)), r_full), (sds((8, full)), sums_full)],
            [pltpu.VMEM((pitch, full), F32)],
        )
        s_split = group(s_split)
        part2, main, main2, z_inner, s_inner = call(
            inner_body,
            [(z_split, r_full), fixed(s_split), fixed(split_gain), fixed(split_shift), (mask, r_mask), fixed(inner_kernel)],
            [
                (sds((2, count, half), BF16), pair_half), (sds((count, half)), r_half), (sds((2, count, half), BF16), pair_half),
                (sds((count, half)), r_half), (sds((8, half)), sums_half),
            ],
        )
        s_inner = group(s_inner)
        tap_spec = pl.BlockSpec((1, half, half), lambda i: (i, 0, 0))
        inner2, z_spread, s_spread = call(
            functools.partial(spread_body, side, slots),
            [fixed(z_inner), fixed(s_split), fixed(s_inner), fixed(inner_gain), fixed(inner_shift), fixed(mask), fixed(edges), (spread_weight, tap_spec)],
            [(sds((2, count, half), BF16), out_whole((2, count, half))), (sds((count, half)), out_whole((count, half))), (sds((8, half)), sums_half)],
            [pltpu.VMEM((count + 2 * GUARD, half), F32), pltpu.VMEM((2, count, half), BF16)],
            (9,),
        )
        s_spread = group(s_spread)
        joined2, z_trans, s_trans = call(
            transition_body,
            [(z_spread, r_half), fixed(s_split), fixed(s_spread), fixed(spread_gain), fixed(spread_shift), (mask, r_mask), (main, r_half), fixed(transition_kernel)],
            [(sds((2, count, half), BF16), pair_half), (sds((count, half)), r_half), (sds((8, half)), sums_half)],
        )
        s_trans = group(s_trans)
        trans2, z_out, s_out = call(
            output_body,
            [(z_trans, r_half), fixed(s_split), fixed(s_trans), fixed(transition_gain), fixed(transition_shift), (mask, r_mask), (part2, pair_half), fixed(output_kernel)],
            [(sds((2, count, half), BF16), pair_half), (sds((count, full)), r_full), (sds((8, full)), sums_full)],
        )
        s_out = group(s_out)
        result, dy_out, q_out = call(
            result_body,
            [(z_out, r_full), fixed(s_split), fixed(s_out), fixed(output_gain), fixed(output_shift), (mask, r_mask), (cotangent, pixels(pitch, cotangent.shape))],
            [(sds(cotangent.shape), pixels(pitch, cotangent.shape)), (sds((count, full)), r_full), (sds((8, full)), sums_full)],
            [pltpu.VMEM((pitch, full), F32)],
        )
        q_out = group(q_out)
        dz_out, dy_trans, dy_part, q_mid = call(
            output_back_body,
            [
                (dy_out, r_full), (z_out, r_full), fixed(s_out), fixed(output_gain), fixed(q_out), fixed(s_split), (mask, r_mask), fixed(output_kernel),
                (z_trans, r_half), fixed(s_trans), fixed(transition_gain), fixed(transition_shift), (z_split, rows(pitch, half, 0)), fixed(split_gain), fixed(split_shift),
            ],
            [(sds((2, count, full), BF16), pair_full), (sds((count, half)), r_half), (sds((count, half)), r_half), (sds((8, full)), sums_full)],
            [pltpu.VMEM((pitch, full), F32)],
        )
        q_mid = group(q_mid)
        dz_trans, dz_part, grad_joined, dy_spread, q_spread = call(
            transition_back_body,
            [
                (dy_trans, r_half), (dy_part, r_half), (z_trans, r_half), fixed(s_trans), fixed(transition_gain), fixed(q_mid), fixed(s_split), (mask, r_mask), fixed(transition_kernel),
                (z_split, rows(pitch, half, 0)), fixed(split_gain), (z_spread, r_half), fixed(s_spread), fixed(spread_gain), fixed(spread_shift),
            ],
            [
                (sds((2, count, half), BF16), pair_half), (sds((2, count, half), BF16), pair_half), (sds((count, half)), r_half),
                (sds((count, half)), r_half), (sds((8, half)), sums_half),
            ],
        )
        q_spread = group(q_spread)
        moved_spec = pl.BlockSpec((1, 2, count, half), lambda i: (i, 0, 0, 0))
        moved, dy_inner, q_inner = call(
            functools.partial(spread_back_body, side, slots),
            [
                fixed(dy_spread), fixed(z_spread), fixed(s_spread), fixed(spread_gain), fixed(q_spread), fixed(s_split), fixed(mask), fixed(edges), (spread_weight, tap_spec),
                fixed(z_inner), fixed(s_inner), fixed(inner_gain), fixed(inner_shift),
            ],
            [(sds((9, 2, count, half), BF16), moved_spec), (sds((count, half)), out_whole((count, half))), (sds((8, half)), sums_half)],
            [pltpu.VMEM((count + 2 * GUARD, half), F32), pltpu.VMEM((count, half), F32)],
            (9,),
        )
        q_inner = group(q_inner)
        dz_inner, dy_main, q_main = call(
            inner_back_body,
            [
                (dy_inner, r_half), (z_inner, r_half), fixed(s_inner), fixed(inner_gain), fixed(q_inner), fixed(s_split), (mask, r_mask), fixed(inner_kernel),
                (grad_joined, r_half), (z_split, rows(pitch, half, 1)), fixed(split_gain), fixed(split_shift),
            ],
            [(sds((2, count, half), BF16), pair_half), (sds((count, half)), r_half), (sds((8, half)), sums_half)],
            [pltpu.VMEM((pitch, half), F32)],
        )
        q_main = group(q_main)
        dz_main, grad_features = call(
            split_back_body,
            [(dy_main, r_half), (z_split, rows(pitch, half, 1)), fixed(q_main), fixed(s_split), fixed(split_gain), (mask, r_mask), (dz_part, pair_half), fixed(split_kernel)],
            [(sds((2, count, half), BF16), pair_half), (sds(cotangent.shape), pixels(pitch, cotangent.shape))],
            [pltpu.VMEM((pitch, full), F32)],
        )
        small = jnp.concatenate([q_mid[0:2, half:], q_main[0:2], q_inner[0:2], q_spread[0:2], q_mid[0:2, :half], q_out[0:2]], axis=1)
        grad_output = jnp.concatenate([weight_grad(trans2, dz_out), weight_grad(part2, dz_out)], axis=0)
        grad_transition, grad_inner = weight_grad(joined2, dz_trans), weight_grad(main2, dz_inner)
        grad_split = jnp.concatenate([weight_grad(x0[None], dz_part), weight_grad(x0[None], dz_main)], axis=1)
        grad_spread = jnp.stack([weight_grad(inner2, moved[tap]) for tap in range(9)])
        grad_split, grad_inner, grad_spread, grad_transition, grad_output = lax.psum(
            (grad_split, grad_inner, grad_spread, grad_transition, grad_output), ("dp", "bn")
        )
        small = lax.psum(small, "dp")
    cuts = [0, full, full + half, full + 2 * half, full + 3 * half, 2 * full + 3 * half]
    shifts = [small[0, a:b] for a, b in zip(cuts[:-1], cuts[1:])]
    gains = [small[1, a:b] for a, b in zip(cuts[:-1], cuts[1:])]
    result, grad_features = (item.reshape(side, side, slots, full).transpose(2, 0, 1, 3) for item in (result, grad_features))
    return (
        result, grad_features,
        grad_split, gains[0], shifts[0], grad_inner, gains[1], shifts[1],
        grad_spread.reshape(3, 3, half, half), gains[2], shifts[2], grad_transition, gains[3], shifts[3], grad_output, gains[4], shifts[4],
    )


def solution(mesh):
    shard, copy = P(("dp", "bn")), P()
    return jax.shard_map(
        functools.partial(local, (mesh.shape["dp"], mesh.shape["bn"])),
        mesh=mesh,
        in_specs=(shard, shard, shard) + (copy,) * 15 + (shard,),
        out_specs=(shard, shard) + (copy,) * 15,
        check_vma=False,
    )
```

```python
import functools

import jax
import jax.numpy as jnp
import numpy as np
from jax import lax
from jax.experimental import pallas as pl
from jax.experimental.pallas import tpu as pltpu
from jax.sharding import PartitionSpec as P

EPS = 1e-05
GUARD = 80
CHUNK = 16
TILES = 4
MESH = pl.DeviceIdType.MESH
F32 = jnp.float32
BF16 = jnp.bfloat16


def round_up(value, step):
    return -(-value // step) * step


def params(megabytes=56):
    return pltpu.CompilerParams(vmem_limit_bytes=megabytes * 1024 * 1024)


def whole(array):
    zeros = (0,) * len(array.shape)
    return pl.BlockSpec(array.shape, lambda *_: zeros, pipeline_mode=pl.Buffered(1))


def out_whole(shape):
    zeros = (0,) * len(shape)
    return pl.BlockSpec(shape, lambda *_: zeros)


def rows(pitch, width, column=0):
    return pl.BlockSpec((pitch, width), lambda i: (i, column))


def rows2(pitch, width):
    return pl.BlockSpec((2, pitch, width), lambda i: (0, i, 0))


def pixels(pitch, shape):
    return pl.BlockSpec((pitch // shape[1],) + tuple(shape[1:]), lambda i: (i, 0, 0))


def sds(shape, dtype=F32):
    return jax.ShapeDtypeStruct(tuple(shape), dtype)


def dot(left, right):
    return jnp.dot(left, right, preferred_element_type=F32)


def dot_t(left, right):
    return lax.dot_general(left, right, (((1,), (1,)), ((), ())), preferred_element_type=F32)


def split_store(ref, place, value):
    high = value.astype(BF16)
    ref[(0,) + place] = high
    ref[(1,) + place] = (value - high.astype(F32)).astype(BF16)


def moments(stats_ref, total, columns):
    mean = stats_ref[0:1, columns] / total
    square = stats_ref[1:2, columns] / total
    return mean, lax.rsqrt(square - mean * mean + EPS)


def mish(y):
    t = jnp.exp(jnp.minimum(y, 30.0))
    n = t * (t + 2.0)
    return y * (n / (n + 2.0))


def mish_slope(y):
    t = jnp.exp(jnp.minimum(y, 30.0))
    n = t * (t + 2.0)
    r = 1.0 / (n + 2.0)
    return n * r + y * (((4.0 * t) * (t + 1.0) * r) * r)


def fold(value):
    return jnp.sum(value.reshape(value.shape[0] // 8, 8, value.shape[1]), axis=0)


def over_rows(count, body, carry=None, unroll=4):
    def step(k, c):
        return body(pl.ds(pl.multiple_of(k * CHUNK, CHUNK), CHUNK), c)

    return lax.fori_loop(0, count // CHUNK, step, carry, unroll=unroll)


def column_blocks(width, block=512):
    return [slice(c, c + block) for c in range(0, width, block)]


def add_sums(sums_ref, columns, pieces):
    for k, piece in enumerate(pieces):
        sums_ref[k : k + 1, columns] += jnp.sum(piece, axis=0, keepdims=True)


def start_sums(sums_ref):
    @pl.when(pl.program_id(0) == 0)
    def _():
        sums_ref[...] = jnp.zeros_like(sums_ref)


def sum_squares(z_ref, sums_ref, mask_ref=None):
    for columns in column_blocks(z_ref.shape[1]):
        width = columns.stop - columns.start

        def body(r, carry):
            value = z_ref[r, columns]
            kept = value if mask_ref is None else value * mask_ref[r, 0:1]
            return (carry[0] + fold(kept), carry[1] + fold(kept * value))

        zero = jnp.zeros((8, width), F32)
        add_sums(sums_ref, columns, over_rows(z_ref.shape[0], body, (zero, zero)))


def product2(ref, place, weight):
    high = ref[(0,) + place]
    low = ref[(1,) + place]
    return dot(high, weight) + dot(low, weight)


def product2_t(ref, place, weight):
    high = ref[(0,) + place]
    low = ref[(1,) + place]
    return dot_t(high, weight) + dot_t(low, weight)


def compact(source_ref, scratch_ref):
    places, slots, _ = source_ref.shape
    for p in range(places):
        scratch_ref[p * slots : (p + 1) * slots, :] = source_ref[p].astype(F32)


def spread_out(scratch_ref, target_ref):
    places, slots, _ = target_ref.shape
    for p in range(places):
        target_ref[p] = scratch_ref[p * slots : (p + 1) * slots, :]


def split_kernel_body(features_ref, mask_ref, w_ref, x_ref, z_ref, sums_ref, scratch_ref):
    compact(features_ref, scratch_ref)

    def body(r, _):
        x_ref[r, :] = jnp.where(mask_ref[r, 0:1] > 0.0, scratch_ref[r, :], 0.0).astype(BF16)

    over_rows(x_ref.shape[0], body)
    z_ref[...] = dot(x_ref[...], w_ref[...])
    start_sums(sums_ref)
    sum_squares(z_ref, sums_ref)
    count = jnp.sum(mask_ref[...], axis=0, keepdims=True)
    sums_ref[2:3, 0:128] += count


def inner_body(z_ref, stats_ref, gain_ref, shift_ref, mask_ref, w_ref, part_ref, main_ref, main2_ref, zi_ref, sums_ref):
    total = stats_ref[2:3, 0:1]
    half = w_ref.shape[0]
    for index, columns in enumerate(column_blocks(2 * half, half)):
        mean, inverse = moments(stats_ref, total, columns)
        scale, shift = gain_ref[0:1, columns] * inverse, shift_ref[0:1, columns]

        def body(r, _):
            act = mish((z_ref[r, columns] - mean) * scale + shift) * mask_ref[r, 0:1]
            if index == 0:
                split_store(part_ref, (r,), act)
            else:
                main_ref[r, :] = act
                split_store(main2_ref, (r,), act)

        over_rows(z_ref.shape[0], body)
    zi_ref[...] = product2(main2_ref, (), w_ref[...])
    start_sums(sums_ref)
    sum_squares(zi_ref, sums_ref)


def taps(side, slots):
    return [((dy * side + dx) * slots, dx) for dy in (-1, 0, 1) for dx in (-1, 0, 1)]


def move_rows(padded_ref, edge_ref, pair_ref, side, slots, sign):
    count = pair_ref.shape[1]
    for index, (move, dx) in enumerate(taps(side, slots)):

        @pl.when(pl.program_id(0) == index)
        def _(move=sign * move, dx=sign * dx):
            moved = padded_ref[GUARD + move : GUARD + move + count, :]
            if dx:
                moved = moved * edge_ref[:, dx + 1 : dx + 2]
            split_store(pair_ref, (slice(None),), moved)


def spread_body(side, slots, z_ref, total_ref, stats_ref, gain_ref, shift_ref, mask_ref, edge_ref, w_ref, inner_ref, zs_ref, sums_ref, padded_ref, pair_ref):
    total = total_ref[2:3, 0:1]
    count = z_ref.shape[0]
    tap = pl.program_id(0)

    @pl.when(tap == 0)
    def _():
        mean, inverse = moments(stats_ref, total, slice(None))
        scale, shift = gain_ref[...] * inverse, shift_ref[...]
        padded_ref[0:GUARD, :] = jnp.zeros((GUARD, padded_ref.shape[1]), F32)
        padded_ref[GUARD + count :, :] = jnp.zeros((GUARD, padded_ref.shape[1]), F32)

        def body(r, _):
            act = mish((z_ref[r, :] - mean) * scale + shift) * mask_ref[r, 0:1]
            padded_ref[pl.ds(r.start + GUARD, CHUNK), :] = act
            split_store(inner_ref, (r,), act)

        over_rows(count, body)
        zs_ref[...] = jnp.zeros_like(zs_ref)

    move_rows(padded_ref, edge_ref, pair_ref, side, slots, 1)
    zs_ref[...] += product2(pair_ref, (), w_ref[0])

    @pl.when(tap == pl.num_programs(0) - 1)
    def _():
        sums_ref[...] = jnp.zeros_like(sums_ref)
        sum_squares(zs_ref, sums_ref, mask_ref)


def transition_body(z_ref, total_ref, stats_ref, gain_ref, shift_ref, mask_ref, main_ref, w_ref, joined_ref, zt_ref, sums_ref):
    total = total_ref[2:3, 0:1]
    mean, inverse = moments(stats_ref, total, slice(None))
    scale, shift = gain_ref[...] * inverse, shift_ref[...]

    def body(r, _):
        act = mish((z_ref[r, :] - mean) * scale + shift) * mask_ref[r, 0:1]
        split_store(joined_ref, (r,), act + main_ref[r, :])

    over_rows(z_ref.shape[0], body)
    zt_ref[...] = product2(joined_ref, (), w_ref[...])
    start_sums(sums_ref)
    sum_squares(zt_ref, sums_ref)


def output_body(z_ref, total_ref, stats_ref, gain_ref, shift_ref, mask_ref, part_ref, w_ref, trans_ref, zo_ref, sums_ref):
    total = total_ref[2:3, 0:1]
    mean, inverse = moments(stats_ref, total, slice(None))
    scale, shift = gain_ref[...] * inverse, shift_ref[...]
    half = z_ref.shape[1]

    def body(r, _):
        act = mish((z_ref[r, :] - mean) * scale + shift) * mask_ref[r, 0:1]
        split_store(trans_ref, (r,), act)

    over_rows(z_ref.shape[0], body)
    zo_ref[...] = product2(part_ref, (), w_ref[half:, :])
    zo_ref[...] += product2(trans_ref, (), w_ref[:half, :])
    start_sums(sums_ref)
    sum_squares(zo_ref, sums_ref)


def result_body(z_ref, total_ref, stats_ref, gain_ref, shift_ref, mask_ref, cotangent_ref, result_ref, dy_ref, sums_ref, scratch_ref):
    total = total_ref[2:3, 0:1]
    compact(cotangent_ref, scratch_ref)
    start_sums(sums_ref)
    for columns in column_blocks(z_ref.shape[1]):
        mean, inverse = moments(stats_ref, total, columns)
        gain, shift = gain_ref[0:1, columns], shift_ref[0:1, columns]

        def body(r, carry):
            mask = mask_ref[r, 0:1]
            scaled = (z_ref[r, columns] - mean) * inverse
            y = scaled * gain + shift
            t = jnp.exp(jnp.minimum(y, 30.0))
            n = t * (t + 2.0)
            inv = 1.0 / (n + 2.0)
            ratio = n * inv
            slope = ratio + y * (((4.0 * t) * (t + 1.0) * inv) * inv)
            dy = jnp.where(mask > 0.0, scratch_ref[r, columns], 0.0) * slope
            scratch_ref[r, columns] = y * ratio * mask
            dy_ref[r, columns] = dy
            return (carry[0] + fold(dy), carry[1] + fold(dy * scaled))

        zero = jnp.zeros((8, columns.stop - columns.start), F32)
        add_sums(sums_ref, columns, over_rows(z_ref.shape[0], body, (zero, zero)))
    spread_out(scratch_ref, result_ref)


def norm_slope(z_ref, grad, mask_ref, r, columns, mean, inverse, gain, shift):
    scaled = (z_ref[r, columns] - mean) * inverse
    dy = grad * mask_ref[r, 0:1] * mish_slope(scaled * gain + shift)
    return dy, (fold(dy), fold(dy * scaled))


def settle(dy, z, mask, mean, inverse, factor, first, second):
    scaled = (z - mean) * inverse
    return mask * factor * (dy - (first + scaled * second))


def output_back_body(dy_ref, zo_ref, so_ref, go_ref, qo_ref, total_ref, mask_ref, w_ref, zt_ref, st_ref, gt_ref, bt_ref, zp_ref, gp_ref, bp_ref, dz_ref, dyt_ref, dyp_ref, sums_ref, grad_ref):
    total = total_ref[2:3, 0:1]
    for columns in column_blocks(zo_ref.shape[1]):
        mean, inverse = moments(so_ref, total, columns)
        factor = go_ref[0:1, columns] * inverse
        first, second = qo_ref[0:1, columns] / total, qo_ref[1:2, columns] / total

        def body(r, _):
            dz = settle(dy_ref[r, columns], zo_ref[r, columns], mask_ref[r, 0:1], mean, inverse, factor, first, second)
            split_store(dz_ref, (r, columns), dz)

        over_rows(zo_ref.shape[0], body)
    grad_ref[...] = product2_t(dz_ref, (), w_ref[...])
    start_sums(sums_ref)
    half = zt_ref.shape[1]
    for index, (z_ref, s_ref, g_ref, b_ref, out_ref) in enumerate(((zt_ref, st_ref, gt_ref, bt_ref, dyt_ref), (zp_ref, total_ref, gp_ref, bp_ref, dyp_ref))):
        columns = slice(index * half, (index + 1) * half)
        own = slice(0, half)
        mean, inverse = moments(s_ref, total, own)
        gain, shift = g_ref[0:1, own], b_ref[0:1, own]

        def body(r, carry):
            dy, sums = norm_slope(z_ref, grad_ref[r, columns], mask_ref, r, own, mean, inverse, gain, shift)
            out_ref[r, :] = dy
            return (carry[0] + sums[0], carry[1] + sums[1])

        zero = jnp.zeros((8, half), F32)
        add_sums(sums_ref, columns, over_rows(zt_ref.shape[0], body, (zero, zero)))


def transition_back_body(dyt_ref, dyp_ref, zt_ref, st_ref, gt_ref, q_ref, total_ref, mask_ref, w_ref, zp_ref, gp_ref, zs_ref, ss_ref, gs_ref, bs_ref, dz_ref, dzp_ref, grad_ref, dys_ref, sums_ref):
    total = total_ref[2:3, 0:1]
    half = zt_ref.shape[1]
    own = slice(0, half)
    for index, (dy_ref, z_ref, s_ref, g_ref, out_ref) in enumerate(((dyt_ref, zt_ref, st_ref, gt_ref, dz_ref), (dyp_ref, zp_ref, total_ref, gp_ref, dzp_ref))):
        columns = slice(index * half, (index + 1) * half)
        mean, inverse = moments(s_ref, total, own)
        factor = g_ref[0:1, own] * inverse
        first, second = q_ref[0:1, columns] / total, q_ref[1:2, columns] / total

        def body(r, _):
            dz = settle(dy_ref[r, :], z_ref[r, :], mask_ref[r, 0:1], mean, inverse, factor, first, second)
            split_store(out_ref, (r,), dz)

        over_rows(zt_ref.shape[0], body)
    grad_ref[...] = product2_t(dz_ref, (), w_ref[...])
    start_sums(sums_ref)
    mean, inverse = moments(ss_ref, total, own)
    gain, shift = gs_ref[...], bs_ref[...]

    def tail(r, carry):
        dy, sums = norm_slope(zs_ref, grad_ref[r, :], mask_ref, r, own, mean, inverse, gain, shift)
        dys_ref[r, :] = dy
        return (carry[0] + sums[0], carry[1] + sums[1])

    zero = jnp.zeros((8, half), F32)
    add_sums(sums_ref, own, over_rows(zt_ref.shape[0], tail, (zero, zero)))


def spread_back_body(side, slots, dy_ref, z_ref, s_ref, g_ref, q_ref, total_ref, mask_ref, edge_ref, w_ref, zi_ref, si_ref, gi_ref, bi_ref, moved_ref, dyi_ref, sums_ref, padded_ref, grad_ref):
    total = total_ref[2:3, 0:1]
    count, half = z_ref.shape
    tap = pl.program_id(0)

    @pl.when(tap == 0)
    def _():
        padded_ref[0:GUARD, :] = jnp.zeros((GUARD, half), F32)
        padded_ref[GUARD + count :, :] = jnp.zeros((GUARD, half), F32)
        mean, inverse = moments(s_ref, total, slice(None))
        factor = g_ref[...] * inverse
        first, second = q_ref[0:1, :] / total, q_ref[1:2, :] / total

        def body(r, _):
            dz = settle(dy_ref[r, :], z_ref[r, :], mask_ref[r, 0:1], mean, inverse, factor, first, second)
            padded_ref[pl.ds(r.start + GUARD, CHUNK), :] = dz

        over_rows(count, body)
        grad_ref[...] = jnp.zeros_like(grad_ref)

    move_rows(padded_ref, edge_ref, moved_ref.at[0], side, slots, -1)
    grad_ref[...] += product2_t(moved_ref.at[0], (), w_ref[0])

    @pl.when(tap == pl.num_programs(0) - 1)
    def _():
        sums_ref[...] = jnp.zeros_like(sums_ref)
        own = slice(0, half)
        mean, inverse = moments(si_ref, total, own)
        gain, shift = gi_ref[...], bi_ref[...]

        def tail(r, carry):
            dy, sums = norm_slope(zi_ref, grad_ref[r, :], mask_ref, r, own, mean, inverse, gain, shift)
            dyi_ref[r, :] = dy
            return (carry[0] + sums[0], carry[1] + sums[1])

        zero = jnp.zeros((8, half), F32)
        add_sums(sums_ref, own, over_rows(count, tail, (zero, zero)))


def inner_back_body(dy_ref, zi_ref, si_ref, gi_ref, q_ref, total_ref, mask_ref, w_ref, joined_ref, zm_ref, gm_ref, bm_ref, dz_ref, dym_ref, sums_ref, grad_ref):
    total = total_ref[2:3, 0:1]
    half = zi_ref.shape[1]
    own = slice(0, half)
    upper = slice(half, 2 * half)
    mean, inverse = moments(si_ref, total, own)
    factor = gi_ref[...] * inverse
    first, second = q_ref[0:1, :] / total, q_ref[1:2, :] / total

    def body(r, _):
        dz = settle(dy_ref[r, :], zi_ref[r, :], mask_ref[r, 0:1], mean, inverse, factor, first, second)
        split_store(dz_ref, (r,), dz)

    over_rows(zi_ref.shape[0], body)
    grad_ref[...] = product2_t(dz_ref, (), w_ref[...])
    start_sums(sums_ref)
    mean, inverse = moments(total_ref, total, upper)
    gain, shift = gm_ref[0:1, upper], bm_ref[0:1, upper]

    def tail(r, carry):
        dy, sums = norm_slope(zm_ref, grad_ref[r, :] + joined_ref[r, :], mask_ref, r, own, mean, inverse, gain, shift)
        dym_ref[r, :] = dy
        return (carry[0] + sums[0], carry[1] + sums[1])

    zero = jnp.zeros((8, half), F32)
    add_sums(sums_ref, own, over_rows(zi_ref.shape[0], tail, (zero, zero)))


def split_back_body(dy_ref, zm_ref, q_ref, total_ref, g_ref, mask_ref, dzp_ref, w_ref, dz_ref, grad_ref, scratch_ref):
    total = total_ref[2:3, 0:1]
    half = zm_ref.shape[1]
    upper = slice(half, 2 * half)
    mean, inverse = moments(total_ref, total, upper)
    factor = g_ref[0:1, upper] * inverse
    first, second = q_ref[0:1, :] / total, q_ref[1:2, :] / total

    def body(r, _):
        dz = settle(dy_ref[r, :], zm_ref[r, :], mask_ref[r, 0:1], mean, inverse, factor, first, second)
        split_store(dz_ref, (r,), dz)

    over_rows(zm_ref.shape[0], body)
    scratch_ref[...] = product2_t(dzp_ref, (), w_ref[:, :half])
    scratch_ref[...] += product2_t(dz_ref, (), w_ref[:, half:])
    spread_out(scratch_ref, grad_ref)


def final_body(pieces, *refs):
    count = len(pieces)
    sources, dzp_hbm, dzm_hbm, w_hbm, refs = refs[:count], refs[count], refs[count + 1], refs[count + 2], refs[count + 3 :]
    targets, grad_hbm, refs = refs[:count], refs[count], refs[count + 1 :]
    buffers, (dzp_ref, dzm_ref, w_ref, wide_ref, staged_ref, load_sem, store_sem, own_sem, grad_sem) = refs[:count], refs[count:]
    half = dzp_ref.shape[2]
    pitch = wide_ref.shape[0]
    places = staged_ref.shape[1]
    tiles = dzp_ref.shape[1] // pitch
    own = [pltpu.make_async_copy(w_hbm, w_ref, own_sem.at[0])]
    for k in range(tiles):
        rows_k = slice(k * pitch, (k + 1) * pitch)
        own.append(pltpu.make_async_copy(dzp_hbm.at[:, rows_k], dzp_ref.at[:, rows_k], own_sem.at[1 + 2 * k]))
        own.append(pltpu.make_async_copy(dzm_hbm.at[:, rows_k], dzm_ref.at[:, rows_k], own_sem.at[2 + 2 * k]))
    loads, stores = [], []
    for source, buffer, target, cuts in zip(sources, buffers, targets, pieces):
        for begin, end in cuts:
            k = len(loads)
            loads.append(pltpu.make_async_copy(source.at[begin:end], buffer.at[begin:end], load_sem.at[k]))
            stores.append(pltpu.make_async_copy(buffer.at[begin:end], target.at[begin:end], store_sem.at[k]))
    for copy in own[:3]:
        copy.start()
    ahead = len(loads) // 2
    for copy in loads[:ahead]:
        copy.start()
    for copy in own[3:]:
        copy.start()
    for copy in loads[ahead:]:
        copy.start()

    def forward(begin, end):
        for k in range(begin, end):
            loads[k].wait()
            stores[k].start()

    def grad_store(k):
        size = min(places, grad_hbm.shape[0] - k * places)
        return pltpu.make_async_copy(staged_ref.at[k % 2, 0:size], grad_hbm.at[k * places : k * places + size], grad_sem.at[k % 2])

    own[0].wait()
    step = -(-len(loads) // (tiles + 1))
    for k in range(tiles):
        own[1 + 2 * k].wait()
        own[2 + 2 * k].wait()
        rows_k = slice(k * pitch, (k + 1) * pitch)
        wide_ref[...] = product2_t(dzp_ref, (rows_k,), w_ref[:, :half]) + product2_t(dzm_ref, (rows_k,), w_ref[:, half:])
        if k >= 2:
            grad_store(k - 2).wait()
        spread_out(wide_ref, staged_ref.at[k % 2])
        grad_store(k).start()
        forward(min(k * step, len(loads)), min((k + 1) * step, len(loads)))
    forward(min(tiles * step, len(loads)), len(loads))
    for k in range(max(0, tiles - 2), tiles):
        grad_store(k).wait()
    for copy in stores:
        copy.wait()


def final_call(arrays, dzp, dzm, weight, slots):
    hbm = pl.BlockSpec(memory_space=pl.ANY)
    vmem, dma = pltpu.VMEM, pltpu.SemaphoreType.DMA
    full, count = weight.shape[0], dzp.shape[1]
    pitch = count // TILES
    pieces = []
    for array in arrays:
        length = array.shape[0]
        row_bytes = 4 * array.size // length
        step = min(length, max(1, (1 << 20) // row_bytes))
        pieces.append([(begin, min(begin + step, length)) for begin in range(0, length, step)])
    number = sum(len(cuts) for cuts in pieces)
    pixel_shape = arrays[0].shape
    scratch = [vmem(array.shape, F32) for array in arrays]
    scratch += [
        vmem(dzp.shape, BF16), vmem(dzm.shape, BF16), vmem(weight.shape, BF16), vmem((pitch, full), F32), vmem((2, pitch // slots, slots, full), F32),
        dma((number,)), dma((number,)), dma((1 + 2 * TILES,)), dma((2,)),
    ]
    return pl.pallas_call(
        functools.partial(final_body, pieces),
        in_specs=[hbm] * (len(arrays) + 3),
        out_specs=[hbm] * (len(arrays) + 1),
        out_shape=[sds(array.shape) for array in arrays] + [sds(pixel_shape)],
        scratch_shapes=scratch,
        compiler_params=params(60),
    )(*arrays, dzp, dzm, weight)


def weight_body(x_ref, dz_ref, dw_ref):
    turned = x_ref[0].T
    value = dot(turned, dz_ref[0]) + dot(turned, dz_ref[1])
    if x_ref.shape[0] == 2:
        value += dot(x_ref[1].T, dz_ref[0])
    dw_ref[...] = value


def weight_grad(x, dz, block=256):
    parts, count, width = x.shape
    wide = dz.shape[2]
    return pl.pallas_call(
        weight_body,
        grid=(width // block,),
        in_specs=[pl.BlockSpec((parts, count, block), lambda i: (0, 0, i)), whole(dz)],
        out_specs=pl.BlockSpec((block, wide), lambda i: (i, 0)),
        out_shape=sds((width, wide)),
        compiler_params=params(),
    )(x, dz)


SPLIT, INNER, SPREAD, TRANS, OUT, BACK_OUT = range(6)


def front_body(side, slots, *refs):
    (features_hbm, cotangent_hbm, w_split_hbm, w_inner_hbm, w_spread_hbm, w_trans_hbm, w_out_hbm), refs = refs[:7], refs[7:]
    (g_split, b_split, g_inner, b_inner, g_spread, b_spread, g_trans, b_trans, g_out, b_out, edge_ref, counts_ref, sides_ref), refs = refs[:13], refs[13:]
    (x_out, zp_out, zm_out, main_out, part_out, zi_out, inner_out, zs_out, joined_out, zt_out, trans_out, result_hbm, dlow_out, dhigh_out, total_ref, mask_ref), refs = refs[:16], refs[16:]
    (p0, p1, p2, p3, p4, p5, p6, p7, q0, q1, q2, q3, wide_ref, feature_ref, cot_ref, staged_ref), refs = refs[:16], refs[16:]
    (w_split, w_inner, w_spread, w_trans, w_out, local_ref, packed_ref, shared_ref), refs = refs[:8], refs[8:]
    weight_sem, feature_sem, cot_sem, staged_sem, out_sem, sum_send, sum_recv = refs
    count, half = p0.shape
    pitch = count // TILES
    places = pitch // slots
    low, high, everything = slice(0, half), slice(half, 2 * half), slice(None)
    dp, bn = lax.axis_index("dp"), lax.axis_index("bn")
    members = shared_ref.shape[1]
    group = [lax.rem(bn + k, members) for k in range(1, members)]

    weights = [
        pltpu.make_async_copy(source, target, weight_sem.at[k])
        for k, (source, target) in enumerate(
            ((w_split_hbm, w_split), (w_inner_hbm, w_inner), (w_spread_hbm, w_spread), (w_trans_hbm, w_trans), (w_out_hbm, w_out))
        )
    ]

    def rows_of(k):
        return min(places, features_hbm.shape[0] - k * places)

    def feature_load(k):
        size = rows_of(k)
        return pltpu.make_async_copy(features_hbm.at[k * places : k * places + size], feature_ref.at[k % 2, 0:size], feature_sem.at[k % 2])

    def cot_load(k):
        size = rows_of(k)
        return pltpu.make_async_copy(cotangent_hbm.at[k * places : k * places + size], cot_ref.at[0:size], cot_sem)

    def result_store(k):
        size = rows_of(k)
        return pltpu.make_async_copy(staged_ref.at[0:size], result_hbm.at[k * places : k * places + size], staged_sem)

    pending = {}

    def write(name, source, target):
        copy = pltpu.make_async_copy(source, target, out_sem.at[len(pending)])
        copy.start()
        pending[name] = [copy, True]

    def written(name):
        if pending[name][1]:
            pending[name][0].wait()
            pending[name][1] = False

    def sum_copies(which):
        wide = slice(0, 384 if which == SPLIT else 256)
        return wide, [
            pltpu.make_async_remote_copy(
                src_ref=packed_ref.at[which, :, wide], dst_ref=shared_ref.at[which, bn, :, wide],
                send_sem=sum_send.at[which, k], recv_sem=sum_recv.at[which, k], device_id={"bn": peer}, device_id_type=MESH,
            )
            for k, peer in enumerate(group)
        ]

    def exchange(which, width, beside=None):
        wide, copies = sum_copies(which)
        pieces = [(j, slice(j * 128, (j + 1) * 128)) for j in range(width // 128)]
        for j, piece in pieces:
            packed_ref[which, j : j + 1, 0:128] = local_ref[which, 0:1, piece]
            packed_ref[which, j : j + 1, 128:256] = local_ref[which, 1:2, piece]
        if which == SPLIT:
            packed_ref[which, 0:1, 256:384] = local_ref[which, 2:3, 0:128]
        for copy in copies:
            copy.start()
        shared_ref[which, bn, :, wide] = packed_ref[which, :, wide]
        if beside is not None:
            beside()
        for copy in copies:
            copy.wait()
        value = shared_ref[which, 0, :, wide]
        for k in range(1, members):
            value = value + shared_ref[which, k, :, wide]
        for j, piece in pieces:
            total_ref[which, 0:1, piece] = value[j : j + 1, 0:128]
            total_ref[which, 1:2, piece] = value[j : j + 1, 128:256]
        if which == SPLIT:
            total_ref[which, 2:3, 0:128] = value[0:1, 256:384]

    def stats(which):
        return total_ref.at[which]

    def affine(which, gain_ref, shift_ref, columns):
        mean, inverse = moments(stats(which), total_ref[SPLIT, 2:3, 0:1], columns)
        return mean, gain_ref[0:1, columns] * inverse, shift_ref[0:1, columns]

    def activate(z_ref, r, mean, scale, shift):
        return mish((z_ref[r, :] - mean) * scale + shift) * mask_ref[r, 0:1]

    feature_load(0).start()
    for k in (0, 1):
        weights[k].start()
    feature_load(1).start()
    barrier = pltpu.get_barrier_semaphore()
    for peer in group:
        pl.semaphore_signal(barrier, inc=1, device_id={"bn": peer}, device_id_type=MESH)
    local_ref[...] = jnp.zeros_like(local_ref)
    packed_ref[...] = jnp.zeros_like(packed_ref)
    total_ref[...] = jnp.zeros_like(total_ref)
    limits = [jnp.where(k < counts_ref[0], sides_ref[k], 0).astype(F32) for k in range(slots)]

    def mask_rows(r, _):
        index = (r.start + lax.broadcasted_iota(jnp.int32, (CHUNK, 128), 0)).astype(F32)
        place = jnp.floor((index + 0.5) * (1.0 / slots))
        slot = index - place * slots
        y = jnp.floor((place + 0.5) * (1.0 / side))
        x = place - y * side
        limit = jnp.zeros_like(index)
        for k in range(slots):
            limit = jnp.where(slot == k, limits[k], limit)
        mask_ref[r, :] = jnp.where(jnp.maximum(x, y) < limit, 1.0, 0.0)

    over_rows(count, mask_rows)
    for k in range(TILES):
        feature_load(k).wait()
        compact(feature_ref.at[k % 2], wide_ref)
        if k + 2 < TILES:
            feature_load(k + 2).start()
        here = pl.ds(k * pitch, pitch)

        def body(r, _, k=k):
            q = pl.ds(pl.multiple_of(r.start + k * pitch, CHUNK), CHUNK)
            for h, columns in enumerate((low, high)):
                q0[h, q, :] = jnp.where(mask_ref[q, 0:1] > 0.0, wide_ref[r, columns], 0.0).astype(BF16)

        over_rows(pitch, body)
    for k in (2, 3, 4):
        weights[k].start()
    cot_load(0).start()
    write("x", q0, x_out)
    weights[0].wait()
    p0[...] = dot(q0[0], w_split[low, low]) + dot(q0[1], w_split[high, low])
    p1[0:count, :] = dot(q0[0], w_split[low, high]) + dot(q0[1], w_split[high, high])
    write("zm", p1.at[0:count], zm_out)
    write("zp", p0, zp_out)

    def add_squares(which, z_ref, columns, masked=False):
        def body(r, carry):
            value = z_ref[r, :]
            kept = value * mask_ref[r, 0:1] if masked else value
            return (carry[0] + fold(kept), carry[1] + fold(kept * value))

        zero = jnp.zeros((8, half), F32)
        add_sums(local_ref.at[which], columns, over_rows(count, body, (zero, zero)))

    add_squares(SPLIT, p0, low)
    add_squares(SPLIT, p1, high)
    local_ref[SPLIT, 2:3, 0:128] = jnp.sum(mask_ref[...], axis=0, keepdims=True)
    pl.semaphore_wait(barrier, members - 1)
    exchange(SPLIT, 2 * half)

    mean, scale, shift = affine(SPLIT, g_split, b_split, high)

    def main_rows(r, _):
        act = activate(p1, r, mean, scale, shift)
        p2[r, :] = act
        split_store(q2, (r,), act)

    over_rows(count, main_rows)
    write("main", q2, main_out)
    weights[1].wait()
    p3[...] = product2(q2, (), w_inner[...])
    write("zi", p3, zi_out)
    add_squares(INNER, p3, low)
    mean_p, scale_p, shift_p = affine(SPLIT, g_split, b_split, low)

    def part_rows(r, _):
        split_store(q1, (r,), activate(p0, r, mean_p, scale_p, shift_p))

    exchange(INNER, half, lambda: over_rows(count, part_rows))
    write("part", q1, part_out)

    written("zm")
    written("x")
    mean_i, scale_i, shift_i = affine(INNER, g_inner, b_inner, low)
    p1[0:GUARD, :] = jnp.zeros((GUARD, half), F32)
    p1[GUARD + count :, :] = jnp.zeros((GUARD, half), F32)

    def inner_rows(r, _):
        act = activate(p3, r, mean_i, scale_i, shift_i)
        p1[pl.ds(r.start + GUARD, CHUNK), :] = act
        split_store(q0, (r,), act)

    over_rows(count, inner_rows)
    write("inner", q0, inner_out)
    weights[2].wait()
    written("zi")
    written("main")
    for tap, (move, dx) in enumerate(taps(side, slots)):
        if move:
            pair_ref = (q2, q3)[tap % 2]
            moved = p1[GUARD + move : GUARD + move + count, :]
            if dx:
                moved = moved * edge_ref[:, dx + 1 : dx + 2]
            split_store(pair_ref, (slice(None),), moved)
        else:
            pair_ref = q0
        part = product2(pair_ref, (), w_spread[tap])
        if tap == 0:
            p3[...] = part
        else:
            p3[...] += part
    write("zs", p3, zs_out)
    add_squares(SPREAD, p3, low, True)
    exchange(SPREAD, half)

    mean_s, scale_s, shift_s = affine(SPREAD, g_spread, b_spread, low)

    def joined_rows(r, _):
        split_store(q2, (r,), activate(p3, r, mean_s, scale_s, shift_s) + p2[r, :])

    over_rows(count, joined_rows)
    write("joined", q2, joined_out)
    weights[3].wait()
    p2[...] = product2(q2, (), w_trans[...])
    write("zt", p2, zt_out)
    add_squares(TRANS, p2, low)
    exchange(TRANS, half)

    mean_t, scale_t, shift_t = affine(TRANS, g_trans, b_trans, low)

    def trans_rows(r, _):
        split_store(q3, (r,), activate(p2, r, mean_t, scale_t, shift_t))

    over_rows(count, trans_rows)
    write("trans", q3, trans_out)
    weights[4].wait()
    for page, columns in ((p4, low), (p5, high)):
        page[...] = product2(q3, (), w_out[low, columns]) + product2(q1, (), w_out[high, columns])
        add_squares(OUT, page, columns)
    exchange(OUT, 2 * half)

    total = total_ref[SPLIT, 2:3, 0:1]
    for k in range(TILES):
        cot_load(k).wait()
        compact(cot_ref, wide_ref)
        if k + 1 < TILES:
            cot_load(k + 1).start()
        for page, slope_page, columns in ((p4, p6, low), (p5, p7, high)):
            mean_o, inverse_o = moments(stats(OUT), total, columns)
            gain, shift_o = g_out[0:1, columns], b_out[0:1, columns]

            def body(r, carry, k=k, page=page, slope_page=slope_page, columns=columns):
                q = pl.ds(pl.multiple_of(r.start + k * pitch, CHUNK), CHUNK)
                mask = mask_ref[q, 0:1]
                scaled = (page[q, :] - mean_o) * inverse_o
                y = scaled * gain + shift_o
                t = jnp.exp(jnp.minimum(y, 30.0))
                n = t * (t + 2.0)
                inv = 1.0 / (n + 2.0)
                ratio = n * inv
                slope = ratio + y * (((4.0 * t) * (t + 1.0) * inv) * inv)
                dy = jnp.where(mask > 0.0, wide_ref[r, columns], 0.0) * slope
                wide_ref[r, columns] = y * ratio * mask
                slope_page[q, :] = dy
                return (carry[0] + fold(dy), carry[1] + fold(dy * scaled))

            zero = jnp.zeros((8, half), F32)
            add_sums(local_ref.at[BACK_OUT], columns, over_rows(pitch, body, (zero, zero)))
        if k:
            result_store(k - 1).wait()
        spread_out(wide_ref, staged_ref)
        result_store(k).start()
    exchange(BACK_OUT, 2 * half)

    def settled(page, z_page, pair_ref, which, back, gain_ref, columns, back_columns):
        mean_k, inverse_k = moments(stats(which), total, columns)
        factor = gain_ref[0:1, columns] * inverse_k
        first, second = total_ref[back, 0:1, back_columns] / total, total_ref[back, 1:2, back_columns] / total

        def body(r, _):
            split_store(pair_ref, (r,), settle(page[r, :], z_page[r, :], mask_ref[r, 0:1], mean_k, inverse_k, factor, first, second))

        over_rows(count, body)

    written("inner")
    written("joined")
    settled(p6, p4, q0, OUT, BACK_OUT, g_out, low, low)
    settled(p7, p5, q2, OUT, BACK_OUT, g_out, high, high)
    write("dlow", q0, dlow_out)
    write("dhigh", q2, dhigh_out)
    result_store(TILES - 1).wait()
    for name in list(pending):
        written(name)


def front_call(arrays, constants, scalars, slots, side, count, members):
    hbm, vmem_spec = pl.BlockSpec(memory_space=pl.ANY), pl.BlockSpec(memory_space=pltpu.VMEM)
    vmem, dma = pltpu.VMEM, pltpu.SemaphoreType.DMA
    full = arrays[0].shape[2]
    half = full // 2
    pitch = count // TILES
    pair, page = sds((2, count, half), BF16), sds((count, half))
    outs = [pair, page, page, pair, pair, page, pair, page, pair, page, pair, sds(arrays[1].shape), pair, pair]
    scratch = [vmem((count, half), F32), vmem((count + 2 * GUARD, half), F32)] + [vmem((count, half), F32)] * 6
    scratch += [vmem((2, count, half), BF16)] * 4
    scratch += [
        vmem((pitch, full), F32), vmem((2, pitch // slots, slots, full), BF16), vmem((pitch // slots, slots, full), F32), vmem((pitch // slots, slots, full), F32),
        vmem((full, full), BF16), vmem((half, half), BF16), vmem((9, half, half), BF16), vmem((half, half), BF16), vmem((full, full), BF16),
        vmem((6, 8, full), F32), vmem((6, 8, 384), F32), vmem((6, members, 8, 384), F32),
        dma((5,)), dma((2,)), dma(()), dma(()), dma((16,)), dma((6, members - 1)), dma((6, members - 1)),
    ]
    return pl.pallas_call(
        functools.partial(front_body, side, slots),
        in_specs=[hbm] * len(arrays) + [vmem_spec] * len(constants) + [pl.BlockSpec(memory_space=pltpu.SMEM)] * 2,
        out_specs=[hbm] * len(outs) + [vmem_spec] * 2,
        out_shape=outs + [sds((6, 8, full)), sds((count, 128))],
        scratch_shapes=scratch,
        compiler_params=pltpu.CompilerParams(collective_id=1, has_side_effects=True, vmem_limit_bytes=60 * 1024 * 1024),
    )(*arrays, *constants, *scalars)


LAG = 8
KEPT = 6


def reduce_body(jobs, side, slots, *refs):
    lefts, rights, refs = refs[:6], refs[6:8], refs[8:]
    (zt_hbm, zp_hbm, zs_hbm, zi_hbm, zm_hbm, ws_hbm), refs = refs[:6], refs[6:]
    (totals_ref, g_split, b_split, g_inner, b_inner, g_spread, b_spread, g_trans, b_trans, mask_ref, edge_ref, wi_ref, wt_ref, wo_ref), refs = refs[:14], refs[14:]
    outs, dpart_out, dmain_out, vectors_ref, refs = refs[:5], refs[5], refs[6], refs[7], refs[8:]
    (x_ref, z_ref, turned_ref, own_ref, r0_ref, half_ref, r1_ref, quarter_ref, r2_ref, eighth_ref, r3_ref, full_ref, load_sem, store_sem) = refs[:14]
    (padded_ref, grad_ref, page_ref, joined_ref, zm_ref, pair_ref, part_ref, wide_ref, tap_ref, sums_ref, shared_ref, small_ref, spread_ref) = refs[14:27]
    (page_sem, tap_sem, write_sem, sum_send, sum_recv, small_send, small_recv) = refs[27:34]
    sems = refs[34:]
    count, half = grad_ref.shape
    pitch = wide_ref.shape[0]
    tiles = count // pitch
    s_split, q_out = totals_ref.at[SPLIT], totals_ref.at[BACK_OUT]
    s_spread, s_trans, s_inner = (totals_ref.at[k, :, 0:half] for k in (SPREAD, TRANS, INNER))
    stats_total = s_split[2:3, 0:1]
    block = own_ref.shape[1]
    mid = block // 2
    dp, bn = lax.axis_index("dp"), lax.axis_index("bn")
    z, x, y, core = dp // 2, dp % 2, bn // 2, bn % 2

    def at(new_z, new_x, new_y, new_core):
        return {"dp": new_z * 2 + new_x, "bn": new_y * 2 + new_core}

    to_core, to_x, to_y = at(z, x, y, 1 - core), at(z, 1 - x, y, core), at(z, x, 1 - y, core)
    depth = [(z + k) % 4 for k in (1, 2, 3)]
    to_z = [at(new_z, x, y, core) for new_z in depth]
    to_far = [at(new_z, 1 - x, y, core) for new_z in depth]
    to_diagonal = at(z, x, 1 - y, 1 - core)
    columns = (pl.ds(0, mid), pl.ds(mid, mid))

    def part(start, size):
        return pl.ds(pl.multiple_of(start, size), size)

    def far(stage, k, slot, source, target, peer):
        send, recv = sems[2 * stage], sems[2 * stage + 1]
        return pltpu.make_async_remote_copy(
            src_ref=source, dst_ref=target, send_sem=send.at[k, slot], recv_sem=recv.at[k, slot], device_id=peer, device_id_type=MESH
        )

    first = (x, y)
    second = (y, x)
    sides = (to_x, to_y)

    def copies(stage, c):
        slot, keep = c % 2, c % KEPT
        base = core * (block // 2)
        if stage == 0:
            return [far(0, 0, slot, own_ref.at[slot, part((1 - core) * (block // 2), block // 2)], r0_ref.at[slot], to_core)]
        if stage == 1:
            return [
                far(1, k, slot, half_ref.at[slot, part((1 - first[k]) * (block // 4), block // 4), columns[k]], r1_ref.at[slot, :, columns[k]], sides[k])
                for k in (0, 1)
            ]
        if stage == 2:
            return [
                far(2, k, slot, quarter_ref.at[slot, part((1 - second[k]) * (block // 8), block // 8), columns[k]], r2_ref.at[slot, :, columns[k]], sides[1 - k])
                for k in (0, 1)
            ]
        if stage == 3:
            return [
                far(3, k, slot, eighth_ref.at[slot, part(depth[k] * (block // 32), block // 32)], r3_ref.at[slot, k], to_z[k]) for k in (0, 1, 2)
            ]
        made = []
        for k in (0, 1):
            eighth = base + first[k] * (block // 4) + second[k] * (block // 8)
            if stage == 4:
                spot = full_ref.at[keep, part(eighth + z * (block // 32), block // 32), columns[k]]
                made += [far(4, 3 * k + d, slot, spot, spot, to_z[d]) for d in (0, 1, 2)]
            elif stage == 5:
                spot = full_ref.at[keep, part(eighth, block // 8), columns[k]]
                made.append(far(5, k, slot, spot, spot, sides[1 - k]))
            elif stage == 6:
                spot = full_ref.at[keep, part(base + first[k] * (block // 4), block // 4), columns[k]]
                made.append(far(6, k, slot, spot, spot, sides[k]))
        if stage == 7:
            spot = full_ref.at[keep, part(base, block // 2)]
            made.append(far(7, 0, slot, spot, spot, to_core))
        return made

    def begin(stage, c):
        for copy in copies(stage, c):
            copy.start()

    def finish(stage, c):
        for copy in copies(stage, c):
            copy.wait()

    def load(j):
        if jobs[j] is None:
            return []
        (left, begin_part, parts), right, _ = jobs[j]
        slot = j % 2
        made = [pltpu.make_async_copy(lefts[left].at[begin_part : begin_part + parts], x_ref.at[slot, 0:parts], load_sem.at[slot, 0])]
        source = {"pair": pair_ref, "part": part_ref, 0: rights[0], 1: rights[1]}.get(right)
        if source is not None:
            made.append(pltpu.make_async_copy(source, z_ref.at[slot], load_sem.at[slot, 1]))
        return made

    def store(j):
        out, spot = jobs[j][2]
        return pltpu.make_async_copy(full_ref.at[j % KEPT], outs[out].at[spot], store_sem.at[j % KEPT])


    everything = slice(None)

    def page(source, target, k):
        return pltpu.make_async_copy(source, target, page_sem.at[k])

    def tap_load(tap):
        return pltpu.make_async_copy(ws_hbm.at[tap], tap_ref.at[tap % 2], tap_sem.at[tap % 2])

    upper = slice(half, 2 * half)
    load_zt, load_zp, load_zs = page(zt_hbm, page_ref, 0), page(zp_hbm, joined_ref, 1), page(zs_hbm, page_ref, 0)
    load_zi, load_zm = page(zi_hbm, page_ref, 0), page(zm_hbm, zm_ref, 2)
    write_part = pltpu.make_async_copy(part_ref, dpart_out, write_sem.at[0])
    write_main = pltpu.make_async_copy(z_ref.at[1], dmain_out, write_sem.at[1])

    group = [at(z, x, y, 1 - core), at(z, x, 1 - y, core), to_diagonal]

    def sum_copies(which):
        return [
            pltpu.make_async_remote_copy(
                src_ref=sums_ref.at[which], dst_ref=shared_ref.at[which, bn], send_sem=sum_send.at[which, k], recv_sem=sum_recv.at[which, k], device_id=peer, device_id_type=MESH
            )
            for k, peer in enumerate(group)
        ]

    def sum_start(which):
        for copy in sum_copies(which):
            copy.start()
        shared_ref[which, bn] = sums_ref[which]

    def sum_finish(which):
        for copy in sum_copies(which):
            copy.wait()
        value = shared_ref[which, 0]
        for k in range(1, shared_ref.shape[1]):
            value = value + shared_ref[which, k]
        sums_ref[which] = value

    everyone = [to_x] + to_z + to_far

    def small_copies():
        return [
            pltpu.make_async_remote_copy(
                src_ref=small_ref, dst_ref=spread_ref.at[dp], send_sem=small_send.at[k], recv_sem=small_recv.at[k], device_id=peer, device_id_type=MESH
            )
            for k, peer in enumerate(everyone)
        ]

    def settled(dy_ref, z_page, which, back, gain_ref, columns, keep):
        mean, inverse = moments(which, stats_total, columns)
        factor = gain_ref[0:1, columns] * inverse
        first_sum, second_sum = sums_ref[back, 0:1, :] / stats_total, sums_ref[back, 1:2, :] / stats_total

        def body(r, _):
            keep(r, settle(dy_ref[r, :], z_page[r, :], mask_ref[r, 0:1], mean, inverse, factor, first_sum, second_sum))

        over_rows(count, body)

    def sloped(grad, target_ref, z_page, which, back, gain_ref, shift_ref, columns):
        mean, inverse = moments(which, stats_total, columns)
        gain, shift = gain_ref[0:1, columns], shift_ref[0:1, columns]

        def body(r, carry):
            dy, sums = norm_slope(z_page, grad[r, :], mask_ref, r, everything, mean, inverse, gain, shift)
            target_ref[r, :] = dy
            return (carry[0] + sums[0], carry[1] + sums[1])

        zero = jnp.zeros((8, half), F32)
        add_sums(sums_ref.at[back], everything, over_rows(count, body, (zero, zero)))
        sum_start(back)

    own, lower = everything, slice(0, half)

    def stacked(step):
        columns_k = slice(step * half, (step + 1) * half)
        for target_ref, rows_k in ((grad_ref, lower), (zm_ref, upper)):
            value = product2_t(z_ref.at[step % 2], (), wo_ref[rows_k, columns_k])
            if step == 0:
                target_ref[...] = value
            else:
                target_ref[...] += value

    def middle_slopes():
        load_zt.wait()
        load_zp.wait()
        sloped(grad_ref, grad_ref, page_ref, s_trans, 2, g_trans, b_trans, own)
        sloped(zm_ref, zm_ref, joined_ref, s_split, 3, g_split, b_split, lower)

    def middle():
        sum_finish(2)
        sum_finish(3)
        settled(grad_ref, page_ref, s_trans, 2, g_trans, own, lambda r, dz: split_store(pair_ref, (r,), dz))
        load_zs.start()
        settled(zm_ref, joined_ref, s_split, 3, g_split, lower, lambda r, dz: split_store(part_ref, (r,), dz))
        load_zm.start()
        write_part.start()
        joined_ref[...] = product2_t(pair_ref, (), wt_ref[...])
        load_zs.wait()
        sloped(joined_ref, grad_ref, page_ref, s_spread, 4, g_spread, b_spread, own)

    def prepare():
        sum_finish(4)
        padded_ref[0:GUARD, :] = jnp.zeros((GUARD, half), F32)
        padded_ref[GUARD + count :, :] = jnp.zeros((GUARD, half), F32)

        def keep(r, dz):
            padded_ref[pl.ds(r.start + GUARD, CHUNK), :] = dz

        settled(grad_ref, page_ref, s_spread, 4, g_spread, own, keep)
        load_zi.start()
        grad_ref[...] = jnp.zeros_like(grad_ref)

    def tap_work(tap):
        move, dx = taps(side, slots)[tap]
        slot = tap % 2
        moved = padded_ref[GUARD - move : GUARD - move + count, :]
        if dx:
            moved = moved * edge_ref[:, 1 - dx : 2 - dx]
        high = moved.astype(BF16)
        z_ref[slot, 0] = high
        z_ref[slot, 1] = (moved - high.astype(F32)).astype(BF16)
        tap_load(tap).wait()
        if tap < 8:
            tap_load(tap + 1).start()

    def tap_gradient(slot):
        grad_ref[...] += dot_t(z_ref[slot, 0], tap_ref[slot]) + dot_t(z_ref[slot, 1], tap_ref[slot])

    def inner_slope():
        load_zi.wait()
        sloped(grad_ref, grad_ref, page_ref, s_inner, 0, g_inner, b_inner, own)

    def shifted(k):
        return lambda r: pl.ds(pl.multiple_of(r.start + k * pitch, CHUNK), CHUNK)

    def inner_tile(k):
        mean, inverse = moments(s_inner, stats_total, everything)
        factor = g_inner[...] * inverse
        first_sum, second_sum = sums_ref[0, 0:1, :] / stats_total, sums_ref[0, 1:2, :] / stats_total
        here = shifted(k)

        def body(r, _):
            q = here(r)
            dz = settle(grad_ref[q, :], page_ref[q, :], mask_ref[q, 0:1], mean, inverse, factor, first_sum, second_sum)
            split_store(pair_ref, (q,), dz)

        over_rows(pitch, body)
        rows_k = slice(k * pitch, (k + 1) * pitch)
        wide_ref[...] = product2_t(pair_ref, (rows_k,), wi_ref[...])
        mean, inverse = moments(s_split, stats_total, upper)
        gain, shift = g_split[0:1, upper], b_split[0:1, upper]

        def tail(r, carry):
            q = here(r)
            dy, sums = norm_slope(zm_ref, wide_ref[r, :] + joined_ref[q, :], mask_ref, q, everything, mean, inverse, gain, shift)
            grad_ref[q, :] = dy
            return (carry[0] + sums[0], carry[1] + sums[1])

        zero = jnp.zeros((8, half), F32)
        add_sums(sums_ref.at[1], everything, over_rows(pitch, tail, (zero, zero)))

    def small_start():
        pieces = [
            (sums_ref.at[3], everything), (sums_ref.at[1], everything), (sums_ref.at[0], everything), (sums_ref.at[4], everything),
            (sums_ref.at[2], everything), (q_out, slice(0, half)), (q_out, slice(half, 2 * half)),
        ]
        small_ref[...] = jnp.zeros_like(small_ref)
        for k, (ref, columns_k) in enumerate(pieces):
            small_ref[k : k + 1, :] = ref[0:1, columns_k]
            small_ref[8 + k : 9 + k, :] = ref[1:2, columns_k]
        for copy in small_copies():
            copy.start()
        spread_ref[dp] = small_ref[...]

    def small_finish():
        for copy in small_copies():
            copy.wait()
        value = spread_ref[0]
        for k in range(1, spread_ref.shape[0]):
            value = value + spread_ref[k]
        vectors_ref[...] = value

    def main_settle():
        def keep(r, dz):
            high = dz.astype(BF16)
            rest = (dz - high.astype(F32)).astype(BF16)
            for slot in (0, 1):
                z_ref[slot, 0, r, :] = high
                z_ref[slot, 1, r, :] = rest

        settled(grad_ref, zm_ref, s_split, 1, g_split, upper, keep)
        write_main.start()

    FIRST_TAP = 6
    hosted = {
        2: [functools.partial(stacked, 0)],
        3: [functools.partial(stacked, 1), middle_slopes],
        4: [middle],
        5: [prepare],
        15: [inner_slope],
        16: [load_zm.wait, lambda: sum_finish(0), functools.partial(inner_tile, 0), functools.partial(inner_tile, 1)],
        17: [functools.partial(inner_tile, 2), functools.partial(inner_tile, 3), lambda: sum_start(1)],
        18: [lambda: sum_finish(1), small_start],
        19: [main_settle],
        20: [small_finish, write_part.wait, write_main.wait],
    }

    sums_ref[...] = jnp.zeros_like(sums_ref)
    load_zt.start()
    load_zp.start()
    tap_load(0).start()
    for copy in load(0):
        copy.start()
    barrier = pltpu.get_barrier_semaphore()
    peers = [to_core, to_x, to_y] + to_z + to_far + [to_diagonal]
    for peer in peers:
        pl.semaphore_signal(barrier, inc=1, device_id=peer, device_id_type=MESH)
    pl.semaphore_wait(barrier, len(peers))
    total = len(jobs)
    taken = [j for j in range(total) if jobs[j] is not None]
    empty = [j for j in range(total) if jobs[j] is None]

    @pl.loop(0, total + LAG + 1)
    def _(t):
        for j in taken:

            @pl.when(t == j + LAG + 1)
            def _(j=j):
                store(j).wait()

        def stage(number, lag):
            def wrap(body):
                c = t - lag
                valid = jnp.logical_and(c >= 0, c < total)
                if empty:
                    valid = jnp.logical_and(valid, jnp.logical_or(c < empty[0], c > empty[-1]))
                pl.when(valid)(lambda: body(c))

            return wrap

        @stage(7, 8)
        def _(c):
            finish(7, c)

        for j in taken:

            @pl.when(t == j + LAG)
            def _(j=j):
                store(j).start()

        for number in (6, 5, 4):

            @stage(number, number + 1)
            def _(c, number=number):
                finish(number, c)
                begin(number + 1, c)

        for j in range(total):

            @pl.when(t == j)
            def _(j=j):
                for copy in load(j):
                    copy.wait()
                for task in hosted.get(j, ()):
                    task()
                if j + 1 < total:
                    for copy in load(j + 1):
                        copy.start()
                if 0 <= j - FIRST_TAP < 9:
                    tap_work(j - FIRST_TAP)

        @pl.when(jnp.logical_and(t >= FIRST_TAP, t < FIRST_TAP + 9))
        def _():
            tap_gradient(t % 2)

        @stage(3, 4)
        def _(c):
            finish(3, c)
            slot, keep = c % 2, c % KEPT
            value = eighth_ref[slot, part(z * (block // 32), block // 32), :]
            for k in (0, 1, 2):
                value = value + r3_ref[slot, k]
            for k in (0, 1):
                row = core * (block // 2) + first[k] * (block // 4) + second[k] * (block // 8) + z * (block // 32)
                full_ref[keep, part(row, block // 32), k * mid : (k + 1) * mid] = value[:, k * mid : (k + 1) * mid]
            begin(4, c)

        @stage(2, 3)
        def _(c):
            finish(2, c)
            slot = c % 2
            for k in (0, 1):
                eighth_ref[slot, :, columns[k]] = quarter_ref[slot, part(second[k] * (block // 8), block // 8), columns[k]] + r2_ref[slot, :, columns[k]]
            begin(3, c)

        @stage(1, 2)
        def _(c):
            finish(1, c)
            slot = c % 2
            for k in (0, 1):
                quarter_ref[slot, :, columns[k]] = half_ref[slot, part(first[k] * (block // 4), block // 4), columns[k]] + r1_ref[slot, :, columns[k]]
            begin(2, c)

        @stage(0, 1)
        def _(c):
            finish(0, c)
            slot = c % 2
            half_ref[slot] = own_ref[slot, part(core * (block // 2), block // 2), :] + r0_ref[slot]
            begin(1, c)

        exact = functools.reduce(jnp.logical_or, [t == j for j in taken if jobs[j][0][2] == 1])

        @stage(None, 0)
        def _(c):
            slot = c % 2
            turned_ref[...] = x_ref[slot, 0].T
            own_ref[slot] = dot(turned_ref[...], z_ref[slot, 0]) + dot(turned_ref[...], z_ref[slot, 1])

            @pl.when(jnp.logical_not(exact))
            def _():
                turned_ref[...] = x_ref[slot, 1].T
                own_ref[slot] += dot(turned_ref[...], z_ref[slot, 0])

            begin(0, c)


def reduce_call(jobs, lefts, rights, hosted, constants, shapes, side, slots):
    hbm, vmem_spec = pl.BlockSpec(memory_space=pl.ANY), pl.BlockSpec(memory_space=pltpu.VMEM)
    vmem, dma = pltpu.VMEM, pltpu.SemaphoreType.DMA
    count, block = hosted[0].shape
    pitch = count // TILES
    scratch = [
        vmem((2, 2, count, block), BF16), vmem((2, 2, count, block), BF16), vmem((block, count), BF16),
        vmem((2, block, block), F32), vmem((2, block // 2, block), F32), vmem((2, block // 2, block), F32),
        vmem((2, block // 4, block), F32), vmem((2, block // 4, block), F32), vmem((2, block // 8, block), F32), vmem((2, block // 8, block), F32),
        vmem((2, 3, block // 32, block), F32), vmem((KEPT, block, block), F32),
        dma((2, 2)), dma((KEPT,)),
        vmem((count + 2 * GUARD, block), F32), vmem((count, block), F32), vmem((count, block), F32), vmem((count, block), F32),
        vmem((count, block), F32), vmem((2, count, block), BF16), vmem((2, count, block), BF16), vmem((pitch, block), F32),
        vmem((2, block, block), BF16), vmem((5, 8, block), F32), vmem((5, 4, 8, block), F32),
        vmem((16, block), F32), vmem((8, 16, block), F32),
        dma((3,)), dma((2,)), dma((2,)), dma((5, 3)), dma((5, 3)), dma((7,)), dma((7,)),
    ]
    for width in (1, 2, 2, 3, 6, 2, 2, 1):
        scratch += [dma((width, 2)), dma((width, 2))]
    return pl.pallas_call(
        functools.partial(reduce_body, jobs, side, slots),
        in_specs=[hbm] * (len(lefts) + len(rights) + len(hosted)) + [vmem_spec] * len(constants),
        out_specs=[hbm] * (len(shapes) + 2) + [vmem_spec],
        out_shape=[sds(shape) for shape in shapes] + [sds((2, count, block), BF16)] * 2 + [sds((16, block))],
        scratch_shapes=scratch,
        compiler_params=pltpu.CompilerParams(collective_id=3, has_side_effects=True, vmem_limit_bytes=60 * 1024 * 1024),
    )(*lefts, *rights, *hosted, *constants)


def gather_sums_body(axis, sums_ref, out_ref, slots_ref, send_sem, recv_sem):
    members = slots_ref.shape[0]
    me = lax.axis_index(axis)
    peers = [lax.rem(me + k, members) for k in range(1, members)]
    barrier = pltpu.get_barrier_semaphore()
    for peer in peers:
        pl.semaphore_signal(barrier, inc=1, device_id={axis: peer}, device_id_type=MESH)
    pl.semaphore_wait(barrier, members - 1)
    copies = [
        pltpu.make_async_remote_copy(
            src_ref=sums_ref, dst_ref=slots_ref.at[me], send_sem=send_sem.at[k], recv_sem=recv_sem.at[k], device_id={axis: peer}, device_id_type=MESH
        )
        for k, peer in enumerate(peers)
    ]
    for copy in copies:
        copy.start()
    slots_ref[me] = sums_ref[...]
    for copy in copies:
        copy.wait()
    value = slots_ref[0]
    for k in range(1, members):
        value = value + slots_ref[k]
    out_ref[...] = value


def gather_sums(sums, members, collective, axis="bn"):
    if members == 1:
        return sums
    spec = pl.BlockSpec(memory_space=pltpu.VMEM)
    return pl.pallas_call(
        functools.partial(gather_sums_body, axis),
        in_specs=[spec],
        out_specs=spec,
        out_shape=sds(sums.shape),
        scratch_shapes=[pltpu.VMEM((members,) + sums.shape, F32), pltpu.SemaphoreType.DMA((members - 1,)), pltpu.SemaphoreType.DMA((members - 1,))],
        compiler_params=pltpu.CompilerParams(collective_id=collective, has_side_effects=True),
    )(sums)


def local(
    shape,
    features, image_counts, map_sides,
    split_kernel, split_gain, split_shift, inner_kernel, inner_gain, inner_shift,
    spread_kernel, spread_gain, spread_shift, transition_kernel, transition_gain, transition_shift,
    output_kernel, output_gain, output_shift, cotangent,
):
    slots, side, _, full = features.shape
    half = inner_kernel.shape[0]
    pitch = round_up(-(-slots * side * side // TILES), 16)
    count = TILES * pitch
    grid = (TILES,)
    columns = np.arange(count)[:, None] // slots % side
    lanes = np.arange(128)[None, :]
    edges = jnp.asarray(np.where(lanes == 0, columns > 0, np.where(lanes == 2, columns < side - 1, True)).astype(np.float32))
    features = features.transpose(1, 2, 0, 3).reshape(side * side, slots, full)
    cotangent = cotangent.transpose(1, 2, 0, 3).reshape(side * side, slots, full)
    (split_gain, split_shift, inner_gain, inner_shift, spread_gain, spread_shift, transition_gain, transition_shift, output_gain, output_shift) = (
        item.reshape(1, -1)
        for item in (split_gain, split_shift, inner_gain, inner_shift, spread_gain, spread_shift, transition_gain, transition_shift, output_gain, output_shift)
    )
    spread_weight = spread_kernel.reshape(9, half, half)

    def group(sums):
        return gather_sums(sums, shape[1], 1 if sums.shape[1] == full else 2)

    sums_full, sums_half = out_whole((8, full)), out_whole((8, half))
    r_half, r_full, r_mask = rows(pitch, half), rows(pitch, full), rows(pitch, 128)
    pair_half, pair_full = rows2(pitch, half), rows2(pitch, full)

    def call(body, ins, outs, scratch=(), steps=grid):
        return pl.pallas_call(
            body,
            grid=steps,
            in_specs=[spec for _, spec in ins],
            out_specs=[spec for _, spec in outs],
            out_shape=[shape for shape, _ in outs],
            scratch_shapes=list(scratch),
            compiler_params=params(),
        )(*[array for array, _ in ins])

    def fixed(array):
        return (array, whole(array))

    if shape == (8, 4):
        low, high = slice(0, half), slice(half, full)
        every = slice(None)
        (x0, z_part, z_main, main2, part2, z_inner, inner2, z_spread, joined2, z_trans, trans2, result, dz_low, dz_high, totals, mask) = front_call(
            [features, cotangent, split_kernel, inner_kernel, spread_weight, transition_kernel, output_kernel],
            [split_gain, split_shift, inner_gain, inner_shift, spread_gain, spread_shift, transition_gain, transition_shift, output_gain, output_shift, edges],
            [image_counts, map_sides],
            slots, side, count, shape[1],
        )
        jobs = [((0, 0, 2), 0, (4, (low, low))), ((0, 0, 2), 1, (4, (low, high)))]
        jobs += [((1, 0, 2), 0, (4, (high, low))), ((1, 0, 2), 1, (4, (high, high)))]
        jobs += [None, None]
        jobs += [((4, 0, 2), None, (2, (tap,))) for tap in range(9)]
        jobs += [((2, 0, 2), "pair", (3, (every, every)))]
        jobs += [((3, 0, 1), "part", (0, (low, low))), ((3, 1, 1), "part", (0, (high, low)))]
        jobs += [((5, 0, 2), "pair", (1, (every, every)))]
        jobs += [((3, 0, 1), None, (0, (low, high))), ((3, 1, 1), None, (0, (high, high)))]
        grad_split, grad_inner, grad_spread, grad_transition, grad_output, dz_part, dz_main, vectors = reduce_call(
            jobs,
            [trans2, part2, joined2, x0, inner2, main2],
            [dz_low, dz_high],
            [z_trans, z_part, z_spread, z_inner, z_main, spread_weight],
            [
                totals, split_gain, split_shift, inner_gain, inner_shift, spread_gain, spread_shift, transition_gain, transition_shift,
                mask, edges, inner_kernel, transition_kernel, output_kernel,
            ],
            [(full, full), (half, half), (9, half, half), (half, half), (full, full)],
            side, slots,
        )
        result, grad_split, grad_inner, grad_spread, grad_transition, grad_output, grad_features = final_call(
            [result, grad_split, grad_inner, grad_spread, grad_transition, grad_output], dz_part, dz_main, split_kernel, slots
        )
        small = vectors.reshape(2, 8 * half)
    else:
        row = jnp.arange(count)[:, None] + jnp.zeros((1, 128), jnp.int32)
        slot, place = row % slots, row // slots
        y, x = place // side, place % side
        sides = sum(jnp.where(slot == k, map_sides[k], 0) for k in range(slots))
        keep = (slot < image_counts[0]) & (y < sides) & (x < sides) & (place < side * side)
        mask = keep.astype(F32)
        x0, z_split, s_split = call(
            split_kernel_body,
            [(features, pixels(pitch, features.shape)), (mask, r_mask), fixed(split_kernel)],
            [(sds((count, full), BF16), r_full), (sds((count, full)), r_full), (sds((8, full)), sums_full)],
            [pltpu.VMEM((pitch, full), F32)],
        )
        s_split = group(s_split)
        part2, main, main2, z_inner, s_inner = call(
            inner_body,
            [(z_split, r_full), fixed(s_split), fixed(split_gain), fixed(split_shift), (mask, r_mask), fixed(inner_kernel)],
            [
                (sds((2, count, half), BF16), pair_half), (sds((count, half)), r_half), (sds((2, count, half), BF16), pair_half),
                (sds((count, half)), r_half), (sds((8, half)), sums_half),
            ],
        )
        s_inner = group(s_inner)
        tap_spec = pl.BlockSpec((1, half, half), lambda i: (i, 0, 0))
        inner2, z_spread, s_spread = call(
            functools.partial(spread_body, side, slots),
            [fixed(z_inner), fixed(s_split), fixed(s_inner), fixed(inner_gain), fixed(inner_shift), fixed(mask), fixed(edges), (spread_weight, tap_spec)],
            [(sds((2, count, half), BF16), out_whole((2, count, half))), (sds((count, half)), out_whole((count, half))), (sds((8, half)), sums_half)],
            [pltpu.VMEM((count + 2 * GUARD, half), F32), pltpu.VMEM((2, count, half), BF16)],
            (9,),
        )
        s_spread = group(s_spread)
        joined2, z_trans, s_trans = call(
            transition_body,
            [(z_spread, r_half), fixed(s_split), fixed(s_spread), fixed(spread_gain), fixed(spread_shift), (mask, r_mask), (main, r_half), fixed(transition_kernel)],
            [(sds((2, count, half), BF16), pair_half), (sds((count, half)), r_half), (sds((8, half)), sums_half)],
        )
        s_trans = group(s_trans)
        trans2, z_out, s_out = call(
            output_body,
            [(z_trans, r_half), fixed(s_split), fixed(s_trans), fixed(transition_gain), fixed(transition_shift), (mask, r_mask), (part2, pair_half), fixed(output_kernel)],
            [(sds((2, count, half), BF16), pair_half), (sds((count, full)), r_full), (sds((8, full)), sums_full)],
        )
        s_out = group(s_out)
        result, dy_out, q_out = call(
            result_body,
            [(z_out, r_full), fixed(s_split), fixed(s_out), fixed(output_gain), fixed(output_shift), (mask, r_mask), (cotangent, pixels(pitch, cotangent.shape))],
            [(sds(cotangent.shape), pixels(pitch, cotangent.shape)), (sds((count, full)), r_full), (sds((8, full)), sums_full)],
            [pltpu.VMEM((pitch, full), F32)],
        )
        q_out = group(q_out)
        dz_out, dy_trans, dy_part, q_mid = call(
            output_back_body,
            [
                (dy_out, r_full), (z_out, r_full), fixed(s_out), fixed(output_gain), fixed(q_out), fixed(s_split), (mask, r_mask), fixed(output_kernel),
                (z_trans, r_half), fixed(s_trans), fixed(transition_gain), fixed(transition_shift), (z_split, rows(pitch, half, 0)), fixed(split_gain), fixed(split_shift),
            ],
            [(sds((2, count, full), BF16), pair_full), (sds((count, half)), r_half), (sds((count, half)), r_half), (sds((8, full)), sums_full)],
            [pltpu.VMEM((pitch, full), F32)],
        )
        q_mid = group(q_mid)
        dz_trans, dz_part, grad_joined, dy_spread, q_spread = call(
            transition_back_body,
            [
                (dy_trans, r_half), (dy_part, r_half), (z_trans, r_half), fixed(s_trans), fixed(transition_gain), fixed(q_mid), fixed(s_split), (mask, r_mask), fixed(transition_kernel),
                (z_split, rows(pitch, half, 0)), fixed(split_gain), (z_spread, r_half), fixed(s_spread), fixed(spread_gain), fixed(spread_shift),
            ],
            [
                (sds((2, count, half), BF16), pair_half), (sds((2, count, half), BF16), pair_half), (sds((count, half)), r_half),
                (sds((count, half)), r_half), (sds((8, half)), sums_half),
            ],
        )
        q_spread = group(q_spread)
        moved_spec = pl.BlockSpec((1, 2, count, half), lambda i: (i, 0, 0, 0))
        moved, dy_inner, q_inner = call(
            functools.partial(spread_back_body, side, slots),
            [
                fixed(dy_spread), fixed(z_spread), fixed(s_spread), fixed(spread_gain), fixed(q_spread), fixed(s_split), fixed(mask), fixed(edges), (spread_weight, tap_spec),
                fixed(z_inner), fixed(s_inner), fixed(inner_gain), fixed(inner_shift),
            ],
            [(sds((9, 2, count, half), BF16), moved_spec), (sds((count, half)), out_whole((count, half))), (sds((8, half)), sums_half)],
            [pltpu.VMEM((count + 2 * GUARD, half), F32), pltpu.VMEM((count, half), F32)],
            (9,),
        )
        q_inner = group(q_inner)
        dz_inner, dy_main, q_main = call(
            inner_back_body,
            [
                (dy_inner, r_half), (z_inner, r_half), fixed(s_inner), fixed(inner_gain), fixed(q_inner), fixed(s_split), (mask, r_mask), fixed(inner_kernel),
                (grad_joined, r_half), (z_split, rows(pitch, half, 1)), fixed(split_gain), fixed(split_shift),
            ],
            [(sds((2, count, half), BF16), pair_half), (sds((count, half)), r_half), (sds((8, half)), sums_half)],
            [pltpu.VMEM((pitch, half), F32)],
        )
        q_main = group(q_main)
        dz_main, grad_features = call(
            split_back_body,
            [(dy_main, r_half), (z_split, rows(pitch, half, 1)), fixed(q_main), fixed(s_split), fixed(split_gain), (mask, r_mask), (dz_part, pair_half), fixed(split_kernel)],
            [(sds((2, count, half), BF16), pair_half), (sds(cotangent.shape), pixels(pitch, cotangent.shape))],
            [pltpu.VMEM((pitch, full), F32)],
        )
        small = jnp.concatenate([q_mid[0:2, half:], q_main[0:2], q_inner[0:2], q_spread[0:2], q_mid[0:2, :half], q_out[0:2]], axis=1)
        grad_output = jnp.concatenate([weight_grad(trans2, dz_out), weight_grad(part2, dz_out)], axis=0)
        grad_transition, grad_inner = weight_grad(joined2, dz_trans), weight_grad(main2, dz_inner)
        grad_split = jnp.concatenate([weight_grad(x0[None], dz_part), weight_grad(x0[None], dz_main)], axis=1)
        grad_spread = jnp.stack([weight_grad(inner2, moved[tap]) for tap in range(9)])
        grad_split, grad_inner, grad_spread, grad_transition, grad_output = lax.psum(
            (grad_split, grad_inner, grad_spread, grad_transition, grad_output), ("dp", "bn")
        )
        small = lax.psum(small, "dp")
    cuts = [0, full, full + half, full + 2 * half, full + 3 * half, 2 * full + 3 * half]
    shifts = [small[0, a:b] for a, b in zip(cuts[:-1], cuts[1:])]
    gains = [small[1, a:b] for a, b in zip(cuts[:-1], cuts[1:])]
    result, grad_features = (item.reshape(side, side, slots, full).transpose(2, 0, 1, 3) for item in (result, grad_features))
    return (
        result, grad_features,
        grad_split, gains[0], shifts[0], grad_inner, gains[1], shifts[1],
        grad_spread.reshape(3, 3, half, half), gains[2], shifts[2], grad_transition, gains[3], shifts[3], grad_output, gains[4], shifts[4],
    )


def solution(mesh):
    shard, copy = P(("dp", "bn")), P()
    return jax.shard_map(
        functools.partial(local, (mesh.shape["dp"], mesh.shape["bn"])),
        mesh=mesh,
        in_specs=(shard, shard, shard) + (copy,) * 15 + (shard,),
        out_specs=(shard, shard) + (copy,) * 15,
        check_vma=False,
    )
```

```python
import functools

import jax
import jax.numpy as jnp
import numpy as np
from jax import lax
from jax.experimental import pallas as pl
from jax.experimental.pallas import tpu as pltpu
from jax.sharding import PartitionSpec as P

EPS = 1e-05
GUARD = 80
CHUNK = 16
TILES = 4
MESH = pl.DeviceIdType.MESH
F32 = jnp.float32
BF16 = jnp.bfloat16


def round_up(value, step):
    return -(-value // step) * step


def params(megabytes=56):
    return pltpu.CompilerParams(vmem_limit_bytes=megabytes * 1024 * 1024)


def whole(array):
    zeros = (0,) * len(array.shape)
    return pl.BlockSpec(array.shape, lambda *_: zeros, pipeline_mode=pl.Buffered(1))


def out_whole(shape):
    zeros = (0,) * len(shape)
    return pl.BlockSpec(shape, lambda *_: zeros)


def rows(pitch, width, column=0):
    return pl.BlockSpec((pitch, width), lambda i: (i, column))


def rows2(pitch, width):
    return pl.BlockSpec((2, pitch, width), lambda i: (0, i, 0))


def pixels(pitch, shape):
    return pl.BlockSpec((pitch // shape[1],) + tuple(shape[1:]), lambda i: (i, 0, 0))


def sds(shape, dtype=F32):
    return jax.ShapeDtypeStruct(tuple(shape), dtype)


def dot(left, right):
    return jnp.dot(left, right, preferred_element_type=F32)


def dot_t(left, right):
    return lax.dot_general(left, right, (((1,), (1,)), ((), ())), preferred_element_type=F32)


def split_store(ref, place, value):
    high = value.astype(BF16)
    ref[(0,) + place] = high
    ref[(1,) + place] = (value - high.astype(F32)).astype(BF16)


def moments(stats_ref, total, columns):
    mean = stats_ref[0:1, columns] / total
    square = stats_ref[1:2, columns] / total
    return mean, lax.rsqrt(square - mean * mean + EPS)


def mish(y):
    t = jnp.exp(jnp.minimum(y, 30.0))
    n = t * (t + 2.0)
    return y * (n / (n + 2.0))


def mish_slope(y):
    t = jnp.exp(jnp.minimum(y, 30.0))
    n = t * (t + 2.0)
    r = 1.0 / (n + 2.0)
    return n * r + y * (((4.0 * t) * (t + 1.0) * r) * r)


def fold(value):
    return jnp.sum(value.reshape(value.shape[0] // 8, 8, value.shape[1]), axis=0)


def over_rows(count, body, carry=None, unroll=4):
    def step(k, c):
        return body(pl.ds(pl.multiple_of(k * CHUNK, CHUNK), CHUNK), c)

    return lax.fori_loop(0, count // CHUNK, step, carry, unroll=unroll)


def column_blocks(width, block=512):
    return [slice(c, c + block) for c in range(0, width, block)]


def add_sums(sums_ref, columns, pieces):
    for k, piece in enumerate(pieces):
        sums_ref[k : k + 1, columns] += jnp.sum(piece, axis=0, keepdims=True)


def start_sums(sums_ref):
    @pl.when(pl.program_id(0) == 0)
    def _():
        sums_ref[...] = jnp.zeros_like(sums_ref)


def sum_squares(z_ref, sums_ref, mask_ref=None):
    for columns in column_blocks(z_ref.shape[1]):
        width = columns.stop - columns.start

        def body(r, carry):
            value = z_ref[r, columns]
            kept = value if mask_ref is None else value * mask_ref[r, 0:1]
            return (carry[0] + fold(kept), carry[1] + fold(kept * value))

        zero = jnp.zeros((8, width), F32)
        add_sums(sums_ref, columns, over_rows(z_ref.shape[0], body, (zero, zero)))


def product2(ref, place, weight):
    high = ref[(0,) + place]
    low = ref[(1,) + place]
    return dot(high, weight) + dot(low, weight)


def product2_t(ref, place, weight):
    high = ref[(0,) + place]
    low = ref[(1,) + place]
    return dot_t(high, weight) + dot_t(low, weight)


def compact(source_ref, scratch_ref):
    places, slots, _ = source_ref.shape
    for p in range(places):
        scratch_ref[p * slots : (p + 1) * slots, :] = source_ref[p].astype(F32)


def spread_out(scratch_ref, target_ref):
    places, slots, _ = target_ref.shape
    for p in range(places):
        target_ref[p] = scratch_ref[p * slots : (p + 1) * slots, :]


def split_kernel_body(features_ref, mask_ref, w_ref, x_ref, z_ref, sums_ref, scratch_ref):
    compact(features_ref, scratch_ref)

    def body(r, _):
        x_ref[r, :] = jnp.where(mask_ref[r, 0:1] > 0.0, scratch_ref[r, :], 0.0).astype(BF16)

    over_rows(x_ref.shape[0], body)
    z_ref[...] = dot(x_ref[...], w_ref[...])
    start_sums(sums_ref)
    sum_squares(z_ref, sums_ref)
    count = jnp.sum(mask_ref[...], axis=0, keepdims=True)
    sums_ref[2:3, 0:128] += count


def inner_body(z_ref, stats_ref, gain_ref, shift_ref, mask_ref, w_ref, part_ref, main_ref, main2_ref, zi_ref, sums_ref):
    total = stats_ref[2:3, 0:1]
    half = w_ref.shape[0]
    for index, columns in enumerate(column_blocks(2 * half, half)):
        mean, inverse = moments(stats_ref, total, columns)
        scale, shift = gain_ref[0:1, columns] * inverse, shift_ref[0:1, columns]

        def body(r, _):
            act = mish((z_ref[r, columns] - mean) * scale + shift) * mask_ref[r, 0:1]
            if index == 0:
                split_store(part_ref, (r,), act)
            else:
                main_ref[r, :] = act
                split_store(main2_ref, (r,), act)

        over_rows(z_ref.shape[0], body)
    zi_ref[...] = product2(main2_ref, (), w_ref[...])
    start_sums(sums_ref)
    sum_squares(zi_ref, sums_ref)


def taps(side, slots):
    return [((dy * side + dx) * slots, dx) for dy in (-1, 0, 1) for dx in (-1, 0, 1)]


def move_rows(padded_ref, edge_ref, pair_ref, side, slots, sign):
    count = pair_ref.shape[1]
    for index, (move, dx) in enumerate(taps(side, slots)):

        @pl.when(pl.program_id(0) == index)
        def _(move=sign * move, dx=sign * dx):
            moved = padded_ref[GUARD + move : GUARD + move + count, :]
            if dx:
                moved = moved * edge_ref[:, dx + 1 : dx + 2]
            split_store(pair_ref, (slice(None),), moved)


def spread_body(side, slots, z_ref, total_ref, stats_ref, gain_ref, shift_ref, mask_ref, edge_ref, w_ref, inner_ref, zs_ref, sums_ref, padded_ref, pair_ref):
    total = total_ref[2:3, 0:1]
    count = z_ref.shape[0]
    tap = pl.program_id(0)

    @pl.when(tap == 0)
    def _():
        mean, inverse = moments(stats_ref, total, slice(None))
        scale, shift = gain_ref[...] * inverse, shift_ref[...]
        padded_ref[0:GUARD, :] = jnp.zeros((GUARD, padded_ref.shape[1]), F32)
        padded_ref[GUARD + count :, :] = jnp.zeros((GUARD, padded_ref.shape[1]), F32)

        def body(r, _):
            act = mish((z_ref[r, :] - mean) * scale + shift) * mask_ref[r, 0:1]
            padded_ref[pl.ds(r.start + GUARD, CHUNK), :] = act
            split_store(inner_ref, (r,), act)

        over_rows(count, body)
        zs_ref[...] = jnp.zeros_like(zs_ref)

    move_rows(padded_ref, edge_ref, pair_ref, side, slots, 1)
    zs_ref[...] += product2(pair_ref, (), w_ref[0])

    @pl.when(tap == pl.num_programs(0) - 1)
    def _():
        sums_ref[...] = jnp.zeros_like(sums_ref)
        sum_squares(zs_ref, sums_ref, mask_ref)


def transition_body(z_ref, total_ref, stats_ref, gain_ref, shift_ref, mask_ref, main_ref, w_ref, joined_ref, zt_ref, sums_ref):
    total = total_ref[2:3, 0:1]
    mean, inverse = moments(stats_ref, total, slice(None))
    scale, shift = gain_ref[...] * inverse, shift_ref[...]

    def body(r, _):
        act = mish((z_ref[r, :] - mean) * scale + shift) * mask_ref[r, 0:1]
        split_store(joined_ref, (r,), act + main_ref[r, :])

    over_rows(z_ref.shape[0], body)
    zt_ref[...] = product2(joined_ref, (), w_ref[...])
    start_sums(sums_ref)
    sum_squares(zt_ref, sums_ref)


def output_body(z_ref, total_ref, stats_ref, gain_ref, shift_ref, mask_ref, part_ref, w_ref, trans_ref, zo_ref, sums_ref):
    total = total_ref[2:3, 0:1]
    mean, inverse = moments(stats_ref, total, slice(None))
    scale, shift = gain_ref[...] * inverse, shift_ref[...]
    half = z_ref.shape[1]

    def body(r, _):
        act = mish((z_ref[r, :] - mean) * scale + shift) * mask_ref[r, 0:1]
        split_store(trans_ref, (r,), act)

    over_rows(z_ref.shape[0], body)
    zo_ref[...] = product2(part_ref, (), w_ref[half:, :])
    zo_ref[...] += product2(trans_ref, (), w_ref[:half, :])
    start_sums(sums_ref)
    sum_squares(zo_ref, sums_ref)


def result_body(z_ref, total_ref, stats_ref, gain_ref, shift_ref, mask_ref, cotangent_ref, result_ref, dy_ref, sums_ref, scratch_ref):
    total = total_ref[2:3, 0:1]
    compact(cotangent_ref, scratch_ref)
    start_sums(sums_ref)
    for columns in column_blocks(z_ref.shape[1]):
        mean, inverse = moments(stats_ref, total, columns)
        gain, shift = gain_ref[0:1, columns], shift_ref[0:1, columns]

        def body(r, carry):
            mask = mask_ref[r, 0:1]
            scaled = (z_ref[r, columns] - mean) * inverse
            y = scaled * gain + shift
            t = jnp.exp(jnp.minimum(y, 30.0))
            n = t * (t + 2.0)
            inv = 1.0 / (n + 2.0)
            ratio = n * inv
            slope = ratio + y * (((4.0 * t) * (t + 1.0) * inv) * inv)
            dy = jnp.where(mask > 0.0, scratch_ref[r, columns], 0.0) * slope
            scratch_ref[r, columns] = y * ratio * mask
            dy_ref[r, columns] = dy
            return (carry[0] + fold(dy), carry[1] + fold(dy * scaled))

        zero = jnp.zeros((8, columns.stop - columns.start), F32)
        add_sums(sums_ref, columns, over_rows(z_ref.shape[0], body, (zero, zero)))
    spread_out(scratch_ref, result_ref)


def norm_slope(z_ref, grad, mask_ref, r, columns, mean, inverse, gain, shift):
    scaled = (z_ref[r, columns] - mean) * inverse
    dy = grad * mask_ref[r, 0:1] * mish_slope(scaled * gain + shift)
    return dy, (fold(dy), fold(dy * scaled))


def settle(dy, z, mask, mean, inverse, factor, first, second):
    scaled = (z - mean) * inverse
    return mask * factor * (dy - (first + scaled * second))


def output_back_body(dy_ref, zo_ref, so_ref, go_ref, qo_ref, total_ref, mask_ref, w_ref, zt_ref, st_ref, gt_ref, bt_ref, zp_ref, gp_ref, bp_ref, dz_ref, dyt_ref, dyp_ref, sums_ref, grad_ref):
    total = total_ref[2:3, 0:1]
    for columns in column_blocks(zo_ref.shape[1]):
        mean, inverse = moments(so_ref, total, columns)
        factor = go_ref[0:1, columns] * inverse
        first, second = qo_ref[0:1, columns] / total, qo_ref[1:2, columns] / total

        def body(r, _):
            dz = settle(dy_ref[r, columns], zo_ref[r, columns], mask_ref[r, 0:1], mean, inverse, factor, first, second)
            split_store(dz_ref, (r, columns), dz)

        over_rows(zo_ref.shape[0], body)
    grad_ref[...] = product2_t(dz_ref, (), w_ref[...])
    start_sums(sums_ref)
    half = zt_ref.shape[1]
    for index, (z_ref, s_ref, g_ref, b_ref, out_ref) in enumerate(((zt_ref, st_ref, gt_ref, bt_ref, dyt_ref), (zp_ref, total_ref, gp_ref, bp_ref, dyp_ref))):
        columns = slice(index * half, (index + 1) * half)
        own = slice(0, half)
        mean, inverse = moments(s_ref, total, own)
        gain, shift = g_ref[0:1, own], b_ref[0:1, own]

        def body(r, carry):
            dy, sums = norm_slope(z_ref, grad_ref[r, columns], mask_ref, r, own, mean, inverse, gain, shift)
            out_ref[r, :] = dy
            return (carry[0] + sums[0], carry[1] + sums[1])

        zero = jnp.zeros((8, half), F32)
        add_sums(sums_ref, columns, over_rows(zt_ref.shape[0], body, (zero, zero)))


def transition_back_body(dyt_ref, dyp_ref, zt_ref, st_ref, gt_ref, q_ref, total_ref, mask_ref, w_ref, zp_ref, gp_ref, zs_ref, ss_ref, gs_ref, bs_ref, dz_ref, dzp_ref, grad_ref, dys_ref, sums_ref):
    total = total_ref[2:3, 0:1]
    half = zt_ref.shape[1]
    own = slice(0, half)
    for index, (dy_ref, z_ref, s_ref, g_ref, out_ref) in enumerate(((dyt_ref, zt_ref, st_ref, gt_ref, dz_ref), (dyp_ref, zp_ref, total_ref, gp_ref, dzp_ref))):
        columns = slice(index * half, (index + 1) * half)
        mean, inverse = moments(s_ref, total, own)
        factor = g_ref[0:1, own] * inverse
        first, second = q_ref[0:1, columns] / total, q_ref[1:2, columns] / total

        def body(r, _):
            dz = settle(dy_ref[r, :], z_ref[r, :], mask_ref[r, 0:1], mean, inverse, factor, first, second)
            split_store(out_ref, (r,), dz)

        over_rows(zt_ref.shape[0], body)
    grad_ref[...] = product2_t(dz_ref, (), w_ref[...])
    start_sums(sums_ref)
    mean, inverse = moments(ss_ref, total, own)
    gain, shift = gs_ref[...], bs_ref[...]

    def tail(r, carry):
        dy, sums = norm_slope(zs_ref, grad_ref[r, :], mask_ref, r, own, mean, inverse, gain, shift)
        dys_ref[r, :] = dy
        return (carry[0] + sums[0], carry[1] + sums[1])

    zero = jnp.zeros((8, half), F32)
    add_sums(sums_ref, own, over_rows(zt_ref.shape[0], tail, (zero, zero)))


def spread_back_body(side, slots, dy_ref, z_ref, s_ref, g_ref, q_ref, total_ref, mask_ref, edge_ref, w_ref, zi_ref, si_ref, gi_ref, bi_ref, moved_ref, dyi_ref, sums_ref, padded_ref, grad_ref):
    total = total_ref[2:3, 0:1]
    count, half = z_ref.shape
    tap = pl.program_id(0)

    @pl.when(tap == 0)
    def _():
        padded_ref[0:GUARD, :] = jnp.zeros((GUARD, half), F32)
        padded_ref[GUARD + count :, :] = jnp.zeros((GUARD, half), F32)
        mean, inverse = moments(s_ref, total, slice(None))
        factor = g_ref[...] * inverse
        first, second = q_ref[0:1, :] / total, q_ref[1:2, :] / total

        def body(r, _):
            dz = settle(dy_ref[r, :], z_ref[r, :], mask_ref[r, 0:1], mean, inverse, factor, first, second)
            padded_ref[pl.ds(r.start + GUARD, CHUNK), :] = dz

        over_rows(count, body)
        grad_ref[...] = jnp.zeros_like(grad_ref)

    move_rows(padded_ref, edge_ref, moved_ref.at[0], side, slots, -1)
    grad_ref[...] += product2_t(moved_ref.at[0], (), w_ref[0])

    @pl.when(tap == pl.num_programs(0) - 1)
    def _():
        sums_ref[...] = jnp.zeros_like(sums_ref)
        own = slice(0, half)
        mean, inverse = moments(si_ref, total, own)
        gain, shift = gi_ref[...], bi_ref[...]

        def tail(r, carry):
            dy, sums = norm_slope(zi_ref, grad_ref[r, :], mask_ref, r, own, mean, inverse, gain, shift)
            dyi_ref[r, :] = dy
            return (carry[0] + sums[0], carry[1] + sums[1])

        zero = jnp.zeros((8, half), F32)
        add_sums(sums_ref, own, over_rows(count, tail, (zero, zero)))


def inner_back_body(dy_ref, zi_ref, si_ref, gi_ref, q_ref, total_ref, mask_ref, w_ref, joined_ref, zm_ref, gm_ref, bm_ref, dz_ref, dym_ref, sums_ref, grad_ref):
    total = total_ref[2:3, 0:1]
    half = zi_ref.shape[1]
    own = slice(0, half)
    upper = slice(half, 2 * half)
    mean, inverse = moments(si_ref, total, own)
    factor = gi_ref[...] * inverse
    first, second = q_ref[0:1, :] / total, q_ref[1:2, :] / total

    def body(r, _):
        dz = settle(dy_ref[r, :], zi_ref[r, :], mask_ref[r, 0:1], mean, inverse, factor, first, second)
        split_store(dz_ref, (r,), dz)

    over_rows(zi_ref.shape[0], body)
    grad_ref[...] = product2_t(dz_ref, (), w_ref[...])
    start_sums(sums_ref)
    mean, inverse = moments(total_ref, total, upper)
    gain, shift = gm_ref[0:1, upper], bm_ref[0:1, upper]

    def tail(r, carry):
        dy, sums = norm_slope(zm_ref, grad_ref[r, :] + joined_ref[r, :], mask_ref, r, own, mean, inverse, gain, shift)
        dym_ref[r, :] = dy
        return (carry[0] + sums[0], carry[1] + sums[1])

    zero = jnp.zeros((8, half), F32)
    add_sums(sums_ref, own, over_rows(zi_ref.shape[0], tail, (zero, zero)))


def split_back_body(dy_ref, zm_ref, q_ref, total_ref, g_ref, mask_ref, dzp_ref, w_ref, dz_ref, grad_ref, scratch_ref):
    total = total_ref[2:3, 0:1]
    half = zm_ref.shape[1]
    upper = slice(half, 2 * half)
    mean, inverse = moments(total_ref, total, upper)
    factor = g_ref[0:1, upper] * inverse
    first, second = q_ref[0:1, :] / total, q_ref[1:2, :] / total

    def body(r, _):
        dz = settle(dy_ref[r, :], zm_ref[r, :], mask_ref[r, 0:1], mean, inverse, factor, first, second)
        split_store(dz_ref, (r,), dz)

    over_rows(zm_ref.shape[0], body)
    scratch_ref[...] = product2_t(dzp_ref, (), w_ref[:, :half])
    scratch_ref[...] += product2_t(dz_ref, (), w_ref[:, half:])
    spread_out(scratch_ref, grad_ref)


def final_body(pieces, *refs):
    count = len(pieces)
    sources, dzp_hbm, dzm_hbm, w_hbm, refs = refs[:count], refs[count], refs[count + 1], refs[count + 2], refs[count + 3 :]
    targets, grad_hbm, refs = refs[:count], refs[count], refs[count + 1 :]
    buffers, (dzp_ref, dzm_ref, w_ref, wide_ref, staged_ref, load_sem, store_sem, own_sem, grad_sem) = refs[:count], refs[count:]
    half = dzp_ref.shape[2]
    pitch = wide_ref.shape[0]
    places = staged_ref.shape[1]
    tiles = dzp_ref.shape[1] // pitch
    own = [pltpu.make_async_copy(w_hbm, w_ref, own_sem.at[0])]
    for k in range(tiles):
        rows_k = slice(k * pitch, (k + 1) * pitch)
        own.append(pltpu.make_async_copy(dzp_hbm.at[:, rows_k], dzp_ref.at[:, rows_k], own_sem.at[1 + 2 * k]))
        own.append(pltpu.make_async_copy(dzm_hbm.at[:, rows_k], dzm_ref.at[:, rows_k], own_sem.at[2 + 2 * k]))
    loads, stores = [], []
    for source, buffer, target, cuts in zip(sources, buffers, targets, pieces):
        for begin, end in cuts:
            k = len(loads)
            loads.append(pltpu.make_async_copy(source.at[begin:end], buffer.at[begin:end], load_sem.at[k]))
            stores.append(pltpu.make_async_copy(buffer.at[begin:end], target.at[begin:end], store_sem.at[k]))
    for copy in own[:3]:
        copy.start()
    ahead = len(loads) // 2
    for copy in loads[:ahead]:
        copy.start()
    for copy in own[3:]:
        copy.start()
    for copy in loads[ahead:]:
        copy.start()

    def forward(begin, end):
        for k in range(begin, end):
            loads[k].wait()
            stores[k].start()

    def grad_store(k):
        size = min(places, grad_hbm.shape[0] - k * places)
        return pltpu.make_async_copy(staged_ref.at[k % 2, 0:size], grad_hbm.at[k * places : k * places + size], grad_sem.at[k % 2])

    own[0].wait()
    step = -(-len(loads) // (tiles + 1))
    for k in range(tiles):
        own[1 + 2 * k].wait()
        own[2 + 2 * k].wait()
        rows_k = slice(k * pitch, (k + 1) * pitch)
        wide_ref[...] = product2_t(dzp_ref, (rows_k,), w_ref[:, :half]) + product2_t(dzm_ref, (rows_k,), w_ref[:, half:])
        if k >= 2:
            grad_store(k - 2).wait()
        spread_out(wide_ref, staged_ref.at[k % 2])
        grad_store(k).start()
        forward(min(k * step, len(loads)), min((k + 1) * step, len(loads)))
    forward(min(tiles * step, len(loads)), len(loads))
    for k in range(max(0, tiles - 2), tiles):
        grad_store(k).wait()
    for copy in stores:
        copy.wait()


def final_call(arrays, dzp, dzm, weight, slots):
    hbm = pl.BlockSpec(memory_space=pl.ANY)
    vmem, dma = pltpu.VMEM, pltpu.SemaphoreType.DMA
    full, count = weight.shape[0], dzp.shape[1]
    pitch = count // TILES
    pieces = []
    for array in arrays:
        length = array.shape[0]
        row_bytes = 4 * array.size // length
        step = min(length, max(1, (1 << 20) // row_bytes))
        pieces.append([(begin, min(begin + step, length)) for begin in range(0, length, step)])
    number = sum(len(cuts) for cuts in pieces)
    pixel_shape = arrays[0].shape
    scratch = [vmem(array.shape, F32) for array in arrays]
    scratch += [
        vmem(dzp.shape, BF16), vmem(dzm.shape, BF16), vmem(weight.shape, BF16), vmem((pitch, full), F32), vmem((2, pitch // slots, slots, full), F32),
        dma((number,)), dma((number,)), dma((1 + 2 * TILES,)), dma((2,)),
    ]
    return pl.pallas_call(
        functools.partial(final_body, pieces),
        in_specs=[hbm] * (len(arrays) + 3),
        out_specs=[hbm] * (len(arrays) + 1),
        out_shape=[sds(array.shape) for array in arrays] + [sds(pixel_shape)],
        scratch_shapes=scratch,
        compiler_params=params(60),
    )(*arrays, dzp, dzm, weight)


def weight_body(x_ref, dz_ref, dw_ref):
    turned = x_ref[0].T
    value = dot(turned, dz_ref[0]) + dot(turned, dz_ref[1])
    if x_ref.shape[0] == 2:
        value += dot(x_ref[1].T, dz_ref[0])
    dw_ref[...] = value


def weight_grad(x, dz, block=256):
    parts, count, width = x.shape
    wide = dz.shape[2]
    return pl.pallas_call(
        weight_body,
        grid=(width // block,),
        in_specs=[pl.BlockSpec((parts, count, block), lambda i: (0, 0, i)), whole(dz)],
        out_specs=pl.BlockSpec((block, wide), lambda i: (i, 0)),
        out_shape=sds((width, wide)),
        compiler_params=params(),
    )(x, dz)


SPLIT, INNER, SPREAD, TRANS, OUT, BACK_OUT = range(6)


def front_body(side, slots, *refs):
    (features_hbm, cotangent_hbm, w_split_hbm, w_inner_hbm, w_spread_hbm, w_trans_hbm, w_out_hbm), refs = refs[:7], refs[7:]
    (g_split, b_split, g_inner, b_inner, g_spread, b_spread, g_trans, b_trans, g_out, b_out, edge_ref, counts_ref, sides_ref), refs = refs[:13], refs[13:]
    (x_out, zp_out, zm_out, main_out, part_out, zi_out, inner_out, zs_out, joined_out, zt_out, trans_out, result_hbm, dlow_out, dhigh_out, total_ref, mask_ref), refs = refs[:16], refs[16:]
    (p0, p1, p2, p3, p4, p5, p6, p7, q0, q1, q2, q3, wide_ref, feature_ref, cot_ref, staged_ref), refs = refs[:16], refs[16:]
    (w_split, w_inner, w_spread, w_trans, w_out, local_ref, packed_ref, shared_ref), refs = refs[:8], refs[8:]
    weight_sem, feature_sem, cot_sem, staged_sem, out_sem, sum_send, sum_recv = refs
    count, half = p0.shape
    pitch = count // TILES
    places = pitch // slots
    low, high, everything = slice(0, half), slice(half, 2 * half), slice(None)
    dp, bn = lax.axis_index("dp"), lax.axis_index("bn")
    members = shared_ref.shape[1]
    group = [lax.rem(bn + k, members) for k in range(1, members)]

    weights = [
        pltpu.make_async_copy(source, target, weight_sem.at[k])
        for k, (source, target) in enumerate(
            ((w_split_hbm, w_split), (w_inner_hbm, w_inner), (w_spread_hbm, w_spread), (w_trans_hbm, w_trans), (w_out_hbm, w_out))
        )
    ]

    def rows_of(k):
        return min(places, features_hbm.shape[0] - k * places)

    def feature_load(k):
        size = rows_of(k)
        return pltpu.make_async_copy(features_hbm.at[k * places : k * places + size], feature_ref.at[k % 2, 0:size], feature_sem.at[k % 2])

    def cot_load(k):
        size = rows_of(k)
        return pltpu.make_async_copy(cotangent_hbm.at[k * places : k * places + size], cot_ref.at[0:size], cot_sem)

    def result_store(k):
        size = rows_of(k)
        return pltpu.make_async_copy(staged_ref.at[0:size], result_hbm.at[k * places : k * places + size], staged_sem)

    pending = {}

    def write(name, source, target):
        copy = pltpu.make_async_copy(source, target, out_sem.at[len(pending)])
        copy.start()
        pending[name] = [copy, True]

    def written(name):
        if pending[name][1]:
            pending[name][0].wait()
            pending[name][1] = False

    def sum_copies(which):
        wide = slice(0, 384 if which == SPLIT else 256)
        return wide, [
            pltpu.make_async_remote_copy(
                src_ref=packed_ref.at[which, :, wide], dst_ref=shared_ref.at[which, bn, :, wide],
                send_sem=sum_send.at[which, k], recv_sem=sum_recv.at[which, k], device_id={"bn": peer}, device_id_type=MESH,
            )
            for k, peer in enumerate(group)
        ]

    def exchange(which, width, beside=None):
        wide, copies = sum_copies(which)
        pieces = [(j, slice(j * 128, (j + 1) * 128)) for j in range(width // 128)]
        for j, piece in pieces:
            packed_ref[which, j : j + 1, 0:128] = local_ref[which, 0:1, piece]
            packed_ref[which, j : j + 1, 128:256] = local_ref[which, 1:2, piece]
        if which == SPLIT:
            packed_ref[which, 0:1, 256:384] = local_ref[which, 2:3, 0:128]
        for copy in copies:
            copy.start()
        shared_ref[which, bn, :, wide] = packed_ref[which, :, wide]
        if beside is not None:
            beside()
        for copy in copies:
            copy.wait()
        value = shared_ref[which, 0, :, wide]
        for k in range(1, members):
            value = value + shared_ref[which, k, :, wide]
        for j, piece in pieces:
            total_ref[which, 0:1, piece] = value[j : j + 1, 0:128]
            total_ref[which, 1:2, piece] = value[j : j + 1, 128:256]
        if which == SPLIT:
            total_ref[which, 2:3, 0:128] = value[0:1, 256:384]

    def stats(which):
        return total_ref.at[which]

    def affine(which, gain_ref, shift_ref, columns):
        mean, inverse = moments(stats(which), total_ref[SPLIT, 2:3, 0:1], columns)
        return mean, gain_ref[0:1, columns] * inverse, shift_ref[0:1, columns]

    def activate(z_ref, r, mean, scale, shift):
        return mish((z_ref[r, :] - mean) * scale + shift) * mask_ref[r, 0:1]

    feature_load(0).start()
    for k in (0, 1):
        weights[k].start()
    feature_load(1).start()
    barrier = pltpu.get_barrier_semaphore()
    for peer in group:
        pl.semaphore_signal(barrier, inc=1, device_id={"bn": peer}, device_id_type=MESH)
    local_ref[...] = jnp.zeros_like(local_ref)
    packed_ref[...] = jnp.zeros_like(packed_ref)
    total_ref[...] = jnp.zeros_like(total_ref)
    limits = [jnp.where(k < counts_ref[0], sides_ref[k], 0).astype(F32) for k in range(slots)]

    def mask_rows(r, _):
        index = (r.start + lax.broadcasted_iota(jnp.int32, (CHUNK, 128), 0)).astype(F32)
        place = jnp.floor((index + 0.5) * (1.0 / slots))
        slot = index - place * slots
        y = jnp.floor((place + 0.5) * (1.0 / side))
        x = place - y * side
        limit = jnp.zeros_like(index)
        for k in range(slots):
            limit = jnp.where(slot == k, limits[k], limit)
        mask_ref[r, :] = jnp.where(jnp.maximum(x, y) < limit, 1.0, 0.0)

    over_rows(count, mask_rows)
    for k in range(TILES):
        feature_load(k).wait()
        compact(feature_ref.at[k % 2], wide_ref)
        if k + 2 < TILES:
            feature_load(k + 2).start()
        here = pl.ds(k * pitch, pitch)

        def body(r, _, k=k):
            q = pl.ds(pl.multiple_of(r.start + k * pitch, CHUNK), CHUNK)
            for h, columns in enumerate((low, high)):
                q0[h, q, :] = jnp.where(mask_ref[q, 0:1] > 0.0, wide_ref[r, columns], 0.0).astype(BF16)

        over_rows(pitch, body)
    for k in (2, 3, 4):
        weights[k].start()
    cot_load(0).start()
    write("x", q0, x_out)
    weights[0].wait()
    p0[...] = dot(q0[0], w_split[low, low]) + dot(q0[1], w_split[high, low])
    p1[0:count, :] = dot(q0[0], w_split[low, high]) + dot(q0[1], w_split[high, high])
    write("zm", p1.at[0:count], zm_out)
    write("zp", p0, zp_out)

    def add_squares(which, z_ref, columns, masked=False):
        def body(r, carry):
            value = z_ref[r, :]
            kept = value * mask_ref[r, 0:1] if masked else value
            return (carry[0] + fold(kept), carry[1] + fold(kept * value))

        zero = jnp.zeros((8, half), F32)
        add_sums(local_ref.at[which], columns, over_rows(count, body, (zero, zero)))

    add_squares(SPLIT, p0, low)
    add_squares(SPLIT, p1, high)
    local_ref[SPLIT, 2:3, 0:128] = jnp.sum(mask_ref[...], axis=0, keepdims=True)
    pl.semaphore_wait(barrier, members - 1)
    exchange(SPLIT, 2 * half)

    mean, scale, shift = affine(SPLIT, g_split, b_split, high)

    def main_rows(r, _):
        act = activate(p1, r, mean, scale, shift)
        p2[r, :] = act
        split_store(q2, (r,), act)

    over_rows(count, main_rows)
    write("main", q2, main_out)
    weights[1].wait()
    p3[...] = product2(q2, (), w_inner[...])
    write("zi", p3, zi_out)
    add_squares(INNER, p3, low)
    mean_p, scale_p, shift_p = affine(SPLIT, g_split, b_split, low)

    def part_rows(r, _):
        split_store(q1, (r,), activate(p0, r, mean_p, scale_p, shift_p))

    exchange(INNER, half, lambda: over_rows(count, part_rows))
    write("part", q1, part_out)

    written("zm")
    written("x")
    mean_i, scale_i, shift_i = affine(INNER, g_inner, b_inner, low)
    p1[0:GUARD, :] = jnp.zeros((GUARD, half), F32)
    p1[GUARD + count :, :] = jnp.zeros((GUARD, half), F32)

    def inner_rows(r, _):
        act = activate(p3, r, mean_i, scale_i, shift_i)
        p1[pl.ds(r.start + GUARD, CHUNK), :] = act
        split_store(q0, (r,), act)

    over_rows(count, inner_rows)
    write("inner", q0, inner_out)
    weights[2].wait()
    written("zi")
    written("main")
    for tap, (move, dx) in enumerate(taps(side, slots)):
        if move:
            pair_ref = (q2, q3)[tap % 2]
            moved = p1[GUARD + move : GUARD + move + count, :]
            if dx:
                moved = moved * edge_ref[:, dx + 1 : dx + 2]
            split_store(pair_ref, (slice(None),), moved)
        else:
            pair_ref = q0
        part = product2(pair_ref, (), w_spread[tap])
        if tap == 0:
            p3[...] = part
        else:
            p3[...] += part
    write("zs", p3, zs_out)
    add_squares(SPREAD, p3, low, True)
    exchange(SPREAD, half)

    mean_s, scale_s, shift_s = affine(SPREAD, g_spread, b_spread, low)

    def joined_rows(r, _):
        split_store(q2, (r,), activate(p3, r, mean_s, scale_s, shift_s) + p2[r, :])

    over_rows(count, joined_rows)
    write("joined", q2, joined_out)
    weights[3].wait()
    p2[...] = product2(q2, (), w_trans[...])
    write("zt", p2, zt_out)
    add_squares(TRANS, p2, low)
    exchange(TRANS, half)

    mean_t, scale_t, shift_t = affine(TRANS, g_trans, b_trans, low)

    def trans_rows(r, _):
        split_store(q3, (r,), activate(p2, r, mean_t, scale_t, shift_t))

    over_rows(count, trans_rows)
    write("trans", q3, trans_out)
    weights[4].wait()
    for page, columns in ((p4, low), (p5, high)):
        page[...] = product2(q3, (), w_out[low, columns]) + product2(q1, (), w_out[high, columns])
        add_squares(OUT, page, columns)
    exchange(OUT, 2 * half)

    total = total_ref[SPLIT, 2:3, 0:1]
    for k in range(TILES):
        cot_load(k).wait()
        compact(cot_ref, wide_ref)
        if k + 1 < TILES:
            cot_load(k + 1).start()
        for page, slope_page, columns in ((p4, p6, low), (p5, p7, high)):
            mean_o, inverse_o = moments(stats(OUT), total, columns)
            gain, shift_o = g_out[0:1, columns], b_out[0:1, columns]

            def body(r, carry, k=k, page=page, slope_page=slope_page, columns=columns):
                q = pl.ds(pl.multiple_of(r.start + k * pitch, CHUNK), CHUNK)
                mask = mask_ref[q, 0:1]
                scaled = (page[q, :] - mean_o) * inverse_o
                y = scaled * gain + shift_o
                t = jnp.exp(jnp.minimum(y, 30.0))
                n = t * (t + 2.0)
                inv = 1.0 / (n + 2.0)
                ratio = n * inv
                slope = ratio + y * (((4.0 * t) * (t + 1.0) * inv) * inv)
                dy = jnp.where(mask > 0.0, wide_ref[r, columns], 0.0) * slope
                wide_ref[r, columns] = y * ratio * mask
                slope_page[q, :] = dy
                return (carry[0] + fold(dy), carry[1] + fold(dy * scaled))

            zero = jnp.zeros((8, half), F32)
            add_sums(local_ref.at[BACK_OUT], columns, over_rows(pitch, body, (zero, zero)))
        if k:
            result_store(k - 1).wait()
        spread_out(wide_ref, staged_ref)
        result_store(k).start()
    exchange(BACK_OUT, 2 * half)

    def settled(page, z_page, pair_ref, which, back, gain_ref, columns, back_columns):
        mean_k, inverse_k = moments(stats(which), total, columns)
        factor = gain_ref[0:1, columns] * inverse_k
        first, second = total_ref[back, 0:1, back_columns] / total, total_ref[back, 1:2, back_columns] / total

        def body(r, _):
            split_store(pair_ref, (r,), settle(page[r, :], z_page[r, :], mask_ref[r, 0:1], mean_k, inverse_k, factor, first, second))

        over_rows(count, body)

    written("inner")
    written("joined")
    settled(p6, p4, q0, OUT, BACK_OUT, g_out, low, low)
    settled(p7, p5, q2, OUT, BACK_OUT, g_out, high, high)
    write("dlow", q0, dlow_out)
    write("dhigh", q2, dhigh_out)
    result_store(TILES - 1).wait()
    for name in list(pending):
        written(name)


def front_call(arrays, constants, scalars, slots, side, count, members):
    hbm, vmem_spec = pl.BlockSpec(memory_space=pl.ANY), pl.BlockSpec(memory_space=pltpu.VMEM)
    vmem, dma = pltpu.VMEM, pltpu.SemaphoreType.DMA
    full = arrays[0].shape[2]
    half = full // 2
    pitch = count // TILES
    pair, page = sds((2, count, half), BF16), sds((count, half))
    outs = [pair, page, page, pair, pair, page, pair, page, pair, page, pair, sds(arrays[1].shape), pair, pair]
    scratch = [vmem((count, half), F32), vmem((count + 2 * GUARD, half), F32)] + [vmem((count, half), F32)] * 6
    scratch += [vmem((2, count, half), BF16)] * 4
    scratch += [
        vmem((pitch, full), F32), vmem((2, pitch // slots, slots, full), BF16), vmem((pitch // slots, slots, full), F32), vmem((pitch // slots, slots, full), F32),
        vmem((full, full), BF16), vmem((half, half), BF16), vmem((9, half, half), BF16), vmem((half, half), BF16), vmem((full, full), BF16),
        vmem((6, 8, full), F32), vmem((6, 8, 384), F32), vmem((6, members, 8, 384), F32),
        dma((5,)), dma((2,)), dma(()), dma(()), dma((16,)), dma((6, members - 1)), dma((6, members - 1)),
    ]
    return pl.pallas_call(
        functools.partial(front_body, side, slots),
        in_specs=[hbm] * len(arrays) + [vmem_spec] * len(constants) + [pl.BlockSpec(memory_space=pltpu.SMEM)] * 2,
        out_specs=[hbm] * len(outs) + [vmem_spec] * 2,
        out_shape=outs + [sds((6, 8, full)), sds((count, 128))],
        scratch_shapes=scratch,
        compiler_params=pltpu.CompilerParams(collective_id=1, has_side_effects=True, vmem_limit_bytes=60 * 1024 * 1024),
    )(*arrays, *constants, *scalars)


LAGS = (1, 2, 3, 4, 5, 6, 7, 8)
LAG = LAGS[-1]
KEPT = 6


def reduce_body(jobs, side, slots, *refs):
    lefts, rights, refs = refs[:6], refs[6:8], refs[8:]
    (zt_hbm, zp_hbm, zs_hbm, zi_hbm, zm_hbm, ws_hbm), refs = refs[:6], refs[6:]
    (totals_ref, g_split, b_split, g_inner, b_inner, g_spread, b_spread, g_trans, b_trans, mask_ref, edge_ref, wi_ref, wt_ref, wo_ref), refs = refs[:14], refs[14:]
    outs, dpart_out, dmain_out, vectors_ref, refs = refs[:5], refs[5], refs[6], refs[7], refs[8:]
    (x_ref, z_ref, turned_ref, own_ref, r0_ref, half_ref, r1_ref, quarter_ref, r2_ref, eighth_ref, r3_ref, gathered_ref, full_ref, load_sem, store_sem) = refs[:15]
    (padded_ref, grad_ref, page_ref, joined_ref, zm_ref, pair_ref, part_ref, wide_ref, tap_ref, sums_ref, shared_ref, small_ref, spread_ref) = refs[15:28]
    (page_sem, tap_sem, write_sem, sum_send, sum_recv, small_send, small_recv) = refs[28:35]
    sems = refs[35:]
    count, half = grad_ref.shape
    pitch = wide_ref.shape[0]
    tiles = count // pitch
    s_split, q_out = totals_ref.at[SPLIT], totals_ref.at[BACK_OUT]
    s_spread, s_trans, s_inner = (totals_ref.at[k, :, 0:half] for k in (SPREAD, TRANS, INNER))
    stats_total = s_split[2:3, 0:1]
    block = own_ref.shape[1]
    mid = block // 2
    dp, bn = lax.axis_index("dp"), lax.axis_index("bn")
    z, x, y, core = dp // 2, dp % 2, bn // 2, bn % 2

    def at(new_z, new_x, new_y, new_core):
        return {"dp": new_z * 2 + new_x, "bn": new_y * 2 + new_core}

    to_core, to_x, to_y = at(z, x, y, 1 - core), at(z, 1 - x, y, core), at(z, x, 1 - y, core)
    depth = [(z + k) % 4 for k in (1, 2, 3)]
    to_z = [at(new_z, x, y, core) for new_z in depth]
    to_far = [at(new_z, 1 - x, y, core) for new_z in depth]
    to_diagonal = at(z, x, 1 - y, 1 - core)
    columns = (pl.ds(0, mid), pl.ds(mid, mid))

    def part(start, size):
        return pl.ds(pl.multiple_of(start, size), size)

    def far(stage, k, turn, source, target, peer):
        send, recv = sems[2 * stage], sems[2 * stage + 1]
        return pltpu.make_async_remote_copy(
            src_ref=source, dst_ref=target, send_sem=send.at[k, turn], recv_sem=recv.at[k, turn], device_id=peer, device_id_type=MESH
        )

    first = (x, y)
    second = (y, x)
    sides = (to_x, to_y)

    def copies(stage, c):
        slot, turn, keep = c % 2, c % 4, c % KEPT
        base = core * (block // 2)
        if stage == 0:
            return [far(0, 0, turn, own_ref.at[slot, part((1 - core) * (block // 2), block // 2)], r0_ref.at[slot], to_core)]
        if stage == 1:
            return [
                far(1, k, turn, half_ref.at[slot, part((1 - first[k]) * (block // 4), block // 4), columns[k]], r1_ref.at[turn, :, columns[k]], sides[k])
                for k in (0, 1)
            ]
        if stage == 2:
            return [
                far(2, k, turn, quarter_ref.at[slot, part((1 - second[k]) * (block // 8), block // 8), columns[k]], r2_ref.at[turn, :, columns[k]], sides[1 - k])
                for k in (0, 1)
            ]
        if stage == 3:
            return [
                far(3, k, turn, eighth_ref.at[slot, part(depth[k] * (block // 32), block // 32)], r3_ref.at[slot, k], to_z[k]) for k in (0, 1, 2)
            ]
        if stage == 4:
            spot = gathered_ref.at[slot, part(z * (block // 32), block // 32)]
            return [far(4, k, turn, spot, spot, to_z[k]) for k in (0, 1, 2)]
        made = []
        for k in (0, 1):
            eighth = base + first[k] * (block // 4) + second[k] * (block // 8)
            if stage == 5:
                spot = full_ref.at[keep, part(eighth, block // 8), columns[k]]
                made.append(far(5, k, turn, spot, spot, sides[1 - k]))
            elif stage == 6:
                spot = full_ref.at[keep, part(base + first[k] * (block // 4), block // 4), columns[k]]
                made.append(far(6, k, turn, spot, spot, sides[k]))
        if stage == 7:
            spot = full_ref.at[keep, part(base, block // 2)]
            made.append(far(7, 0, turn, spot, spot, to_core))
        return made

    def begin(stage, c):
        for copy in copies(stage, c):
            copy.start()

    def finish(stage, c):
        for copy in copies(stage, c):
            copy.wait()

    def load(j):
        if jobs[j] is None:
            return []
        (left, begin_part, parts), right, _ = jobs[j]
        slot = j % 2
        made = []
        if j < 2 or jobs[j - 2] is None or jobs[j - 2][0] != jobs[j][0]:
            made.append(pltpu.make_async_copy(lefts[left].at[begin_part : begin_part + parts], x_ref.at[slot, 0:parts], load_sem.at[slot, 0]))
        source = {"pair": pair_ref, "part": part_ref, 0: rights[0], 1: rights[1]}.get(right)
        if source is not None:
            made.append(pltpu.make_async_copy(source, z_ref.at[slot], load_sem.at[slot, 1]))
        return made

    def store(j):
        out, spot = jobs[j][2]
        return pltpu.make_async_copy(full_ref.at[j % KEPT], outs[out].at[spot], store_sem.at[j % KEPT])


    everything = slice(None)

    def page(source, target, k):
        return pltpu.make_async_copy(source, target, page_sem.at[k])

    def tap_load(tap):
        return pltpu.make_async_copy(ws_hbm.at[tap], tap_ref.at[tap % 2], tap_sem.at[tap % 2])

    upper = slice(half, 2 * half)
    load_zt, load_zp, load_zs = page(zt_hbm, page_ref, 0), page(zp_hbm, joined_ref, 1), page(zs_hbm, page_ref, 0)
    load_zi, load_zm = page(zi_hbm, page_ref, 0), page(zm_hbm, zm_ref, 2)
    write_part = pltpu.make_async_copy(part_ref, dpart_out, write_sem.at[0])
    write_main = pltpu.make_async_copy(z_ref.at[1], dmain_out, write_sem.at[1])

    group = [at(z, x, y, 1 - core), at(z, x, 1 - y, core), to_diagonal]

    def sum_copies(which):
        return [
            pltpu.make_async_remote_copy(
                src_ref=sums_ref.at[which], dst_ref=shared_ref.at[which, bn], send_sem=sum_send.at[which, k], recv_sem=sum_recv.at[which, k], device_id=peer, device_id_type=MESH
            )
            for k, peer in enumerate(group)
        ]

    def sum_start(which):
        for copy in sum_copies(which):
            copy.start()
        shared_ref[which, bn] = sums_ref[which]

    def sum_finish(which):
        for copy in sum_copies(which):
            copy.wait()
        value = shared_ref[which, 0]
        for k in range(1, shared_ref.shape[1]):
            value = value + shared_ref[which, k]
        sums_ref[which] = value

    everyone = [to_x] + to_z + to_far

    def small_copies():
        return [
            pltpu.make_async_remote_copy(
                src_ref=small_ref, dst_ref=spread_ref.at[dp], send_sem=small_send.at[k], recv_sem=small_recv.at[k], device_id=peer, device_id_type=MESH
            )
            for k, peer in enumerate(everyone)
        ]

    def settled(dy_ref, z_page, which, back, gain_ref, columns, keep):
        mean, inverse = moments(which, stats_total, columns)
        factor = gain_ref[0:1, columns] * inverse
        first_sum, second_sum = sums_ref[back, 0:1, :] / stats_total, sums_ref[back, 1:2, :] / stats_total

        def body(r, _):
            keep(r, settle(dy_ref[r, :], z_page[r, :], mask_ref[r, 0:1], mean, inverse, factor, first_sum, second_sum))

        over_rows(count, body)

    def sloped(grad, target_ref, z_page, which, back, gain_ref, shift_ref, columns):
        mean, inverse = moments(which, stats_total, columns)
        gain, shift = gain_ref[0:1, columns], shift_ref[0:1, columns]

        def body(r, carry):
            dy, sums = norm_slope(z_page, grad[r, :], mask_ref, r, everything, mean, inverse, gain, shift)
            target_ref[r, :] = dy
            return (carry[0] + sums[0], carry[1] + sums[1])

        zero = jnp.zeros((8, half), F32)
        add_sums(sums_ref.at[back], everything, over_rows(count, body, (zero, zero)))
        sum_start(back)

    own, lower = everything, slice(0, half)

    def stacked(step):
        columns_k = slice(step * half, (step + 1) * half)
        for target_ref, rows_k in ((grad_ref, lower), (zm_ref, upper)):
            value = product2_t(z_ref.at[step % 2], (), wo_ref[rows_k, columns_k])
            if step == 0:
                target_ref[...] = value
            else:
                target_ref[...] += value

    def middle_slopes():
        load_zt.wait()
        load_zp.wait()
        sloped(grad_ref, grad_ref, page_ref, s_trans, 2, g_trans, b_trans, own)
        sloped(zm_ref, zm_ref, joined_ref, s_split, 3, g_split, b_split, lower)

    def middle():
        sum_finish(2)
        sum_finish(3)
        settled(grad_ref, page_ref, s_trans, 2, g_trans, own, lambda r, dz: split_store(pair_ref, (r,), dz))
        load_zs.start()
        settled(zm_ref, joined_ref, s_split, 3, g_split, lower, lambda r, dz: split_store(part_ref, (r,), dz))
        load_zm.start()
        write_part.start()
        joined_ref[...] = product2_t(pair_ref, (), wt_ref[...])
        load_zs.wait()
        sloped(joined_ref, grad_ref, page_ref, s_spread, 4, g_spread, b_spread, own)

    def prepare():
        sum_finish(4)
        padded_ref[0:GUARD, :] = jnp.zeros((GUARD, half), F32)
        padded_ref[GUARD + count :, :] = jnp.zeros((GUARD, half), F32)

        def keep(r, dz):
            padded_ref[pl.ds(r.start + GUARD, CHUNK), :] = dz

        settled(grad_ref, page_ref, s_spread, 4, g_spread, own, keep)
        load_zi.start()
        grad_ref[...] = jnp.zeros_like(grad_ref)

    def tap_work(tap):
        move, dx = taps(side, slots)[tap]
        slot = tap % 2
        moved = padded_ref[GUARD - move : GUARD - move + count, :]
        if dx:
            moved = moved * edge_ref[:, 1 - dx : 2 - dx]
        high = moved.astype(BF16)
        z_ref[slot, 0] = high
        z_ref[slot, 1] = (moved - high.astype(F32)).astype(BF16)
        tap_load(tap).wait()
        if tap < 8:
            tap_load(tap + 1).start()

    def tap_gradient(slot):
        grad_ref[...] += dot_t(z_ref[slot, 0], tap_ref[slot]) + dot_t(z_ref[slot, 1], tap_ref[slot])

    def inner_slope():
        load_zi.wait()
        sloped(grad_ref, grad_ref, page_ref, s_inner, 0, g_inner, b_inner, own)

    def shifted(k):
        return lambda r: pl.ds(pl.multiple_of(r.start + k * pitch, CHUNK), CHUNK)

    def inner_tile(k):
        mean, inverse = moments(s_inner, stats_total, everything)
        factor = g_inner[...] * inverse
        first_sum, second_sum = sums_ref[0, 0:1, :] / stats_total, sums_ref[0, 1:2, :] / stats_total
        here = shifted(k)

        def body(r, _):
            q = here(r)
            dz = settle(grad_ref[q, :], page_ref[q, :], mask_ref[q, 0:1], mean, inverse, factor, first_sum, second_sum)
            split_store(pair_ref, (q,), dz)

        over_rows(pitch, body)
        rows_k = slice(k * pitch, (k + 1) * pitch)
        wide_ref[...] = product2_t(pair_ref, (rows_k,), wi_ref[...])
        mean, inverse = moments(s_split, stats_total, upper)
        gain, shift = g_split[0:1, upper], b_split[0:1, upper]

        def tail(r, carry):
            q = here(r)
            dy, sums = norm_slope(zm_ref, wide_ref[r, :] + joined_ref[q, :], mask_ref, q, everything, mean, inverse, gain, shift)
            grad_ref[q, :] = dy
            return (carry[0] + sums[0], carry[1] + sums[1])

        zero = jnp.zeros((8, half), F32)
        add_sums(sums_ref.at[1], everything, over_rows(pitch, tail, (zero, zero)))

    def small_start():
        pieces = [
            (sums_ref.at[3], everything), (sums_ref.at[1], everything), (sums_ref.at[0], everything), (sums_ref.at[4], everything),
            (sums_ref.at[2], everything), (q_out, slice(0, half)), (q_out, slice(half, 2 * half)),
        ]
        small_ref[...] = jnp.zeros_like(small_ref)
        for k, (ref, columns_k) in enumerate(pieces):
            small_ref[k : k + 1, :] = ref[0:1, columns_k]
            small_ref[8 + k : 9 + k, :] = ref[1:2, columns_k]
        for copy in small_copies():
            copy.start()
        spread_ref[dp] = small_ref[...]

    def small_finish():
        for copy in small_copies():
            copy.wait()
        value = spread_ref[0]
        for k in range(1, spread_ref.shape[0]):
            value = value + spread_ref[k]
        vectors_ref[...] = value

    def main_settle():
        def keep(r, dz):
            high = dz.astype(BF16)
            rest = (dz - high.astype(F32)).astype(BF16)
            for slot in (0, 1):
                z_ref[slot, 0, r, :] = high
                z_ref[slot, 1, r, :] = rest

        settled(grad_ref, zm_ref, s_split, 1, g_split, upper, keep)
        write_main.start()

    FIRST_TAP = 4
    hosted = {
        0: [functools.partial(stacked, 0)],
        1: [functools.partial(stacked, 1), middle_slopes],
        2: [middle],
        3: [prepare],
        13: [inner_slope],
        14: [load_zm.wait, lambda: sum_finish(0), functools.partial(inner_tile, 0), functools.partial(inner_tile, 1)],
        15: [functools.partial(inner_tile, 2), functools.partial(inner_tile, 3), lambda: sum_start(1)],
        16: [lambda: sum_finish(1), small_start],
        17: [main_settle],
        18: [small_finish, write_part.wait, write_main.wait],
    }

    sums_ref[...] = jnp.zeros_like(sums_ref)
    load_zt.start()
    load_zp.start()
    tap_load(0).start()
    for copy in load(0):
        copy.start()
    barrier = pltpu.get_barrier_semaphore()
    peers = [to_core, to_x, to_y] + to_z + to_far + [to_diagonal]
    for peer in peers:
        pl.semaphore_signal(barrier, inc=1, device_id=peer, device_id_type=MESH)
    pl.semaphore_wait(barrier, len(peers))
    total = len(jobs)
    taken = [j for j in range(total) if jobs[j] is not None]
    empty = [j for j in range(total) if jobs[j] is None]

    @pl.loop(0, total + LAG + 1)
    def _(t):
        for j in taken:

            @pl.when(t == j + LAG + 1)
            def _(j=j):
                store(j).wait()

        def stage(number, lag):
            def wrap(body):
                c = t - lag
                valid = jnp.logical_and(c >= 0, c < total)
                if empty:
                    valid = jnp.logical_and(valid, jnp.logical_or(c < empty[0], c > empty[-1]))
                pl.when(valid)(lambda: body(c))

            return wrap

        @stage(7, LAGS[7])
        def _(c):
            finish(7, c)

        for j in taken:

            @pl.when(t == j + LAG)
            def _(j=j):
                store(j).start()

        for number in (6, 5, 4):

            @stage(number, LAGS[number])
            def _(c, number=number):
                finish(number, c)
                if number == 4:
                    for k in (0, 1):
                        row = core * (block // 2) + first[k] * (block // 4) + second[k] * (block // 8)
                        full_ref[c % KEPT, part(row, block // 8), columns[k]] = gathered_ref[c % 2, :, columns[k]]
                begin(number + 1, c)

        for j in range(total):

            @pl.when(t == j)
            def _(j=j):
                for copy in load(j):
                    copy.wait()
                for task in hosted.get(j, ()):
                    task()
                if j + 1 < total:
                    for copy in load(j + 1):
                        copy.start()
                if 0 <= j - FIRST_TAP < 9:
                    tap_work(j - FIRST_TAP)

        @pl.when(jnp.logical_and(t >= FIRST_TAP, t < FIRST_TAP + 9))
        def _():
            tap_gradient(t % 2)

        @stage(3, LAGS[3])
        def _(c):
            finish(3, c)
            slot = c % 2
            value = eighth_ref[slot, part(z * (block // 32), block // 32), :]
            for k in (0, 1, 2):
                value = value + r3_ref[slot, k]
            gathered_ref[slot, part(z * (block // 32), block // 32), :] = value
            begin(4, c)

        @stage(2, LAGS[2])
        def _(c):
            finish(2, c)
            slot = c % 2
            for k in (0, 1):
                eighth_ref[slot, :, columns[k]] = quarter_ref[slot, part(second[k] * (block // 8), block // 8), columns[k]] + r2_ref[c % 4, :, columns[k]]
            begin(3, c)

        @stage(1, LAGS[1])
        def _(c):
            finish(1, c)
            slot = c % 2
            for k in (0, 1):
                quarter_ref[slot, :, columns[k]] = half_ref[slot, part(first[k] * (block // 4), block // 4), columns[k]] + r1_ref[c % 4, :, columns[k]]
            begin(2, c)

        @stage(0, LAGS[0])
        def _(c):
            finish(0, c)
            slot = c % 2
            half_ref[slot] = own_ref[slot, part(core * (block // 2), block // 2), :] + r0_ref[slot]
            begin(1, c)

        exact = functools.reduce(jnp.logical_or, [t == j for j in taken if jobs[j][0][2] == 1])

        @stage(None, 0)
        def _(c):
            slot = c % 2
            turned_ref[...] = x_ref[slot, 0].T
            own_ref[slot] = dot(turned_ref[...], z_ref[slot, 0]) + dot(turned_ref[...], z_ref[slot, 1])

            @pl.when(jnp.logical_not(exact))
            def _():
                turned_ref[...] = x_ref[slot, 1].T
                own_ref[slot] += dot(turned_ref[...], z_ref[slot, 0])

            begin(0, c)


def reduce_call(jobs, lefts, rights, hosted, constants, shapes, side, slots):
    hbm, vmem_spec = pl.BlockSpec(memory_space=pl.ANY), pl.BlockSpec(memory_space=pltpu.VMEM)
    vmem, dma = pltpu.VMEM, pltpu.SemaphoreType.DMA
    count, block = hosted[0].shape
    pitch = count // TILES
    scratch = [
        vmem((2, 2, count, block), BF16), vmem((2, 2, count, block), BF16), vmem((block, count), BF16),
        vmem((2, block, block), F32), vmem((2, block // 2, block), F32), vmem((2, block // 2, block), F32),
        vmem((4, block // 4, block), F32), vmem((2, block // 4, block), F32), vmem((4, block // 8, block), F32), vmem((2, block // 8, block), F32),
        vmem((2, 3, block // 32, block), F32), vmem((2, block // 8, block), F32), vmem((KEPT, block, block), F32),
        dma((2, 2)), dma((KEPT,)),
        vmem((count + 2 * GUARD, block), F32), vmem((count, block), F32), vmem((count, block), F32), vmem((count, block), F32),
        vmem((count, block), F32), vmem((2, count, block), BF16), vmem((2, count, block), BF16), vmem((pitch, block), F32),
        vmem((2, block, block), BF16), vmem((5, 8, block), F32), vmem((5, 4, 8, block), F32),
        vmem((16, block), F32), vmem((8, 16, block), F32),
        dma((3,)), dma((2,)), dma((2,)), dma((5, 3)), dma((5, 3)), dma((7,)), dma((7,)),
    ]
    for width in (1, 2, 2, 3, 3, 2, 2, 1):
        scratch += [dma((width, 4)), dma((width, 4))]
    return pl.pallas_call(
        functools.partial(reduce_body, jobs, side, slots),
        in_specs=[hbm] * (len(lefts) + len(rights) + len(hosted)) + [vmem_spec] * len(constants),
        out_specs=[hbm] * (len(shapes) + 2) + [vmem_spec],
        out_shape=[sds(shape) for shape in shapes] + [sds((2, count, block), BF16)] * 2 + [sds((16, block))],
        scratch_shapes=scratch,
        compiler_params=pltpu.CompilerParams(collective_id=3, has_side_effects=True, vmem_limit_bytes=60 * 1024 * 1024),
    )(*lefts, *rights, *hosted, *constants)


def gather_sums_body(axis, sums_ref, out_ref, slots_ref, send_sem, recv_sem):
    members = slots_ref.shape[0]
    me = lax.axis_index(axis)
    peers = [lax.rem(me + k, members) for k in range(1, members)]
    barrier = pltpu.get_barrier_semaphore()
    for peer in peers:
        pl.semaphore_signal(barrier, inc=1, device_id={axis: peer}, device_id_type=MESH)
    pl.semaphore_wait(barrier, members - 1)
    copies = [
        pltpu.make_async_remote_copy(
            src_ref=sums_ref, dst_ref=slots_ref.at[me], send_sem=send_sem.at[k], recv_sem=recv_sem.at[k], device_id={axis: peer}, device_id_type=MESH
        )
        for k, peer in enumerate(peers)
    ]
    for copy in copies:
        copy.start()
    slots_ref[me] = sums_ref[...]
    for copy in copies:
        copy.wait()
    value = slots_ref[0]
    for k in range(1, members):
        value = value + slots_ref[k]
    out_ref[...] = value


def gather_sums(sums, members, collective, axis="bn"):
    if members == 1:
        return sums
    spec = pl.BlockSpec(memory_space=pltpu.VMEM)
    return pl.pallas_call(
        functools.partial(gather_sums_body, axis),
        in_specs=[spec],
        out_specs=spec,
        out_shape=sds(sums.shape),
        scratch_shapes=[pltpu.VMEM((members,) + sums.shape, F32), pltpu.SemaphoreType.DMA((members - 1,)), pltpu.SemaphoreType.DMA((members - 1,))],
        compiler_params=pltpu.CompilerParams(collective_id=collective, has_side_effects=True),
    )(sums)


def local(
    shape,
    features, image_counts, map_sides,
    split_kernel, split_gain, split_shift, inner_kernel, inner_gain, inner_shift,
    spread_kernel, spread_gain, spread_shift, transition_kernel, transition_gain, transition_shift,
    output_kernel, output_gain, output_shift, cotangent,
):
    slots, side, _, full = features.shape
    half = inner_kernel.shape[0]
    pitch = round_up(-(-slots * side * side // TILES), 16)
    count = TILES * pitch
    grid = (TILES,)
    columns = np.arange(count)[:, None] // slots % side
    lanes = np.arange(128)[None, :]
    edges = jnp.asarray(np.where(lanes == 0, columns > 0, np.where(lanes == 2, columns < side - 1, True)).astype(np.float32))
    features = features.transpose(1, 2, 0, 3).reshape(side * side, slots, full)
    cotangent = cotangent.transpose(1, 2, 0, 3).reshape(side * side, slots, full)
    (split_gain, split_shift, inner_gain, inner_shift, spread_gain, spread_shift, transition_gain, transition_shift, output_gain, output_shift) = (
        item.reshape(1, -1)
        for item in (split_gain, split_shift, inner_gain, inner_shift, spread_gain, spread_shift, transition_gain, transition_shift, output_gain, output_shift)
    )
    spread_weight = spread_kernel.reshape(9, half, half)

    def group(sums):
        return gather_sums(sums, shape[1], 1 if sums.shape[1] == full else 2)

    sums_full, sums_half = out_whole((8, full)), out_whole((8, half))
    r_half, r_full, r_mask = rows(pitch, half), rows(pitch, full), rows(pitch, 128)
    pair_half, pair_full = rows2(pitch, half), rows2(pitch, full)

    def call(body, ins, outs, scratch=(), steps=grid):
        return pl.pallas_call(
            body,
            grid=steps,
            in_specs=[spec for _, spec in ins],
            out_specs=[spec for _, spec in outs],
            out_shape=[shape for shape, _ in outs],
            scratch_shapes=list(scratch),
            compiler_params=params(),
        )(*[array for array, _ in ins])

    def fixed(array):
        return (array, whole(array))

    if shape == (8, 4):
        low, high = slice(0, half), slice(half, full)
        every = slice(None)
        (x0, z_part, z_main, main2, part2, z_inner, inner2, z_spread, joined2, z_trans, trans2, result, dz_low, dz_high, totals, mask) = front_call(
            [features, cotangent, split_kernel, inner_kernel, spread_weight, transition_kernel, output_kernel],
            [split_gain, split_shift, inner_gain, inner_shift, spread_gain, spread_shift, transition_gain, transition_shift, output_gain, output_shift, edges],
            [image_counts, map_sides],
            slots, side, count, shape[1],
        )
        jobs = [((0, 0, 2), 0, (4, (low, low))), ((0, 0, 2), 1, (4, (low, high)))]
        jobs += [((1, 0, 2), 0, (4, (high, low))), ((1, 0, 2), 1, (4, (high, high)))]
        jobs += [((4, 0, 2), None, (2, (tap,))) for tap in range(9)]
        jobs += [((2, 0, 2), "pair", (3, (every, every)))]
        jobs += [((3, 0, 1), "part", (0, (low, low))), ((3, 1, 1), "part", (0, (high, low)))]
        jobs += [((5, 0, 2), "pair", (1, (every, every)))]
        jobs += [((3, 0, 1), None, (0, (low, high))), ((3, 1, 1), None, (0, (high, high)))]
        grad_split, grad_inner, grad_spread, grad_transition, grad_output, dz_part, dz_main, vectors = reduce_call(
            jobs,
            [trans2, part2, joined2, x0, inner2, main2],
            [dz_low, dz_high],
            [z_trans, z_part, z_spread, z_inner, z_main, spread_weight],
            [
                totals, split_gain, split_shift, inner_gain, inner_shift, spread_gain, spread_shift, transition_gain, transition_shift,
                mask, edges, inner_kernel, transition_kernel, output_kernel,
            ],
            [(full, full), (half, half), (9, half, half), (half, half), (full, full)],
            side, slots,
        )
        result, grad_split, grad_inner, grad_spread, grad_transition, grad_output, grad_features = final_call(
            [result, grad_split, grad_inner, grad_spread, grad_transition, grad_output], dz_part, dz_main, split_kernel, slots
        )
        small = vectors.reshape(2, 8 * half)
    else:
        row = jnp.arange(count)[:, None] + jnp.zeros((1, 128), jnp.int32)
        slot, place = row % slots, row // slots
        y, x = place // side, place % side
        sides = sum(jnp.where(slot == k, map_sides[k], 0) for k in range(slots))
        keep = (slot < image_counts[0]) & (y < sides) & (x < sides) & (place < side * side)
        mask = keep.astype(F32)
        x0, z_split, s_split = call(
            split_kernel_body,
            [(features, pixels(pitch, features.shape)), (mask, r_mask), fixed(split_kernel)],
            [(sds((count, full), BF16), r_full), (sds((count, full)), r_full), (sds((8, full)), sums_full)],
            [pltpu.VMEM((pitch, full), F32)],
        )
        s_split = group(s_split)
        part2, main, main2, z_inner, s_inner = call(
            inner_body,
            [(z_split, r_full), fixed(s_split), fixed(split_gain), fixed(split_shift), (mask, r_mask), fixed(inner_kernel)],
            [
                (sds((2, count, half), BF16), pair_half), (sds((count, half)), r_half), (sds((2, count, half), BF16), pair_half),
                (sds((count, half)), r_half), (sds((8, half)), sums_half),
            ],
        )
        s_inner = group(s_inner)
        tap_spec = pl.BlockSpec((1, half, half), lambda i: (i, 0, 0))
        inner2, z_spread, s_spread = call(
            functools.partial(spread_body, side, slots),
            [fixed(z_inner), fixed(s_split), fixed(s_inner), fixed(inner_gain), fixed(inner_shift), fixed(mask), fixed(edges), (spread_weight, tap_spec)],
            [(sds((2, count, half), BF16), out_whole((2, count, half))), (sds((count, half)), out_whole((count, half))), (sds((8, half)), sums_half)],
            [pltpu.VMEM((count + 2 * GUARD, half), F32), pltpu.VMEM((2, count, half), BF16)],
            (9,),
        )
        s_spread = group(s_spread)
        joined2, z_trans, s_trans = call(
            transition_body,
            [(z_spread, r_half), fixed(s_split), fixed(s_spread), fixed(spread_gain), fixed(spread_shift), (mask, r_mask), (main, r_half), fixed(transition_kernel)],
            [(sds((2, count, half), BF16), pair_half), (sds((count, half)), r_half), (sds((8, half)), sums_half)],
        )
        s_trans = group(s_trans)
        trans2, z_out, s_out = call(
            output_body,
            [(z_trans, r_half), fixed(s_split), fixed(s_trans), fixed(transition_gain), fixed(transition_shift), (mask, r_mask), (part2, pair_half), fixed(output_kernel)],
            [(sds((2, count, half), BF16), pair_half), (sds((count, full)), r_full), (sds((8, full)), sums_full)],
        )
        s_out = group(s_out)
        result, dy_out, q_out = call(
            result_body,
            [(z_out, r_full), fixed(s_split), fixed(s_out), fixed(output_gain), fixed(output_shift), (mask, r_mask), (cotangent, pixels(pitch, cotangent.shape))],
            [(sds(cotangent.shape), pixels(pitch, cotangent.shape)), (sds((count, full)), r_full), (sds((8, full)), sums_full)],
            [pltpu.VMEM((pitch, full), F32)],
        )
        q_out = group(q_out)
        dz_out, dy_trans, dy_part, q_mid = call(
            output_back_body,
            [
                (dy_out, r_full), (z_out, r_full), fixed(s_out), fixed(output_gain), fixed(q_out), fixed(s_split), (mask, r_mask), fixed(output_kernel),
                (z_trans, r_half), fixed(s_trans), fixed(transition_gain), fixed(transition_shift), (z_split, rows(pitch, half, 0)), fixed(split_gain), fixed(split_shift),
            ],
            [(sds((2, count, full), BF16), pair_full), (sds((count, half)), r_half), (sds((count, half)), r_half), (sds((8, full)), sums_full)],
            [pltpu.VMEM((pitch, full), F32)],
        )
        q_mid = group(q_mid)
        dz_trans, dz_part, grad_joined, dy_spread, q_spread = call(
            transition_back_body,
            [
                (dy_trans, r_half), (dy_part, r_half), (z_trans, r_half), fixed(s_trans), fixed(transition_gain), fixed(q_mid), fixed(s_split), (mask, r_mask), fixed(transition_kernel),
                (z_split, rows(pitch, half, 0)), fixed(split_gain), (z_spread, r_half), fixed(s_spread), fixed(spread_gain), fixed(spread_shift),
            ],
            [
                (sds((2, count, half), BF16), pair_half), (sds((2, count, half), BF16), pair_half), (sds((count, half)), r_half),
                (sds((count, half)), r_half), (sds((8, half)), sums_half),
            ],
        )
        q_spread = group(q_spread)
        moved_spec = pl.BlockSpec((1, 2, count, half), lambda i: (i, 0, 0, 0))
        moved, dy_inner, q_inner = call(
            functools.partial(spread_back_body, side, slots),
            [
                fixed(dy_spread), fixed(z_spread), fixed(s_spread), fixed(spread_gain), fixed(q_spread), fixed(s_split), fixed(mask), fixed(edges), (spread_weight, tap_spec),
                fixed(z_inner), fixed(s_inner), fixed(inner_gain), fixed(inner_shift),
            ],
            [(sds((9, 2, count, half), BF16), moved_spec), (sds((count, half)), out_whole((count, half))), (sds((8, half)), sums_half)],
            [pltpu.VMEM((count + 2 * GUARD, half), F32), pltpu.VMEM((count, half), F32)],
            (9,),
        )
        q_inner = group(q_inner)
        dz_inner, dy_main, q_main = call(
            inner_back_body,
            [
                (dy_inner, r_half), (z_inner, r_half), fixed(s_inner), fixed(inner_gain), fixed(q_inner), fixed(s_split), (mask, r_mask), fixed(inner_kernel),
                (grad_joined, r_half), (z_split, rows(pitch, half, 1)), fixed(split_gain), fixed(split_shift),
            ],
            [(sds((2, count, half), BF16), pair_half), (sds((count, half)), r_half), (sds((8, half)), sums_half)],
            [pltpu.VMEM((pitch, half), F32)],
        )
        q_main = group(q_main)
        dz_main, grad_features = call(
            split_back_body,
            [(dy_main, r_half), (z_split, rows(pitch, half, 1)), fixed(q_main), fixed(s_split), fixed(split_gain), (mask, r_mask), (dz_part, pair_half), fixed(split_kernel)],
            [(sds((2, count, half), BF16), pair_half), (sds(cotangent.shape), pixels(pitch, cotangent.shape))],
            [pltpu.VMEM((pitch, full), F32)],
        )
        small = jnp.concatenate([q_mid[0:2, half:], q_main[0:2], q_inner[0:2], q_spread[0:2], q_mid[0:2, :half], q_out[0:2]], axis=1)
        grad_output = jnp.concatenate([weight_grad(trans2, dz_out), weight_grad(part2, dz_out)], axis=0)
        grad_transition, grad_inner = weight_grad(joined2, dz_trans), weight_grad(main2, dz_inner)
        grad_split = jnp.concatenate([weight_grad(x0[None], dz_part), weight_grad(x0[None], dz_main)], axis=1)
        grad_spread = jnp.stack([weight_grad(inner2, moved[tap]) for tap in range(9)])
        grad_split, grad_inner, grad_spread, grad_transition, grad_output = lax.psum(
            (grad_split, grad_inner, grad_spread, grad_transition, grad_output), ("dp", "bn")
        )
        small = lax.psum(small, "dp")
    cuts = [0, full, full + half, full + 2 * half, full + 3 * half, 2 * full + 3 * half]
    shifts = [small[0, a:b] for a, b in zip(cuts[:-1], cuts[1:])]
    gains = [small[1, a:b] for a, b in zip(cuts[:-1], cuts[1:])]
    result, grad_features = (item.reshape(side, side, slots, full).transpose(2, 0, 1, 3) for item in (result, grad_features))
    return (
        result, grad_features,
        grad_split, gains[0], shifts[0], grad_inner, gains[1], shifts[1],
        grad_spread.reshape(3, 3, half, half), gains[2], shifts[2], grad_transition, gains[3], shifts[3], grad_output, gains[4], shifts[4],
    )


def solution(mesh):
    shard, copy = P(("dp", "bn")), P()
    return jax.shard_map(
        functools.partial(local, (mesh.shape["dp"], mesh.shape["bn"])),
        mesh=mesh,
        in_specs=(shard, shard, shard) + (copy,) * 15 + (shard,),
        out_specs=(shard, shard) + (copy,) * 15,
        check_vma=False,
    )
```

```python
import functools

import jax
import jax.numpy as jnp
import numpy as np
from jax import lax
from jax.experimental import pallas as pl
from jax.experimental.pallas import tpu as pltpu
from jax.sharding import PartitionSpec as P

EPS = 1e-05
GUARD = 80
CHUNK = 16
TILES = 4
MESH = pl.DeviceIdType.MESH
F32 = jnp.float32
BF16 = jnp.bfloat16


def round_up(value, step):
    return -(-value // step) * step


def params(megabytes=56):
    return pltpu.CompilerParams(vmem_limit_bytes=megabytes * 1024 * 1024)


def whole(array):
    zeros = (0,) * len(array.shape)
    return pl.BlockSpec(array.shape, lambda *_: zeros, pipeline_mode=pl.Buffered(1))


def out_whole(shape):
    zeros = (0,) * len(shape)
    return pl.BlockSpec(shape, lambda *_: zeros)


def rows(pitch, width, column=0):
    return pl.BlockSpec((pitch, width), lambda i: (i, column))


def rows2(pitch, width):
    return pl.BlockSpec((2, pitch, width), lambda i: (0, i, 0))


def pixels(pitch, shape):
    return pl.BlockSpec((pitch // shape[1],) + tuple(shape[1:]), lambda i: (i, 0, 0))


def sds(shape, dtype=F32):
    return jax.ShapeDtypeStruct(tuple(shape), dtype)


def dot(left, right):
    return jnp.dot(left, right, preferred_element_type=F32)


def dot_t(left, right):
    return lax.dot_general(left, right, (((1,), (1,)), ((), ())), preferred_element_type=F32)


def split_store(ref, place, value):
    high = value.astype(BF16)
    ref[(0,) + place] = high
    ref[(1,) + place] = (value - high.astype(F32)).astype(BF16)


def moments(stats_ref, total, columns):
    mean = stats_ref[0:1, columns] / total
    square = stats_ref[1:2, columns] / total
    return mean, lax.rsqrt(square - mean * mean + EPS)


def mish(y):
    t = jnp.exp(jnp.minimum(y, 30.0))
    n = t * (t + 2.0)
    return y * (n / (n + 2.0))


def mish_slope(y):
    t = jnp.exp(jnp.minimum(y, 30.0))
    n = t * (t + 2.0)
    r = 1.0 / (n + 2.0)
    return n * r + y * (((4.0 * t) * (t + 1.0) * r) * r)


def fold(value):
    return jnp.sum(value.reshape(value.shape[0] // 8, 8, value.shape[1]), axis=0)


def over_rows(count, body, carry=None, unroll=4):
    def step(k, c):
        return body(pl.ds(pl.multiple_of(k * CHUNK, CHUNK), CHUNK), c)

    return lax.fori_loop(0, count // CHUNK, step, carry, unroll=unroll)


def column_blocks(width, block=512):
    return [slice(c, c + block) for c in range(0, width, block)]


def add_sums(sums_ref, columns, pieces):
    for k, piece in enumerate(pieces):
        sums_ref[k : k + 1, columns] += jnp.sum(piece, axis=0, keepdims=True)


def start_sums(sums_ref):
    @pl.when(pl.program_id(0) == 0)
    def _():
        sums_ref[...] = jnp.zeros_like(sums_ref)


def sum_squares(z_ref, sums_ref, mask_ref=None):
    for columns in column_blocks(z_ref.shape[1]):
        width = columns.stop - columns.start

        def body(r, carry):
            value = z_ref[r, columns]
            kept = value if mask_ref is None else value * mask_ref[r, 0:1]
            return (carry[0] + fold(kept), carry[1] + fold(kept * value))

        zero = jnp.zeros((8, width), F32)
        add_sums(sums_ref, columns, over_rows(z_ref.shape[0], body, (zero, zero)))


def product2(ref, place, weight):
    high = ref[(0,) + place]
    low = ref[(1,) + place]
    return dot(high, weight) + dot(low, weight)


def product2_t(ref, place, weight):
    high = ref[(0,) + place]
    low = ref[(1,) + place]
    return dot_t(high, weight) + dot_t(low, weight)


def compact(source_ref, scratch_ref):
    places, slots, _ = source_ref.shape
    for p in range(places):
        scratch_ref[p * slots : (p + 1) * slots, :] = source_ref[p].astype(F32)


def spread_out(scratch_ref, target_ref):
    places, slots, _ = target_ref.shape
    for p in range(places):
        target_ref[p] = scratch_ref[p * slots : (p + 1) * slots, :]


def split_kernel_body(features_ref, mask_ref, w_ref, x_ref, z_ref, sums_ref, scratch_ref):
    compact(features_ref, scratch_ref)

    def body(r, _):
        x_ref[r, :] = jnp.where(mask_ref[r, 0:1] > 0.0, scratch_ref[r, :], 0.0).astype(BF16)

    over_rows(x_ref.shape[0], body)
    z_ref[...] = dot(x_ref[...], w_ref[...])
    start_sums(sums_ref)
    sum_squares(z_ref, sums_ref)
    count = jnp.sum(mask_ref[...], axis=0, keepdims=True)
    sums_ref[2:3, 0:128] += count


def inner_body(z_ref, stats_ref, gain_ref, shift_ref, mask_ref, w_ref, part_ref, main_ref, main2_ref, zi_ref, sums_ref):
    total = stats_ref[2:3, 0:1]
    half = w_ref.shape[0]
    for index, columns in enumerate(column_blocks(2 * half, half)):
        mean, inverse = moments(stats_ref, total, columns)
        scale, shift = gain_ref[0:1, columns] * inverse, shift_ref[0:1, columns]

        def body(r, _):
            act = mish((z_ref[r, columns] - mean) * scale + shift) * mask_ref[r, 0:1]
            if index == 0:
                split_store(part_ref, (r,), act)
            else:
                main_ref[r, :] = act
                split_store(main2_ref, (r,), act)

        over_rows(z_ref.shape[0], body)
    zi_ref[...] = product2(main2_ref, (), w_ref[...])
    start_sums(sums_ref)
    sum_squares(zi_ref, sums_ref)


def taps(side, slots):
    return [((dy * side + dx) * slots, dx) for dy in (-1, 0, 1) for dx in (-1, 0, 1)]


def move_rows(padded_ref, edge_ref, pair_ref, side, slots, sign):
    count = pair_ref.shape[1]
    for index, (move, dx) in enumerate(taps(side, slots)):

        @pl.when(pl.program_id(0) == index)
        def _(move=sign * move, dx=sign * dx):
            moved = padded_ref[GUARD + move : GUARD + move + count, :]
            if dx:
                moved = moved * edge_ref[:, dx + 1 : dx + 2]
            split_store(pair_ref, (slice(None),), moved)


def spread_body(side, slots, z_ref, total_ref, stats_ref, gain_ref, shift_ref, mask_ref, edge_ref, w_ref, inner_ref, zs_ref, sums_ref, padded_ref, pair_ref):
    total = total_ref[2:3, 0:1]
    count = z_ref.shape[0]
    tap = pl.program_id(0)

    @pl.when(tap == 0)
    def _():
        mean, inverse = moments(stats_ref, total, slice(None))
        scale, shift = gain_ref[...] * inverse, shift_ref[...]
        padded_ref[0:GUARD, :] = jnp.zeros((GUARD, padded_ref.shape[1]), F32)
        padded_ref[GUARD + count :, :] = jnp.zeros((GUARD, padded_ref.shape[1]), F32)

        def body(r, _):
            act = mish((z_ref[r, :] - mean) * scale + shift) * mask_ref[r, 0:1]
            padded_ref[pl.ds(r.start + GUARD, CHUNK), :] = act
            split_store(inner_ref, (r,), act)

        over_rows(count, body)
        zs_ref[...] = jnp.zeros_like(zs_ref)

    move_rows(padded_ref, edge_ref, pair_ref, side, slots, 1)
    zs_ref[...] += product2(pair_ref, (), w_ref[0])

    @pl.when(tap == pl.num_programs(0) - 1)
    def _():
        sums_ref[...] = jnp.zeros_like(sums_ref)
        sum_squares(zs_ref, sums_ref, mask_ref)


def transition_body(z_ref, total_ref, stats_ref, gain_ref, shift_ref, mask_ref, main_ref, w_ref, joined_ref, zt_ref, sums_ref):
    total = total_ref[2:3, 0:1]
    mean, inverse = moments(stats_ref, total, slice(None))
    scale, shift = gain_ref[...] * inverse, shift_ref[...]

    def body(r, _):
        act = mish((z_ref[r, :] - mean) * scale + shift) * mask_ref[r, 0:1]
        split_store(joined_ref, (r,), act + main_ref[r, :])

    over_rows(z_ref.shape[0], body)
    zt_ref[...] = product2(joined_ref, (), w_ref[...])
    start_sums(sums_ref)
    sum_squares(zt_ref, sums_ref)


def output_body(z_ref, total_ref, stats_ref, gain_ref, shift_ref, mask_ref, part_ref, w_ref, trans_ref, zo_ref, sums_ref):
    total = total_ref[2:3, 0:1]
    mean, inverse = moments(stats_ref, total, slice(None))
    scale, shift = gain_ref[...] * inverse, shift_ref[...]
    half = z_ref.shape[1]

    def body(r, _):
        act = mish((z_ref[r, :] - mean) * scale + shift) * mask_ref[r, 0:1]
        split_store(trans_ref, (r,), act)

    over_rows(z_ref.shape[0], body)
    zo_ref[...] = product2(part_ref, (), w_ref[half:, :])
    zo_ref[...] += product2(trans_ref, (), w_ref[:half, :])
    start_sums(sums_ref)
    sum_squares(zo_ref, sums_ref)


def result_body(z_ref, total_ref, stats_ref, gain_ref, shift_ref, mask_ref, cotangent_ref, result_ref, dy_ref, sums_ref, scratch_ref):
    total = total_ref[2:3, 0:1]
    compact(cotangent_ref, scratch_ref)
    start_sums(sums_ref)
    for columns in column_blocks(z_ref.shape[1]):
        mean, inverse = moments(stats_ref, total, columns)
        gain, shift = gain_ref[0:1, columns], shift_ref[0:1, columns]

        def body(r, carry):
            mask = mask_ref[r, 0:1]
            scaled = (z_ref[r, columns] - mean) * inverse
            y = scaled * gain + shift
            t = jnp.exp(jnp.minimum(y, 30.0))
            n = t * (t + 2.0)
            inv = 1.0 / (n + 2.0)
            ratio = n * inv
            slope = ratio + y * (((4.0 * t) * (t + 1.0) * inv) * inv)
            dy = jnp.where(mask > 0.0, scratch_ref[r, columns], 0.0) * slope
            scratch_ref[r, columns] = y * ratio * mask
            dy_ref[r, columns] = dy
            return (carry[0] + fold(dy), carry[1] + fold(dy * scaled))

        zero = jnp.zeros((8, columns.stop - columns.start), F32)
        add_sums(sums_ref, columns, over_rows(z_ref.shape[0], body, (zero, zero)))
    spread_out(scratch_ref, result_ref)


def norm_slope(z_ref, grad, mask_ref, r, columns, mean, inverse, gain, shift):
    scaled = (z_ref[r, columns] - mean) * inverse
    dy = grad * mask_ref[r, 0:1] * mish_slope(scaled * gain + shift)
    return dy, (fold(dy), fold(dy * scaled))


def settle(dy, z, mask, mean, inverse, factor, first, second):
    scaled = (z - mean) * inverse
    return mask * factor * (dy - (first + scaled * second))


def output_back_body(dy_ref, zo_ref, so_ref, go_ref, qo_ref, total_ref, mask_ref, w_ref, zt_ref, st_ref, gt_ref, bt_ref, zp_ref, gp_ref, bp_ref, dz_ref, dyt_ref, dyp_ref, sums_ref, grad_ref):
    total = total_ref[2:3, 0:1]
    for columns in column_blocks(zo_ref.shape[1]):
        mean, inverse = moments(so_ref, total, columns)
        factor = go_ref[0:1, columns] * inverse
        first, second = qo_ref[0:1, columns] / total, qo_ref[1:2, columns] / total

        def body(r, _):
            dz = settle(dy_ref[r, columns], zo_ref[r, columns], mask_ref[r, 0:1], mean, inverse, factor, first, second)
            split_store(dz_ref, (r, columns), dz)

        over_rows(zo_ref.shape[0], body)
    grad_ref[...] = product2_t(dz_ref, (), w_ref[...])
    start_sums(sums_ref)
    half = zt_ref.shape[1]
    for index, (z_ref, s_ref, g_ref, b_ref, out_ref) in enumerate(((zt_ref, st_ref, gt_ref, bt_ref, dyt_ref), (zp_ref, total_ref, gp_ref, bp_ref, dyp_ref))):
        columns = slice(index * half, (index + 1) * half)
        own = slice(0, half)
        mean, inverse = moments(s_ref, total, own)
        gain, shift = g_ref[0:1, own], b_ref[0:1, own]

        def body(r, carry):
            dy, sums = norm_slope(z_ref, grad_ref[r, columns], mask_ref, r, own, mean, inverse, gain, shift)
            out_ref[r, :] = dy
            return (carry[0] + sums[0], carry[1] + sums[1])

        zero = jnp.zeros((8, half), F32)
        add_sums(sums_ref, columns, over_rows(zt_ref.shape[0], body, (zero, zero)))


def transition_back_body(dyt_ref, dyp_ref, zt_ref, st_ref, gt_ref, q_ref, total_ref, mask_ref, w_ref, zp_ref, gp_ref, zs_ref, ss_ref, gs_ref, bs_ref, dz_ref, dzp_ref, grad_ref, dys_ref, sums_ref):
    total = total_ref[2:3, 0:1]
    half = zt_ref.shape[1]
    own = slice(0, half)
    for index, (dy_ref, z_ref, s_ref, g_ref, out_ref) in enumerate(((dyt_ref, zt_ref, st_ref, gt_ref, dz_ref), (dyp_ref, zp_ref, total_ref, gp_ref, dzp_ref))):
        columns = slice(index * half, (index + 1) * half)
        mean, inverse = moments(s_ref, total, own)
        factor = g_ref[0:1, own] * inverse
        first, second = q_ref[0:1, columns] / total, q_ref[1:2, columns] / total

        def body(r, _):
            dz = settle(dy_ref[r, :], z_ref[r, :], mask_ref[r, 0:1], mean, inverse, factor, first, second)
            split_store(out_ref, (r,), dz)

        over_rows(zt_ref.shape[0], body)
    grad_ref[...] = product2_t(dz_ref, (), w_ref[...])
    start_sums(sums_ref)
    mean, inverse = moments(ss_ref, total, own)
    gain, shift = gs_ref[...], bs_ref[...]

    def tail(r, carry):
        dy, sums = norm_slope(zs_ref, grad_ref[r, :], mask_ref, r, own, mean, inverse, gain, shift)
        dys_ref[r, :] = dy
        return (carry[0] + sums[0], carry[1] + sums[1])

    zero = jnp.zeros((8, half), F32)
    add_sums(sums_ref, own, over_rows(zt_ref.shape[0], tail, (zero, zero)))


def spread_back_body(side, slots, dy_ref, z_ref, s_ref, g_ref, q_ref, total_ref, mask_ref, edge_ref, w_ref, zi_ref, si_ref, gi_ref, bi_ref, moved_ref, dyi_ref, sums_ref, padded_ref, grad_ref):
    total = total_ref[2:3, 0:1]
    count, half = z_ref.shape
    tap = pl.program_id(0)

    @pl.when(tap == 0)
    def _():
        padded_ref[0:GUARD, :] = jnp.zeros((GUARD, half), F32)
        padded_ref[GUARD + count :, :] = jnp.zeros((GUARD, half), F32)
        mean, inverse = moments(s_ref, total, slice(None))
        factor = g_ref[...] * inverse
        first, second = q_ref[0:1, :] / total, q_ref[1:2, :] / total

        def body(r, _):
            dz = settle(dy_ref[r, :], z_ref[r, :], mask_ref[r, 0:1], mean, inverse, factor, first, second)
            padded_ref[pl.ds(r.start + GUARD, CHUNK), :] = dz

        over_rows(count, body)
        grad_ref[...] = jnp.zeros_like(grad_ref)

    move_rows(padded_ref, edge_ref, moved_ref.at[0], side, slots, -1)
    grad_ref[...] += product2_t(moved_ref.at[0], (), w_ref[0])

    @pl.when(tap == pl.num_programs(0) - 1)
    def _():
        sums_ref[...] = jnp.zeros_like(sums_ref)
        own = slice(0, half)
        mean, inverse = moments(si_ref, total, own)
        gain, shift = gi_ref[...], bi_ref[...]

        def tail(r, carry):
            dy, sums = norm_slope(zi_ref, grad_ref[r, :], mask_ref, r, own, mean, inverse, gain, shift)
            dyi_ref[r, :] = dy
            return (carry[0] + sums[0], carry[1] + sums[1])

        zero = jnp.zeros((8, half), F32)
        add_sums(sums_ref, own, over_rows(count, tail, (zero, zero)))


def inner_back_body(dy_ref, zi_ref, si_ref, gi_ref, q_ref, total_ref, mask_ref, w_ref, joined_ref, zm_ref, gm_ref, bm_ref, dz_ref, dym_ref, sums_ref, grad_ref):
    total = total_ref[2:3, 0:1]
    half = zi_ref.shape[1]
    own = slice(0, half)
    upper = slice(half, 2 * half)
    mean, inverse = moments(si_ref, total, own)
    factor = gi_ref[...] * inverse
    first, second = q_ref[0:1, :] / total, q_ref[1:2, :] / total

    def body(r, _):
        dz = settle(dy_ref[r, :], zi_ref[r, :], mask_ref[r, 0:1], mean, inverse, factor, first, second)
        split_store(dz_ref, (r,), dz)

    over_rows(zi_ref.shape[0], body)
    grad_ref[...] = product2_t(dz_ref, (), w_ref[...])
    start_sums(sums_ref)
    mean, inverse = moments(total_ref, total, upper)
    gain, shift = gm_ref[0:1, upper], bm_ref[0:1, upper]

    def tail(r, carry):
        dy, sums = norm_slope(zm_ref, grad_ref[r, :] + joined_ref[r, :], mask_ref, r, own, mean, inverse, gain, shift)
        dym_ref[r, :] = dy
        return (carry[0] + sums[0], carry[1] + sums[1])

    zero = jnp.zeros((8, half), F32)
    add_sums(sums_ref, own, over_rows(zi_ref.shape[0], tail, (zero, zero)))


def split_back_body(dy_ref, zm_ref, q_ref, total_ref, g_ref, mask_ref, dzp_ref, w_ref, dz_ref, grad_ref, scratch_ref):
    total = total_ref[2:3, 0:1]
    half = zm_ref.shape[1]
    upper = slice(half, 2 * half)
    mean, inverse = moments(total_ref, total, upper)
    factor = g_ref[0:1, upper] * inverse
    first, second = q_ref[0:1, :] / total, q_ref[1:2, :] / total

    def body(r, _):
        dz = settle(dy_ref[r, :], zm_ref[r, :], mask_ref[r, 0:1], mean, inverse, factor, first, second)
        split_store(dz_ref, (r,), dz)

    over_rows(zm_ref.shape[0], body)
    scratch_ref[...] = product2_t(dzp_ref, (), w_ref[:, :half])
    scratch_ref[...] += product2_t(dz_ref, (), w_ref[:, half:])
    spread_out(scratch_ref, grad_ref)


def final_body(pieces, *refs):
    count = len(pieces)
    sources, dzp_hbm, dzm_hbm, w_hbm, refs = refs[:count], refs[count], refs[count + 1], refs[count + 2], refs[count + 3 :]
    targets, grad_hbm, refs = refs[:count], refs[count], refs[count + 1 :]
    buffers, (dzp_ref, dzm_ref, w_ref, wide_ref, staged_ref, load_sem, store_sem, own_sem, grad_sem) = refs[:count], refs[count:]
    half = dzp_ref.shape[2]
    pitch = wide_ref.shape[0]
    places = staged_ref.shape[1]
    tiles = dzp_ref.shape[1] // pitch
    own = [pltpu.make_async_copy(w_hbm, w_ref, own_sem.at[0])]
    for k in range(tiles):
        rows_k = slice(k * pitch, (k + 1) * pitch)
        own.append(pltpu.make_async_copy(dzp_hbm.at[:, rows_k], dzp_ref.at[:, rows_k], own_sem.at[1 + 2 * k]))
        own.append(pltpu.make_async_copy(dzm_hbm.at[:, rows_k], dzm_ref.at[:, rows_k], own_sem.at[2 + 2 * k]))
    loads, stores = [], []
    for source, buffer, target, cuts in zip(sources, buffers, targets, pieces):
        for begin, end in cuts:
            k = len(loads)
            loads.append(pltpu.make_async_copy(source.at[begin:end], buffer.at[begin:end], load_sem.at[k]))
            stores.append(pltpu.make_async_copy(buffer.at[begin:end], target.at[begin:end], store_sem.at[k]))
    for copy in own[:3]:
        copy.start()
    ahead = len(loads) // 2
    for copy in loads[:ahead]:
        copy.start()
    for copy in own[3:]:
        copy.start()
    for copy in loads[ahead:]:
        copy.start()

    def forward(begin, end):
        for k in range(begin, end):
            loads[k].wait()
            stores[k].start()

    def grad_store(k):
        size = min(places, grad_hbm.shape[0] - k * places)
        return pltpu.make_async_copy(staged_ref.at[k % 2, 0:size], grad_hbm.at[k * places : k * places + size], grad_sem.at[k % 2])

    own[0].wait()
    step = -(-len(loads) // (tiles + 1))
    for k in range(tiles):
        own[1 + 2 * k].wait()
        own[2 + 2 * k].wait()
        rows_k = slice(k * pitch, (k + 1) * pitch)
        wide_ref[...] = product2_t(dzp_ref, (rows_k,), w_ref[:, :half]) + product2_t(dzm_ref, (rows_k,), w_ref[:, half:])
        if k >= 2:
            grad_store(k - 2).wait()
        spread_out(wide_ref, staged_ref.at[k % 2])
        grad_store(k).start()
        forward(min(k * step, len(loads)), min((k + 1) * step, len(loads)))
    forward(min(tiles * step, len(loads)), len(loads))
    for k in range(max(0, tiles - 2), tiles):
        grad_store(k).wait()
    for copy in stores:
        copy.wait()


def final_call(arrays, dzp, dzm, weight, slots):
    hbm = pl.BlockSpec(memory_space=pl.ANY)
    vmem, dma = pltpu.VMEM, pltpu.SemaphoreType.DMA
    full, count = weight.shape[0], dzp.shape[1]
    pitch = count // TILES
    pieces = []
    for array in arrays:
        length = array.shape[0]
        row_bytes = 4 * array.size // length
        step = min(length, max(1, (1 << 20) // row_bytes))
        pieces.append([(begin, min(begin + step, length)) for begin in range(0, length, step)])
    number = sum(len(cuts) for cuts in pieces)
    pixel_shape = arrays[0].shape
    scratch = [vmem(array.shape, F32) for array in arrays]
    scratch += [
        vmem(dzp.shape, BF16), vmem(dzm.shape, BF16), vmem(weight.shape, BF16), vmem((pitch, full), F32), vmem((2, pitch // slots, slots, full), F32),
        dma((number,)), dma((number,)), dma((1 + 2 * TILES,)), dma((2,)),
    ]
    return pl.pallas_call(
        functools.partial(final_body, pieces),
        in_specs=[hbm] * (len(arrays) + 3),
        out_specs=[hbm] * (len(arrays) + 1),
        out_shape=[sds(array.shape) for array in arrays] + [sds(pixel_shape)],
        scratch_shapes=scratch,
        compiler_params=params(60),
    )(*arrays, dzp, dzm, weight)


def weight_body(x_ref, dz_ref, dw_ref):
    turned = x_ref[0].T
    value = dot(turned, dz_ref[0]) + dot(turned, dz_ref[1])
    if x_ref.shape[0] == 2:
        value += dot(x_ref[1].T, dz_ref[0])
    dw_ref[...] = value


def weight_grad(x, dz, block=256):
    parts, count, width = x.shape
    wide = dz.shape[2]
    return pl.pallas_call(
        weight_body,
        grid=(width // block,),
        in_specs=[pl.BlockSpec((parts, count, block), lambda i: (0, 0, i)), whole(dz)],
        out_specs=pl.BlockSpec((block, wide), lambda i: (i, 0)),
        out_shape=sds((width, wide)),
        compiler_params=params(),
    )(x, dz)


SPLIT, INNER, SPREAD, TRANS, OUT, BACK_OUT, SPLIT_LOW = range(7)


def front_body(side, slots, *refs):
    (features_hbm, cotangent_hbm, w_split_hbm, w_inner_hbm, w_spread_hbm, w_trans_hbm, w_out_hbm), refs = refs[:7], refs[7:]
    (g_split, b_split, g_inner, b_inner, g_spread, b_spread, g_trans, b_trans, g_out, b_out, edge_ref, counts_ref, sides_ref), refs = refs[:13], refs[13:]
    (x_out, zp_out, zm_out, main_out, part_out, zi_out, inner_out, zs_out, joined_out, zt_out, trans_out, result_hbm, dlow_out, dhigh_out, total_ref, mask_ref), refs = refs[:16], refs[16:]
    (p0, p1, p2, p3, p4, p5, p6, p7, q0, q1, q2, q3, wide_ref, feature_ref, cot_ref, staged_ref), refs = refs[:16], refs[16:]
    (w_split, w_inner, w_spread, w_trans, w_out, local_ref, packed_ref, shared_ref), refs = refs[:8], refs[8:]
    weight_sem, feature_sem, cot_sem, staged_sem, out_sem, sum_send, sum_recv = refs
    count, half = p0.shape
    pitch = count // TILES
    places = pitch // slots
    low, high, everything = slice(0, half), slice(half, 2 * half), slice(None)
    dp, bn = lax.axis_index("dp"), lax.axis_index("bn")
    members = shared_ref.shape[1]
    group = [lax.rem(bn + k, members) for k in range(1, members)]

    weights = [
        pltpu.make_async_copy(source, target, weight_sem.at[k])
        for k, (source, target) in enumerate(
            ((w_split_hbm, w_split), (w_inner_hbm, w_inner), (w_spread_hbm, w_spread), (w_trans_hbm, w_trans), (w_out_hbm, w_out))
        )
    ]

    def rows_of(k):
        return min(places, features_hbm.shape[0] - k * places)

    def feature_load(k):
        size = rows_of(k)
        return pltpu.make_async_copy(features_hbm.at[k * places : k * places + size], feature_ref.at[k % 2, 0:size], feature_sem.at[k % 2])

    def cot_load(k):
        size = rows_of(k)
        return pltpu.make_async_copy(cotangent_hbm.at[k * places : k * places + size], cot_ref.at[0:size], cot_sem)

    def result_store(k):
        size = rows_of(k)
        return pltpu.make_async_copy(staged_ref.at[0:size], result_hbm.at[k * places : k * places + size], staged_sem)

    pending = {}

    def write(name, source, target):
        copy = pltpu.make_async_copy(source, target, out_sem.at[len(pending)])
        copy.start()
        pending[name] = [copy, True]

    def written(name):
        if pending[name][1]:
            pending[name][0].wait()
            pending[name][1] = False

    def sum_copies(which):
        wide = slice(0, 384 if which == SPLIT else 256)
        return wide, [
            pltpu.make_async_remote_copy(
                src_ref=packed_ref.at[which, :, wide], dst_ref=shared_ref.at[which, bn, :, wide],
                send_sem=sum_send.at[which, k], recv_sem=sum_recv.at[which, k], device_id={"bn": peer}, device_id_type=MESH,
            )
            for k, peer in enumerate(group)
        ]

    def exchange(which, width, beside=None, start=0, target=None):
        wide, copies = sum_copies(which)
        pieces = [(j, slice(start + j * 128, start + (j + 1) * 128)) for j in range(width // 128)]
        kept = which if target is None else target
        for j, piece in pieces:
            packed_ref[which, j : j + 1, 0:128] = local_ref[kept, 0:1, piece]
            packed_ref[which, j : j + 1, 128:256] = local_ref[kept, 1:2, piece]
        if which == SPLIT:
            packed_ref[which, 0:1, 256:384] = local_ref[which, 2:3, 0:128]
        for copy in copies:
            copy.start()
        shared_ref[which, bn, :, wide] = packed_ref[which, :, wide]
        if beside is not None:
            beside()
        for copy in copies:
            copy.wait()
        value = shared_ref[which, 0, :, wide]
        for k in range(1, members):
            value = value + shared_ref[which, k, :, wide]
        for j, piece in pieces:
            total_ref[kept, 0:1, piece] = value[j : j + 1, 0:128]
            total_ref[kept, 1:2, piece] = value[j : j + 1, 128:256]
        if which == SPLIT:
            total_ref[which, 2:3, 0:128] = value[0:1, 256:384]

    def stats(which):
        return total_ref.at[which]

    def affine(which, gain_ref, shift_ref, columns):
        mean, inverse = moments(stats(which), total_ref[SPLIT, 2:3, 0:1], columns)
        return mean, gain_ref[0:1, columns] * inverse, shift_ref[0:1, columns]

    def activate(z_ref, r, mean, scale, shift):
        return mish((z_ref[r, :] - mean) * scale + shift) * mask_ref[r, 0:1]

    feature_load(0).start()
    for k in (0, 1):
        weights[k].start()
    feature_load(1).start()
    barrier = pltpu.get_barrier_semaphore()
    for peer in group:
        pl.semaphore_signal(barrier, inc=1, device_id={"bn": peer}, device_id_type=MESH)
    local_ref[...] = jnp.zeros_like(local_ref)
    packed_ref[...] = jnp.zeros_like(packed_ref)
    total_ref[...] = jnp.zeros_like(total_ref)
    limits = [jnp.where(k < counts_ref[0], sides_ref[k], 0).astype(F32) for k in range(slots)]

    def mask_rows(r, _):
        index = (r.start + lax.broadcasted_iota(jnp.int32, (CHUNK, 128), 0)).astype(F32)
        place = jnp.floor((index + 0.5) * (1.0 / slots))
        slot = index - place * slots
        y = jnp.floor((place + 0.5) * (1.0 / side))
        x = place - y * side
        limit = jnp.zeros_like(index)
        for k in range(slots):
            limit = jnp.where(slot == k, limits[k], limit)
        mask_ref[r, :] = jnp.where(jnp.maximum(x, y) < limit, 1.0, 0.0)

    over_rows(count, mask_rows)
    for k in range(TILES):
        feature_load(k).wait()
        compact(feature_ref.at[k % 2], wide_ref)
        if k + 2 < TILES:
            feature_load(k + 2).start()
        here = pl.ds(k * pitch, pitch)

        def body(r, _, k=k):
            q = pl.ds(pl.multiple_of(r.start + k * pitch, CHUNK), CHUNK)
            for h, columns in enumerate((low, high)):
                q0[h, q, :] = jnp.where(mask_ref[q, 0:1] > 0.0, wide_ref[r, columns], 0.0).astype(BF16)

        over_rows(pitch, body)
    for k in (2, 3, 4):
        weights[k].start()
    cot_load(0).start()
    write("x", q0, x_out)
    weights[0].wait()
    p1[0:count, :] = dot(q0[0], w_split[low, high]) + dot(q0[1], w_split[high, high])
    write("zm", p1.at[0:count], zm_out)

    def add_squares(which, z_ref, columns, masked=False):
        def body(r, carry):
            value = z_ref[r, :]
            kept = value * mask_ref[r, 0:1] if masked else value
            return (carry[0] + fold(kept), carry[1] + fold(kept * value))

        zero = jnp.zeros((8, half), F32)
        add_sums(local_ref.at[which], columns, over_rows(count, body, (zero, zero)))

    add_squares(SPLIT, p1, high)
    local_ref[SPLIT, 2:3, 0:128] = jnp.sum(mask_ref[...], axis=0, keepdims=True)
    pl.semaphore_wait(barrier, members - 1)

    def split_low():
        p0[...] = dot(q0[0], w_split[low, low]) + dot(q0[1], w_split[high, low])
        write("zp", p0, zp_out)
        add_squares(SPLIT, p0, low)

    exchange(SPLIT, half, split_low, half)

    def inner():
        mean, scale, shift = affine(SPLIT, g_split, b_split, high)

        def main_rows(r, _):
            act = activate(p1, r, mean, scale, shift)
            p2[r, :] = act
            split_store(q2, (r,), act)

        over_rows(count, main_rows)
        write("main", q2, main_out)
        weights[1].wait()
        p3[...] = product2(q2, (), w_inner[...])
        write("zi", p3, zi_out)
        add_squares(INNER, p3, low)

    exchange(SPLIT_LOW, half, inner, 0, SPLIT)
    mean_p, scale_p, shift_p = affine(SPLIT, g_split, b_split, low)

    def part_rows(r, _):
        split_store(q1, (r,), activate(p0, r, mean_p, scale_p, shift_p))

    exchange(INNER, half, lambda: over_rows(count, part_rows))
    write("part", q1, part_out)

    written("zm")
    written("x")
    mean_i, scale_i, shift_i = affine(INNER, g_inner, b_inner, low)
    p1[0:GUARD, :] = jnp.zeros((GUARD, half), F32)
    p1[GUARD + count :, :] = jnp.zeros((GUARD, half), F32)

    def inner_rows(r, _):
        act = activate(p3, r, mean_i, scale_i, shift_i)
        p1[pl.ds(r.start + GUARD, CHUNK), :] = act
        split_store(q0, (r,), act)

    over_rows(count, inner_rows)
    write("inner", q0, inner_out)
    weights[2].wait()
    written("zi")
    written("main")
    for tap, (move, dx) in enumerate(taps(side, slots)):
        if move:
            pair_ref = (q2, q3)[tap % 2]
            moved = p1[GUARD + move : GUARD + move + count, :]
            if dx:
                moved = moved * edge_ref[:, dx + 1 : dx + 2]
            split_store(pair_ref, (slice(None),), moved)
        else:
            pair_ref = q0
        part = product2(pair_ref, (), w_spread[tap])
        if tap == 0:
            p3[...] = part
        else:
            p3[...] += part
    write("zs", p3, zs_out)
    add_squares(SPREAD, p3, low, True)
    exchange(SPREAD, half)

    mean_s, scale_s, shift_s = affine(SPREAD, g_spread, b_spread, low)

    def joined_rows(r, _):
        split_store(q2, (r,), activate(p3, r, mean_s, scale_s, shift_s) + p2[r, :])

    over_rows(count, joined_rows)
    write("joined", q2, joined_out)
    weights[3].wait()
    p2[...] = product2(q2, (), w_trans[...])
    write("zt", p2, zt_out)
    add_squares(TRANS, p2, low)
    exchange(TRANS, half)

    mean_t, scale_t, shift_t = affine(TRANS, g_trans, b_trans, low)

    def trans_rows(r, _):
        split_store(q3, (r,), activate(p2, r, mean_t, scale_t, shift_t))

    over_rows(count, trans_rows)
    write("trans", q3, trans_out)
    weights[4].wait()
    for page, columns in ((p4, low), (p5, high)):
        page[...] = product2(q3, (), w_out[low, columns]) + product2(q1, (), w_out[high, columns])
        add_squares(OUT, page, columns)
    exchange(OUT, 2 * half)

    total = total_ref[SPLIT, 2:3, 0:1]
    for k in range(TILES):
        cot_load(k).wait()
        compact(cot_ref, wide_ref)
        if k + 1 < TILES:
            cot_load(k + 1).start()
        for page, slope_page, columns in ((p4, p6, low), (p5, p7, high)):
            mean_o, inverse_o = moments(stats(OUT), total, columns)
            gain, shift_o = g_out[0:1, columns], b_out[0:1, columns]

            def body(r, carry, k=k, page=page, slope_page=slope_page, columns=columns):
                q = pl.ds(pl.multiple_of(r.start + k * pitch, CHUNK), CHUNK)
                mask = mask_ref[q, 0:1]
                scaled = (page[q, :] - mean_o) * inverse_o
                y = scaled * gain + shift_o
                t = jnp.exp(jnp.minimum(y, 30.0))
                n = t * (t + 2.0)
                inv = 1.0 / (n + 2.0)
                ratio = n * inv
                slope = ratio + y * (((4.0 * t) * (t + 1.0) * inv) * inv)
                dy = jnp.where(mask > 0.0, wide_ref[r, columns], 0.0) * slope
                wide_ref[r, columns] = y * ratio * mask
                slope_page[q, :] = dy
                return (carry[0] + fold(dy), carry[1] + fold(dy * scaled))

            zero = jnp.zeros((8, half), F32)
            add_sums(local_ref.at[BACK_OUT], columns, over_rows(pitch, body, (zero, zero)))
        if k:
            result_store(k - 1).wait()
        spread_out(wide_ref, staged_ref)
        result_store(k).start()
    exchange(BACK_OUT, 2 * half)

    def settled(page, z_page, pair_ref, which, back, gain_ref, columns, back_columns):
        mean_k, inverse_k = moments(stats(which), total, columns)
        factor = gain_ref[0:1, columns] * inverse_k
        first, second = total_ref[back, 0:1, back_columns] / total, total_ref[back, 1:2, back_columns] / total

        def body(r, _):
            split_store(pair_ref, (r,), settle(page[r, :], z_page[r, :], mask_ref[r, 0:1], mean_k, inverse_k, factor, first, second))

        over_rows(count, body)

    written("inner")
    written("joined")
    settled(p6, p4, q0, OUT, BACK_OUT, g_out, low, low)
    settled(p7, p5, q2, OUT, BACK_OUT, g_out, high, high)
    write("dlow", q0, dlow_out)
    write("dhigh", q2, dhigh_out)
    result_store(TILES - 1).wait()
    for name in list(pending):
        written(name)


def front_call(arrays, constants, scalars, slots, side, count, members):
    hbm, vmem_spec = pl.BlockSpec(memory_space=pl.ANY), pl.BlockSpec(memory_space=pltpu.VMEM)
    vmem, dma = pltpu.VMEM, pltpu.SemaphoreType.DMA
    full = arrays[0].shape[2]
    half = full // 2
    pitch = count // TILES
    pair, page = sds((2, count, half), BF16), sds((count, half))
    outs = [pair, page, page, pair, pair, page, pair, page, pair, page, pair, sds(arrays[1].shape), pair, pair]
    scratch = [vmem((count, half), F32), vmem((count + 2 * GUARD, half), F32)] + [vmem((count, half), F32)] * 6
    scratch += [vmem((2, count, half), BF16)] * 4
    scratch += [
        vmem((pitch, full), F32), vmem((2, pitch // slots, slots, full), BF16), vmem((pitch // slots, slots, full), F32), vmem((pitch // slots, slots, full), F32),
        vmem((full, full), BF16), vmem((half, half), BF16), vmem((9, half, half), BF16), vmem((half, half), BF16), vmem((full, full), BF16),
        vmem((6, 8, full), F32), vmem((7, 8, 384), F32), vmem((7, members, 8, 384), F32),
        dma((5,)), dma((2,)), dma(()), dma(()), dma((16,)), dma((7, members - 1)), dma((7, members - 1)),
    ]
    return pl.pallas_call(
        functools.partial(front_body, side, slots),
        in_specs=[hbm] * len(arrays) + [vmem_spec] * len(constants) + [pl.BlockSpec(memory_space=pltpu.SMEM)] * 2,
        out_specs=[hbm] * len(outs) + [vmem_spec] * 2,
        out_shape=outs + [sds((6, 8, full)), sds((count, 128))],
        scratch_shapes=scratch,
        compiler_params=pltpu.CompilerParams(collective_id=1, has_side_effects=True, vmem_limit_bytes=60 * 1024 * 1024),
    )(*arrays, *constants, *scalars)


LAGS = (1, 2, 3, 4, 5, 6, 7, 8)
LAG = LAGS[-1]
KEPT = 6


def reduce_body(jobs, side, slots, *refs):
    lefts, rights, refs = refs[:6], refs[6:8], refs[8:]
    (zt_hbm, zp_hbm, zs_hbm, zi_hbm, zm_hbm, ws_hbm), refs = refs[:6], refs[6:]
    (totals_ref, g_split, b_split, g_inner, b_inner, g_spread, b_spread, g_trans, b_trans, mask_ref, edge_ref, wi_ref, wt_ref, wo_ref), refs = refs[:14], refs[14:]
    outs, dpart_out, dmain_out, vectors_ref, refs = refs[:5], refs[5], refs[6], refs[7], refs[8:]
    (x_ref, z_ref, turned_ref, own_ref, r0_ref, half_ref, r1_ref, quarter_ref, r2_ref, eighth_ref, r3_ref, gathered_ref, full_ref, load_sem, store_sem) = refs[:15]
    (padded_ref, grad_ref, page_ref, joined_ref, zm_ref, pair_ref, part_ref, wide_ref, tap_ref, sums_ref, shared_ref, small_ref, spread_ref) = refs[15:28]
    (page_sem, tap_sem, write_sem, sum_send, sum_recv, small_send, small_recv) = refs[28:35]
    sems = refs[35:]
    count, half = grad_ref.shape
    pitch = wide_ref.shape[0]
    tiles = count // pitch
    s_split, q_out = totals_ref.at[SPLIT], totals_ref.at[BACK_OUT]
    s_spread, s_trans, s_inner = (totals_ref.at[k, :, 0:half] for k in (SPREAD, TRANS, INNER))
    stats_total = s_split[2:3, 0:1]
    block = own_ref.shape[1]
    mid = block // 2
    dp, bn = lax.axis_index("dp"), lax.axis_index("bn")
    z, x, y, core = dp // 2, dp % 2, bn // 2, bn % 2

    def at(new_z, new_x, new_y, new_core):
        return {"dp": new_z * 2 + new_x, "bn": new_y * 2 + new_core}

    to_core, to_x, to_y = at(z, x, y, 1 - core), at(z, 1 - x, y, core), at(z, x, 1 - y, core)
    depth = [(z + k) % 4 for k in (1, 2, 3)]
    to_z = [at(new_z, x, y, core) for new_z in depth]
    to_far = [at(new_z, 1 - x, y, core) for new_z in depth]
    to_diagonal = at(z, x, 1 - y, 1 - core)
    columns = (pl.ds(0, mid), pl.ds(mid, mid))

    def part(start, size):
        return pl.ds(pl.multiple_of(start, size), size)

    def far(stage, k, turn, source, target, peer):
        send, recv = sems[2 * stage], sems[2 * stage + 1]
        return pltpu.make_async_remote_copy(
            src_ref=source, dst_ref=target, send_sem=send.at[k, turn], recv_sem=recv.at[k, turn], device_id=peer, device_id_type=MESH
        )

    first = (x, y)
    second = (y, x)
    sides = (to_x, to_y)

    def copies(stage, c):
        slot, turn, keep = c % 2, c % 4, c % KEPT
        base = core * (block // 2)
        if stage == 0:
            return [far(0, 0, turn, own_ref.at[slot, part((1 - core) * (block // 2), block // 2)], r0_ref.at[slot], to_core)]
        if stage == 1:
            return [
                far(1, k, turn, half_ref.at[slot, part((1 - first[k]) * (block // 4), block // 4), columns[k]], r1_ref.at[turn, :, columns[k]], sides[k])
                for k in (0, 1)
            ]
        if stage == 2:
            return [
                far(2, k, turn, quarter_ref.at[slot, part((1 - second[k]) * (block // 8), block // 8), columns[k]], r2_ref.at[turn, :, columns[k]], sides[1 - k])
                for k in (0, 1)
            ]
        if stage == 3:
            return [
                far(3, k, turn, eighth_ref.at[slot, part(depth[k] * (block // 32), block // 32)], r3_ref.at[slot, k], to_z[k]) for k in (0, 1, 2)
            ]
        if stage == 4:
            spot = gathered_ref.at[slot, part(z * (block // 32), block // 32)]
            return [far(4, k, turn, spot, spot, to_z[k]) for k in (0, 1, 2)]
        made = []
        for k in (0, 1):
            eighth = base + first[k] * (block // 4) + second[k] * (block // 8)
            if stage == 5:
                spot = full_ref.at[keep, part(eighth, block // 8), columns[k]]
                made.append(far(5, k, turn, spot, spot, sides[1 - k]))
            elif stage == 6:
                spot = full_ref.at[keep, part(base + first[k] * (block // 4), block // 4), columns[k]]
                made.append(far(6, k, turn, spot, spot, sides[k]))
        if stage == 7:
            spot = full_ref.at[keep, part(base, block // 2)]
            made.append(far(7, 0, turn, spot, spot, to_core))
        return made

    def begin(stage, c):
        for copy in copies(stage, c):
            copy.start()

    def finish(stage, c):
        for copy in copies(stage, c):
            copy.wait()

    def load(j):
        if jobs[j] is None:
            return []
        (left, begin_part, parts), right, _ = jobs[j]
        slot = j % 2
        made = []
        if j < 2 or jobs[j - 2] is None or jobs[j - 2][0] != jobs[j][0]:
            made.append(pltpu.make_async_copy(lefts[left].at[begin_part : begin_part + parts], x_ref.at[slot, 0:parts], load_sem.at[slot, 0]))
        source = {"pair": pair_ref, "part": part_ref, 0: rights[0], 1: rights[1]}.get(right)
        if source is not None:
            made.append(pltpu.make_async_copy(source, z_ref.at[slot], load_sem.at[slot, 1]))
        return made

    def store(j):
        out, spot = jobs[j][2]
        return pltpu.make_async_copy(full_ref.at[j % KEPT], outs[out].at[spot], store_sem.at[j % KEPT])


    everything = slice(None)

    def page(source, target, k):
        return pltpu.make_async_copy(source, target, page_sem.at[k])

    def tap_load(tap):
        return pltpu.make_async_copy(ws_hbm.at[tap], tap_ref.at[tap % 2], tap_sem.at[tap % 2])

    upper = slice(half, 2 * half)
    load_zt, load_zp, load_zs = page(zt_hbm, page_ref, 0), page(zp_hbm, joined_ref, 1), page(zs_hbm, page_ref, 0)
    load_zi, load_zm = page(zi_hbm, page_ref, 0), page(zm_hbm, zm_ref, 2)
    write_part = pltpu.make_async_copy(part_ref, dpart_out, write_sem.at[0])
    write_main = pltpu.make_async_copy(z_ref.at[1], dmain_out, write_sem.at[1])

    group = [at(z, x, y, 1 - core), at(z, x, 1 - y, core), to_diagonal]

    def sum_copies(which):
        return [
            pltpu.make_async_remote_copy(
                src_ref=sums_ref.at[which], dst_ref=shared_ref.at[which, bn], send_sem=sum_send.at[which, k], recv_sem=sum_recv.at[which, k], device_id=peer, device_id_type=MESH
            )
            for k, peer in enumerate(group)
        ]

    def sum_start(which):
        for copy in sum_copies(which):
            copy.start()
        shared_ref[which, bn] = sums_ref[which]

    def sum_finish(which):
        for copy in sum_copies(which):
            copy.wait()
        value = shared_ref[which, 0]
        for k in range(1, shared_ref.shape[1]):
            value = value + shared_ref[which, k]
        sums_ref[which] = value

    everyone = [to_x] + to_z + to_far

    def small_copies():
        return [
            pltpu.make_async_remote_copy(
                src_ref=small_ref, dst_ref=spread_ref.at[dp], send_sem=small_send.at[k], recv_sem=small_recv.at[k], device_id=peer, device_id_type=MESH
            )
            for k, peer in enumerate(everyone)
        ]

    def settled(dy_ref, z_page, which, back, gain_ref, columns, keep):
        mean, inverse = moments(which, stats_total, columns)
        factor = gain_ref[0:1, columns] * inverse
        first_sum, second_sum = sums_ref[back, 0:1, :] / stats_total, sums_ref[back, 1:2, :] / stats_total

        def body(r, _):
            keep(r, settle(dy_ref[r, :], z_page[r, :], mask_ref[r, 0:1], mean, inverse, factor, first_sum, second_sum))

        over_rows(count, body)

    def sloped(grad, target_ref, z_page, which, back, gain_ref, shift_ref, columns):
        mean, inverse = moments(which, stats_total, columns)
        gain, shift = gain_ref[0:1, columns], shift_ref[0:1, columns]

        def body(r, carry):
            dy, sums = norm_slope(z_page, grad[r, :], mask_ref, r, everything, mean, inverse, gain, shift)
            target_ref[r, :] = dy
            return (carry[0] + sums[0], carry[1] + sums[1])

        zero = jnp.zeros((8, half), F32)
        add_sums(sums_ref.at[back], everything, over_rows(count, body, (zero, zero)))
        sum_start(back)

    own, lower = everything, slice(0, half)

    def stacked(step):
        columns_k = slice(step * half, (step + 1) * half)
        for target_ref, rows_k in ((grad_ref, lower), (zm_ref, upper)):
            value = product2_t(z_ref.at[step % 2], (), wo_ref[rows_k, columns_k])
            if step == 0:
                target_ref[...] = value
            else:
                target_ref[...] += value

    def middle_slopes():
        load_zt.wait()
        load_zp.wait()
        sloped(grad_ref, grad_ref, page_ref, s_trans, 2, g_trans, b_trans, own)
        sloped(zm_ref, zm_ref, joined_ref, s_split, 3, g_split, b_split, lower)

    def middle():
        sum_finish(2)
        sum_finish(3)
        settled(grad_ref, page_ref, s_trans, 2, g_trans, own, lambda r, dz: split_store(pair_ref, (r,), dz))
        load_zs.start()
        settled(zm_ref, joined_ref, s_split, 3, g_split, lower, lambda r, dz: split_store(part_ref, (r,), dz))
        load_zm.start()
        write_part.start()
        joined_ref[...] = product2_t(pair_ref, (), wt_ref[...])
        load_zs.wait()
        sloped(joined_ref, grad_ref, page_ref, s_spread, 4, g_spread, b_spread, own)

    def prepare():
        sum_finish(4)
        padded_ref[0:GUARD, :] = jnp.zeros((GUARD, half), F32)
        padded_ref[GUARD + count :, :] = jnp.zeros((GUARD, half), F32)

        def keep(r, dz):
            padded_ref[pl.ds(r.start + GUARD, CHUNK), :] = dz

        settled(grad_ref, page_ref, s_spread, 4, g_spread, own, keep)
        load_zi.start()
        grad_ref[...] = jnp.zeros_like(grad_ref)

    def tap_work(tap):
        move, dx = taps(side, slots)[tap]
        slot = tap % 2
        moved = padded_ref[GUARD - move : GUARD - move + count, :]
        if dx:
            moved = moved * edge_ref[:, 1 - dx : 2 - dx]
        high = moved.astype(BF16)
        z_ref[slot, 0] = high
        z_ref[slot, 1] = (moved - high.astype(F32)).astype(BF16)
        tap_load(tap).wait()
        if tap < 8:
            tap_load(tap + 1).start()

    def tap_gradient(slot):
        grad_ref[...] += dot_t(z_ref[slot, 0], tap_ref[slot]) + dot_t(z_ref[slot, 1], tap_ref[slot])

    def inner_slope():
        load_zi.wait()
        sloped(grad_ref, grad_ref, page_ref, s_inner, 0, g_inner, b_inner, own)

    def shifted(k):
        return lambda r: pl.ds(pl.multiple_of(r.start + k * pitch, CHUNK), CHUNK)

    def inner_tile(k):
        mean, inverse = moments(s_inner, stats_total, everything)
        factor = g_inner[...] * inverse
        first_sum, second_sum = sums_ref[0, 0:1, :] / stats_total, sums_ref[0, 1:2, :] / stats_total
        here = shifted(k)

        def body(r, _):
            q = here(r)
            dz = settle(grad_ref[q, :], page_ref[q, :], mask_ref[q, 0:1], mean, inverse, factor, first_sum, second_sum)
            split_store(pair_ref, (q,), dz)

        over_rows(pitch, body)
        rows_k = slice(k * pitch, (k + 1) * pitch)
        wide_ref[...] = product2_t(pair_ref, (rows_k,), wi_ref[...])
        mean, inverse = moments(s_split, stats_total, upper)
        gain, shift = g_split[0:1, upper], b_split[0:1, upper]

        def tail(r, carry):
            q = here(r)
            dy, sums = norm_slope(zm_ref, wide_ref[r, :] + joined_ref[q, :], mask_ref, q, everything, mean, inverse, gain, shift)
            grad_ref[q, :] = dy
            return (carry[0] + sums[0], carry[1] + sums[1])

        zero = jnp.zeros((8, half), F32)
        add_sums(sums_ref.at[1], everything, over_rows(pitch, tail, (zero, zero)))

    def small_start():
        pieces = [
            (sums_ref.at[3], everything), (sums_ref.at[1], everything), (sums_ref.at[0], everything), (sums_ref.at[4], everything),
            (sums_ref.at[2], everything), (q_out, slice(0, half)), (q_out, slice(half, 2 * half)),
        ]
        small_ref[...] = jnp.zeros_like(small_ref)
        for k, (ref, columns_k) in enumerate(pieces):
            small_ref[k : k + 1, :] = ref[0:1, columns_k]
            small_ref[8 + k : 9 + k, :] = ref[1:2, columns_k]
        for copy in small_copies():
            copy.start()
        spread_ref[dp] = small_ref[...]

    def small_finish():
        for copy in small_copies():
            copy.wait()
        value = spread_ref[0]
        for k in range(1, spread_ref.shape[0]):
            value = value + spread_ref[k]
        vectors_ref[...] = value

    def main_settle():
        def keep(r, dz):
            high = dz.astype(BF16)
            rest = (dz - high.astype(F32)).astype(BF16)
            for slot in (0, 1):
                z_ref[slot, 0, r, :] = high
                z_ref[slot, 1, r, :] = rest

        settled(grad_ref, zm_ref, s_split, 1, g_split, upper, keep)
        write_main.start()

    FIRST_TAP = 4
    hosted = {
        0: [functools.partial(stacked, 0)],
        1: [functools.partial(stacked, 1), middle_slopes],
        2: [middle],
        3: [prepare],
        13: [inner_slope],
        14: [load_zm.wait, lambda: sum_finish(0), functools.partial(inner_tile, 0), functools.partial(inner_tile, 1)],
        15: [functools.partial(inner_tile, 2), functools.partial(inner_tile, 3), lambda: sum_start(1)],
        16: [lambda: sum_finish(1), small_start],
        17: [main_settle],
        18: [small_finish, write_part.wait, write_main.wait],
    }

    sums_ref[...] = jnp.zeros_like(sums_ref)
    load_zt.start()
    load_zp.start()
    tap_load(0).start()
    for copy in load(0):
        copy.start()
    barrier = pltpu.get_barrier_semaphore()
    peers = [to_core, to_x, to_y] + to_z + to_far + [to_diagonal]
    for peer in peers:
        pl.semaphore_signal(barrier, inc=1, device_id=peer, device_id_type=MESH)
    pl.semaphore_wait(barrier, len(peers))
    total = len(jobs)
    taken = [j for j in range(total) if jobs[j] is not None]
    empty = [j for j in range(total) if jobs[j] is None]

    @pl.loop(0, total + LAG + 1)
    def _(t):
        for j in taken:

            @pl.when(t == j + LAG + 1)
            def _(j=j):
                store(j).wait()

        def stage(number, lag):
            def wrap(body):
                c = t - lag
                valid = jnp.logical_and(c >= 0, c < total)
                if empty:
                    valid = jnp.logical_and(valid, jnp.logical_or(c < empty[0], c > empty[-1]))
                pl.when(valid)(lambda: body(c))

            return wrap

        @stage(7, LAGS[7])
        def _(c):
            finish(7, c)

        for j in taken:

            @pl.when(t == j + LAG)
            def _(j=j):
                store(j).start()

        for number in (6, 5, 4):

            @stage(number, LAGS[number])
            def _(c, number=number):
                finish(number, c)
                if number == 4:
                    for k in (0, 1):
                        row = core * (block // 2) + first[k] * (block // 4) + second[k] * (block // 8)
                        full_ref[c % KEPT, part(row, block // 8), columns[k]] = gathered_ref[c % 2, :, columns[k]]
                begin(number + 1, c)

        for j in range(total):

            @pl.when(t == j)
            def _(j=j):
                for copy in load(j):
                    copy.wait()
                for task in hosted.get(j, ()):
                    task()
                if j + 1 < total:
                    for copy in load(j + 1):
                        copy.start()
                if 0 <= j - FIRST_TAP < 9:
                    tap_work(j - FIRST_TAP)

        @pl.when(jnp.logical_and(t >= FIRST_TAP, t < FIRST_TAP + 9))
        def _():
            tap_gradient(t % 2)

        @stage(3, LAGS[3])
        def _(c):
            finish(3, c)
            slot = c % 2
            value = eighth_ref[slot, part(z * (block // 32), block // 32), :]
            for k in (0, 1, 2):
                value = value + r3_ref[slot, k]
            gathered_ref[slot, part(z * (block // 32), block // 32), :] = value
            begin(4, c)

        @stage(2, LAGS[2])
        def _(c):
            finish(2, c)
            slot = c % 2
            for k in (0, 1):
                eighth_ref[slot, :, columns[k]] = quarter_ref[slot, part(second[k] * (block // 8), block // 8), columns[k]] + r2_ref[c % 4, :, columns[k]]
            begin(3, c)

        @stage(1, LAGS[1])
        def _(c):
            finish(1, c)
            slot = c % 2
            for k in (0, 1):
                quarter_ref[slot, :, columns[k]] = half_ref[slot, part(first[k] * (block // 4), block // 4), columns[k]] + r1_ref[c % 4, :, columns[k]]
            begin(2, c)

        @stage(0, LAGS[0])
        def _(c):
            finish(0, c)
            slot = c % 2
            half_ref[slot] = own_ref[slot, part(core * (block // 2), block // 2), :] + r0_ref[slot]
            begin(1, c)

        exact = functools.reduce(jnp.logical_or, [t == j for j in taken if jobs[j][0][2] == 1])

        @stage(None, 0)
        def _(c):
            slot = c % 2
            turned_ref[...] = x_ref[slot, 0].T
            own_ref[slot] = dot(turned_ref[...], z_ref[slot, 0]) + dot(turned_ref[...], z_ref[slot, 1])

            @pl.when(jnp.logical_not(exact))
            def _():
                turned_ref[...] = x_ref[slot, 1].T
                own_ref[slot] += dot(turned_ref[...], z_ref[slot, 0])

            begin(0, c)


def reduce_call(jobs, lefts, rights, hosted, constants, shapes, side, slots):
    hbm, vmem_spec = pl.BlockSpec(memory_space=pl.ANY), pl.BlockSpec(memory_space=pltpu.VMEM)
    vmem, dma = pltpu.VMEM, pltpu.SemaphoreType.DMA
    count, block = hosted[0].shape
    pitch = count // TILES
    scratch = [
        vmem((2, 2, count, block), BF16), vmem((2, 2, count, block), BF16), vmem((block, count), BF16),
        vmem((2, block, block), F32), vmem((2, block // 2, block), F32), vmem((2, block // 2, block), F32),
        vmem((4, block // 4, block), F32), vmem((2, block // 4, block), F32), vmem((4, block // 8, block), F32), vmem((2, block // 8, block), F32),
        vmem((2, 3, block // 32, block), F32), vmem((2, block // 8, block), F32), vmem((KEPT, block, block), F32),
        dma((2, 2)), dma((KEPT,)),
        vmem((count + 2 * GUARD, block), F32), vmem((count, block), F32), vmem((count, block), F32), vmem((count, block), F32),
        vmem((count, block), F32), vmem((2, count, block), BF16), vmem((2, count, block), BF16), vmem((pitch, block), F32),
        vmem((2, block, block), BF16), vmem((5, 8, block), F32), vmem((5, 4, 8, block), F32),
        vmem((16, block), F32), vmem((8, 16, block), F32),
        dma((3,)), dma((2,)), dma((2,)), dma((5, 3)), dma((5, 3)), dma((7,)), dma((7,)),
    ]
    for width in (1, 2, 2, 3, 3, 2, 2, 1):
        scratch += [dma((width, 4)), dma((width, 4))]
    return pl.pallas_call(
        functools.partial(reduce_body, jobs, side, slots),
        in_specs=[hbm] * (len(lefts) + len(rights) + len(hosted)) + [vmem_spec] * len(constants),
        out_specs=[hbm] * (len(shapes) + 2) + [vmem_spec],
        out_shape=[sds(shape) for shape in shapes] + [sds((2, count, block), BF16)] * 2 + [sds((16, block))],
        scratch_shapes=scratch,
        compiler_params=pltpu.CompilerParams(collective_id=3, has_side_effects=True, vmem_limit_bytes=60 * 1024 * 1024),
    )(*lefts, *rights, *hosted, *constants)


def gather_sums_body(axis, sums_ref, out_ref, slots_ref, send_sem, recv_sem):
    members = slots_ref.shape[0]
    me = lax.axis_index(axis)
    peers = [lax.rem(me + k, members) for k in range(1, members)]
    barrier = pltpu.get_barrier_semaphore()
    for peer in peers:
        pl.semaphore_signal(barrier, inc=1, device_id={axis: peer}, device_id_type=MESH)
    pl.semaphore_wait(barrier, members - 1)
    copies = [
        pltpu.make_async_remote_copy(
            src_ref=sums_ref, dst_ref=slots_ref.at[me], send_sem=send_sem.at[k], recv_sem=recv_sem.at[k], device_id={axis: peer}, device_id_type=MESH
        )
        for k, peer in enumerate(peers)
    ]
    for copy in copies:
        copy.start()
    slots_ref[me] = sums_ref[...]
    for copy in copies:
        copy.wait()
    value = slots_ref[0]
    for k in range(1, members):
        value = value + slots_ref[k]
    out_ref[...] = value


def gather_sums(sums, members, collective, axis="bn"):
    if members == 1:
        return sums
    spec = pl.BlockSpec(memory_space=pltpu.VMEM)
    return pl.pallas_call(
        functools.partial(gather_sums_body, axis),
        in_specs=[spec],
        out_specs=spec,
        out_shape=sds(sums.shape),
        scratch_shapes=[pltpu.VMEM((members,) + sums.shape, F32), pltpu.SemaphoreType.DMA((members - 1,)), pltpu.SemaphoreType.DMA((members - 1,))],
        compiler_params=pltpu.CompilerParams(collective_id=collective, has_side_effects=True),
    )(sums)


def local(
    shape,
    features, image_counts, map_sides,
    split_kernel, split_gain, split_shift, inner_kernel, inner_gain, inner_shift,
    spread_kernel, spread_gain, spread_shift, transition_kernel, transition_gain, transition_shift,
    output_kernel, output_gain, output_shift, cotangent,
):
    slots, side, _, full = features.shape
    half = inner_kernel.shape[0]
    pitch = round_up(-(-slots * side * side // TILES), 16)
    count = TILES * pitch
    grid = (TILES,)
    columns = np.arange(count)[:, None] // slots % side
    lanes = np.arange(128)[None, :]
    edges = jnp.asarray(np.where(lanes == 0, columns > 0, np.where(lanes == 2, columns < side - 1, True)).astype(np.float32))
    features = features.transpose(1, 2, 0, 3).reshape(side * side, slots, full)
    cotangent = cotangent.transpose(1, 2, 0, 3).reshape(side * side, slots, full)
    (split_gain, split_shift, inner_gain, inner_shift, spread_gain, spread_shift, transition_gain, transition_shift, output_gain, output_shift) = (
        item.reshape(1, -1)
        for item in (split_gain, split_shift, inner_gain, inner_shift, spread_gain, spread_shift, transition_gain, transition_shift, output_gain, output_shift)
    )
    spread_weight = spread_kernel.reshape(9, half, half)

    def group(sums):
        return gather_sums(sums, shape[1], 1 if sums.shape[1] == full else 2)

    sums_full, sums_half = out_whole((8, full)), out_whole((8, half))
    r_half, r_full, r_mask = rows(pitch, half), rows(pitch, full), rows(pitch, 128)
    pair_half, pair_full = rows2(pitch, half), rows2(pitch, full)

    def call(body, ins, outs, scratch=(), steps=grid):
        return pl.pallas_call(
            body,
            grid=steps,
            in_specs=[spec for _, spec in ins],
            out_specs=[spec for _, spec in outs],
            out_shape=[shape for shape, _ in outs],
            scratch_shapes=list(scratch),
            compiler_params=params(),
        )(*[array for array, _ in ins])

    def fixed(array):
        return (array, whole(array))

    if shape == (8, 4):
        low, high = slice(0, half), slice(half, full)
        every = slice(None)
        (x0, z_part, z_main, main2, part2, z_inner, inner2, z_spread, joined2, z_trans, trans2, result, dz_low, dz_high, totals, mask) = front_call(
            [features, cotangent, split_kernel, inner_kernel, spread_weight, transition_kernel, output_kernel],
            [split_gain, split_shift, inner_gain, inner_shift, spread_gain, spread_shift, transition_gain, transition_shift, output_gain, output_shift, edges],
            [image_counts, map_sides],
            slots, side, count, shape[1],
        )
        jobs = [((0, 0, 2), 0, (4, (low, low))), ((0, 0, 2), 1, (4, (low, high)))]
        jobs += [((1, 0, 2), 0, (4, (high, low))), ((1, 0, 2), 1, (4, (high, high)))]
        jobs += [((4, 0, 2), None, (2, (tap,))) for tap in range(9)]
        jobs += [((2, 0, 2), "pair", (3, (every, every)))]
        jobs += [((3, 0, 1), "part", (0, (low, low))), ((3, 1, 1), "part", (0, (high, low)))]
        jobs += [((5, 0, 2), "pair", (1, (every, every)))]
        jobs += [((3, 0, 1), None, (0, (low, high))), ((3, 1, 1), None, (0, (high, high)))]
        grad_split, grad_inner, grad_spread, grad_transition, grad_output, dz_part, dz_main, vectors = reduce_call(
            jobs,
            [trans2, part2, joined2, x0, inner2, main2],
            [dz_low, dz_high],
            [z_trans, z_part, z_spread, z_inner, z_main, spread_weight],
            [
                totals, split_gain, split_shift, inner_gain, inner_shift, spread_gain, spread_shift, transition_gain, transition_shift,
                mask, edges, inner_kernel, transition_kernel, output_kernel,
            ],
            [(full, full), (half, half), (9, half, half), (half, half), (full, full)],
            side, slots,
        )
        result, grad_split, grad_inner, grad_spread, grad_transition, grad_output, grad_features = final_call(
            [result, grad_split, grad_inner, grad_spread, grad_transition, grad_output], dz_part, dz_main, split_kernel, slots
        )
        small = vectors.reshape(2, 8 * half)
    else:
        row = jnp.arange(count)[:, None] + jnp.zeros((1, 128), jnp.int32)
        slot, place = row % slots, row // slots
        y, x = place // side, place % side
        sides = sum(jnp.where(slot == k, map_sides[k], 0) for k in range(slots))
        keep = (slot < image_counts[0]) & (y < sides) & (x < sides) & (place < side * side)
        mask = keep.astype(F32)
        x0, z_split, s_split = call(
            split_kernel_body,
            [(features, pixels(pitch, features.shape)), (mask, r_mask), fixed(split_kernel)],
            [(sds((count, full), BF16), r_full), (sds((count, full)), r_full), (sds((8, full)), sums_full)],
            [pltpu.VMEM((pitch, full), F32)],
        )
        s_split = group(s_split)
        part2, main, main2, z_inner, s_inner = call(
            inner_body,
            [(z_split, r_full), fixed(s_split), fixed(split_gain), fixed(split_shift), (mask, r_mask), fixed(inner_kernel)],
            [
                (sds((2, count, half), BF16), pair_half), (sds((count, half)), r_half), (sds((2, count, half), BF16), pair_half),
                (sds((count, half)), r_half), (sds((8, half)), sums_half),
            ],
        )
        s_inner = group(s_inner)
        tap_spec = pl.BlockSpec((1, half, half), lambda i: (i, 0, 0))
        inner2, z_spread, s_spread = call(
            functools.partial(spread_body, side, slots),
            [fixed(z_inner), fixed(s_split), fixed(s_inner), fixed(inner_gain), fixed(inner_shift), fixed(mask), fixed(edges), (spread_weight, tap_spec)],
            [(sds((2, count, half), BF16), out_whole((2, count, half))), (sds((count, half)), out_whole((count, half))), (sds((8, half)), sums_half)],
            [pltpu.VMEM((count + 2 * GUARD, half), F32), pltpu.VMEM((2, count, half), BF16)],
            (9,),
        )
        s_spread = group(s_spread)
        joined2, z_trans, s_trans = call(
            transition_body,
            [(z_spread, r_half), fixed(s_split), fixed(s_spread), fixed(spread_gain), fixed(spread_shift), (mask, r_mask), (main, r_half), fixed(transition_kernel)],
            [(sds((2, count, half), BF16), pair_half), (sds((count, half)), r_half), (sds((8, half)), sums_half)],
        )
        s_trans = group(s_trans)
        trans2, z_out, s_out = call(
            output_body,
            [(z_trans, r_half), fixed(s_split), fixed(s_trans), fixed(transition_gain), fixed(transition_shift), (mask, r_mask), (part2, pair_half), fixed(output_kernel)],
            [(sds((2, count, half), BF16), pair_half), (sds((count, full)), r_full), (sds((8, full)), sums_full)],
        )
        s_out = group(s_out)
        result, dy_out, q_out = call(
            result_body,
            [(z_out, r_full), fixed(s_split), fixed(s_out), fixed(output_gain), fixed(output_shift), (mask, r_mask), (cotangent, pixels(pitch, cotangent.shape))],
            [(sds(cotangent.shape), pixels(pitch, cotangent.shape)), (sds((count, full)), r_full), (sds((8, full)), sums_full)],
            [pltpu.VMEM((pitch, full), F32)],
        )
        q_out = group(q_out)
        dz_out, dy_trans, dy_part, q_mid = call(
            output_back_body,
            [
                (dy_out, r_full), (z_out, r_full), fixed(s_out), fixed(output_gain), fixed(q_out), fixed(s_split), (mask, r_mask), fixed(output_kernel),
                (z_trans, r_half), fixed(s_trans), fixed(transition_gain), fixed(transition_shift), (z_split, rows(pitch, half, 0)), fixed(split_gain), fixed(split_shift),
            ],
            [(sds((2, count, full), BF16), pair_full), (sds((count, half)), r_half), (sds((count, half)), r_half), (sds((8, full)), sums_full)],
            [pltpu.VMEM((pitch, full), F32)],
        )
        q_mid = group(q_mid)
        dz_trans, dz_part, grad_joined, dy_spread, q_spread = call(
            transition_back_body,
            [
                (dy_trans, r_half), (dy_part, r_half), (z_trans, r_half), fixed(s_trans), fixed(transition_gain), fixed(q_mid), fixed(s_split), (mask, r_mask), fixed(transition_kernel),
                (z_split, rows(pitch, half, 0)), fixed(split_gain), (z_spread, r_half), fixed(s_spread), fixed(spread_gain), fixed(spread_shift),
            ],
            [
                (sds((2, count, half), BF16), pair_half), (sds((2, count, half), BF16), pair_half), (sds((count, half)), r_half),
                (sds((count, half)), r_half), (sds((8, half)), sums_half),
            ],
        )
        q_spread = group(q_spread)
        moved_spec = pl.BlockSpec((1, 2, count, half), lambda i: (i, 0, 0, 0))
        moved, dy_inner, q_inner = call(
            functools.partial(spread_back_body, side, slots),
            [
                fixed(dy_spread), fixed(z_spread), fixed(s_spread), fixed(spread_gain), fixed(q_spread), fixed(s_split), fixed(mask), fixed(edges), (spread_weight, tap_spec),
                fixed(z_inner), fixed(s_inner), fixed(inner_gain), fixed(inner_shift),
            ],
            [(sds((9, 2, count, half), BF16), moved_spec), (sds((count, half)), out_whole((count, half))), (sds((8, half)), sums_half)],
            [pltpu.VMEM((count + 2 * GUARD, half), F32), pltpu.VMEM((count, half), F32)],
            (9,),
        )
        q_inner = group(q_inner)
        dz_inner, dy_main, q_main = call(
            inner_back_body,
            [
                (dy_inner, r_half), (z_inner, r_half), fixed(s_inner), fixed(inner_gain), fixed(q_inner), fixed(s_split), (mask, r_mask), fixed(inner_kernel),
                (grad_joined, r_half), (z_split, rows(pitch, half, 1)), fixed(split_gain), fixed(split_shift),
            ],
            [(sds((2, count, half), BF16), pair_half), (sds((count, half)), r_half), (sds((8, half)), sums_half)],
            [pltpu.VMEM((pitch, half), F32)],
        )
        q_main = group(q_main)
        dz_main, grad_features = call(
            split_back_body,
            [(dy_main, r_half), (z_split, rows(pitch, half, 1)), fixed(q_main), fixed(s_split), fixed(split_gain), (mask, r_mask), (dz_part, pair_half), fixed(split_kernel)],
            [(sds((2, count, half), BF16), pair_half), (sds(cotangent.shape), pixels(pitch, cotangent.shape))],
            [pltpu.VMEM((pitch, full), F32)],
        )
        small = jnp.concatenate([q_mid[0:2, half:], q_main[0:2], q_inner[0:2], q_spread[0:2], q_mid[0:2, :half], q_out[0:2]], axis=1)
        grad_output = jnp.concatenate([weight_grad(trans2, dz_out), weight_grad(part2, dz_out)], axis=0)
        grad_transition, grad_inner = weight_grad(joined2, dz_trans), weight_grad(main2, dz_inner)
        grad_split = jnp.concatenate([weight_grad(x0[None], dz_part), weight_grad(x0[None], dz_main)], axis=1)
        grad_spread = jnp.stack([weight_grad(inner2, moved[tap]) for tap in range(9)])
        grad_split, grad_inner, grad_spread, grad_transition, grad_output = lax.psum(
            (grad_split, grad_inner, grad_spread, grad_transition, grad_output), ("dp", "bn")
        )
        small = lax.psum(small, "dp")
    cuts = [0, full, full + half, full + 2 * half, full + 3 * half, 2 * full + 3 * half]
    shifts = [small[0, a:b] for a, b in zip(cuts[:-1], cuts[1:])]
    gains = [small[1, a:b] for a, b in zip(cuts[:-1], cuts[1:])]
    result, grad_features = (item.reshape(side, side, slots, full).transpose(2, 0, 1, 3) for item in (result, grad_features))
    return (
        result, grad_features,
        grad_split, gains[0], shifts[0], grad_inner, gains[1], shifts[1],
        grad_spread.reshape(3, 3, half, half), gains[2], shifts[2], grad_transition, gains[3], shifts[3], grad_output, gains[4], shifts[4],
    )


def solution(mesh):
    shard, copy = P(("dp", "bn")), P()
    return jax.shard_map(
        functools.partial(local, (mesh.shape["dp"], mesh.shape["bn"])),
        mesh=mesh,
        in_specs=(shard, shard, shard) + (copy,) * 15 + (shard,),
        out_specs=(shard, shard) + (copy,) * 15,
        check_vma=False,
    )
```
